32 devices in a mesh: seq: 8 (over z, y), head: 4 (over x, core).
Axes of the slice: x: 2, y: 2, z: 4, core: 2. Of those that a mesh axis runs over, the one named last changes fastest.
Arguments:
- tokens: bfloat16 [2048, 1024], P('seq'), may hold values from -6 to 6
- w_qkv: bfloat16 [1024, 3, 1024], P('seq', None, 'head'), may hold values from -0.1875 to 0.1875
- w_out: bfloat16 [1024, 1024], P('head', 'seq'), may hold values from -1 to 1
- ln1_gain: bfloat16 [1024], P('seq'), may hold values from 0.5 to 1.5
- ln1_bias: bfloat16 [1024], P('seq'), may hold values from -1.796875 to 1.796875
- ln2_gain: bfloat16 [1024], P('seq'), may hold values from 0.5 to 1.5
- ln2_bias: bfloat16 [1024], P('seq'), may hold values from -1.796875 to 1.796875
- w_up: bfloat16 [1024, 4096], P('seq', 'head'), may hold values from -0.1875 to 0.1875
- up_bias: bfloat16 [4096], P('head'), may hold values from -1.796875 to 1.796875
- w_down: bfloat16 [4096, 1024], P('head', 'seq'), may hold values from -0.09375 to 0.09375
- down_bias: bfloat16 [1024], P('seq'), may hold values from -1.796875 to 1.796875
- seq_units: int32 [4], replicated, may hold values from 1 to 4, 8 in all
- seq_pad: int32 [4], replicated, may hold values from 0 to 127
- rand_picks: int32 [32, 16, 3], P('seq', 'head'), may hold values from 0 to 65535
- cotangent: bfloat16 [2048, 1024], P('seq'), may hold values from -6 to 6
Outputs:
- output: bfloat16 [2048, 1024], P('seq')
- x_grad: float32 [2048, 1024], P('seq')
- w_qkv_grad: float32 [1024, 3, 1024], P('seq', None, 'head')
- w_out_grad: float32 [1024, 1024], P('head', 'seq')
- ln1_gain_grad: float32 [1024], P('seq')
- ln1_bias_grad: float32 [1024], P('seq')
- ln2_gain_grad: float32 [1024], P('seq')
- ln2_bias_grad: float32 [1024], P('seq')
- w_up_grad: float32 [1024, 4096], P('seq', 'head')
- up_bias_grad: float32 [4096], P('head')
- w_down_grad: float32 [4096, 1024], P('head', 'seq')
- down_bias_grad: float32 [1024], P('seq')
The draws below stay inside these ranges and needn't reach their ends.
Inputs may be any that keep to these rules, and one draw needn't show every extreme that they name: `seq_units`: each sequence covers whole units; the values add up to the number of units in the stream, and some sequence covers 4 units.
All inputs are finite; a program needn't handle non-finite values.
Results may differ from the reference program's by a relative error of at most 0.012.
Values may be sent and summed in bfloat16 or wider, within the bound.
A program may use at most 128 MiB of HBM per device.

```python
import math
import jax
import jax.numpy as jnp
import numpy as np
from jax import lax

D = 1024
HEADS = 16
HEAD_DIM = 64
FF = 4096
BLK = 64
RAND = 3
SPAN = 4
BLK_DEV = 4
NSEQ = 4
NBLK = 32
TOKENS = 2048
N_SEQ = 8


def place_ends(entries, own_key, least, high):
    place = [jax.random.randint(jax.random.fold_in(own_key, axis), (), 0, length) for axis, length in enumerate(entries.shape)]
    main_axis = entries.shape.index(max(entries.shape))
    next_to = place[:main_axis] + [(place[main_axis] + 1) % entries.shape[main_axis]] + place[main_axis + 1:]
    return entries.at[tuple(place)].set(least).at[tuple(next_to)].set(high)


def strengthened(array, own_key, source, target, shards_of, factor):
    owner, partner = [(jnp.arange(array.shape[dim]) // (array.shape[dim] // shards_of)).reshape([-1 if axis == dim else 1 for axis in range(array.ndim)]) for dim in (source, target)]
    chosen = jax.random.permutation(own_key, shards_of)[partner]
    strong = (owner == chosen) | (owner == (partner + shards_of // 2) % shards_of)
    return jnp.where(strong, factor * array, array)


def shard_levels(own_key, shape, cuts, low, largest):
    factor_of, own = 1.0, jax.random.fold_in(own_key, 6)
    for dim, parts in cuts:
        heights = jnp.exp(jax.random.uniform(jax.random.fold_in(own, dim), (parts,), jnp.float32, low / len(cuts), largest / len(cuts)))
        factor_of = factor_of * jnp.repeat(heights, shape[dim] // parts).reshape([-1 if axis == dim else 1 for axis in range(len(shape))])
    return factor_of


def length_profile(count, total, bound, skew):
    weights = [(1 << 20) // math.isqrt(standing ** skew) + 1 for standing in range(2, count + 1)]
    rest, counts = total - bound - (count - 1), [1] * (count - 1)
    while rest > 0:
        movable = [i for i in range(count - 1) if counts[i] < bound]
        whole, budget = sum([weights[i] for i in movable]), rest
        for i in movable:
            more = min(bound - counts[i], max(1, budget * weights[i] // whole), rest)
            counts[i] = counts[i] + more
            rest = rest - more
    return np.array([bound] + counts)


def uneven_parts(stream_key, count, total, bound, lean):
    if count == 2:
        one = jax.random.randint(stream_key, (), max(1, total - bound), min(bound, total - 1) + 1)
        return jnp.stack([one, total - one])
    tallies = jnp.asarray(length_profile(count, total, bound, lean), jnp.int32)
    couples = (count - 1) // 2
    donor, sink = tallies[1:1 + 2 * couples:2], tallies[2:2 + 2 * couples:2]
    room = jnp.minimum(donor - 1, bound - sink)
    passed = jax.random.randint(jax.random.fold_in(stream_key, 1), (couples,), 0, 1 << 20) % (room + 1)
    tallies = tallies.at[1:1 + 2 * couples:2].set(donor - passed).at[2:2 + 2 * couples:2].set(sink + passed)
    return tallies[jax.random.permutation(jax.random.fold_in(stream_key, 2), count)]


def bell_draw(key, dims, width, reach, cuts=(), kind=jnp.bfloat16):
    gain = shard_levels(key, dims, cuts, -0.22, 0.18) if cuts else 1.0
    values = jax.random.normal(key, dims, jnp.float32) * width * gain
    return jnp.minimum(jnp.maximum(values, -reach), reach).astype(kind)


def heavy_noise(stream_key, shape, width, most, shards, heavy, kind=jnp.bfloat16):
    values = width * jax.random.normal(stream_key, shape, jnp.float32)
    if shards:
        values = values * shard_levels(stream_key, shape, shards, -0.22, 0.18)
    return jnp.clip(strengthened(values, jax.random.fold_in(stream_key, 3), *heavy), -most, most).astype(kind)


def setup_inputs(seed: int = 0) -> dict:
    arg_keys = jax.random.split(jax.random.key(seed), 16)
    tokens = bell_draw(arg_keys[0], (TOKENS, D), 1.0, 6.0, ((0, 8),))
    w_qkv = bell_draw(arg_keys[1], (D, 3, D), D ** -0.5, 0.1875, ((0, 8), (2, 4)))
    w_out = bell_draw(arg_keys[2], (D, D), (D // 32) ** -0.5, 1.0, ((0, 4), (1, 8)))
    ln1_gain = jnp.clip(1.0 + 0.1 * jax.random.normal(arg_keys[3], (D,), jnp.float32), 0.5, 1.5).astype(jnp.bfloat16)
    ln1_bias = bell_draw(arg_keys[4], (D,), 0.3, 1.796875, ((0, 8),))
    ln2_gain = jnp.clip(1.0 + 0.1 * jax.random.normal(arg_keys[5], (D,), jnp.float32), 0.5, 1.5).astype(jnp.bfloat16)
    ln2_bias = bell_draw(arg_keys[6], (D,), 0.3, 1.796875, ((0, 8),))
    w_up = bell_draw(arg_keys[7], (D, FF), D ** -0.5, 0.1875, ((0, 8), (1, 4)))
    up_bias = bell_draw(arg_keys[8], (FF,), 0.3, 1.796875, ((0, 4),))
    w_down = bell_draw(arg_keys[9], (FF, D), FF ** -0.5, 0.09375, ((0, 4), (1, 8)))
    down_bias = bell_draw(arg_keys[10], (D,), 0.3, 1.796875, ((0, 8),))
    seq_units = uneven_parts(arg_keys[11], NSEQ, N_SEQ, SPAN, 2).astype(jnp.int32)
    seq_pad = place_ends(jax.random.randint(arg_keys[12], (NSEQ,), 0, BLK_DEV * BLK // 2), jax.random.fold_in(arg_keys[12], 1), 0, (BLK_DEV * BLK // 2) - 1).astype(jnp.int32)
    rand_picks = place_ends(jax.random.randint(arg_keys[13], (NBLK, HEADS, RAND), 0, 65536), jax.random.fold_in(arg_keys[13], 1), 0, 65535).astype(jnp.int32)
    cotangent = heavy_noise(arg_keys[14], (TOKENS, D), 1.0, 6.0, ((0, 8),), (0, 1, 8, 2.0))
    return dict(tokens=tokens, w_qkv=w_qkv, w_out=w_out, ln1_gain=ln1_gain, ln1_bias=ln1_bias, ln2_gain=ln2_gain, ln2_bias=ln2_bias, w_up=w_up, up_bias=up_bias, w_down=w_down, down_bias=down_bias, seq_units=seq_units, seq_pad=seq_pad, rand_picks=rand_picks, cotangent=cotangent)


EPSILON = 1e-05
NEGATIVE = -1e+30
HIGHEST = lax.Precision.HIGHEST

@jax.custom_vjp
def low(v):
    return lax.optimization_barrier(v.astype(jnp.bfloat16)).astype(jnp.float32)

@jax.custom_vjp
def low_back(v):
    return v

def low_keep(v):
    return (low(v), None)

def low_pass(kept, grad):
    return (grad,)

def back_keep(v):
    return (v, None)

def back_low(kept, grad):
    return (low(grad),)
low.defvjp(low_keep, low_pass)
low_back.defvjp(back_keep, back_low)

def layer_norm(features, norm_gain, norm_shift):
    average = lax.optimization_barrier(jnp.mean(features, axis=-1, keepdims=True))
    centred = features - average
    spread = lax.optimization_barrier(jnp.mean(centred * centred, axis=-1, keepdims=True))
    return centred * lax.rsqrt(spread + EPSILON) * norm_gain + norm_shift

def gelu_tanh(values):
    return jax.nn.gelu(values, approximate=True)

def both_ways(values):
    return low_back(low(values))

def softmax_low(logits, usable, over_axes):
    logits = low_back(logits)
    logits = jnp.where(usable, logits, NEGATIVE)
    row_max = lax.optimization_barrier(jnp.max(logits, axis=over_axes, keepdims=True))
    scaled = jnp.exp(logits - row_max)
    return low(scaled / lax.optimization_barrier(jnp.sum(scaled, axis=over_axes, keepdims=True)))

def unit_attention(key_rows, value_rows, inputs):
    unit_id, queries, picked_raw, position, span_dev, live_tokens = inputs
    tok_dev = BLK_DEV * BLK
    near_count = (2 * SPAN - 1) * BLK_DEV
    scaling = HEAD_DIM ** (-0.5)
    root = (unit_id * tok_dev).astype(jnp.int32)
    near_keys = lax.dynamic_slice_in_dim(key_rows, root, near_count * BLK, 0).reshape(near_count, BLK, HEADS, HEAD_DIM)
    near_values = lax.dynamic_slice_in_dim(value_rows, root, near_count * BLK, 0).reshape(near_count, BLK, HEADS, HEAD_DIM)
    offsets = jnp.arange(2 * SPAN - 1, dtype=jnp.int32) - (SPAN - 1)
    relative = (position + offsets).astype(jnp.int32)
    inside = (relative >= 0) & (relative < span_dev)
    places = relative[:, None] * tok_dev + jnp.arange(tok_dev, dtype=jnp.int32)[None, :]
    usable = (inside[:, None] & (places < live_tokens)).reshape(near_count, BLK)
    root_block = ((SPAN - 1 - position) * BLK_DEV).astype(jnp.int32)
    query_blocks = (position * BLK_DEV + jnp.arange(BLK_DEV, dtype=jnp.int32)).astype(jnp.int32)
    window = query_blocks[:, None] + jnp.arange(3, dtype=jnp.int32)[None, :] - 1 + root_block
    anchors = jnp.stack([root_block, root_block + span_dev * BLK_DEV - 1]).astype(jnp.int32)
    chosen = (picked_raw % (span_dev * BLK_DEV) + root_block).astype(jnp.int32)
    window = jnp.broadcast_to(window[:, None, :], (BLK_DEV, HEADS, 3))
    anchors = jnp.broadcast_to(anchors[None, None, :], (BLK_DEV, HEADS, 2))
    indices = jnp.concatenate([window, anchors, chosen], axis=-1).astype(jnp.int32)
    head_ids = jnp.arange(HEADS, dtype=jnp.int32)[None, :, None]
    key_heads = jnp.transpose(near_keys, (2, 0, 1, 3))
    value_heads = jnp.transpose(near_values, (2, 0, 1, 3))
    picked_keys = key_heads[head_ids, indices]
    picked_values = value_heads[head_ids, indices]
    grouped = queries.reshape(BLK_DEV, BLK, HEADS, HEAD_DIM)
    logits = jnp.einsum('bqhd,bhrkd->bhqrk', grouped, picked_keys, precision=HIGHEST) * scaling
    weights = softmax_low(logits, usable[indices][:, :, None], (3, 4))
    sparse = jnp.einsum('bhqrk,bhrkd->bqhd', weights, picked_values, precision=HIGHEST).reshape(tok_dev, HEADS, HEAD_DIM)
    seq_keys = lax.dynamic_slice_in_dim(near_keys, root_block, SPAN * BLK_DEV, 0)
    seq_values = lax.dynamic_slice_in_dim(near_values, root_block, SPAN * BLK_DEV, 0)
    seq_usable = lax.dynamic_slice_in_dim(usable, root_block, SPAN * BLK_DEV, 0)
    edge_queries = jnp.concatenate([queries[:BLK], queries[tok_dev - BLK:]], axis=0)
    lead_logits = jnp.einsum('qhd,nkhd->hqnk', edge_queries, seq_keys, precision=HIGHEST) * scaling
    lead_weights = softmax_low(lead_logits, seq_usable[None, None], (2, 3))
    lead_out = jnp.einsum('hqnk,nkhd->qhd', lead_weights, seq_values, precision=HIGHEST)
    first_rows = jnp.where(position == 0, lead_out[:BLK], sparse[:BLK])
    last_rows = jnp.where(position == span_dev - 1, lead_out[BLK:], sparse[tok_dev - BLK:])
    return jnp.concatenate([first_rows, sparse[BLK:tok_dev - BLK], last_rows], axis=0)

def reference(tokens, w_qkv, w_out, ln1_gain, ln1_bias, ln2_gain, ln2_bias, w_up, up_bias, w_down, down_bias, seq_units, seq_pad, rand_picks, cotangent):
    tok_dev = BLK_DEV * BLK
    seq_count = seq_units.shape[0]
    starts = (jnp.cumsum(seq_units) - seq_units).astype(jnp.int32)
    devices = jnp.arange(N_SEQ, dtype=jnp.int32)
    member = (lax.optimization_barrier(jnp.sum((starts[None, :] <= devices[:, None]).astype(jnp.int32), axis=1)) - 1).astype(jnp.int32)
    pick_one = (jnp.arange(seq_count, dtype=jnp.int32)[None, :] == member[:, None]).astype(jnp.int32)
    leaders = lax.optimization_barrier(jnp.sum(pick_one * starts[None, :], axis=1)).astype(jnp.int32)
    span_units = lax.optimization_barrier(jnp.sum(pick_one * seq_units[None, :], axis=1)).astype(jnp.int32)
    pad_tokens = lax.optimization_barrier(jnp.sum(pick_one * seq_pad[None, :], axis=1)).astype(jnp.int32)
    positions = (devices - leaders).astype(jnp.int32)
    live_tokens = (span_units * tok_dev - pad_tokens).astype(jnp.int32)
    margin = (SPAN - 1) * tok_dev
    unit_picks = rand_picks.reshape(N_SEQ, BLK_DEV, HEADS, RAND)
    checked_unit = jax.checkpoint(unit_attention)

    def forward(inputs, qkv_weight, out_weight, gain_one, shift_one, gain_two, shift_two, up_weight, up_shift, down_weight, down_shift):
        normed = low(layer_norm(inputs, gain_one, shift_one))
        triple = both_ways(jnp.einsum('td,dcf->tcf', normed, qkv_weight, precision=HIGHEST))
        queries = triple[:, 0].reshape(N_SEQ, tok_dev, HEADS, HEAD_DIM)
        key_rows = jnp.pad(triple[:, 1].reshape(TOKENS, HEADS, HEAD_DIM), ((margin, margin), (0, 0), (0, 0)))
        value_rows = jnp.pad(triple[:, 2].reshape(TOKENS, HEADS, HEAD_DIM), ((margin, margin), (0, 0), (0, 0)))
        attended = lax.map(lambda unit_inputs: checked_unit(key_rows, value_rows, unit_inputs), (devices, queries, unit_picks, positions, span_units, live_tokens))
        attended = both_ways(attended.reshape(TOKENS, D))
        middle = inputs + low_back(jnp.dot(attended, out_weight, precision=HIGHEST))

        def feed_forward(block_rows):
            normed_two = low(layer_norm(block_rows, gain_two, shift_two))
            pre_act = low_back(jnp.dot(normed_two, up_weight, precision=HIGHEST) + up_shift)
            hidden = low(gelu_tanh(pre_act))
            return low_back(jnp.dot(hidden, down_weight, precision=HIGHEST) + down_shift)
        branch = lax.map(jax.checkpoint(feed_forward), middle.reshape(N_SEQ, tok_dev, D)).reshape(TOKENS, D)
        return middle + branch
    result, pullback = jax.vjp(forward, tokens.astype(jnp.float32), w_qkv.astype(jnp.float32), w_out.astype(jnp.float32), ln1_gain.astype(jnp.float32), ln1_bias.astype(jnp.float32), ln2_gain.astype(jnp.float32), ln2_bias.astype(jnp.float32), w_up.astype(jnp.float32), up_bias.astype(jnp.float32), w_down.astype(jnp.float32), down_bias.astype(jnp.float32))
    gradients = pullback(cotangent.astype(jnp.float32))
    return (result.astype(jnp.bfloat16), gradients[0], gradients[1], gradients[2], gradients[3], gradients[4], gradients[5], gradients[6], gradients[7], gradients[8], gradients[9], gradients[10])
```

```python
import jax
import jax.numpy as jnp
from jax import lax
from jax.sharding import PartitionSpec as P

HEAD_DIM = 64
BLK = 64
SPAN = 4
BLK_DEV = 4
EPSILON = 1e-05
NEGATIVE = -1e30
F32 = jnp.float32
BF16 = jnp.bfloat16


def shifted(value, axis, steps):
    count = lax.axis_size(axis)
    first, last = max(0, -steps), min(count, count - steps)
    return lax.ppermute(value, axis, [(i, i + steps) for i in range(first, last)])


def norm_parts(features):
    average = jnp.mean(features, axis=-1, keepdims=True)
    centred = features - average
    spread = jnp.mean(centred * centred, axis=-1, keepdims=True)
    inverse = lax.rsqrt(spread + EPSILON)
    return centred * inverse, inverse


def norm_backward(xhat, inverse, scaled):
    first = jnp.mean(scaled, axis=-1, keepdims=True)
    second = jnp.mean(scaled * xhat, axis=-1, keepdims=True)
    return inverse * (scaled - first - xhat * second)


def dot(a, b, dims):
    return lax.dot_general(a, b, (dims, ((), ())), preferred_element_type=F32)


def sequence_place(seq_units, seq_pad):
    device = lax.axis_index("seq")
    start, leader, span, pad = 0, 0, 0, 0
    for k in range(seq_units.shape[0]):
        units = seq_units[k]
        inside = (device >= start) & (device < start + units)
        leader = jnp.where(inside, start, leader)
        span = jnp.where(inside, units, span)
        pad = jnp.where(inside, seq_pad[k], pad)
        start = start + units
    return device - leader, span, pad


def key_counts(position, span, picks):
    blocks = lax.broadcasted_iota(jnp.int32, (1, 1, SPAN * BLK_DEV), 2)
    query = position * BLK_DEV + lax.broadcasted_iota(jnp.int32, (BLK_DEV, 1, 1), 0)
    total = span * BLK_DEV
    count = jnp.zeros((BLK_DEV, picks.shape[1], SPAN * BLK_DEV), F32)
    for wanted in (query - 1, query, query + 1, 0, total - 1):
        count = count + (blocks == wanted).astype(F32)
    chosen = picks % total
    for r in range(picks.shape[2]):
        count = count + (blocks == chosen[:, :, r : r + 1]).astype(F32)
    return jnp.where((query == 0) | (query == total - 1), 1.0, count)


def local_general(
    tokens, w_qkv, w_out, ln1_gain, ln1_bias, ln2_gain, ln2_bias, w_up, up_bias, w_down, down_bias,
    seq_units, seq_pad, rand_picks, cotangent,
):
    tok, width = tokens.shape
    heads = w_qkv.shape[2] // HEAD_DIM
    rows = lambda v: lax.all_gather(v, "seq", axis=0, tiled=True)
    cols = lambda v: lax.all_gather(v, "seq", axis=1, tiled=True)
    vectors = jnp.stack([ln1_gain, ln1_bias, ln2_gain, ln2_bias, down_bias], axis=0)
    gain_one, shift_one, gain_two, shift_two, down_shift = [
        v[None].astype(F32) for v in cols(vectors)
    ]
    qkv = rows(w_qkv)
    out_w, up_w, down_w = cols(w_out), rows(w_up), cols(w_down)
    position, span, pad = sequence_place(seq_units, seq_pad)
    root = SPAN - 1 - position
    inputs = tokens.astype(F32)
    xhat_one, inv_one = norm_parts(inputs)
    normed = (xhat_one * gain_one + shift_one).astype(BF16)
    triple = jnp.einsum("td,dcf->tcf", normed, qkv, preferred_element_type=F32).astype(BF16)
    own = jnp.stack([triple[:, 1], triple[:, 2]], axis=0)
    pieces = [own if o == 0 else shifted(own, "seq", -o) for o in range(1 - SPAN, SPAN)]
    nearby = jnp.stack(pieces, axis=0)
    window = lax.dynamic_slice_in_dim(nearby, root, SPAN, 0)
    split = lambda v: v.reshape(v.shape[0], heads, HEAD_DIM)
    keys = split(window[:, 0].reshape(SPAN * tok, -1))
    values = split(window[:, 1].reshape(SPAN * tok, -1))
    queries = split(triple[:, 0])
    scaling = HEAD_DIM ** (-0.5)
    live = jnp.arange(SPAN * tok, dtype=jnp.int32) < span * tok - pad
    count = jnp.repeat(key_counts(position, span, rand_picks), BLK, axis=2)
    count = jnp.where(live[None, None], count, 0.0)
    count = jnp.transpose(jnp.repeat(count, BLK, axis=0), (1, 0, 2))
    logits = jnp.einsum("qhd,khd->hqk", queries, keys, preferred_element_type=F32) * scaling
    logits = jnp.where(count > 0, logits, NEGATIVE)
    grown = jnp.exp(logits - jnp.max(logits, axis=-1, keepdims=True)) * count
    chances = grown / jnp.sum(grown, axis=-1, keepdims=True)
    chances_low = chances.astype(BF16)
    attended = jnp.einsum("hqk,khd->qhd", chances_low, values, preferred_element_type=F32)
    attended = attended.astype(BF16).reshape(tok, heads * HEAD_DIM)
    middle = inputs + lax.psum(dot(attended, out_w, ((1,), (0,))), "head")
    xhat_two, inv_two = norm_parts(middle)
    normed_two = (xhat_two * gain_two + shift_two).astype(BF16)
    pre_act = dot(normed_two, up_w, ((1,), (0,))) + up_bias.astype(F32)[None]
    hidden, pull = jax.vjp(lambda v: jax.nn.gelu(v, approximate=True), pre_act)
    hidden = hidden.astype(BF16)
    ffn = lax.psum(dot(hidden, down_w, ((1,), (0,))).astype(BF16), "head").astype(F32)
    output = (middle + ffn + down_shift).astype(BF16)
    grad_out = cotangent.astype(F32)
    grad_w_down = dot(hidden, cotangent, ((0,), (0,)))
    grad_pre = pull(dot(cotangent, down_w, ((1,), (1,))))[0].astype(BF16)
    grad_w_up = dot(normed_two, grad_pre, ((0,), (0,)))
    grad_up_bias = lax.psum(jnp.sum(grad_pre.astype(F32), axis=0), "seq")
    grad_two = lax.psum(dot(grad_pre, up_w, ((1,), (1,))), "head")
    grad_middle = grad_out + norm_backward(xhat_two, inv_two, grad_two * gain_two)
    grad_branch = grad_middle.astype(BF16)
    grad_w_out = dot(attended, grad_branch, ((0,), (0,)))
    grad_att = split(dot(grad_branch, out_w, ((1,), (1,))).astype(BF16))
    grad_prob = jnp.einsum("qhd,khd->hqk", grad_att, values, preferred_element_type=F32)
    inner = jnp.sum(chances * grad_prob, axis=-1, keepdims=True)
    grad_logit = (chances * (grad_prob - inner)).astype(BF16)
    dq = scaling * jnp.einsum("hqk,khd->qhd", grad_logit, keys, preferred_element_type=F32)
    dk = scaling * jnp.einsum("hqk,qhd->khd", grad_logit, queries, preferred_element_type=F32)
    dv = jnp.einsum("hqk,qhd->khd", chances_low, grad_att, preferred_element_type=F32)
    part = jnp.stack([dk.reshape(SPAN, tok, -1), dv.reshape(SPAN, tok, -1)], axis=1)
    near = jnp.zeros((2 * SPAN - 1,) + part.shape[1:], F32)
    near = lax.dynamic_update_slice_in_dim(near, part, root, 0)
    owned = near[SPAN - 1]
    for offset in range(1 - SPAN, SPAN):
        if offset:
            owned = owned + shifted(near[offset + SPAN - 1], "seq", offset)
    owned = owned.astype(BF16)
    grad_triple = jnp.stack([dq.reshape(tok, -1).astype(BF16), owned[0], owned[1]], axis=1)
    grad_w_qkv = jnp.einsum("td,tcf->dcf", normed, grad_triple, preferred_element_type=F32)
    grad_one = lax.psum(
        jnp.einsum("tcf,dcf->td", grad_triple, qkv, preferred_element_type=F32), "head"
    )
    x_grad = grad_middle + norm_backward(xhat_one, inv_one, grad_one * gain_one)
    sums = jnp.stack(
        [
            jnp.sum(grad_one * xhat_one, axis=0), jnp.sum(grad_one, axis=0),
            jnp.sum(grad_two * xhat_two, axis=0), jnp.sum(grad_two, axis=0),
            jnp.sum(grad_out, axis=0),
        ],
        axis=0,
    )
    scatter = lambda v, d: lax.psum_scatter(v, "seq", scatter_dimension=d, tiled=True)
    sums = scatter(sums, 1)
    return (
        output, x_grad, scatter(grad_w_qkv, 0), scatter(grad_w_out, 1), sums[0], sums[1], sums[2],
        sums[3], scatter(grad_w_up, 0), grad_up_bias, scatter(grad_w_down, 1), sums[4],
    )


IN_SPECS = (
    P("seq", None), P("seq", None, "head"), P("head", "seq"), P("seq"), P("seq"), P("seq"),
    P("seq"), P("seq", "head"), P("head"), P("head", "seq"), P("seq"), P(), P(),
    P("seq", "head", None), P("seq", None),
)
OUT_SPECS = (
    P("seq", None), P("seq", None), P("seq", None, "head"), P("head", "seq"), P("seq"), P("seq"),
    P("seq"), P("seq"), P("seq", "head"), P("head"), P("head", "seq"), P("seq"),
)


def solution(mesh):
    return jax.shard_map(
        local_general, mesh=mesh, in_specs=IN_SPECS, out_specs=OUT_SPECS, check_vma=False
    )
```

```python
import jax
import jax.numpy as jnp
from jax import lax
from jax.experimental import pallas as pl
from jax.experimental.pallas import tpu as pltpu
from jax.sharding import PartitionSpec as P

HEAD_DIM = 64
BLK = 64
SPAN = 4
BLK_DEV = 4
EPSILON = 1e-05
NEGATIVE = -1e30
F32 = jnp.float32
BF16 = jnp.bfloat16


def shifted(value, axis, steps):
    count = lax.axis_size(axis)
    first, last = max(0, -steps), min(count, count - steps)
    return lax.ppermute(value, axis, [(i, i + steps) for i in range(first, last)])


def norm_parts(features):
    average = jnp.mean(features, axis=-1, keepdims=True)
    centred = features - average
    spread = jnp.mean(centred * centred, axis=-1, keepdims=True)
    inverse = lax.rsqrt(spread + EPSILON)
    return centred * inverse, inverse


def norm_backward(xhat, inverse, scaled):
    first = jnp.mean(scaled, axis=-1, keepdims=True)
    second = jnp.mean(scaled * xhat, axis=-1, keepdims=True)
    return inverse * (scaled - first - xhat * second)


def dot(a, b, dims):
    return lax.dot_general(a, b, (dims, ((), ())), preferred_element_type=F32)


def sequence_place(seq_units, seq_pad):
    device = lax.axis_index("seq")
    start, leader, span, pad = 0, 0, 0, 0
    for k in range(seq_units.shape[0]):
        units = seq_units[k]
        inside = (device >= start) & (device < start + units)
        leader = jnp.where(inside, start, leader)
        span = jnp.where(inside, units, span)
        pad = jnp.where(inside, seq_pad[k], pad)
        start = start + units
    return device - leader, span, pad


def key_counts(position, span, picks):
    blocks = lax.broadcasted_iota(jnp.int32, (1, 1, SPAN * BLK_DEV), 2)
    query = position * BLK_DEV + lax.broadcasted_iota(jnp.int32, (BLK_DEV, 1, 1), 0)
    total = span * BLK_DEV
    count = jnp.zeros((BLK_DEV, picks.shape[1], SPAN * BLK_DEV), F32)
    for wanted in (query - 1, query, query + 1, 0, total - 1):
        count = count + (blocks == wanted).astype(F32)
    chosen = picks % total
    for r in range(picks.shape[2]):
        count = count + (blocks == chosen[:, :, r : r + 1]).astype(F32)
    return jnp.where((query == 0) | (query == total - 1), 1.0, count)


def local_general(
    tokens, w_qkv, w_out, ln1_gain, ln1_bias, ln2_gain, ln2_bias, w_up, up_bias, w_down, down_bias,
    seq_units, seq_pad, rand_picks, cotangent,
):
    tok, width = tokens.shape
    heads = w_qkv.shape[2] // HEAD_DIM
    rows = lambda v: lax.all_gather(v, "seq", axis=0, tiled=True)
    cols = lambda v: lax.all_gather(v, "seq", axis=1, tiled=True)
    vectors = jnp.stack([ln1_gain, ln1_bias, ln2_gain, ln2_bias, down_bias], axis=0)
    gain_one, shift_one, gain_two, shift_two, down_shift = [
        v[None].astype(F32) for v in cols(vectors)
    ]
    qkv = rows(w_qkv)
    out_w, up_w, down_w = cols(w_out), rows(w_up), cols(w_down)
    position, span, pad = sequence_place(seq_units, seq_pad)
    root = SPAN - 1 - position
    inputs = tokens.astype(F32)
    xhat_one, inv_one = norm_parts(inputs)
    normed = (xhat_one * gain_one + shift_one).astype(BF16)
    triple = jnp.einsum("td,dcf->tcf", normed, qkv, preferred_element_type=F32).astype(BF16)
    own = jnp.stack([triple[:, 1], triple[:, 2]], axis=0)
    pieces = [own if o == 0 else shifted(own, "seq", -o) for o in range(1 - SPAN, SPAN)]
    nearby = jnp.stack(pieces, axis=0)
    window = lax.dynamic_slice_in_dim(nearby, root, SPAN, 0)
    split = lambda v: v.reshape(v.shape[0], heads, HEAD_DIM)
    keys = split(window[:, 0].reshape(SPAN * tok, -1))
    values = split(window[:, 1].reshape(SPAN * tok, -1))
    queries = split(triple[:, 0])
    scaling = HEAD_DIM ** (-0.5)
    live = jnp.arange(SPAN * tok, dtype=jnp.int32) < span * tok - pad
    count = jnp.repeat(key_counts(position, span, rand_picks), BLK, axis=2)
    count = jnp.where(live[None, None], count, 0.0)
    count = jnp.transpose(jnp.repeat(count, BLK, axis=0), (1, 0, 2))
    logits = jnp.einsum("qhd,khd->hqk", queries, keys, preferred_element_type=F32) * scaling
    logits = jnp.where(count > 0, logits, NEGATIVE)
    grown = jnp.exp(logits - jnp.max(logits, axis=-1, keepdims=True)) * count
    chances = grown / jnp.sum(grown, axis=-1, keepdims=True)
    chances_low = chances.astype(BF16)
    attended = jnp.einsum("hqk,khd->qhd", chances_low, values, preferred_element_type=F32)
    attended = attended.astype(BF16).reshape(tok, heads * HEAD_DIM)
    middle = inputs + lax.psum(dot(attended, out_w, ((1,), (0,))), "head")
    xhat_two, inv_two = norm_parts(middle)
    normed_two = (xhat_two * gain_two + shift_two).astype(BF16)
    pre_act = dot(normed_two, up_w, ((1,), (0,))) + up_bias.astype(F32)[None]
    hidden, pull = jax.vjp(lambda v: jax.nn.gelu(v, approximate=True), pre_act)
    hidden = hidden.astype(BF16)
    ffn = lax.psum(dot(hidden, down_w, ((1,), (0,))).astype(BF16), "head").astype(F32)
    output = (middle + ffn + down_shift).astype(BF16)
    grad_out = cotangent.astype(F32)
    grad_w_down = dot(hidden, cotangent, ((0,), (0,)))
    grad_pre = pull(dot(cotangent, down_w, ((1,), (1,))))[0].astype(BF16)
    grad_w_up = dot(normed_two, grad_pre, ((0,), (0,)))
    grad_up_bias = lax.psum(jnp.sum(grad_pre.astype(F32), axis=0), "seq")
    grad_two = lax.psum(dot(grad_pre, up_w, ((1,), (1,))), "head")
    grad_middle = grad_out + norm_backward(xhat_two, inv_two, grad_two * gain_two)
    grad_branch = grad_middle.astype(BF16)
    grad_w_out = dot(attended, grad_branch, ((0,), (0,)))
    grad_att = split(dot(grad_branch, out_w, ((1,), (1,))).astype(BF16))
    grad_prob = jnp.einsum("qhd,khd->hqk", grad_att, values, preferred_element_type=F32)
    inner = jnp.sum(chances * grad_prob, axis=-1, keepdims=True)
    grad_logit = (chances * (grad_prob - inner)).astype(BF16)
    dq = scaling * jnp.einsum("hqk,khd->qhd", grad_logit, keys, preferred_element_type=F32)
    dk = scaling * jnp.einsum("hqk,qhd->khd", grad_logit, queries, preferred_element_type=F32)
    dv = jnp.einsum("hqk,qhd->khd", chances_low, grad_att, preferred_element_type=F32)
    part = jnp.stack([dk.reshape(SPAN, tok, -1), dv.reshape(SPAN, tok, -1)], axis=1)
    near = jnp.zeros((2 * SPAN - 1,) + part.shape[1:], F32)
    near = lax.dynamic_update_slice_in_dim(near, part, root, 0)
    owned = near[SPAN - 1]
    for offset in range(1 - SPAN, SPAN):
        if offset:
            owned = owned + shifted(near[offset + SPAN - 1], "seq", offset)
    owned = owned.astype(BF16)
    grad_triple = jnp.stack([dq.reshape(tok, -1).astype(BF16), owned[0], owned[1]], axis=1)
    grad_w_qkv = jnp.einsum("td,tcf->dcf", normed, grad_triple, preferred_element_type=F32)
    grad_one = lax.psum(
        jnp.einsum("tcf,dcf->td", grad_triple, qkv, preferred_element_type=F32), "head"
    )
    x_grad = grad_middle + norm_backward(xhat_one, inv_one, grad_one * gain_one)
    sums = jnp.stack(
        [
            jnp.sum(grad_one * xhat_one, axis=0), jnp.sum(grad_one, axis=0),
            jnp.sum(grad_two * xhat_two, axis=0), jnp.sum(grad_two, axis=0),
            jnp.sum(grad_out, axis=0),
        ],
        axis=0,
    )
    scatter = lambda v, d: lax.psum_scatter(v, "seq", scatter_dimension=d, tiled=True)
    sums = scatter(sums, 1)
    return (
        output, x_grad, scatter(grad_w_qkv, 0), scatter(grad_w_out, 1), sums[0], sums[1], sums[2],
        sums[3], scatter(grad_w_up, 0), grad_up_bias, scatter(grad_w_down, 1), sums[4],
    )


MESH = pl.DeviceIdType.MESH
SEQ = 8
HEAD = 4
LINE = 4
VMEM_BYTES = 60 * 1024 * 1024


def al(value, multiple):
    return pl.multiple_of(value, multiple)


def fused_kernel(
    units, pads, picks, tok, cot, wq, wo, wu, wd, vec, upb,
    out_o, xg_o, gq_o, go_o, gu_o, gd_o, small_o, upbg_o,
    wq_all, wo_all, wu_all, wd_all, gains, normed, qs, kv_all, kwin, vwin, lg, prob, prob_low, ds,
    att, att_low, n2, hid, dgelu, gp, gb, xgb, mid_own, gm_own, gatt, dq, dk, dv, dkv_pad, dkv_send,
    dkv_recv, gt, part_send, part_recv, sum_f, cnt,
    sq, so, su, sd, aq, ao, au, ad, bq, bo, bu, bd, rq, ro, ru, rd,
    sm_send, sm_recv, sm_own, sm_two, up_send, up_recv,
    g_ss, g_rs, v_ss, v_rs, kv_ss, kv_rs, dkv_ss, dkv_rs, rs_ss, rs_rs, ag_ss, ag_rs,
    ra_ss, ra_rs, rb_ss, rb_rs, sm_ss, sm_rs, sm2_ss, sm2_rs, up_ss, up_rs,
):
    s = lax.axis_index("seq")
    h = lax.axis_index("head")
    z, y = lax.div(s, 2), lax.rem(s, 2)
    mate = z * 2 + 1 - y
    tokens = tok.shape[0]
    quarter = tokens // HEAD
    head_w = qs.shape[1]
    width = tok.shape[1]

    def copy(src, dst, ss, rs, **where):
        return pltpu.make_async_remote_copy(
            src_ref=src, dst_ref=dst, send_sem=ss, recv_sem=rs, device_id=where,
            device_id_type=MESH,
        )

    barrier = pltpu.get_barrier_semaphore()
    for d in range(1, SEQ):
        pl.semaphore_signal(
            barrier, inc=1, device_id={"seq": lax.rem(s + d, SEQ)}, device_id_type=MESH
        )
    for d in range(1, HEAD):
        pl.semaphore_signal(
            barrier, inc=1, device_id={"head": lax.rem(h + d, HEAD)}, device_id_type=MESH
        )
    for k in range(2 * SPAN - 1):
        other = s + k - (SPAN - 1)

        @pl.when((other < 0) | (other >= SEQ))
        def _():
            kv_all[k] = jnp.zeros(kv_all.shape[1:], BF16)
            dkv_recv[k] = jnp.zeros(dkv_recv.shape[1:], BF16)

    pl.semaphore_wait(barrier, SEQ - 1 + HEAD - 1)

    shard = [wq, wo, wu, wd]
    d_rows = wq.shape[0]
    slot = [
        lambda o: wq_all.at[pl.ds(al(o * d_rows, d_rows), d_rows), :],
        lambda o: wo_all.at[:, pl.ds(al(o * d_rows, d_rows), d_rows)],
        lambda o: wu_all.at[pl.ds(al(o * d_rows, d_rows), d_rows), :],
        lambda o: wd_all.at[:, pl.ds(al(o * d_rows, d_rows), d_rows)],
    ]

    def own_shard(w):
        here = slot[w](s)
        here[...] = shard[w][...]

    def line_copy(w, d):
        to = lax.rem(z + d, LINE) * 2 + y
        return copy(shard[w], slot[w](s), g_ss.at[w, d - 1], g_rs.at[w, s], seq=to)

    def mate_copy(w):
        return copy(shard[w], slot[w](s), g_ss.at[w, 3], g_rs.at[w, s], seq=mate)

    def forward_copy(w, d):
        o = lax.rem(z + LINE - d, LINE) * 2 + y
        return copy(slot[w](o), slot[w](o), g_ss.at[w, 3 + d], g_rs.at[w, o], seq=mate)

    def gather_start(w):
        mate_copy(w).start()
        for d in range(1, LINE):
            line_copy(w, d).start()

    def gather_forward(w):
        for d in range(1, LINE):
            o = lax.rem(z + LINE - d, LINE) * 2 + y
            copy(shard[w], slot[w](o), g_ss.at[w, d - 1], g_rs.at[w, o], seq=mate).wait_recv()
            forward_copy(w, d).start()

    def gather_finish(w):
        for d in range(LINE):
            o = lax.rem(z + d, LINE) * 2 + 1 - y
            copy(shard[w], slot[w](o), g_ss.at[w, 3], g_rs.at[w, o], seq=mate).wait_recv()

    def gather_drain(w):
        for d in range(1, LINE):
            line_copy(w, d).wait_send()
            forward_copy(w, d).wait_send()
        mate_copy(w).wait_send()

    def vec_copy(d):
        to = lax.rem(s + d, SEQ)
        return copy(
            vec, gains.at[:, pl.ds(al(s * d_rows, d_rows), d_rows)], v_ss.at[d - 1], v_rs.at[s],
            seq=to,
        )

    for d in range(1, SEQ):
        vec_copy(d).start()
    gather_start(0)
    gather_start(1)
    for w in range(4):
        own_shard(w)
    gains[:, pl.ds(al(s * d_rows, d_rows), d_rows)] = vec[...]

    start, leader, span, pad = 0, 0, 0, 0
    for k in range(units.shape[0]):
        here = units[k]
        inside = (s >= start) & (s < start + here)
        leader = jnp.where(inside, start, leader)
        span = jnp.where(inside, here, span)
        pad = jnp.where(inside, pads[k], pad)
        start = start + here
    position = s - leader
    root = jnp.clip(SPAN - 1 - position, 0, SPAN - 1)
    total = span * BLK_DEV
    live = span * tokens - pad

    for d in range(1, SEQ):
        o = lax.rem(s + d, SEQ)
        copy(
            vec, gains.at[:, pl.ds(al(o * d_rows, d_rows), d_rows)], v_ss.at[0], v_rs.at[o],
            seq=mate,
        ).wait_recv()
    for c in range(HEAD):
        r = pl.ds(c * quarter, quarter)
        xhat, _ = norm_parts(tok[r, :].astype(F32))
        normed[r, :] = (xhat * gains[0:1, :] + gains[1:2, :]).astype(BF16)
    gather_forward(0)
    gather_finish(0)
    gather_start(2)
    gather_start(3)
    scaling = HEAD_DIM ** (-0.5)
    for c in range(3):
        r = pl.ds(c * head_w, head_w)
        part = dot(normed[...], wq_all[:, r], ((1,), (0,)))
        if c == 0:
            qs[...] = (part.astype(BF16).astype(F32) * scaling).astype(BF16)
        else:
            kv_all[SPAN - 1, :, pl.ds((c - 1) * head_w, head_w)] = part.astype(BF16)

    def near(k, then):
        other = s + k - (SPAN - 1)
        if k != SPAN - 1:
            pl.when((other >= 0) & (other < SEQ))(lambda: then(other))

    def kv_copy(k, other):
        back = 2 * (SPAN - 1) - k
        return copy(
            kv_all.at[SPAN - 1], kv_all.at[back], kv_ss.at[k], kv_rs.at[back], seq=other
        )

    def kv_arrival(k, other):
        return copy(kv_all.at[SPAN - 1], kv_all.at[k], kv_ss.at[k], kv_rs.at[k], seq=other)

    for k in range(2 * SPAN - 1):
        near(k, lambda other, k=k: kv_copy(k, other).start())

    columns = lax.broadcasted_iota(jnp.int32, (1, SPAN * tokens), 1)
    usable = columns < live
    blocks = lax.div(columns, BLK)
    for hh in range(HEAD):
        for b in range(BLK_DEV):
            query = position * BLK_DEV + b
            count = jnp.zeros((1, SPAN * tokens), F32)
            for wanted in (query - 1, query, query + 1, 0, total - 1):
                count = count + jnp.where(blocks == wanted, 1.0, 0.0)
            for r in range(picks.shape[2]):
                raw = picks[b, hh, r]
                chosen = lax.rem(raw, BLK_DEV)
                for units_held in range(2, SPAN + 1):
                    chosen = jnp.where(
                        span == units_held, lax.rem(raw, BLK_DEV * units_held), chosen
                    )
                count = count + jnp.where(blocks == chosen, 1.0, 0.0)
            edge = (query == 0) | (query == total - 1)
            count = jnp.where(edge, 1.0, count)
            cnt[hh, b : b + 1, :] = jnp.where(usable, count, 0.0)

    for k in range(2 * SPAN - 1):
        near(k, lambda other, k=k: kv_arrival(k, other).wait_recv())
    for j in range(SPAN):
        part = kv_all[root + j]
        kwin[pl.ds(j * tokens, tokens), :] = part[:, :head_w]
        vwin[pl.ds(j * tokens, tokens), :] = part[:, head_w:]
    gather_forward(1)

    lanes = lax.div(lax.broadcasted_iota(jnp.int32, (1, head_w), 1), HEAD_DIM)

    att[...] = jnp.zeros(att.shape, F32)

    def attend(hh, carry):
        mine = lanes == hh
        query = jnp.where(mine, qs[...], jnp.zeros((), BF16))
        for j in range(SPAN):
            c = pl.ds(j * tokens, tokens)
            lg[:, c] = dot(query, kwin[c, :], ((1,), (1,)))
        for b in range(BLK_DEV):
            r = pl.ds(b * BLK, BLK)
            count = cnt[hh, b : b + 1, :]
            logits = jnp.where(count > 0, lg[r, :], NEGATIVE)
            grown = jnp.exp(logits - jnp.max(logits, axis=-1, keepdims=True)) * count
            chance = grown / jnp.sum(grown, axis=-1, keepdims=True)
            prob[hh, r, :] = chance
            prob_low[hh, r, :] = chance.astype(BF16)
        part = dot(prob_low[hh], vwin[...], ((1,), (0,)))
        att[...] += jnp.where(mine, part, 0.0)
        return carry

    lax.fori_loop(0, HEAD, attend, 0)
    att_low[...] = att[...].astype(BF16)
    gather_finish(1)

    def rows_of(k):
        return pl.ds(al(k * quarter, quarter), quarter)

    def rs_copy(op, d):
        to = lax.rem(h + d, HEAD)
        return copy(
            part_send.at[op, rows_of(to), :], part_recv.at[op, h], rs_ss.at[op, d],
            rs_rs.at[op, h], head=to,
        )

    def reduce_start(op):
        part_send[op] = sum_f[...].astype(BF16)
        for d in range(1, HEAD):
            rs_copy(op, d).start()

    def reduce_finish(op):
        result = sum_f[rows_of(h), :]
        for d in range(1, HEAD):
            o = lax.rem(h + d, HEAD)
            copy(
                part_send.at[op, rows_of(o), :], part_recv.at[op, o], rs_ss.at[op, d],
                rs_rs.at[op, o], head=o,
            ).wait_recv()
            result = result + part_recv[op, o].astype(F32)
        return result

    def ag_copy(op, whole, d):
        to = lax.rem(h + d, HEAD)
        return copy(
            whole.at[rows_of(h), :], whole.at[rows_of(h), :], ag_ss.at[op, d], ag_rs.at[op, h],
            head=to,
        )

    def spread_start(op, whole, value):
        whole[rows_of(h), :] = value
        for d in range(1, HEAD):
            ag_copy(op, whole, d).start()

    def spread_finish(op, whole):
        for d in range(1, HEAD):
            o = lax.rem(h + d, HEAD)
            copy(
                whole.at[rows_of(o), :], whole.at[rows_of(o), :], ag_ss.at[op, d],
                ag_rs.at[op, o], head=o,
            ).wait_recv()

    def tiled(n, body):
        def step(j, carry):
            body(al(j * 256, 256))
            return carry

        lax.fori_loop(0, n // 256, step, 0)

    def out_tile(c):
        sum_f[:, pl.ds(c, 256)] = dot(att_low[...], wo_all[:, pl.ds(c, 256)], ((1,), (0,)))

    tiled(width, out_tile)
    reduce_start(0)
    gather_forward(2)
    gather_forward(3)
    middle = tok[rows_of(h), :].astype(F32) + reduce_finish(0)
    mid_own[...] = middle
    xhat, _ = norm_parts(middle)
    spread_start(0, n2, (xhat * gains[2:3, :] + gains[3:4, :]).astype(BF16))
    gather_finish(2)
    gather_finish(3)
    spread_finish(0, n2)

    root_c = (2.0 / 3.141592653589793) ** 0.5

    def ffn_tile(c):
        f = pl.ds(c, 256)
        v = dot(n2[...], wu_all[:, f], ((1,), (0,))) + upb[:, f].astype(F32)
        t = jnp.tanh(root_c * (v + 0.044715 * (v * v * v)))
        hid[:, f] = (0.5 * v * (1.0 + t)).astype(BF16)
        slope = 0.5 * (1.0 + t) + 0.5 * v * (1.0 - t * t) * (root_c * (1.0 + 0.134145 * v * v))
        low = (dot(cot[...], wd_all[f, :], ((1,), (1,))) * slope).astype(BF16)
        gp[:, f] = low
        up_send[:, f] = jnp.broadcast_to(
            jnp.sum(low.astype(F32), axis=0, keepdims=True), (8, 256)
        )

    tiled(wu_all.shape[1], ffn_tile)

    def gn2_tile(c):
        sum_f[:, pl.ds(c, 256)] = dot(gp[...], wu_all[pl.ds(c, 256), :], ((1,), (1,)))

    tiled(width, gn2_tile)
    reduce_start(1)

    def up_copy(d):
        to = lax.rem(s + d, SEQ)
        return copy(up_send, up_recv.at[s], up_ss.at[d], up_rs.at[s], seq=to)

    for d in range(1, SEQ):
        up_copy(d).start()

    send = [sq, so, su, sd]
    arrive = [aq, ao, au, ad]
    again = [bq, bo, bu, bd]
    final = [rq, ro, ru, rd]
    grads = [gq_o, go_o, gu_o, gd_o]

    def cross_copy(w, zz):
        return copy(
            send[w].at[zz * 2 + 1 - y], arrive[w].at[zz], ra_ss.at[w, zz], ra_rs.at[w, zz],
            seq=mate,
        )

    def along_copy(w, d):
        zz = lax.rem(z + d, LINE)
        return copy(
            again[w].at[zz], final[w].at[z], rb_ss.at[w, zz], rb_rs.at[w, z], seq=zz * 2 + y
        )

    def grad_along(w):
        for d in range(1, LINE):
            zz = lax.rem(z + d, LINE)
            cross_copy(w, zz).wait_recv()
            mine = send[w][zz * 2 + y].astype(F32) + arrive[w][zz].astype(F32)
            again[w][zz] = mine.astype(BF16)
            along_copy(w, d).start()

    def grad_finish(w):
        cross_copy(w, z).wait_recv()
        result = send[w][z * 2 + y].astype(F32) + arrive[w][z].astype(F32)
        for d in range(1, LINE):
            o = lax.rem(z + d, LINE)
            copy(
                again[w].at[o], final[w].at[o], rb_ss.at[w, o], rb_rs.at[w, o], seq=mate
            ).wait_recv()
            result = result + final[w][o].astype(F32)
        grads[w][...] = result

    def grad_drain(w):
        for zz in range(LINE):
            cross_copy(w, zz).wait_send()
        for d in range(1, LINE):
            along_copy(w, d).wait_send()

    def down_step(zz, carry):
        c = al(zz * 256, 256)
        part = dot(hid[...], cot[:, pl.ds(c, 256)], ((0,), (0,))).astype(BF16)
        sd[zz * 2] = part[:, :d_rows]
        sd[zz * 2 + 1] = part[:, d_rows:]
        cross_copy(3, zz).start()
        return carry

    def up_step(zz, carry):
        c = al(zz * 256, 256)
        part = dot(n2[:, pl.ds(c, 256)], gp[...], ((0,), (0,))).astype(BF16)
        su[zz * 2] = part[:d_rows]
        su[zz * 2 + 1] = part[d_rows:]
        cross_copy(2, zz).start()
        return carry

    lax.fori_loop(0, LINE, down_step, 0)
    lax.fori_loop(0, LINE, up_step, 0)

    grad_two = reduce_finish(1)
    xhat, inverse = norm_parts(mid_own[...])
    dy = cot[rows_of(h), :].astype(F32)
    sm_send[2:3, :] = jnp.sum(grad_two * xhat, axis=0, keepdims=True)
    sm_send[3:4, :] = jnp.sum(grad_two, axis=0, keepdims=True)
    sm_send[4:5, :] = jnp.sum(dy, axis=0, keepdims=True)
    sm_send[5:8, :] = jnp.zeros((3, width), F32)
    grad_mid = dy + norm_backward(xhat, inverse, grad_two * gains[2:3, :])
    gm_own[...] = grad_mid
    spread_start(1, gb, grad_mid.astype(BF16))

    def down_tile(c):
        sum_f[:, pl.ds(c, 256)] = dot(hid[...], wd_all[:, pl.ds(c, 256)], ((1,), (0,)))

    tiled(width, down_tile)
    reduce_start(2)
    grad_along(3)
    spread_finish(1, gb)

    def wo_step(zz, carry):
        c = al(zz * 256, 256)
        part = dot(att_low[...], gb[:, pl.ds(c, 256)], ((0,), (0,))).astype(BF16)
        so[zz * 2] = part[:, :d_rows]
        so[zz * 2 + 1] = part[:, d_rows:]
        cross_copy(1, zz).start()
        return carry

    gatt[...] = dot(gb[...], wo_all[...], ((1,), (1,))).astype(BF16)
    lax.fori_loop(0, LINE, wo_step, 0)
    ffn = reduce_finish(2)
    spread_start(2, out_o, (mid_own[...] + ffn + gains[4:5, :]).astype(BF16))

    dq[...] = jnp.zeros(dq.shape, F32)
    dk[...] = jnp.zeros(dk.shape, F32)
    dv[...] = jnp.zeros(dv.shape, F32)

    def attend_back(hh, carry):
        mine = lanes == hh
        none = jnp.zeros((), BF16)
        query = jnp.where(mine, qs[...], none)
        grad = jnp.where(mine, gatt[...], none)
        for j in range(SPAN):
            c = pl.ds(j * tokens, tokens)
            lg[:, c] = dot(grad, vwin[c, :], ((1,), (1,)))
        for b in range(BLK_DEV):
            r = pl.ds(b * BLK, BLK)
            chance, grown = prob[hh, r, :], lg[r, :]
            inner = jnp.sum(chance * grown, axis=-1, keepdims=True)
            ds[r, :] = (chance * (grown - inner)).astype(BF16)
        dq[...] += jnp.where(mine, dot(ds[...], kwin[...], ((1,), (0,))), 0.0)
        for j in range(SPAN):
            c = pl.ds(j * tokens, tokens)
            dk[c, :] += dot(ds[:, c], query, ((0,), (0,)))
            dv[c, :] += dot(prob_low[hh, :, c], grad, ((0,), (0,)))
        return carry

    lax.fori_loop(0, HEAD, attend_back, 0)
    for k in range(2 * (SPAN - 1) + SPAN):
        j = k - (SPAN - 1)
        if 0 <= j < SPAN:
            c = pl.ds(j * tokens, tokens)
            dkv_pad[k, :, :head_w] = dk[c, :].astype(BF16)
            dkv_pad[k, :, head_w:] = dv[c, :].astype(BF16)
        else:
            dkv_pad[k] = jnp.zeros(dkv_pad.shape[1:], BF16)

    def dkv_copy(k, other):
        back = 2 * (SPAN - 1) - k
        return copy(
            dkv_send.at[k], dkv_recv.at[back], dkv_ss.at[k], dkv_rs.at[back], seq=other
        )

    def dkv_arrival(k, other):
        return copy(dkv_send.at[k], dkv_recv.at[k], dkv_ss.at[k], dkv_rs.at[k], seq=other)

    for k in range(2 * SPAN - 1):
        dkv_send[k] = dkv_pad[k + SPAN - 1 - root]
        near(k, lambda other, k=k: dkv_copy(k, other).start())

    gt[:, :head_w] = (dq[...] * scaling).astype(BF16)
    grad_along(2)
    grad_along(1)
    for k in range(2 * SPAN - 1):
        near(k, lambda other, k=k: dkv_arrival(k, other).wait_recv())
    whole = dkv_send[SPAN - 1].astype(F32)
    for k in range(2 * SPAN - 1):
        if k != SPAN - 1:
            whole = whole + dkv_recv[k].astype(F32)
    gt[:, head_w:] = whole.astype(BF16)

    def gn1_tile(c):
        sum_f[:, pl.ds(c, 256)] = dot(gt[...], wq_all[pl.ds(c, 256), :], ((1,), (1,)))

    tiled(width, gn1_tile)
    reduce_start(3)

    def wq_step(zz, carry):
        c = al(zz * 256, 256)
        part = dot(normed[:, pl.ds(c, 256)], gt[...], ((0,), (0,))).astype(BF16)
        sq[zz * 2] = part[:d_rows]
        sq[zz * 2 + 1] = part[d_rows:]
        cross_copy(0, zz).start()
        return carry

    lax.fori_loop(0, LINE, wq_step, 0)
    grad_one = reduce_finish(3)
    xhat, inverse = norm_parts(tok[rows_of(h), :].astype(F32))
    sm_send[0:1, :] = jnp.sum(grad_one * xhat, axis=0, keepdims=True)
    sm_send[1:2, :] = jnp.sum(grad_one, axis=0, keepdims=True)

    def small_copy(d):
        to = lax.rem(s + d, SEQ)
        return copy(
            sm_send.at[:, pl.ds(al(to * d_rows, d_rows), d_rows)], sm_recv.at[s], sm_ss.at[d],
            sm_rs.at[s], seq=to,
        )

    for d in range(1, SEQ):
        small_copy(d).start()
    grad_x = gm_own[...] + norm_backward(xhat, inverse, grad_one * gains[0:1, :])
    spread_start(3, xgb, grad_x.astype(BF16))
    grad_along(0)

    sm_recv[s] = sm_send[:, pl.ds(al(s * d_rows, d_rows), d_rows)]
    up_recv[s] = up_send[...]
    for d in range(1, SEQ):
        o = lax.rem(s + d, SEQ)
        copy(
            sm_send.at[:, pl.ds(0, d_rows)], sm_recv.at[o], sm_ss.at[d], sm_rs.at[o], seq=o
        ).wait_recv()
        copy(up_send, up_recv.at[o], up_ss.at[d], up_rs.at[o], seq=o).wait_recv()
    part, ups = sm_recv[0], up_recv[0]
    for o in range(1, SEQ):
        part, ups = part + sm_recv[o], ups + up_recv[o]
    upbg_o[...] = ups
    sm_own[...] = part

    def two_copy(d):
        to = lax.rem(h + d, HEAD)
        return copy(sm_own, sm_two.at[h], sm2_ss.at[d], sm2_rs.at[h], head=to)

    for d in range(1, HEAD):
        two_copy(d).start()
    sm_two[h] = part
    for w in (3, 2, 1):
        grad_finish(w)
    spread_finish(2, out_o)
    spread_finish(3, xgb)
    xg_o[...] = xgb[...].astype(F32)
    for d in range(1, HEAD):
        o = lax.rem(h + d, HEAD)
        copy(sm_own, sm_two.at[o], sm2_ss.at[d], sm2_rs.at[o], head=o).wait_recv()
    small_o[...] = (sm_two[0] + sm_two[1]) + (sm_two[2] + sm_two[3])
    grad_finish(0)

    for w in range(4):
        gather_drain(w)
        grad_drain(w)
    for d in range(1, SEQ):
        vec_copy(d).wait_send()
        up_copy(d).wait_send()
        small_copy(d).wait_send()
    for k in range(2 * SPAN - 1):
        near(k, lambda other, k=k: kv_copy(k, other).wait_send())
        near(k, lambda other, k=k: dkv_copy(k, other).wait_send())
    for d in range(1, HEAD):
        two_copy(d).wait_send()
        for op, ref in enumerate((n2, gb, out_o, xgb)):
            rs_copy(op, d).wait_send()
            ag_copy(op, ref, d).wait_send()


def local_fused(
    tokens, w_qkv, w_out, ln1_gain, ln1_bias, ln2_gain, ln2_bias, w_up, up_bias, w_down, down_bias,
    seq_units, seq_pad, rand_picks, cotangent,
):
    tok, width = tokens.shape
    rows, _, head_w = w_qkv.shape
    hidden = w_up.shape[1]
    vectors = jnp.stack([ln1_gain, ln1_bias, ln2_gain, ln2_bias, down_bias], axis=0)
    vectors = jnp.pad(vectors.astype(F32), ((0, 3), (0, 0)))
    near = 2 * SPAN - 1
    quarter = tok // HEAD
    v = pltpu.VMEM
    dma = pltpu.SemaphoreType.DMA
    shards = [(rows, 3 * head_w), (head_w, rows), (rows, hidden), (hidden, rows)]
    scratch = [
        v((width, 3 * head_w), BF16), v((head_w, width), BF16), v((width, hidden), BF16),
        v((hidden, width), BF16), v((8, width), F32), v((tok, width), BF16),
        v((tok, head_w), BF16), v((near, tok, 2 * head_w), BF16), v((SPAN * tok, head_w), BF16),
        v((SPAN * tok, head_w), BF16), v((tok, SPAN * tok), F32), v((HEAD, tok, SPAN * tok), F32),
        v((HEAD, tok, SPAN * tok), BF16), v((tok, SPAN * tok), BF16),
        v((tok, head_w), F32), v((tok, head_w), BF16), v((tok, width), BF16),
        v((tok, hidden), BF16), v((8, 128), F32), v((tok, hidden), BF16), v((tok, width), BF16),
        v((tok, width), BF16), v((quarter, width), F32), v((quarter, width), F32),
        v((tok, head_w), BF16), v((tok, head_w), F32), v((SPAN * tok, head_w), F32),
        v((SPAN * tok, head_w), F32), v((near + SPAN - 1, tok, 2 * head_w), BF16),
        v((near, tok, 2 * head_w), BF16), v((near, tok, 2 * head_w), BF16),
        v((tok, 3 * head_w), BF16), v((4, tok, width), BF16), v((4, HEAD, quarter, width), BF16),
        v((tok, width), F32), v((HEAD, 8, SPAN * tok), F32),
    ]
    for lead in (SEQ, LINE, LINE, LINE):
        scratch += [v((lead,) + shape, BF16) for shape in shards]
    scratch += [
        v((8, width), F32), v((SEQ, 8, rows), F32), v((8, rows), F32), v((HEAD, 8, rows), F32),
        v((8, hidden), F32), v((SEQ, 8, hidden), F32),
    ]
    scratch += [
        dma(shape)
        for shape in (
            (4, 7), (4, SEQ), (7,), (SEQ,), (near,), (near,), (near,), (near,),
            (4, HEAD), (4, HEAD), (4, HEAD), (4, HEAD), (4, LINE), (4, LINE), (4, LINE), (4, LINE),
            (SEQ,), (SEQ,), (HEAD,), (HEAD,), (SEQ,), (SEQ,),
        )
    ]
    outs = [
        ((tok, width), BF16), ((tok, width), F32), (shards[0], F32), (shards[1], F32),
        (shards[2], F32), (shards[3], F32), ((8, rows), F32), ((8, hidden), F32),
    ]
    smem, vmem = pl.BlockSpec(memory_space=pltpu.SMEM), pl.BlockSpec(memory_space=pltpu.VMEM)
    out, xg, gq, go, gu, gd, small, upg = pl.pallas_call(
        fused_kernel,
        out_shape=[jax.ShapeDtypeStruct(*o) for o in outs],
        in_specs=[smem] * 3 + [vmem] * 8,
        out_specs=[vmem] * 8,
        scratch_shapes=scratch,
        compiler_params=pltpu.CompilerParams(
            collective_id=0, has_side_effects=True, vmem_limit_bytes=VMEM_BYTES
        ),
        name="fused_layer",
    )(
        seq_units, seq_pad, rand_picks, tokens, cotangent, w_qkv.reshape(rows, 3 * head_w), w_out,
        w_up, w_down, vectors, up_bias.reshape(1, hidden),
    )
    return (
        out, xg, gq.reshape(rows, 3, head_w), go, small[0], small[1], small[2], small[3], gu,
        upg[0], gd, small[4],
    )


IN_SPECS = (
    P("seq", None), P("seq", None, "head"), P("head", "seq"), P("seq"), P("seq"), P("seq"),
    P("seq"), P("seq", "head"), P("head"), P("head", "seq"), P("seq"), P(), P(),
    P("seq", "head", None), P("seq", None),
)
OUT_SPECS = (
    P("seq", None), P("seq", None), P("seq", None, "head"), P("head", "seq"), P("seq"), P("seq"),
    P("seq"), P("seq"), P("seq", "head"), P("head"), P("head", "seq"), P("seq"),
)


def solution(mesh):
    fits = mesh.shape["seq"] == SEQ and mesh.shape["head"] == HEAD
    return jax.shard_map(
        local_fused if fits else local_general, mesh=mesh, in_specs=IN_SPECS,
        out_specs=OUT_SPECS, check_vma=False,
    )
```

```python
import functools
import types

import jax
import jax.numpy as jnp
from jax import lax
from jax.experimental import pallas as pl
from jax.experimental.pallas import tpu as pltpu
from jax.sharding import PartitionSpec as P

HEAD_DIM = 64
BLK = 64
SPAN = 4
BLK_DEV = 4
EPSILON = 1e-05
NEGATIVE = -1e30
F32 = jnp.float32
BF16 = jnp.bfloat16


def shifted(value, axis, steps):
    count = lax.axis_size(axis)
    first, last = max(0, -steps), min(count, count - steps)
    return lax.ppermute(value, axis, [(i, i + steps) for i in range(first, last)])


def norm_parts(features):
    average = jnp.mean(features, axis=-1, keepdims=True)
    centred = features - average
    spread = jnp.mean(centred * centred, axis=-1, keepdims=True)
    inverse = lax.rsqrt(spread + EPSILON)
    return centred * inverse, inverse


def norm_backward(xhat, inverse, scaled):
    first = jnp.mean(scaled, axis=-1, keepdims=True)
    second = jnp.mean(scaled * xhat, axis=-1, keepdims=True)
    return inverse * (scaled - first - xhat * second)


def dot(a, b, dims):
    return lax.dot_general(a, b, (dims, ((), ())), preferred_element_type=F32)


def sequence_place(seq_units, seq_pad):
    device = lax.axis_index("seq")
    start, leader, span, pad = 0, 0, 0, 0
    for k in range(seq_units.shape[0]):
        units = seq_units[k]
        inside = (device >= start) & (device < start + units)
        leader = jnp.where(inside, start, leader)
        span = jnp.where(inside, units, span)
        pad = jnp.where(inside, seq_pad[k], pad)
        start = start + units
    return device - leader, span, pad


def key_counts(position, span, picks):
    blocks = lax.broadcasted_iota(jnp.int32, (1, 1, SPAN * BLK_DEV), 2)
    query = position * BLK_DEV + lax.broadcasted_iota(jnp.int32, (BLK_DEV, 1, 1), 0)
    total = span * BLK_DEV
    count = jnp.zeros((BLK_DEV, picks.shape[1], SPAN * BLK_DEV), F32)
    for wanted in (query - 1, query, query + 1, 0, total - 1):
        count = count + (blocks == wanted).astype(F32)
    chosen = picks % total
    for r in range(picks.shape[2]):
        count = count + (blocks == chosen[:, :, r : r + 1]).astype(F32)
    return jnp.where((query == 0) | (query == total - 1), 1.0, count)


def local_general(
    tokens, w_qkv, w_out, ln1_gain, ln1_bias, ln2_gain, ln2_bias, w_up, up_bias, w_down, down_bias,
    seq_units, seq_pad, rand_picks, cotangent,
):
    tok, width = tokens.shape
    heads = w_qkv.shape[2] // HEAD_DIM
    rows = lambda v: lax.all_gather(v, "seq", axis=0, tiled=True)
    cols = lambda v: lax.all_gather(v, "seq", axis=1, tiled=True)
    vectors = jnp.stack([ln1_gain, ln1_bias, ln2_gain, ln2_bias, down_bias], axis=0)
    gain_one, shift_one, gain_two, shift_two, down_shift = [
        v[None].astype(F32) for v in cols(vectors)
    ]
    qkv = rows(w_qkv)
    out_w, up_w, down_w = cols(w_out), rows(w_up), cols(w_down)
    position, span, pad = sequence_place(seq_units, seq_pad)
    root = SPAN - 1 - position
    inputs = tokens.astype(F32)
    xhat_one, inv_one = norm_parts(inputs)
    normed = (xhat_one * gain_one + shift_one).astype(BF16)
    triple = jnp.einsum("td,dcf->tcf", normed, qkv, preferred_element_type=F32).astype(BF16)
    own = jnp.stack([triple[:, 1], triple[:, 2]], axis=0)
    pieces = [own if o == 0 else shifted(own, "seq", -o) for o in range(1 - SPAN, SPAN)]
    nearby = jnp.stack(pieces, axis=0)
    window = lax.dynamic_slice_in_dim(nearby, root, SPAN, 0)
    split = lambda v: v.reshape(v.shape[0], heads, HEAD_DIM)
    keys = split(window[:, 0].reshape(SPAN * tok, -1))
    values = split(window[:, 1].reshape(SPAN * tok, -1))
    queries = split(triple[:, 0])
    scaling = HEAD_DIM ** (-0.5)
    live = jnp.arange(SPAN * tok, dtype=jnp.int32) < span * tok - pad
    count = jnp.repeat(key_counts(position, span, rand_picks), BLK, axis=2)
    count = jnp.where(live[None, None], count, 0.0)
    count = jnp.transpose(jnp.repeat(count, BLK, axis=0), (1, 0, 2))
    logits = jnp.einsum("qhd,khd->hqk", queries, keys, preferred_element_type=F32) * scaling
    logits = jnp.where(count > 0, logits, NEGATIVE)
    grown = jnp.exp(logits - jnp.max(logits, axis=-1, keepdims=True)) * count
    chances = grown / jnp.sum(grown, axis=-1, keepdims=True)
    chances_low = chances.astype(BF16)
    attended = jnp.einsum("hqk,khd->qhd", chances_low, values, preferred_element_type=F32)
    attended = attended.astype(BF16).reshape(tok, heads * HEAD_DIM)
    middle = inputs + lax.psum(dot(attended, out_w, ((1,), (0,))), "head")
    xhat_two, inv_two = norm_parts(middle)
    normed_two = (xhat_two * gain_two + shift_two).astype(BF16)
    pre_act = dot(normed_two, up_w, ((1,), (0,))) + up_bias.astype(F32)[None]
    hidden, pull = jax.vjp(lambda v: jax.nn.gelu(v, approximate=True), pre_act)
    hidden = hidden.astype(BF16)
    ffn = lax.psum(dot(hidden, down_w, ((1,), (0,))).astype(BF16), "head").astype(F32)
    output = (middle + ffn + down_shift).astype(BF16)
    grad_out = cotangent.astype(F32)
    grad_w_down = dot(hidden, cotangent, ((0,), (0,)))
    grad_pre = pull(dot(cotangent, down_w, ((1,), (1,))))[0].astype(BF16)
    grad_w_up = dot(normed_two, grad_pre, ((0,), (0,)))
    grad_up_bias = lax.psum(jnp.sum(grad_pre.astype(F32), axis=0), "seq")
    grad_two = lax.psum(dot(grad_pre, up_w, ((1,), (1,))), "head")
    grad_middle = grad_out + norm_backward(xhat_two, inv_two, grad_two * gain_two)
    grad_branch = grad_middle.astype(BF16)
    grad_w_out = dot(attended, grad_branch, ((0,), (0,)))
    grad_att = split(dot(grad_branch, out_w, ((1,), (1,))).astype(BF16))
    grad_prob = jnp.einsum("qhd,khd->hqk", grad_att, values, preferred_element_type=F32)
    inner = jnp.sum(chances * grad_prob, axis=-1, keepdims=True)
    grad_logit = (chances * (grad_prob - inner)).astype(BF16)
    dq = scaling * jnp.einsum("hqk,khd->qhd", grad_logit, keys, preferred_element_type=F32)
    dk = scaling * jnp.einsum("hqk,qhd->khd", grad_logit, queries, preferred_element_type=F32)
    dv = jnp.einsum("hqk,qhd->khd", chances_low, grad_att, preferred_element_type=F32)
    part = jnp.stack([dk.reshape(SPAN, tok, -1), dv.reshape(SPAN, tok, -1)], axis=1)
    near = jnp.zeros((2 * SPAN - 1,) + part.shape[1:], F32)
    near = lax.dynamic_update_slice_in_dim(near, part, root, 0)
    owned = near[SPAN - 1]
    for offset in range(1 - SPAN, SPAN):
        if offset:
            owned = owned + shifted(near[offset + SPAN - 1], "seq", offset)
    owned = owned.astype(BF16)
    grad_triple = jnp.stack([dq.reshape(tok, -1).astype(BF16), owned[0], owned[1]], axis=1)
    grad_w_qkv = jnp.einsum("td,tcf->dcf", normed, grad_triple, preferred_element_type=F32)
    grad_one = lax.psum(
        jnp.einsum("tcf,dcf->td", grad_triple, qkv, preferred_element_type=F32), "head"
    )
    x_grad = grad_middle + norm_backward(xhat_one, inv_one, grad_one * gain_one)
    sums = jnp.stack(
        [
            jnp.sum(grad_one * xhat_one, axis=0), jnp.sum(grad_one, axis=0),
            jnp.sum(grad_two * xhat_two, axis=0), jnp.sum(grad_two, axis=0),
            jnp.sum(grad_out, axis=0),
        ],
        axis=0,
    )
    scatter = lambda v, d: lax.psum_scatter(v, "seq", scatter_dimension=d, tiled=True)
    sums = scatter(sums, 1)
    return (
        output, x_grad, scatter(grad_w_qkv, 0), scatter(grad_w_out, 1), sums[0], sums[1], sums[2],
        sums[3], scatter(grad_w_up, 0), grad_up_bias, scatter(grad_w_down, 1), sums[4],
    )


MESH = pl.DeviceIdType.MESH
SEQ = 8
HEAD = 4
LINE = 4
NEAR = 2 * SPAN - 1
QKV_KV, QKV_Q, OUT, UP, DOWN = range(5)
VMEM_BYTES = 60 * 1024 * 1024


def al(value, multiple):
    return pl.multiple_of(value, multiple)


def fused_kernel(names, *refs):
    r = types.SimpleNamespace(**dict(zip(names, refs)))
    s, h = lax.axis_index("seq"), lax.axis_index("head")
    z, y, x, c = lax.div(s, 2), lax.rem(s, 2), lax.div(h, 2), lax.rem(h, 2)
    e = lax.rem(z, 2)
    pair_z = z + 1 - 2 * e
    mate = z * 2 + 1 - y
    pair = pair_z * 2 + y
    twin = x * 2 + 1 - c
    across = (1 - x) * 2 + c
    tokens, width = r.tok.shape
    quarter = tokens // HEAD
    head_w = r.qs.shape[1]
    rows = r.wq.shape[1]
    half = r.wu_all.shape[1]
    sent = []

    def copy(src, dst, ss, rs, **where):
        return pltpu.make_async_remote_copy(
            src_ref=src, dst_ref=dst, send_sem=ss, recv_sem=rs, device_id=where,
            device_id_type=MESH,
        )

    def when(cond, then):
        if cond is None:
            then()
        else:
            pl.when(cond)(lambda: then())

    def send(cond, *args, **where):
        one = copy(*args, **where)
        when(cond, one.start)
        sent.append((cond, one))

    def arrived(cond, dst, rs, like=None):
        when(cond, copy(dst if like is None else like, dst, r.v_ss.at[0], rs, seq=mate).wait_recv)

    barrier = pltpu.get_barrier_semaphore()
    greeted = [{"seq": lax.rem(s + d, SEQ)} for d in range(1, SEQ)]
    greeted += [{"head": lax.rem(h + d, HEAD)} for d in range(1, HEAD)]
    greeted += [{"seq": pair, "head": across}]
    for where in greeted:
        pl.semaphore_signal(barrier, inc=1, device_id=where, device_id_type=MESH)
    for k, ref in enumerate((r.g1, r.b1, r.g2, r.b2, r.b3)):
        r.vec[k : k + 1, :] = ref[...].reshape(1, rows).astype(F32)
    r.vec[5:8, :] = jnp.zeros((3, rows), F32)
    for k in range(NEAR):
        other = s + k - (SPAN - 1)

        @pl.when((other < 0) | (other >= SEQ))
        def _():
            r.kv_all[k] = jnp.zeros(r.kv_all.shape[1:], BF16)
            r.dkv_recv[k] = jnp.zeros(r.dkv_recv.shape[1:], BF16)

    pl.semaphore_wait(barrier, len(greeted))

    def cols(o, size):
        return pl.ds(al(o * size, size), size)

    relay_slot = [lambda o: r.wq_all.at[:, cols(o, rows), :], lambda o: r.wo_all.at[:, cols(o, rows)]]
    relay_src = [r.wq, r.wo]

    def relay_send(w, src, o, up_k, mate_k):
        def args(k):
            return src, relay_slot[w](o), r.g_ss.at[w, k], r.g_rs.at[w, o]

        return args

    def relay_start(w):
        src, dst, rs = relay_src[w], relay_slot[w](s), r.g_rs.at[w, s]
        send(z < LINE - 1, src, dst, r.g_ss.at[w, 0], rs, seq=s + 2)
        send(z > 0, src, dst, r.g_ss.at[w, 4], rs, seq=s - 2)
        send(None, src, dst, r.g_ss.at[w, 8], rs, seq=mate)

    def relay_round(w, k):
        for sign, first, third in ((-1, 0, 8 + k), (1, 4, 11 + k)):
            from_z = z + sign * k
            there = (from_z >= 0) & (from_z < LINE)
            o = jnp.clip(from_z, 0, LINE - 1) * 2 + y
            ref, rs = relay_slot[w](o), r.g_rs.at[w, o]
            arrived(there, ref, rs)
            onward = (z < LINE - 1) if sign < 0 else (z > 0)
            send(there & onward, ref, ref, r.g_ss.at[w, first + k], rs, seq=s - 2 * sign)
            send(there, ref, ref, r.g_ss.at[w, third], rs, seq=mate)

    def relay_finish(w):
        for d in range(LINE):
            o = lax.rem(z + d, LINE) * 2 + 1 - y
            arrived(None, relay_slot[w](o), r.g_rs.at[w, o])

    for d in range(1, SEQ):
        send(
            None, r.vec, r.gains.at[:, cols(s, rows)], r.v_ss.at[d - 1], r.v_rs.at[s],
            seq=lax.rem(s + d, SEQ),
        )
    relay_start(0)
    r.gains[:, cols(s, rows)] = r.vec[...]
    r.wq_all[:, cols(s, rows), :] = r.wq[...]
    r.wo_all[:, cols(s, rows)] = r.wo[...]

    start, leader, span, pad = 0, 0, 0, 0
    for k in range(r.units.shape[0]):
        here = r.units[k]
        inside = (s >= start) & (s < start + here)
        leader = jnp.where(inside, start, leader)
        span = jnp.where(inside, here, span)
        pad = jnp.where(inside, r.pads[k], pad)
        start = start + here
    position = s - leader
    root = jnp.clip(SPAN - 1 - position, 0, SPAN - 1)
    total = span * BLK_DEV
    live = span * tokens - pad

    for k in range(HEAD):
        q = pl.ds(k * quarter, quarter)
        r.xh[q, :] = norm_parts(r.tok[q, :].astype(F32))[0]
    relay_round(0, 1)
    relay_start(1)

    columns = lax.broadcasted_iota(jnp.int32, (1, SPAN * tokens), 1)
    usable = columns < live
    blocks = lax.div(columns, BLK)
    for hh in range(HEAD):
        if hh == 2:
            relay_round(0, 2)
        for b in range(BLK_DEV):
            query = position * BLK_DEV + b
            count = jnp.zeros((1, SPAN * tokens), F32)
            for wanted in (query - 1, query, query + 1, 0, total - 1):
                count = count + jnp.where(blocks == wanted, 1.0, 0.0)
            for k in range(r.picks.shape[0]):
                raw = r.picks[k, b, hh]
                chosen = lax.rem(raw, BLK_DEV)
                for held in range(2, SPAN + 1):
                    chosen = jnp.where(span == held, lax.rem(raw, BLK_DEV * held), chosen)
                count = count + jnp.where(blocks == chosen, 1.0, 0.0)
            count = jnp.where((query == 0) | (query == total - 1), 1.0, count)
            r.cnt[hh, b : b + 1, :] = jnp.where(usable, count, 0.0)
    relay_round(0, 3)

    ffn_src = {
        UP: lambda k: r.wu.at[:, cols(k, half)],
        DOWN: lambda k: r.wd.at[cols(k, half), :],
    }
    ffn_slot = {
        UP: lambda o: r.wu_all.at[cols(o, rows), :],
        DOWN: lambda o: r.wd_all.at[:, cols(o, rows)],
    }

    def ffn_start(w):
        i = w - UP
        for d in range(1, LINE):
            to = lax.rem(z + d, LINE)
            send(
                None, ffn_src[w](lax.rem(to, 2)), ffn_slot[w](s), r.f_ss.at[i, d - 1],
                r.f_rs.at[i, s], seq=to * 2 + y,
            )
        send(
            None, ffn_src[w](e), ffn_slot[w](s), r.f_ss.at[i, 3], r.f_rs.at[i, s], seq=mate
        )

    def ffn_forward(w):
        i = w - UP
        for d in range(1, LINE):
            o = lax.rem(z + LINE - d, LINE) * 2 + y
            ref = ffn_slot[w](o)
            arrived(None, ref, r.f_rs.at[i, o])
            send(None, ref, ref, r.f_ss.at[i, 3 + d], r.f_rs.at[i, o], seq=mate)

    def ffn_finish(w):
        for d in range(LINE):
            o = lax.rem(z + d, LINE) * 2 + 1 - y
            arrived(None, ffn_slot[w](o), r.f_rs.at[w - UP, o])

    ffn_start(UP)
    for ref, src in ((ffn_slot[UP](s), ffn_src[UP](e)), (ffn_slot[DOWN](s), ffn_src[DOWN](e))):
        ref[...] = src[...]

    for d in range(1, SEQ):
        o = lax.rem(s + d, SEQ)
        arrived(None, r.gains.at[:, cols(o, rows)], r.v_rs.at[o], r.vec)
    for k in range(HEAD):
        q = pl.ds(k * quarter, quarter)
        r.normed[q, :] = (r.xh[q, :] * r.gains[0:1, :] + r.gains[1:2, :]).astype(BF16)
    relay_finish(0)
    scaling = HEAD_DIM ** (-0.5)
    for k in (1, 2):
        part = dot(r.normed[...], r.wq_all[k], ((1,), (0,)))
        r.kv_all[SPAN - 1, :, pl.ds((k - 1) * head_w, head_w)] = part.astype(BF16)

    def kv_send(cond, slot, back, k, to):
        send(cond, r.kv_all.at[slot], r.kv_all.at[back], r.kv_ss.at[k], r.kv_rs.at[back], seq=to)

    def kv_wait(cond, slot):
        arrived(cond, r.kv_all.at[slot], r.kv_rs.at[slot])

    low, high = z > 0, z < LINE - 1
    from_mate = 4 - 2 * y
    kv_send(None, 3, 2 + 2 * y, 0, mate)
    kv_send(high, 3, 1, 1, s + 2)
    kv_send(low, 3, 5, 2, s - 2)
    part = dot(r.normed[...], r.wq_all[0], ((1,), (0,)))
    r.qs[...] = (part.astype(BF16).astype(F32) * scaling).astype(BF16)
    kv_wait(None, from_mate)
    kv_send(high, from_mate, 2 - 2 * y, 3, s + 2)
    kv_send(low, from_mate, 6 - 2 * y, 4, s - 2)
    for k in range(1, LINE):
        relay_round(1, k)
    kv_wait(low, 2 - 2 * y)
    kv_wait(high, 6 - 2 * y)
    kv_send((y == 0) & low & high, 2, 0, 5, s + 2)
    kv_send((y == 1) & low & high, 4, 6, 6, s - 2)
    ffn_start(DOWN)

    half_t = tokens // 2
    r.cotx[cols(e, tokens), :] = r.cot[...]

    def cot_rows(unit, core):
        return r.cotx.at[pl.ds(al(unit * tokens + core * half_t, half_t), half_t), :]

    send(None, r.cot.at[cols(c, half_t), :], cot_rows(e, c), r.c_ss.at[0], r.c_rs.at[0], seq=pair)
    ffn_forward(UP)
    kv_wait(low, 1)
    kv_wait(high, 5)
    kv_wait((y == 0) & (z >= 2), 0)
    kv_wait((y == 1) & (z <= 1), 6)
    for j in range(SPAN):
        part = r.kv_all[root + j]
        r.kwin[pl.ds(j * tokens, tokens), :] = part[:, :head_w]
        r.vwin[pl.ds(j * tokens, tokens), :] = part[:, head_w:]

    lanes = lax.div(lax.broadcasted_iota(jnp.int32, (1, head_w), 1), HEAD_DIM)
    none = jnp.zeros((), BF16)
    r.att[...] = jnp.zeros(r.att.shape, F32)

    def attend(hh, carry):
        mine = lanes == hh
        query = jnp.where(mine, r.qs[...], none)
        for j in range(SPAN):
            k = pl.ds(j * tokens, tokens)
            r.lg[:, k] = dot(query, r.kwin[k, :], ((1,), (1,)))
        for b in range(BLK_DEV):
            q = pl.ds(b * BLK, BLK)
            count = r.cnt[hh, b : b + 1, :]
            logits = jnp.where(count > 0, r.lg[q, :], NEGATIVE)
            grown = jnp.exp(logits - jnp.max(logits, axis=-1, keepdims=True)) * count
            chance = grown / jnp.sum(grown, axis=-1, keepdims=True)
            r.prob[hh, q, :] = chance
            r.prob_low[hh, q, :] = chance.astype(BF16)
        part = dot(r.prob_low[hh], r.vwin[...], ((1,), (0,)))
        r.att[...] += jnp.where(mine, part, 0.0)
        return carry

    lax.fori_loop(0, HEAD, attend, 0)
    r.att_low[...] = r.att[...].astype(BF16)
    relay_finish(1)

    def rows_of(k):
        return cols(k, quarter)

    def reduce_start(op):
        r.part_send[op] = r.sum_f[:tokens, :].astype(BF16)
        for d in range(1, HEAD):
            to = lax.rem(h + d, HEAD)
            send(
                None, r.part_send.at[op, rows_of(to), :], r.part_recv.at[op, h],
                r.rs_ss.at[op, d], r.rs_rs.at[op, h], head=to,
            )

    def reduce_finish(op):
        result = r.sum_f[rows_of(h), :]
        for d in range(1, HEAD):
            o = lax.rem(h + d, HEAD)
            arrived(None, r.part_recv.at[op, o], r.rs_rs.at[op, o])
            result = result + r.part_recv[op, o].astype(F32)
        return result

    def spread_start(op, whole, value):
        whole[rows_of(h), :] = value
        for d in range(1, HEAD):
            ref = whole.at[rows_of(h), :]
            send(
                None, ref, ref, r.ag_ss.at[op, d], r.ag_rs.at[op, h], head=lax.rem(h + d, HEAD)
            )

    def spread_finish(op, whole):
        for d in range(1, HEAD):
            o = lax.rem(h + d, HEAD)
            arrived(None, whole.at[rows_of(o), :], r.ag_rs.at[op, o])

    def block_rows(unit, head):
        return pl.ds(al(unit * tokens + head * quarter, quarter), quarter)

    def pair_start(op):
        for u in range(2):
            for v in range(2):
                block = r.sum_f[block_rows(u, v * 2 + 1 - c), :]
                r.p1_send[op, u * 2 + v] = block.astype(BF16)
        send(None, r.p1_send.at[op], r.p1_recv.at[op], r.p1_ss.at[op], r.p1_rs.at[op], head=twin)

    def pair_middle(op):
        arrived(None, r.p1_recv.at[op], r.p1_rs.at[op])
        for du, dv in ((1, 1), (1, 0), (0, 1), (0, 0)):
            u, v = lax.rem(e + du, 2), lax.rem(x + dv, 2)
            block = r.sum_f[block_rows(u, v * 2 + c), :] + r.p1_recv[op, u * 2 + v].astype(F32)
            if du or dv:
                k = u * 2 + v
                r.p2_send[op, k] = block.astype(BF16)
                send(
                    None, r.p2_send.at[op, k], r.p2_recv.at[op, e * 2 + x], r.p2_ss.at[op, k],
                    r.p2_rs.at[op, e * 2 + x], seq=pair if du else s, head=across if dv else h,
                )
            else:
                r.p_own[op] = block

    def pair_finish(op):
        result = r.p_own[op]
        for du, dv in ((0, 1), (1, 0), (1, 1)):
            k = lax.rem(e + du, 2) * 2 + lax.rem(x + dv, 2)
            arrived(None, r.p2_recv.at[op, k], r.p2_rs.at[op, k])
            result = result + r.p2_recv[op, k].astype(F32)
        return result

    def tiled(n, body):
        def step(j, carry):
            body(al(j * 256, 256))
            return carry

        lax.fori_loop(0, n // 256, step, 0)

    def out_tile(k):
        k = pl.ds(k, 256)
        r.sum_f[:tokens, k] = dot(r.att_low[...], r.wo_all[:, k], ((1,), (0,)))

    tiled(width, out_tile)
    reduce_start(0)
    arrived(None, cot_rows(1 - e, c), r.c_rs.at[0])
    send(
        None, cot_rows(1 - e, c), cot_rows(1 - e, c), r.c_ss.at[1], r.c_rs.at[1], head=twin
    )
    ffn_forward(DOWN)
    middle = r.tok[rows_of(h), :].astype(F32) + reduce_finish(0)
    r.mid_own[...] = middle
    xhat, _ = norm_parts(middle)

    def n2_rows(unit, head):
        return r.n2x.at[block_rows(unit, head), :]

    r.n2x[block_rows(e, h), :] = (xhat * r.gains[2:3, :] + r.gains[3:4, :]).astype(BF16)
    mine, tag = n2_rows(e, h), e * 4 + h
    send(None, mine, mine, r.n2_ss.at[0], r.n2_rs.at[tag], head=across)
    send(None, mine, mine, r.n2_ss.at[1], r.n2_rs.at[tag], seq=pair, head=across)
    send(None, mine, mine, r.n2_ss.at[2], r.n2_rs.at[tag], seq=pair)
    send(None, mine, mine, r.n2_ss.at[3], r.n2_rs.at[tag], head=twin)
    ffn_finish(UP)
    ffn_finish(DOWN)
    for k, (unit, head) in enumerate(((e, across), (1 - e, h), (1 - e, across))):
        ref, tag = n2_rows(unit, head), unit * 4 + head
        arrived(None, ref, r.n2_rs.at[tag])
        send(None, ref, ref, r.n2_ss.at[4 + k], r.n2_rs.at[tag], head=twin)
    for unit in (e, 1 - e):
        for head in (x * 2 + 1 - c, (1 - x) * 2 + 1 - c):
            arrived(None, n2_rows(unit, head), r.n2_rs.at[unit * 4 + head])
    arrived(None, cot_rows(1 - e, 1 - c), r.c_rs.at[1])

    root_c = (2.0 / 3.141592653589793) ** 0.5
    r.up_send[half // 128 :, :] = jnp.zeros((8 - half // 128, 128), F32)
    for j in range(half // 256):
        f = pl.ds(j * 256, 256)
        bias = r.upb[:, pl.ds(al(e * half + j * 256, 256), 256)].astype(F32)
        v = dot(r.n2x[...], r.wu_all[:, f], ((1,), (0,))) + bias
        t = jnp.tanh(root_c * (v + 0.044715 * (v * v * v)))
        r.hid[:, f] = (0.5 * v * (1.0 + t)).astype(BF16)
        slope = 0.5 * (1.0 + t) + 0.5 * v * (1.0 - t * t) * (root_c * (1.0 + 0.134145 * v * v))
        low_p = (dot(r.cotx[...], r.wd_all[f, :], ((1,), (1,))) * slope).astype(BF16)
        r.gp[:, f] = low_p
        sums = jnp.sum(low_p.astype(F32), axis=0, keepdims=True)
        r.up_send[2 * j : 2 * j + 1, :] = sums[:, :128]
        r.up_send[2 * j + 1 : 2 * j + 2, :] = sums[:, 128:]

    def gn2_tile(k):
        k = pl.ds(k, 256)
        r.sum_f[:, k] = dot(r.gp[...], r.wu_all[k, :], ((1,), (1,)))

    tiled(width, gn2_tile)
    pair_start(0)

    grad_send = {QKV_KV: r.skv, QKV_Q: r.sq, OUT: r.so, UP: r.su, DOWN: r.sd}
    grad_arrive = {QKV_KV: r.akv, QKV_Q: r.aq, OUT: r.ao, UP: r.au, DOWN: r.ad}
    grad_again = {QKV_KV: r.bkv, QKV_Q: r.bq, OUT: r.bo, UP: r.bu, DOWN: r.bd}
    grad_final = {QKV_KV: r.rkv, QKV_Q: r.rq, OUT: r.ro, UP: r.ru, DOWN: r.rd}

    def tile_of(i):
        return lax.rem(z + 1 + i, LINE)

    def grad_cross(w, zz):
        send(
            None, grad_send[w].at[zz * 2 + 1 - y], grad_arrive[w].at[zz], r.ra_ss.at[w, zz],
            r.ra_rs.at[w, zz], seq=mate,
        )

    def grad_along(w, ks=(1, 2, 3)):
        for d in ks:
            zz = lax.rem(z + d, LINE)
            arrived(None, grad_arrive[w].at[zz], r.ra_rs.at[w, zz])
            both = grad_send[w][zz * 2 + y].astype(F32) + grad_arrive[w][zz].astype(F32)
            grad_again[w][zz] = both.astype(BF16)
            send(
                None, grad_again[w].at[zz], grad_final[w].at[z], r.rb_ss.at[w, zz],
                r.rb_rs.at[w, z], seq=zz * 2 + y,
            )

    def grad_own(w):
        arrived(None, grad_arrive[w].at[z], r.ra_rs.at[w, z])
        return grad_send[w][z * 2 + y].astype(F32) + grad_arrive[w][z].astype(F32)

    def grad_from(w, o):
        arrived(None, grad_final[w].at[o], r.rb_rs.at[w, o])
        return grad_final[w][o].astype(F32)

    def grad_sum(w):
        result = grad_own(w)
        for d in range(1, LINE):
            result = result + grad_from(w, lax.rem(z + d, LINE))
        return result

    def grad_halves(w):
        same = grad_own(w) + grad_from(w, lax.rem(z + 2, LINE))
        other = grad_from(w, lax.rem(z + 1, LINE)) + grad_from(w, lax.rem(z + 3, LINE))
        return same, other

    def down_step(i):
        zz = tile_of(i)
        part = dot(r.hid[...], r.cotx[:, cols(zz, 256)], ((0,), (0,))).astype(BF16)
        r.sd[zz * 2] = part[:, :rows]
        r.sd[zz * 2 + 1] = part[:, rows:]
        grad_cross(DOWN, zz)

    def up_step(i):
        zz = tile_of(i)
        part = dot(r.n2x[:, cols(zz, 256)], r.gp[...], ((0,), (0,))).astype(BF16)
        r.su[zz * 2] = part[:rows]
        r.su[zz * 2 + 1] = part[rows:]
        grad_cross(UP, zz)

    down_step(0)
    down_step(1)
    pair_middle(0)
    down_step(2)
    down_step(3)
    for i in range(LINE):
        up_step(i)
    for d in range(1, SEQ):
        send(
            None, r.up_send, r.up_recv.at[s], r.up_ss.at[d], r.up_rs.at[s],
            seq=lax.rem(s + d, SEQ),
        )

    grad_two = pair_finish(0)
    xhat, inverse = norm_parts(r.mid_own[...])
    dy = r.cot[rows_of(h), :].astype(F32)
    grad_mid = dy + norm_backward(xhat, inverse, grad_two * r.gains[2:3, :])
    r.gm_own[...] = grad_mid
    spread_start(0, r.gb, grad_mid.astype(BF16))
    r.sm_send[2:3, :] = jnp.sum(grad_two * xhat, axis=0, keepdims=True)
    r.sm_send[3:4, :] = jnp.sum(grad_two, axis=0, keepdims=True)
    r.sm_send[4:5, :] = jnp.sum(dy, axis=0, keepdims=True)
    r.sm_send[5:8, :] = jnp.zeros((3, width), F32)

    def down_tile(k):
        k = pl.ds(k, 256)
        r.sum_f[:, k] = dot(r.hid[...], r.wd_all[:, k], ((1,), (0,)))

    tiled(width, down_tile)
    pair_start(1)
    grad_along(DOWN)
    pair_middle(1)
    spread_finish(0, r.gb)
    r.gatt[...] = dot(r.gb[...], r.wo_all[...], ((1,), (1,))).astype(BF16)
    for i in range(LINE):
        zz = tile_of(i)
        part = dot(r.att_low[...], r.gb[:, cols(zz, 256)], ((0,), (0,))).astype(BF16)
        r.so[zz * 2] = part[:, :rows]
        r.so[zz * 2 + 1] = part[:, rows:]
        grad_cross(OUT, zz)
    grad_along(UP)

    r.dq[...] = jnp.zeros(r.dq.shape, F32)
    r.dk[...] = jnp.zeros(r.dk.shape, F32)
    r.dv[...] = jnp.zeros(r.dv.shape, F32)

    def attend_back(hh, carry):
        mine = lanes == hh
        query = jnp.where(mine, r.qs[...], none)
        grad = jnp.where(mine, r.gatt[...], none)
        for j in range(SPAN):
            k = pl.ds(j * tokens, tokens)
            r.lg[:, k] = dot(grad, r.vwin[k, :], ((1,), (1,)))
        for b in range(BLK_DEV):
            q = pl.ds(b * BLK, BLK)
            chance, grown = r.prob[hh, q, :], r.lg[q, :]
            inner = jnp.sum(chance * grown, axis=-1, keepdims=True)
            r.ds[q, :] = (chance * (grown - inner)).astype(BF16)
        r.dq[...] += jnp.where(mine, dot(r.ds[...], r.kwin[...], ((1,), (0,))), 0.0)
        for j in range(SPAN):
            k = pl.ds(j * tokens, tokens)
            r.dk[k, :] += dot(r.ds[:, k], query, ((0,), (0,)))
            r.dv[k, :] += dot(r.prob_low[hh, :, k], grad, ((0,), (0,)))
        return carry

    lax.fori_loop(0, HEAD, attend_back, 0)
    for k in range(2 * (SPAN - 1) + SPAN):
        j = k - (SPAN - 1)
        if 0 <= j < SPAN:
            q = pl.ds(j * tokens, tokens)
            r.dkv_pad[k, :, :head_w] = r.dk[q, :].astype(BF16)
            r.dkv_pad[k, :, head_w:] = r.dv[q, :].astype(BF16)
        else:
            r.dkv_pad[k] = jnp.zeros(r.dkv_pad.shape[1:], BF16)
    for k in range(NEAR):
        r.dkv_send[k] = r.dkv_pad[k + SPAN - 1 - root]
        other, back = s + k - (SPAN - 1), 2 * (SPAN - 1) - k
        if k != SPAN - 1:
            send(
                (other >= 0) & (other < SEQ), r.dkv_send.at[k], r.dkv_recv.at[back],
                r.dkv_ss.at[k], r.dkv_rs.at[back], seq=other,
            )

    r.gtq[...] = (r.dq[...] * scaling).astype(BF16)
    for i in range(LINE):
        zz = tile_of(i)
        part = dot(r.normed[:, cols(zz, 256)], r.gtq[...], ((0,), (0,))).astype(BF16)
        r.sq[zz * 2] = part[:rows]
        r.sq[zz * 2 + 1] = part[rows:]
        grad_cross(QKV_Q, zz)
    grad_along(OUT)
    ffn = pair_finish(1)
    spread_start(1, r.out_o, (r.mid_own[...] + ffn + r.gains[4:5, :]).astype(BF16))

    whole = r.dkv_send[SPAN - 1].astype(F32)
    for k in range(NEAR):
        if k != SPAN - 1:
            other = s + k - (SPAN - 1)
            arrived((other >= 0) & (other < SEQ), r.dkv_recv.at[k], r.dkv_rs.at[k])
            whole = whole + r.dkv_recv[k].astype(F32)
    r.gtkv[...] = whole.astype(BF16)
    for i in range(LINE):
        zz = tile_of(i)
        part = dot(r.normed[:, cols(zz, 256)], r.gtkv[...], ((0,), (0,))).astype(BF16)
        for v in range(2):
            for k in range(2):
                r.skv[zz * 2 + v, k] = part[v * rows : (v + 1) * rows, k * head_w : (k + 1) * head_w]
        grad_cross(QKV_KV, zz)

    def gn1_tile(k):
        k = pl.ds(k, 256)
        r.sum_f[:tokens, k] = (
            dot(r.gtq[...], r.wq_all[0, k, :], ((1,), (1,)))
            + dot(r.gtkv[:, :head_w], r.wq_all[1, k, :], ((1,), (1,)))
            + dot(r.gtkv[:, head_w:], r.wq_all[2, k, :], ((1,), (1,)))
        )

    tiled(width, gn1_tile)
    reduce_start(1)
    grad_along(QKV_Q)
    grad_along(QKV_KV)
    grad_one = reduce_finish(1)
    xhat, inverse = norm_parts(r.tok[rows_of(h), :].astype(F32))
    r.sm_send[0:1, :] = jnp.sum(grad_one * xhat, axis=0, keepdims=True)
    r.sm_send[1:2, :] = jnp.sum(grad_one, axis=0, keepdims=True)
    for d in range(1, SEQ):
        to = lax.rem(s + d, SEQ)
        send(
            None, r.sm_send.at[:, cols(to, rows)], r.sm_recv.at[s], r.sm_ss.at[d], r.sm_rs.at[s],
            seq=to,
        )
    grad_x = r.gm_own[...] + norm_backward(xhat, inverse, grad_one * r.gains[0:1, :])
    spread_start(2, r.xgb, grad_x.astype(BF16))

    same, other = grad_halves(DOWN)
    r.gd_o[cols(e, half), :] = same
    r.gd_o[cols(1 - e, half), :] = other
    same, other = grad_halves(UP)
    r.gu_o[:, cols(e, half)] = same
    r.gu_o[:, cols(1 - e, half)] = other
    r.go_o[...] = grad_sum(OUT)

    r.sm_recv[s] = r.sm_send[:, cols(s, rows)]
    r.up_recv[s] = r.up_send[...]
    for d in range(1, SEQ):
        o = lax.rem(s + d, SEQ)
        arrived(None, r.sm_recv.at[o], r.sm_rs.at[o], r.vec)
        arrived(None, r.up_recv.at[o], r.up_rs.at[o])
    part = r.sm_recv[0]
    for o in range(1, SEQ):
        part = part + r.sm_recv[o]
    r.sm_own[...] = part
    for d in range(1, HEAD):
        send(
            None, r.sm_own, r.sm_two.at[h], r.sm2_ss.at[d], r.sm2_rs.at[h],
            head=lax.rem(h + d, HEAD),
        )
    r.sm_two[h] = part
    tall = half // 128
    for u in range(2):
        ups = jnp.zeros((tall, 128), F32)
        for o in range(SEQ):
            if (o // 2) % 2 == u:
                ups = ups + r.up_recv[o, :tall, :]
        r.small_o[8 + u * tall : 8 + (u + 1) * tall, :] = ups
    spread_finish(1, r.out_o)
    spread_finish(2, r.xgb)
    r.xg_o[...] = r.xgb[...].astype(F32)
    for d in range(1, HEAD):
        o = lax.rem(h + d, HEAD)
        arrived(None, r.sm_two.at[o], r.sm2_rs.at[o])
    r.small_o[0:8, :] = (r.sm_two[0] + r.sm_two[1]) + (r.sm_two[2] + r.sm_two[3])
    r.gq_o[0] = grad_sum(QKV_Q)
    r.gq_o[1:3] = grad_sum(QKV_KV)

    for cond, one in sent:
        when(cond, one.wait_send)


def local_fused(
    tokens, w_qkv, w_out, ln1_gain, ln1_bias, ln2_gain, ln2_bias, w_up, up_bias, w_down, down_bias,
    seq_units, seq_pad, rand_picks, cotangent,
):
    tok, width = tokens.shape
    rows, _, head_w = w_qkv.shape
    hidden = w_up.shape[1]
    half = hidden // 2
    quarter = tok // HEAD
    keys = SPAN * tok
    smem, vmem = pl.BlockSpec(memory_space=pltpu.SMEM), pl.BlockSpec(memory_space=pltpu.VMEM)
    ins = dict(
        units=seq_units, pads=seq_pad, picks=jnp.transpose(rand_picks, (2, 0, 1)), tok=tokens,
        cot=cotangent, wq=jnp.transpose(w_qkv, (1, 0, 2)), wo=w_out, wu=w_up, wd=w_down,
        g1=ln1_gain, b1=ln1_bias, g2=ln2_gain, b2=ln2_bias, b3=down_bias,
        upb=up_bias.reshape(1, hidden),
    )
    outs = dict(
        out_o=((tok, width), BF16), xg_o=((tok, width), F32), gq_o=((3, rows, head_w), F32),
        go_o=((head_w, rows), F32), gu_o=((rows, hidden), F32), gd_o=((hidden, rows), F32),
        small_o=((16, rows), F32),
    )
    scratch = dict(
        wq_all=((3, width, head_w), BF16), wo_all=((head_w, width), BF16),
        wu_all=((width, half), BF16), wd_all=((half, width), BF16), vec=((8, rows), F32),
        gains=((8, width), F32), xh=((tok, width), F32), normed=((tok, width), BF16),
        qs=((tok, head_w), BF16), kv_all=((NEAR, tok, 2 * head_w), BF16),
        kwin=((keys, head_w), BF16), vwin=((keys, head_w), BF16), lg=((tok, keys), F32),
        prob=((HEAD, tok, keys), F32), prob_low=((HEAD, tok, keys), BF16), ds=((tok, keys), BF16),
        att=((tok, head_w), F32), att_low=((tok, head_w), BF16), n2x=((2 * tok, width), BF16),
        cotx=((2 * tok, width), BF16), hid=((2 * tok, half), BF16), gp=((2 * tok, half), BF16),
        gb=((tok, width), BF16), xgb=((tok, width), BF16), mid_own=((quarter, width), F32),
        gm_own=((quarter, width), F32), gatt=((tok, head_w), BF16), dq=((tok, head_w), F32),
        dk=((keys, head_w), F32), dv=((keys, head_w), F32),
        dkv_pad=((NEAR + SPAN - 1, tok, 2 * head_w), BF16),
        dkv_send=((NEAR, tok, 2 * head_w), BF16), dkv_recv=((NEAR, tok, 2 * head_w), BF16),
        gtq=((tok, head_w), BF16), gtkv=((tok, 2 * head_w), BF16),
        part_send=((2, tok, width), BF16), part_recv=((2, HEAD, quarter, width), BF16),
        sum_f=((2 * tok, width), F32), cnt=((HEAD, 8, keys), F32),
        p1_send=((2, 4, quarter, width), BF16), p1_recv=((2, 4, quarter, width), BF16),
        p2_send=((2, 4, quarter, width), BF16), p2_recv=((2, 4, quarter, width), BF16),
        p_own=((2, quarter, width), F32), sm_send=((8, width), F32),
        sm_recv=((SEQ, 8, rows), F32), sm_own=((8, rows), F32), sm_two=((HEAD, 8, rows), F32),
        up_send=((8, 128), F32), up_recv=((SEQ, 8, 128), F32),
    )
    shards = dict(
        kv=(2, rows, head_w), q=(rows, head_w), o=(head_w, rows), u=(rows, half), d=(half, rows)
    )
    for lead, count in (("s", SEQ), ("a", LINE), ("b", LINE), ("r", LINE)):
        for name, shape in shards.items():
            scratch[lead + name] = ((count,) + shape, BF16)
    semaphores = dict(
        g_ss=(2, 16), g_rs=(2, SEQ), f_ss=(2, 7), f_rs=(2, SEQ), v_ss=(7,), v_rs=(SEQ,),
        kv_ss=(NEAR,), kv_rs=(NEAR,), dkv_ss=(NEAR,), dkv_rs=(NEAR,), c_ss=(2,), c_rs=(2,),
        rs_ss=(2, HEAD), rs_rs=(2, HEAD), ag_ss=(3, HEAD), ag_rs=(3, HEAD), n2_ss=(7,),
        n2_rs=(8,), p1_ss=(2,), p1_rs=(2,), p2_ss=(2, 4), p2_rs=(2, 4), ra_ss=(5, LINE),
        ra_rs=(5, LINE), rb_ss=(5, LINE), rb_rs=(5, LINE), sm_ss=(SEQ,), sm_rs=(SEQ,),
        sm2_ss=(HEAD,), sm2_rs=(HEAD,), up_ss=(SEQ,), up_rs=(SEQ,),
    )
    names = [*ins, *outs, *scratch, *semaphores]
    out, xg, gq, go, gu, gd, small = pl.pallas_call(
        functools.partial(fused_kernel, names),
        out_shape=[jax.ShapeDtypeStruct(*o) for o in outs.values()],
        in_specs=[smem] * 3 + [vmem] * (len(ins) - 3),
        out_specs=[vmem] * len(outs),
        scratch_shapes=[pltpu.VMEM(*v) for v in scratch.values()]
        + [pltpu.SemaphoreType.DMA(v) for v in semaphores.values()],
        compiler_params=pltpu.CompilerParams(
            collective_id=0, has_side_effects=True, vmem_limit_bytes=VMEM_BYTES
        ),
        name="fused_layer",
    )(*ins.values())
    return (
        out, xg, jnp.transpose(gq, (1, 0, 2)), go, small[0], small[1], small[2], small[3], gu,
        small[8:16].reshape(hidden), gd, small[4],
    )


IN_SPECS = (
    P("seq", None), P("seq", None, "head"), P("head", "seq"), P("seq"), P("seq"), P("seq"),
    P("seq"), P("seq", "head"), P("head"), P("head", "seq"), P("seq"), P(), P(),
    P("seq", "head", None), P("seq", None),
)
OUT_SPECS = (
    P("seq", None), P("seq", None), P("seq", None, "head"), P("head", "seq"), P("seq"), P("seq"),
    P("seq"), P("seq"), P("seq", "head"), P("head"), P("head", "seq"), P("seq"),
)


def solution(mesh):
    fits = mesh.shape["seq"] == SEQ and mesh.shape["head"] == HEAD
    return jax.shard_map(
        local_fused if fits else local_general, mesh=mesh, in_specs=IN_SPECS,
        out_specs=OUT_SPECS, check_vma=False,
    )
```

```python
import functools
import types

import jax
import jax.numpy as jnp
from jax import lax
from jax.experimental import pallas as pl
from jax.experimental.pallas import tpu as pltpu
from jax.sharding import PartitionSpec as P

HEAD_DIM = 64
BLK = 64
SPAN = 4
BLK_DEV = 4
EPSILON = 1e-05
NEGATIVE = -1e30
F32 = jnp.float32
BF16 = jnp.bfloat16


def shifted(value, axis, steps):
    count = lax.axis_size(axis)
    first, last = max(0, -steps), min(count, count - steps)
    return lax.ppermute(value, axis, [(i, i + steps) for i in range(first, last)])


def norm_parts(features):
    average = jnp.mean(features, axis=-1, keepdims=True)
    centred = features - average
    spread = jnp.mean(centred * centred, axis=-1, keepdims=True)
    inverse = lax.rsqrt(spread + EPSILON)
    return centred * inverse, inverse


def norm_backward(xhat, inverse, scaled):
    first = jnp.mean(scaled, axis=-1, keepdims=True)
    second = jnp.mean(scaled * xhat, axis=-1, keepdims=True)
    return inverse * (scaled - first - xhat * second)


def dot(a, b, dims):
    return lax.dot_general(a, b, (dims, ((), ())), preferred_element_type=F32)


def sequence_place(seq_units, seq_pad):
    device = lax.axis_index("seq")
    start, leader, span, pad = 0, 0, 0, 0
    for k in range(seq_units.shape[0]):
        units = seq_units[k]
        inside = (device >= start) & (device < start + units)
        leader = jnp.where(inside, start, leader)
        span = jnp.where(inside, units, span)
        pad = jnp.where(inside, seq_pad[k], pad)
        start = start + units
    return device - leader, span, pad


def key_counts(position, span, picks):
    blocks = lax.broadcasted_iota(jnp.int32, (1, 1, SPAN * BLK_DEV), 2)
    query = position * BLK_DEV + lax.broadcasted_iota(jnp.int32, (BLK_DEV, 1, 1), 0)
    total = span * BLK_DEV
    count = jnp.zeros((BLK_DEV, picks.shape[1], SPAN * BLK_DEV), F32)
    for wanted in (query - 1, query, query + 1, 0, total - 1):
        count = count + (blocks == wanted).astype(F32)
    chosen = picks % total
    for r in range(picks.shape[2]):
        count = count + (blocks == chosen[:, :, r : r + 1]).astype(F32)
    return jnp.where((query == 0) | (query == total - 1), 1.0, count)


def local_general(
    tokens, w_qkv, w_out, ln1_gain, ln1_bias, ln2_gain, ln2_bias, w_up, up_bias, w_down, down_bias,
    seq_units, seq_pad, rand_picks, cotangent,
):
    tok, width = tokens.shape
    heads = w_qkv.shape[2] // HEAD_DIM
    rows = lambda v: lax.all_gather(v, "seq", axis=0, tiled=True)
    cols = lambda v: lax.all_gather(v, "seq", axis=1, tiled=True)
    vectors = jnp.stack([ln1_gain, ln1_bias, ln2_gain, ln2_bias, down_bias], axis=0)
    gain_one, shift_one, gain_two, shift_two, down_shift = [
        v[None].astype(F32) for v in cols(vectors)
    ]
    qkv = rows(w_qkv)
    out_w, up_w, down_w = cols(w_out), rows(w_up), cols(w_down)
    position, span, pad = sequence_place(seq_units, seq_pad)
    root = SPAN - 1 - position
    inputs = tokens.astype(F32)
    xhat_one, inv_one = norm_parts(inputs)
    normed = (xhat_one * gain_one + shift_one).astype(BF16)
    triple = jnp.einsum("td,dcf->tcf", normed, qkv, preferred_element_type=F32).astype(BF16)
    own = jnp.stack([triple[:, 1], triple[:, 2]], axis=0)
    pieces = [own if o == 0 else shifted(own, "seq", -o) for o in range(1 - SPAN, SPAN)]
    nearby = jnp.stack(pieces, axis=0)
    window = lax.dynamic_slice_in_dim(nearby, root, SPAN, 0)
    split = lambda v: v.reshape(v.shape[0], heads, HEAD_DIM)
    keys = split(window[:, 0].reshape(SPAN * tok, -1))
    values = split(window[:, 1].reshape(SPAN * tok, -1))
    queries = split(triple[:, 0])
    scaling = HEAD_DIM ** (-0.5)
    live = jnp.arange(SPAN * tok, dtype=jnp.int32) < span * tok - pad
    count = jnp.repeat(key_counts(position, span, rand_picks), BLK, axis=2)
    count = jnp.where(live[None, None], count, 0.0)
    count = jnp.transpose(jnp.repeat(count, BLK, axis=0), (1, 0, 2))
    logits = jnp.einsum("qhd,khd->hqk", queries, keys, preferred_element_type=F32) * scaling
    logits = jnp.where(count > 0, logits, NEGATIVE)
    grown = jnp.exp(logits - jnp.max(logits, axis=-1, keepdims=True)) * count
    chances = grown / jnp.sum(grown, axis=-1, keepdims=True)
    chances_low = chances.astype(BF16)
    attended = jnp.einsum("hqk,khd->qhd", chances_low, values, preferred_element_type=F32)
    attended = attended.astype(BF16).reshape(tok, heads * HEAD_DIM)
    middle = inputs + lax.psum(dot(attended, out_w, ((1,), (0,))), "head")
    xhat_two, inv_two = norm_parts(middle)
    normed_two = (xhat_two * gain_two + shift_two).astype(BF16)
    pre_act = dot(normed_two, up_w, ((1,), (0,))) + up_bias.astype(F32)[None]
    hidden, pull = jax.vjp(lambda v: jax.nn.gelu(v, approximate=True), pre_act)
    hidden = hidden.astype(BF16)
    ffn = lax.psum(dot(hidden, down_w, ((1,), (0,))).astype(BF16), "head").astype(F32)
    output = (middle + ffn + down_shift).astype(BF16)
    grad_out = cotangent.astype(F32)
    grad_w_down = dot(hidden, cotangent, ((0,), (0,)))
    grad_pre = pull(dot(cotangent, down_w, ((1,), (1,))))[0].astype(BF16)
    grad_w_up = dot(normed_two, grad_pre, ((0,), (0,)))
    grad_up_bias = lax.psum(jnp.sum(grad_pre.astype(F32), axis=0), "seq")
    grad_two = lax.psum(dot(grad_pre, up_w, ((1,), (1,))), "head")
    grad_middle = grad_out + norm_backward(xhat_two, inv_two, grad_two * gain_two)
    grad_branch = grad_middle.astype(BF16)
    grad_w_out = dot(attended, grad_branch, ((0,), (0,)))
    grad_att = split(dot(grad_branch, out_w, ((1,), (1,))).astype(BF16))
    grad_prob = jnp.einsum("qhd,khd->hqk", grad_att, values, preferred_element_type=F32)
    inner = jnp.sum(chances * grad_prob, axis=-1, keepdims=True)
    grad_logit = (chances * (grad_prob - inner)).astype(BF16)
    dq = scaling * jnp.einsum("hqk,khd->qhd", grad_logit, keys, preferred_element_type=F32)
    dk = scaling * jnp.einsum("hqk,qhd->khd", grad_logit, queries, preferred_element_type=F32)
    dv = jnp.einsum("hqk,qhd->khd", chances_low, grad_att, preferred_element_type=F32)
    part = jnp.stack([dk.reshape(SPAN, tok, -1), dv.reshape(SPAN, tok, -1)], axis=1)
    near = jnp.zeros((2 * SPAN - 1,) + part.shape[1:], F32)
    near = lax.dynamic_update_slice_in_dim(near, part, root, 0)
    owned = near[SPAN - 1]
    for offset in range(1 - SPAN, SPAN):
        if offset:
            owned = owned + shifted(near[offset + SPAN - 1], "seq", offset)
    owned = owned.astype(BF16)
    grad_triple = jnp.stack([dq.reshape(tok, -1).astype(BF16), owned[0], owned[1]], axis=1)
    grad_w_qkv = jnp.einsum("td,tcf->dcf", normed, grad_triple, preferred_element_type=F32)
    grad_one = lax.psum(
        jnp.einsum("tcf,dcf->td", grad_triple, qkv, preferred_element_type=F32), "head"
    )
    x_grad = grad_middle + norm_backward(xhat_one, inv_one, grad_one * gain_one)
    sums = jnp.stack(
        [
            jnp.sum(grad_one * xhat_one, axis=0), jnp.sum(grad_one, axis=0),
            jnp.sum(grad_two * xhat_two, axis=0), jnp.sum(grad_two, axis=0),
            jnp.sum(grad_out, axis=0),
        ],
        axis=0,
    )
    scatter = lambda v, d: lax.psum_scatter(v, "seq", scatter_dimension=d, tiled=True)
    sums = scatter(sums, 1)
    return (
        output, x_grad, scatter(grad_w_qkv, 0), scatter(grad_w_out, 1), sums[0], sums[1], sums[2],
        sums[3], scatter(grad_w_up, 0), grad_up_bias, scatter(grad_w_down, 1), sums[4],
    )


MESH = pl.DeviceIdType.MESH
SEQ = 8
HEAD = 4
LINE = 4
NEAR = 2 * SPAN - 1
QKV_KV, QKV_Q, OUT, UP, DOWN = range(5)
VMEM_BYTES = 60 * 1024 * 1024


def al(value, multiple):
    return pl.multiple_of(value, multiple)


def fused_kernel(names, *refs):
    r = types.SimpleNamespace(**dict(zip(names, refs)))
    s, h = lax.axis_index("seq"), lax.axis_index("head")
    z, y, x, c = lax.div(s, 2), lax.rem(s, 2), lax.div(h, 2), lax.rem(h, 2)
    e = lax.rem(z, 2)
    pair_z = z + 1 - 2 * e
    mate = z * 2 + 1 - y
    pair = pair_z * 2 + y
    twin = x * 2 + 1 - c
    across = (1 - x) * 2 + c
    tokens, width = r.tok.shape
    quarter = tokens // HEAD
    head_w = r.qs.shape[1]
    rows = r.wq.shape[1]
    half = r.wu_all.shape[1]
    sent = []

    def copy(src, dst, ss, rs, **where):
        return pltpu.make_async_remote_copy(
            src_ref=src, dst_ref=dst, send_sem=ss, recv_sem=rs, device_id=where,
            device_id_type=MESH,
        )

    def when(cond, then):
        if cond is None:
            then()
        else:
            pl.when(cond)(lambda: then())

    def send(cond, *args, **where):
        one = copy(*args, **where)
        when(cond, one.start)
        sent.append((cond, one))

    def arrived(cond, dst, rs, like=None):
        when(cond, copy(dst if like is None else like, dst, r.v_ss.at[0], rs, seq=mate).wait_recv)

    barrier = pltpu.get_barrier_semaphore()
    greeted = [{"seq": lax.rem(s + d, SEQ)} for d in range(1, SEQ)]
    greeted += [{"head": lax.rem(h + d, HEAD)} for d in range(1, HEAD)]
    greeted += [{"seq": pair, "head": across}]
    for where in greeted:
        pl.semaphore_signal(barrier, inc=1, device_id=where, device_id_type=MESH)
    for k, ref in enumerate((r.g1, r.b1, r.g2, r.b2, r.b3)):
        r.vec[k : k + 1, :] = ref[...].reshape(1, rows).astype(F32)
    r.vec[5:8, :] = jnp.zeros((3, rows), F32)
    pl.semaphore_wait(barrier, len(greeted))

    def cols(o, size):
        return pl.ds(al(o * size, size), size)

    relay_slot = [
        lambda o: r.wq_all.at[1:3, cols(o, rows), :],
        lambda o: r.wq_all.at[0, cols(o, rows), :],
        lambda o: r.wo_all.at[:, cols(o, rows)],
    ]
    relay_src = [r.wq.at[1:3], r.wq.at[0], r.wo]

    def relay_start(w):
        src, dst, rs = relay_src[w], relay_slot[w](s), r.g_rs.at[w, s]
        send(z < LINE - 1, src, dst, r.g_ss.at[w, 0], rs, seq=s + 2)
        send(z > 0, src, dst, r.g_ss.at[w, 4], rs, seq=s - 2)
        send(None, src, dst, r.g_ss.at[w, 8], rs, seq=mate)

    def relay_round(w, k):
        for sign, first, third in ((-1, 0, 8 + k), (1, 4, 11 + k)):
            from_z = z + sign * k
            there = (from_z >= 0) & (from_z < LINE)
            o = jnp.clip(from_z, 0, LINE - 1) * 2 + y
            ref, rs = relay_slot[w](o), r.g_rs.at[w, o]
            arrived(there, ref, rs)
            onward = (z < LINE - 1) if sign < 0 else (z > 0)
            send(there & onward, ref, ref, r.g_ss.at[w, first + k], rs, seq=s - 2 * sign)
            send(there, ref, ref, r.g_ss.at[w, third], rs, seq=mate)

    def relay_finish(w):
        for d in range(LINE):
            o = lax.rem(z + d, LINE) * 2 + 1 - y
            arrived(None, relay_slot[w](o), r.g_rs.at[w, o])

    low, high = z > 0, z < LINE - 1
    from_mate = 4 - 2 * y

    def token_rows(slot, head):
        return r.nall.at[slot, cols(head, quarter), :]

    def token_send(cond, slot, back, k, to):
        send(cond, token_rows(slot, h), token_rows(back, h), r.t_ns.at[k], r.t_rs.at[back, h], seq=to)

    def token_share(cond, slot):
        ref = token_rows(slot, h)
        arrived(cond, ref, r.t_rs.at[slot, h])
        send(cond, ref, ref, r.t_ss.at[slot, 0], r.t_rs.at[slot, h], head=across)
        send(cond, ref, ref, r.t_ss.at[slot, 1], r.t_rs.at[slot, h], head=twin)

    def token_pass(cond, slot):
        ref = token_rows(slot, across)
        arrived(cond, ref, r.t_rs.at[slot, across])
        send(cond, ref, ref, r.t_ss.at[slot, 2], r.t_rs.at[slot, across], head=twin)

    def token_ready(cond, slot):
        arrived(cond, token_rows(slot, twin), r.t_rs.at[slot, twin])
        other = (1 - x) * 2 + 1 - c
        arrived(cond, token_rows(slot, other), r.t_rs.at[slot, other])

    far_in = jnp.where(y == 0, z >= 2, z <= 1)
    far_slot = 6 * y
    slots = (
        (None, from_mate), (low, 1), (high, 5), (low, 2 - 2 * y), (high, 6 - 2 * y),
        (far_in, far_slot),
    )
    for d in range(1, SEQ):
        send(
            None, r.vec, r.gains.at[:, cols(s, rows)], r.v_ss.at[d - 1], r.v_rs.at[s],
            seq=lax.rem(s + d, SEQ),
        )
    relay_start(0)
    r.gains[:, cols(s, rows)] = r.vec[...]
    for k in range(NEAR):
        other = s + k - (SPAN - 1)

        @pl.when((other < 0) | (other >= SEQ))
        def _():
            r.nall[k] = jnp.zeros(r.nall.shape[1:], BF16)

    for k, cond in enumerate((low & high, high, low, high, low)):

        @pl.when(jnp.logical_not(cond))
        def _():
            r.dkv_recv[k] = jnp.zeros(r.dkv_recv.shape[1:], BF16)

    for d in range(1, SEQ):
        o = lax.rem(s + d, SEQ)
        arrived(None, r.gains.at[:, cols(o, rows)], r.v_rs.at[o], r.vec)

    def normalise(q):
        xhat, _ = norm_parts(r.tok[q, :].astype(F32))
        r.nall[SPAN - 1, q, :] = (xhat * r.gains[0:1, :] + r.gains[1:2, :]).astype(BF16)

    normalise(cols(h, quarter))
    token_send(None, SPAN - 1, 2 + 2 * y, 0, mate)
    token_send(high, SPAN - 1, 1, 1, s + 2)
    token_send(low, SPAN - 1, 5, 2, s - 2)
    for d in range(1, HEAD):
        normalise(cols(lax.rem(h + d, HEAD), quarter))
    token_share(*slots[0])
    token_send(high, from_mate, 2 - 2 * y, 3, s + 2)
    token_send(low, from_mate, 6 - 2 * y, 4, s - 2)
    relay_round(0, 1)
    token_share(*slots[1])
    token_share(*slots[2])
    r.wq_all[:, cols(s, rows), :] = r.wq[...]
    r.wo_all[:, cols(s, rows)] = r.wo[...]
    token_share(*slots[3])
    token_share(*slots[4])
    token_send((y == 0) & low & high, 2, 0, 5, s + 2)
    token_send((y == 1) & low & high, 4, 6, 5, s - 2)
    relay_round(0, 2)
    relay_start(1)
    relay_round(0, 3)
    token_share(*slots[5])
    for cond, slot in slots[:3]:
        token_pass(cond, slot)
    relay_round(1, 1)
    relay_start(2)

    start, leader, span, pad = 0, 0, 0, 0
    for k in range(r.units.shape[0]):
        here = r.units[k]
        inside = (s >= start) & (s < start + here)
        leader = jnp.where(inside, start, leader)
        span = jnp.where(inside, here, span)
        pad = jnp.where(inside, r.pads[k], pad)
        start = start + here
    position = s - leader
    root = jnp.clip(SPAN - 1 - position, 0, SPAN - 1)
    total = span * BLK_DEV
    live = span * tokens - pad

    columns = lax.broadcasted_iota(jnp.int32, (1, SPAN * tokens), 1)
    usable = columns < live
    blocks = lax.div(columns, BLK)
    for hh in range(HEAD):
        for b in range(BLK_DEV):
            query = position * BLK_DEV + b
            count = jnp.zeros((1, SPAN * tokens), F32)
            for wanted in (query - 1, query, query + 1, 0, total - 1):
                count = count + jnp.where(blocks == wanted, 1.0, 0.0)
            for k in range(r.picks.shape[0]):
                raw = r.picks[k, b, hh]
                chosen = lax.rem(raw, BLK_DEV)
                for k_units in range(2, SPAN + 1):
                    chosen = jnp.where(span == k_units, lax.rem(raw, BLK_DEV * k_units), chosen)
                count = count + jnp.where(blocks == chosen, 1.0, 0.0)
            count = jnp.where((query == 0) | (query == total - 1), 1.0, count)
            held = usable & (count > 0)
            bias = jnp.log(jnp.maximum(count, 1.0))
            r.bias[hh, b : b + 1, :] = jnp.where(held, bias, NEGATIVE)

    ffn_src = {
        UP: lambda k: r.wu.at[:, cols(k, half)],
        DOWN: lambda k: r.wd.at[cols(k, half), :],
    }
    ffn_slot = {
        UP: lambda o: r.wu_all.at[cols(o, rows), :],
        DOWN: lambda o: r.wd_all.at[:, cols(o, rows)],
    }

    def ffn_start(w):
        i = w - UP
        for d in range(1, LINE):
            to = lax.rem(z + d, LINE)
            send(
                None, ffn_src[w](lax.rem(to, 2)), ffn_slot[w](s), r.f_ss.at[i, d - 1],
                r.f_rs.at[i, s], seq=to * 2 + y,
            )
        send(
            None, ffn_src[w](e), ffn_slot[w](s), r.f_ss.at[i, 3], r.f_rs.at[i, s], seq=mate
        )

    def ffn_forward(w):
        i = w - UP
        for d in range(1, LINE):
            o = lax.rem(z + LINE - d, LINE) * 2 + y
            ref = ffn_slot[w](o)
            arrived(None, ref, r.f_rs.at[i, o])
            send(None, ref, ref, r.f_ss.at[i, 3 + d], r.f_rs.at[i, o], seq=mate)

    def ffn_finish(w):
        for d in range(LINE):
            o = lax.rem(z + d, LINE) * 2 + 1 - y
            arrived(None, ffn_slot[w](o), r.f_rs.at[w - UP, o])

    ffn_start(UP)
    relay_round(1, 2)
    relay_round(1, 3)
    for cond, slot in slots[3:]:
        token_pass(cond, slot)
    for ref, src in ((ffn_slot[UP](s), ffn_src[UP](e)), (ffn_slot[DOWN](s), ffn_src[DOWN](e))):
        ref[...] = src[...]

    ffn_start(DOWN)
    for cond, slot in slots:
        token_ready(cond, slot)
    relay_finish(0)
    scaling = HEAD_DIM ** (-0.5)
    for j in range(SPAN):
        q = pl.ds(j * tokens, tokens)
        rows_in = r.nall[root + j]
        r.kwin[q, :] = dot(rows_in, r.wq_all[1], ((1,), (0,))).astype(BF16)
        r.vwin[q, :] = dot(rows_in, r.wq_all[2], ((1,), (0,))).astype(BF16)
    relay_finish(1)
    part = dot(r.nall[SPAN - 1], r.wq_all[0], ((1,), (0,)))
    r.qs[...] = (part.astype(BF16).astype(F32) * scaling).astype(BF16)
    for k in range(1, LINE):
        relay_round(2, k)

    half_t = tokens // 2
    r.cotx[cols(e, tokens), :] = r.cot[...]

    def cot_rows(unit, core):
        return r.cotx.at[pl.ds(al(unit * tokens + core * half_t, half_t), half_t), :]

    send(None, r.cot.at[cols(c, half_t), :], cot_rows(e, c), r.c_ss.at[0], r.c_rs.at[0], seq=pair)
    ffn_forward(UP)

    lanes = lax.div(lax.broadcasted_iota(jnp.int32, (1, head_w), 1), HEAD_DIM)
    none = jnp.zeros((), BF16)
    r.att[...] = jnp.zeros(r.att.shape, F32)

    def attend(hh, carry):
        mine = lanes == hh
        query = jnp.where(mine, r.qs[...], none)
        for j in range(SPAN):
            k = pl.ds(j * tokens, tokens)
            r.lg[:, k] = dot(query, r.kwin[k, :], ((1,), (1,)))
        for b in range(BLK_DEV):
            q = pl.ds(b * BLK, BLK)
            logits = r.lg[q, :] + r.bias[hh, b : b + 1, :]
            grown = jnp.exp(logits - jnp.max(logits, axis=-1, keepdims=True))
            scale = 1.0 / jnp.sum(grown, axis=-1, keepdims=True)
            r.prob[hh, q, :] = (grown * scale).astype(BF16)
        part = dot(r.prob[hh], r.vwin[...], ((1,), (0,)))
        r.att[...] += jnp.where(mine, part, 0.0)
        return carry

    lax.fori_loop(0, HEAD, attend, 0)
    r.att_low[...] = r.att[...].astype(BF16)
    relay_finish(2)

    beyond = (1 - x) * 2 + 1 - c

    def rows_of(k):
        return cols(k, quarter)

    def reduce_start(op):
        for v in range(2):
            r.q1_send[op, v] = r.sum_f[rows_of(v * 2 + 1 - c), :].astype(BF16)
        send(None, r.q1_send.at[op], r.q1_recv.at[op], r.q1_ss.at[op], r.q1_rs.at[op], head=twin)

    def reduce_middle(op):
        arrived(None, r.q1_recv.at[op], r.q1_rs.at[op])
        block = r.sum_f[rows_of(across), :] + r.q1_recv[op, 1 - x].astype(F32)
        r.q2_send[op] = block.astype(BF16)
        send(None, r.q2_send.at[op], r.q2_recv.at[op], r.q2_ss.at[op], r.q2_rs.at[op], head=across)
        r.q_own[op] = r.sum_f[rows_of(h), :] + r.q1_recv[op, x].astype(F32)

    def reduce_finish(op):
        arrived(None, r.q2_recv.at[op], r.q2_rs.at[op])
        return r.q_own[op] + r.q2_recv[op].astype(F32)

    def spread_start(op, whole, value):
        whole[rows_of(h), :] = value
        ref = whole.at[rows_of(h), :]
        send(None, ref, ref, r.ag_ss.at[op, 0], r.ag_rs.at[op, h], head=across)
        send(None, ref, ref, r.ag_ss.at[op, 1], r.ag_rs.at[op, h], head=twin)

    def spread_pass(op, whole):
        ref = whole.at[rows_of(across), :]
        arrived(None, ref, r.ag_rs.at[op, across])
        send(None, ref, ref, r.ag_ss.at[op, 2], r.ag_rs.at[op, across], head=twin)

    def spread_finish(op, whole):
        for o in (twin, beyond):
            arrived(None, whole.at[rows_of(o), :], r.ag_rs.at[op, o])

    def block_rows(unit, head):
        return pl.ds(al(unit * tokens + head * quarter, quarter), quarter)

    def pair_start(op):
        for u in range(2):
            for v in range(2):
                block = r.sum_f[block_rows(u, v * 2 + 1 - c), :]
                r.p1_send[op, u * 2 + v] = block.astype(BF16)
        send(None, r.p1_send.at[op], r.p1_recv.at[op], r.p1_ss.at[op], r.p1_rs.at[op], head=twin)

    def pair_middle(op):
        arrived(None, r.p1_recv.at[op], r.p1_rs.at[op])
        for du, dv in ((1, 1), (1, 0), (0, 1), (0, 0)):
            u, v = lax.rem(e + du, 2), lax.rem(x + dv, 2)
            block = r.sum_f[block_rows(u, v * 2 + c), :] + r.p1_recv[op, u * 2 + v].astype(F32)
            if du or dv:
                k = u * 2 + v
                r.p2_send[op, k] = block.astype(BF16)
                send(
                    None, r.p2_send.at[op, k], r.p2_recv.at[op, e * 2 + x], r.p2_ss.at[op, k],
                    r.p2_rs.at[op, e * 2 + x], seq=pair if du else s, head=across if dv else h,
                )
            else:
                r.p_own[op] = block

    def pair_finish(op):
        result = r.p_own[op]
        for du, dv in ((0, 1), (1, 0), (1, 1)):
            k = lax.rem(e + du, 2) * 2 + lax.rem(x + dv, 2)
            arrived(None, r.p2_recv.at[op, k], r.p2_rs.at[op, k])
            result = result + r.p2_recv[op, k].astype(F32)
        return result

    def tiled(n, body):
        def step(j, carry):
            body(al(j * 256, 256))
            return carry

        lax.fori_loop(0, n // 256, step, 0)

    def out_tile(k):
        k = pl.ds(k, 256)
        r.sum_f[:tokens, k] = dot(r.att_low[...], r.wo_all[:, k], ((1,), (0,)))

    tiled(width, out_tile)
    reduce_start(0)
    reduce_middle(0)
    arrived(None, cot_rows(1 - e, c), r.c_rs.at[0])
    send(
        None, cot_rows(1 - e, c), cot_rows(1 - e, c), r.c_ss.at[1], r.c_rs.at[1], head=twin
    )
    ffn_forward(DOWN)
    middle = r.tok[rows_of(h), :].astype(F32) + reduce_finish(0)
    r.mid_own[...] = middle
    xhat, _ = norm_parts(middle)

    def n2_rows(unit, head):
        return r.n2x.at[block_rows(unit, head), :]

    r.n2x[block_rows(e, h), :] = (xhat * r.gains[2:3, :] + r.gains[3:4, :]).astype(BF16)
    mine, tag = n2_rows(e, h), e * 4 + h
    send(None, mine, mine, r.n2_ss.at[0], r.n2_rs.at[tag], head=across)
    send(None, mine, mine, r.n2_ss.at[1], r.n2_rs.at[tag], seq=pair, head=across)
    send(None, mine, mine, r.n2_ss.at[2], r.n2_rs.at[tag], seq=pair)
    send(None, mine, mine, r.n2_ss.at[3], r.n2_rs.at[tag], head=twin)
    ffn_finish(UP)
    ffn_finish(DOWN)
    for k, (unit, head) in enumerate(((e, across), (1 - e, h), (1 - e, across))):
        ref, tag = n2_rows(unit, head), unit * 4 + head
        arrived(None, ref, r.n2_rs.at[tag])
        send(None, ref, ref, r.n2_ss.at[4 + k], r.n2_rs.at[tag], head=twin)
    for unit in (e, 1 - e):
        for head in (x * 2 + 1 - c, (1 - x) * 2 + 1 - c):
            arrived(None, n2_rows(unit, head), r.n2_rs.at[unit * 4 + head])
    arrived(None, cot_rows(1 - e, 1 - c), r.c_rs.at[1])

    root_c = (2.0 / 3.141592653589793) ** 0.5
    r.up_send[half // 128 :, :] = jnp.zeros((8 - half // 128, 128), F32)
    for j in range(half // 256):
        f = pl.ds(j * 256, 256)
        bias = r.upb[:, pl.ds(al(e * half + j * 256, 256), 256)].astype(F32)
        v = dot(r.n2x[...], r.wu_all[:, f], ((1,), (0,))) + bias
        t = jnp.tanh(root_c * (v + 0.044715 * (v * v * v)))
        r.hid[:, f] = (0.5 * v * (1.0 + t)).astype(BF16)
        slope = 0.5 * (1.0 + t) + 0.5 * v * (1.0 - t * t) * (root_c * (1.0 + 0.134145 * v * v))
        low_p = (dot(r.cotx[...], r.wd_all[f, :], ((1,), (1,))) * slope).astype(BF16)
        r.gp[:, f] = low_p
        sums = jnp.sum(low_p.astype(F32), axis=0, keepdims=True)
        r.up_send[2 * j : 2 * j + 1, :] = sums[:, :128]
        r.up_send[2 * j + 1 : 2 * j + 2, :] = sums[:, 128:]

    def gn2_tile(k):
        k = pl.ds(k, 256)
        r.sum_f[:, k] = dot(r.gp[...], r.wu_all[k, :], ((1,), (1,)))

    tiled(width, gn2_tile)
    pair_start(0)

    grad_send = {QKV_KV: r.skv, QKV_Q: r.sq, OUT: r.so, UP: r.su, DOWN: r.sd}
    grad_arrive = {QKV_KV: r.akv, QKV_Q: r.aq, OUT: r.ao, UP: r.au, DOWN: r.ad}
    grad_again = {QKV_KV: r.bkv, QKV_Q: r.bq, OUT: r.bo, UP: r.bu, DOWN: r.bd}
    grad_final = {QKV_KV: r.rkv, QKV_Q: r.rq, OUT: r.ro, UP: r.ru, DOWN: r.rd}

    def tile_of(i):
        return lax.rem(z + 1 + i, LINE)

    def grad_cross(w, zz):
        send(
            None, grad_send[w].at[zz * 2 + 1 - y], grad_arrive[w].at[zz], r.ra_ss.at[w, zz],
            r.ra_rs.at[w, zz], seq=mate,
        )

    def grad_along(w, ks=(1, 2, 3)):
        for d in ks:
            zz = lax.rem(z + d, LINE)
            arrived(None, grad_arrive[w].at[zz], r.ra_rs.at[w, zz])
            both = grad_send[w][zz * 2 + y].astype(F32) + grad_arrive[w][zz].astype(F32)
            grad_again[w][zz] = both.astype(BF16)
            send(
                None, grad_again[w].at[zz], grad_final[w].at[z], r.rb_ss.at[w, zz],
                r.rb_rs.at[w, z], seq=zz * 2 + y,
            )

    def grad_own(w):
        arrived(None, grad_arrive[w].at[z], r.ra_rs.at[w, z])
        return grad_send[w][z * 2 + y].astype(F32) + grad_arrive[w][z].astype(F32)

    def grad_from(w, o):
        arrived(None, grad_final[w].at[o], r.rb_rs.at[w, o])
        return grad_final[w][o].astype(F32)

    def grad_sum(w):
        result = grad_own(w)
        for d in range(1, LINE):
            result = result + grad_from(w, lax.rem(z + d, LINE))
        return result

    def grad_halves(w):
        same = grad_own(w) + grad_from(w, lax.rem(z + 2, LINE))
        other = grad_from(w, lax.rem(z + 1, LINE)) + grad_from(w, lax.rem(z + 3, LINE))
        return same, other

    def down_step(i):
        zz = tile_of(i)
        part = dot(r.hid[...], r.cotx[:, cols(zz, 256)], ((0,), (0,))).astype(BF16)
        r.sd[zz * 2] = part[:, :rows]
        r.sd[zz * 2 + 1] = part[:, rows:]
        grad_cross(DOWN, zz)

    def up_step(i):
        zz = tile_of(i)
        part = dot(r.n2x[:, cols(zz, 256)], r.gp[...], ((0,), (0,))).astype(BF16)
        r.su[zz * 2] = part[:rows]
        r.su[zz * 2 + 1] = part[rows:]
        grad_cross(UP, zz)

    down_step(0)
    down_step(1)
    pair_middle(0)
    down_step(2)
    down_step(3)
    for i in range(LINE):
        up_step(i)
    for d in range(1, SEQ):
        send(
            None, r.up_send, r.up_recv.at[s], r.up_ss.at[d], r.up_rs.at[s],
            seq=lax.rem(s + d, SEQ),
        )

    grad_two = pair_finish(0)
    xhat, inverse = norm_parts(r.mid_own[...])
    dy = r.cot[rows_of(h), :].astype(F32)
    grad_mid = dy + norm_backward(xhat, inverse, grad_two * r.gains[2:3, :])
    r.gm_own[...] = grad_mid
    spread_start(0, r.gb, grad_mid.astype(BF16))
    r.sm_send[2:3, :] = jnp.sum(grad_two * xhat, axis=0, keepdims=True)
    r.sm_send[3:4, :] = jnp.sum(grad_two, axis=0, keepdims=True)
    r.sm_send[4:5, :] = jnp.sum(dy, axis=0, keepdims=True)
    r.sm_send[5:8, :] = jnp.zeros((3, width), F32)

    def down_tile(k):
        k = pl.ds(k, 256)
        r.sum_f[:, k] = dot(r.hid[...], r.wd_all[:, k], ((1,), (0,)))

    tiled(width, down_tile)
    pair_start(1)
    grad_along(DOWN)
    pair_middle(1)
    spread_pass(0, r.gb)
    spread_finish(0, r.gb)
    r.gatt[...] = dot(r.gb[...], r.wo_all[...], ((1,), (1,))).astype(BF16)
    for i in range(LINE):
        zz = tile_of(i)
        part = dot(r.att_low[...], r.gb[:, cols(zz, 256)], ((0,), (0,))).astype(BF16)
        r.so[zz * 2] = part[:, :rows]
        r.so[zz * 2 + 1] = part[:, rows:]
        grad_cross(OUT, zz)
    grad_along(UP, (1, 2))

    r.dq[...] = jnp.zeros(r.dq.shape, F32)
    r.dk[...] = jnp.zeros(r.dk.shape, F32)
    r.dv[...] = jnp.zeros(r.dv.shape, F32)

    def attend_back(hh, carry):
        mine = lanes == hh
        query = jnp.where(mine, r.qs[...], none)
        grad = jnp.where(mine, r.gatt[...], none)
        for j in range(SPAN):
            k = pl.ds(j * tokens, tokens)
            r.lg[:, k] = dot(grad, r.vwin[k, :], ((1,), (1,)))
        for b in range(BLK_DEV):
            q = pl.ds(b * BLK, BLK)
            chance, grown = r.prob[hh, q, :].astype(F32), r.lg[q, :]
            inner = jnp.sum(chance * grown, axis=-1, keepdims=True)
            r.ds[q, :] = (chance * (grown - inner)).astype(BF16)
        r.dq[...] += jnp.where(mine, dot(r.ds[...], r.kwin[...], ((1,), (0,))), 0.0)
        for j in range(SPAN):
            k = pl.ds(j * tokens, tokens)
            r.dk[k, :] += dot(r.ds[:, k], query, ((0,), (0,)))
            r.dv[k, :] += dot(r.prob[hh, :, k], grad, ((0,), (0,)))
        return carry

    lax.fori_loop(0, HEAD, attend_back, 0)
    for k in range(2 * (SPAN - 1) + SPAN):
        j = k - (SPAN - 1)
        if 0 <= j < SPAN:
            q = pl.ds(j * tokens, tokens)
            r.dkv_pad[k, :, :head_w] = r.dk[q, :].astype(BF16)
            r.dkv_pad[k, :, head_w:] = r.dv[q, :].astype(BF16)
        else:
            r.dkv_pad[k] = jnp.zeros(r.dkv_pad.shape[1:], BF16)
    for k in range(NEAR):
        r.dkv_send[k] = r.dkv_pad[k + SPAN - 1 - root]
    r.gtq[...] = (r.dq[...] * scaling).astype(BF16)

    def grad_hop(cond, slot, into, k, to):
        send(cond, r.dkv_send.at[slot], r.dkv_recv.at[into], r.dkv_ss.at[k], r.dkv_rs.at[into], seq=to)

    def add_to(slot, *froms):
        both = r.dkv_send[slot].astype(F32)
        for k in froms:
            both = both + r.dkv_recv[k].astype(F32)
        r.dkv_send[slot] = both.astype(BF16)

    def grad_wait(cond, into):
        arrived(cond, r.dkv_recv.at[into], r.dkv_rs.at[into])

    FAR, ABOVE, BELOW, LINE_ABOVE, LINE_BELOW, MATE = range(6)
    grad_hop((y == 0) & (z >= 2), 0, FAR, 0, s - 2)
    grad_hop((y == 1) & (z <= 1), 6, FAR, 0, s + 2)
    grad_hop((y == 0) & high, 6, BELOW, 1, s + 2)
    grad_hop((y == 1) & low, 0, ABOVE, 1, s - 2)

    grad_along(UP, (3,))

    for i in range(LINE):
        zz = tile_of(i)
        part = jnp.zeros((256, 2 * head_w), F32)
        for j in range(SPAN):
            part = part + dot(
                r.nall[root + j, :, cols(zz, 256)], r.dkv_pad[j + SPAN - 1], ((0,), (0,))
            )
        part = part.astype(BF16)
        for v in range(2):
            for k in range(2):
                r.skv[zz * 2 + v, k] = part[v * rows : (v + 1) * rows, k * head_w : (k + 1) * head_w]
        grad_cross(QKV_KV, zz)
        if i == 1:
            grad_wait(low & high, FAR)
            add_to(2 + 2 * y, FAR)
            grad_hop((y == 0) & low, 2, ABOVE, 2, s - 2)
            grad_hop((y == 1) & high, 4, BELOW, 2, s + 2)
            grad_hop(low, 1, LINE_ABOVE, 3, s - 2)
            grad_hop(high, 5, LINE_BELOW, 4, s + 2)
    grad_wait(high, ABOVE)
    grad_wait(low, BELOW)
    add_to(from_mate, ABOVE, BELOW)
    grad_hop(None, from_mate, MATE, 5, mate)
    for i in range(LINE):
        zz = tile_of(i)
        part = dot(r.nall[SPAN - 1, :, cols(zz, 256)], r.gtq[...], ((0,), (0,))).astype(BF16)
        r.sq[zz * 2] = part[:rows]
        r.sq[zz * 2 + 1] = part[rows:]
        grad_cross(QKV_Q, zz)
    grad_along(OUT)
    grad_along(QKV_KV)
    ffn = pair_finish(1)
    spread_start(1, r.out_o, (r.mid_own[...] + ffn + r.gains[4:5, :]).astype(BF16))
    grad_wait(high, LINE_ABOVE)
    grad_wait(low, LINE_BELOW)
    grad_wait(None, MATE)
    whole = r.dkv_send[SPAN - 1].astype(F32)
    for k in (LINE_ABOVE, LINE_BELOW, MATE):
        whole = whole + r.dkv_recv[k].astype(F32)
    r.gtkv[...] = whole.astype(BF16)

    def gn1_tile(k):
        k = pl.ds(k, 256)
        r.sum_f[:tokens, k] = (
            dot(r.gtq[...], r.wq_all[0, k, :], ((1,), (1,)))
            + dot(r.gtkv[:, :head_w], r.wq_all[1, k, :], ((1,), (1,)))
            + dot(r.gtkv[:, head_w:], r.wq_all[2, k, :], ((1,), (1,)))
        )

    tiled(width, gn1_tile)
    reduce_start(1)
    reduce_middle(1)
    grad_along(QKV_Q)
    grad_one = reduce_finish(1)
    xhat, inverse = norm_parts(r.tok[rows_of(h), :].astype(F32))
    r.sm_send[0:1, :] = jnp.sum(grad_one * xhat, axis=0, keepdims=True)
    r.sm_send[1:2, :] = jnp.sum(grad_one, axis=0, keepdims=True)
    for d in range(1, SEQ):
        to = lax.rem(s + d, SEQ)
        send(
            None, r.sm_send.at[:, cols(to, rows)], r.sm_recv.at[s], r.sm_ss.at[d], r.sm_rs.at[s],
            seq=to,
        )
    spread_pass(1, r.out_o)
    grad_x = r.gm_own[...] + norm_backward(xhat, inverse, grad_one * r.gains[0:1, :])
    spread_start(2, r.xgb, grad_x.astype(BF16))

    same, other = grad_halves(DOWN)
    r.gd_o[cols(e, half), :] = same
    r.gd_o[cols(1 - e, half), :] = other
    same, other = grad_halves(UP)
    r.gu_o[:, cols(e, half)] = same
    r.gu_o[:, cols(1 - e, half)] = other
    spread_pass(2, r.xgb)
    r.go_o[...] = grad_sum(OUT)

    r.sm_recv[s] = r.sm_send[:, cols(s, rows)]
    r.up_recv[s] = r.up_send[...]
    for d in range(1, SEQ):
        o = lax.rem(s + d, SEQ)
        arrived(None, r.sm_recv.at[o], r.sm_rs.at[o], r.vec)
        arrived(None, r.up_recv.at[o], r.up_rs.at[o])
    part = r.sm_recv[0]
    for o in range(1, SEQ):
        part = part + r.sm_recv[o]
    r.sm_own[...] = part
    for d in range(1, HEAD):
        send(
            None, r.sm_own, r.sm_two.at[h], r.sm2_ss.at[d], r.sm2_rs.at[h],
            head=lax.rem(h + d, HEAD),
        )
    r.sm_two[h] = part
    tall = half // 128
    for u in range(2):
        ups = jnp.zeros((tall, 128), F32)
        for o in range(SEQ):
            if (o // 2) % 2 == u:
                ups = ups + r.up_recv[o, :tall, :]
        r.small_o[8 + u * tall : 8 + (u + 1) * tall, :] = ups
    spread_finish(1, r.out_o)
    spread_finish(2, r.xgb)
    r.xg_o[...] = r.xgb[...].astype(F32)
    for d in range(1, HEAD):
        o = lax.rem(h + d, HEAD)
        arrived(None, r.sm_two.at[o], r.sm2_rs.at[o])
    r.small_o[0:8, :] = (r.sm_two[0] + r.sm_two[1]) + (r.sm_two[2] + r.sm_two[3])
    r.gq_o[0] = grad_sum(QKV_Q)
    r.gq_o[1:3] = grad_sum(QKV_KV)

    for cond, one in sent:
        when(cond, one.wait_send)


def local_fused(
    tokens, w_qkv, w_out, ln1_gain, ln1_bias, ln2_gain, ln2_bias, w_up, up_bias, w_down, down_bias,
    seq_units, seq_pad, rand_picks, cotangent,
):
    tok, width = tokens.shape
    rows, _, head_w = w_qkv.shape
    hidden = w_up.shape[1]
    half = hidden // 2
    quarter = tok // HEAD
    keys = SPAN * tok
    smem, vmem = pl.BlockSpec(memory_space=pltpu.SMEM), pl.BlockSpec(memory_space=pltpu.VMEM)
    ins = dict(
        units=seq_units, pads=seq_pad, picks=jnp.transpose(rand_picks, (2, 0, 1)), tok=tokens,
        cot=cotangent, wq=jnp.transpose(w_qkv, (1, 0, 2)), wo=w_out, wu=w_up, wd=w_down,
        g1=ln1_gain, b1=ln1_bias, g2=ln2_gain, b2=ln2_bias, b3=down_bias,
        upb=up_bias.reshape(1, hidden),
    )
    outs = dict(
        out_o=((tok, width), BF16), xg_o=((tok, width), F32), gq_o=((3, rows, head_w), F32),
        go_o=((head_w, rows), F32), gu_o=((rows, hidden), F32), gd_o=((hidden, rows), F32),
        small_o=((16, rows), F32),
    )
    scratch = dict(
        wq_all=((3, width, head_w), BF16), wo_all=((head_w, width), BF16),
        wu_all=((width, half), BF16), wd_all=((half, width), BF16), vec=((8, rows), F32),
        gains=((8, width), F32), nall=((NEAR, tok, width), BF16),
        qs=((tok, head_w), BF16),
        kwin=((keys, head_w), BF16), vwin=((keys, head_w), BF16), lg=((tok, keys), F32),
        prob=((HEAD, tok, keys), BF16), ds=((tok, keys), BF16),
        att=((tok, head_w), F32), att_low=((tok, head_w), BF16), n2x=((2 * tok, width), BF16),
        cotx=((2 * tok, width), BF16), hid=((2 * tok, half), BF16), gp=((2 * tok, half), BF16),
        gb=((tok, width), BF16), xgb=((tok, width), BF16), mid_own=((quarter, width), F32),
        gm_own=((quarter, width), F32), gatt=((tok, head_w), BF16), dq=((tok, head_w), F32),
        dk=((keys, head_w), F32), dv=((keys, head_w), F32),
        dkv_pad=((NEAR + SPAN - 1, tok, 2 * head_w), BF16),
        dkv_send=((NEAR, tok, 2 * head_w), BF16), dkv_recv=((6, tok, 2 * head_w), BF16),
        gtq=((tok, head_w), BF16), gtkv=((tok, 2 * head_w), BF16),
        q1_send=((2, 2, quarter, width), BF16), q1_recv=((2, 2, quarter, width), BF16),
        q2_send=((2, quarter, width), BF16), q2_recv=((2, quarter, width), BF16),
        q_own=((2, quarter, width), F32),
        sum_f=((2 * tok, width), F32), bias=((HEAD, 8, keys), F32),
        p1_send=((2, 4, quarter, width), BF16), p1_recv=((2, 4, quarter, width), BF16),
        p2_send=((2, 4, quarter, width), BF16), p2_recv=((2, 4, quarter, width), BF16),
        p_own=((2, quarter, width), F32), sm_send=((8, width), F32),
        sm_recv=((SEQ, 8, rows), F32), sm_own=((8, rows), F32), sm_two=((HEAD, 8, rows), F32),
        up_send=((8, 128), F32), up_recv=((SEQ, 8, 128), F32),
    )
    shards = dict(
        kv=(2, rows, head_w), q=(rows, head_w), o=(head_w, rows), u=(rows, half), d=(half, rows)
    )
    for lead, count in (("s", SEQ), ("a", LINE), ("b", LINE), ("r", LINE)):
        for name, shape in shards.items():
            scratch[lead + name] = ((count,) + shape, BF16)
    semaphores = dict(
        g_ss=(3, 16), g_rs=(3, SEQ), f_ss=(2, 7), f_rs=(2, SEQ), v_ss=(7,), v_rs=(SEQ,),
        t_ns=(6,), t_ss=(NEAR, 3), t_rs=(NEAR, HEAD), dkv_ss=(6,), dkv_rs=(6,), c_ss=(2,), c_rs=(2,),
        q1_ss=(2,), q1_rs=(2,), q2_ss=(2,), q2_rs=(2,), ag_ss=(3, 3), ag_rs=(3, HEAD), n2_ss=(7,),
        n2_rs=(8,), p1_ss=(2,), p1_rs=(2,), p2_ss=(2, 4), p2_rs=(2, 4), ra_ss=(5, LINE),
        ra_rs=(5, LINE), rb_ss=(5, LINE), rb_rs=(5, LINE), sm_ss=(SEQ,), sm_rs=(SEQ,),
        sm2_ss=(HEAD,), sm2_rs=(HEAD,), up_ss=(SEQ,), up_rs=(SEQ,),
    )
    names = [*ins, *outs, *scratch, *semaphores]
    results = pl.pallas_call(
        functools.partial(fused_kernel, names),
        out_shape=[jax.ShapeDtypeStruct(*o) for o in outs.values()],
        in_specs=[smem] * 3 + [vmem] * (len(ins) - 3),
        out_specs=[vmem] * len(outs),
        scratch_shapes=[pltpu.VMEM(*v) for v in scratch.values()]
        + [pltpu.SemaphoreType.DMA(v) for v in semaphores.values()],
        compiler_params=pltpu.CompilerParams(
            collective_id=0, has_side_effects=True, vmem_limit_bytes=VMEM_BYTES
        ),
        name="fused_layer",
    )(*ins.values())
    large = list(outs.values())[:-1]
    handed = pl.pallas_call(
        hand_over_kernel,
        out_shape=[jax.ShapeDtypeStruct(*o) for o in large]
        + [jax.ShapeDtypeStruct((rows,), F32)] * 5
        + [jax.ShapeDtypeStruct((hidden,), F32)],
        in_specs=[vmem] * len(outs),
        out_specs=[vmem] * (len(large) + 6),
        name="hand_over",
    )(*results)
    out, xg, gq, go, gu, gd, g1, b1, g2, b2, b3, upg = handed
    return out, xg, jnp.transpose(gq, (1, 0, 2)), go, g1, b1, g2, b2, gu, upg, gd, b3


def hand_over_kernel(*refs):
    large = (len(refs) - 7) // 2
    small, vectors = refs[large], refs[2 * large + 1 :]
    for k in range(large):
        refs[large + 1 + k][...] = refs[k][...]
    for k in range(5):
        vectors[k][...] = small[k, :]
    for k in range(8):
        vectors[5][pl.ds(k * 128, 128)] = small[8 + k, :]


IN_SPECS = (
    P("seq", None), P("seq", None, "head"), P("head", "seq"), P("seq"), P("seq"), P("seq"),
    P("seq"), P("seq", "head"), P("head"), P("head", "seq"), P("seq"), P(), P(),
    P("seq", "head", None), P("seq", None),
)
OUT_SPECS = (
    P("seq", None), P("seq", None), P("seq", None, "head"), P("head", "seq"), P("seq"), P("seq"),
    P("seq"), P("seq"), P("seq", "head"), P("head"), P("head", "seq"), P("seq"),
)


def solution(mesh):
    fits = mesh.shape["seq"] == SEQ and mesh.shape["head"] == HEAD
    return jax.shard_map(
        local_fused if fits else local_general, mesh=mesh, in_specs=IN_SPECS,
        out_specs=OUT_SPECS, check_vma=False,
    )
```

```python
import functools
import types

import jax
import jax.numpy as jnp
from jax import lax
from jax.experimental import pallas as pl
from jax.experimental.pallas import tpu as pltpu
from jax.sharding import PartitionSpec as P

HEAD_DIM = 64
BLK = 64
SPAN = 4
BLK_DEV = 4
EPSILON = 1e-05
NEGATIVE = -1e30
F32 = jnp.float32
BF16 = jnp.bfloat16


def shifted(value, axis, steps):
    count = lax.axis_size(axis)
    first, last = max(0, -steps), min(count, count - steps)
    return lax.ppermute(value, axis, [(i, i + steps) for i in range(first, last)])


def norm_parts(features):
    average = jnp.mean(features, axis=-1, keepdims=True)
    centred = features - average
    spread = jnp.mean(centred * centred, axis=-1, keepdims=True)
    inverse = lax.rsqrt(spread + EPSILON)
    return centred * inverse, inverse


def norm_backward(xhat, inverse, scaled):
    first = jnp.mean(scaled, axis=-1, keepdims=True)
    second = jnp.mean(scaled * xhat, axis=-1, keepdims=True)
    return inverse * (scaled - first - xhat * second)


def dot(a, b, dims):
    return lax.dot_general(a, b, (dims, ((), ())), preferred_element_type=F32)


def sequence_place(seq_units, seq_pad):
    device = lax.axis_index("seq")
    start, leader, span, pad = 0, 0, 0, 0
    for k in range(seq_units.shape[0]):
        units = seq_units[k]
        inside = (device >= start) & (device < start + units)
        leader = jnp.where(inside, start, leader)
        span = jnp.where(inside, units, span)
        pad = jnp.where(inside, seq_pad[k], pad)
        start = start + units
    return device - leader, span, pad


def key_counts(position, span, picks):
    blocks = lax.broadcasted_iota(jnp.int32, (1, 1, SPAN * BLK_DEV), 2)
    query = position * BLK_DEV + lax.broadcasted_iota(jnp.int32, (BLK_DEV, 1, 1), 0)
    total = span * BLK_DEV
    count = jnp.zeros((BLK_DEV, picks.shape[1], SPAN * BLK_DEV), F32)
    for wanted in (query - 1, query, query + 1, 0, total - 1):
        count = count + (blocks == wanted).astype(F32)
    chosen = picks % total
    for r in range(picks.shape[2]):
        count = count + (blocks == chosen[:, :, r : r + 1]).astype(F32)
    return jnp.where((query == 0) | (query == total - 1), 1.0, count)


def local_general(
    tokens, w_qkv, w_out, ln1_gain, ln1_bias, ln2_gain, ln2_bias, w_up, up_bias, w_down, down_bias,
    seq_units, seq_pad, rand_picks, cotangent,
):
    tok, width = tokens.shape
    heads = w_qkv.shape[2] // HEAD_DIM
    rows = lambda v: lax.all_gather(v, "seq", axis=0, tiled=True)
    cols = lambda v: lax.all_gather(v, "seq", axis=1, tiled=True)
    vectors = jnp.stack([ln1_gain, ln1_bias, ln2_gain, ln2_bias, down_bias], axis=0)
    gain_one, shift_one, gain_two, shift_two, down_shift = [
        v[None].astype(F32) for v in cols(vectors)
    ]
    qkv = rows(w_qkv)
    out_w, up_w, down_w = cols(w_out), rows(w_up), cols(w_down)
    position, span, pad = sequence_place(seq_units, seq_pad)
    root = SPAN - 1 - position
    inputs = tokens.astype(F32)
    xhat_one, inv_one = norm_parts(inputs)
    normed = (xhat_one * gain_one + shift_one).astype(BF16)
    triple = jnp.einsum("td,dcf->tcf", normed, qkv, preferred_element_type=F32).astype(BF16)
    own = jnp.stack([triple[:, 1], triple[:, 2]], axis=0)
    pieces = [own if o == 0 else shifted(own, "seq", -o) for o in range(1 - SPAN, SPAN)]
    nearby = jnp.stack(pieces, axis=0)
    window = lax.dynamic_slice_in_dim(nearby, root, SPAN, 0)
    split = lambda v: v.reshape(v.shape[0], heads, HEAD_DIM)
    keys = split(window[:, 0].reshape(SPAN * tok, -1))
    values = split(window[:, 1].reshape(SPAN * tok, -1))
    queries = split(triple[:, 0])
    scaling = HEAD_DIM ** (-0.5)
    live = jnp.arange(SPAN * tok, dtype=jnp.int32) < span * tok - pad
    count = jnp.repeat(key_counts(position, span, rand_picks), BLK, axis=2)
    count = jnp.where(live[None, None], count, 0.0)
    count = jnp.transpose(jnp.repeat(count, BLK, axis=0), (1, 0, 2))
    logits = jnp.einsum("qhd,khd->hqk", queries, keys, preferred_element_type=F32) * scaling
    logits = jnp.where(count > 0, logits, NEGATIVE)
    grown = jnp.exp(logits - jnp.max(logits, axis=-1, keepdims=True)) * count
    chances = grown / jnp.sum(grown, axis=-1, keepdims=True)
    chances_low = chances.astype(BF16)
    attended = jnp.einsum("hqk,khd->qhd", chances_low, values, preferred_element_type=F32)
    attended = attended.astype(BF16).reshape(tok, heads * HEAD_DIM)
    middle = inputs + lax.psum(dot(attended, out_w, ((1,), (0,))), "head")
    xhat_two, inv_two = norm_parts(middle)
    normed_two = (xhat_two * gain_two + shift_two).astype(BF16)
    pre_act = dot(normed_two, up_w, ((1,), (0,))) + up_bias.astype(F32)[None]
    hidden, pull = jax.vjp(lambda v: jax.nn.gelu(v, approximate=True), pre_act)
    hidden = hidden.astype(BF16)
    ffn = lax.psum(dot(hidden, down_w, ((1,), (0,))).astype(BF16), "head").astype(F32)
    output = (middle + ffn + down_shift).astype(BF16)
    grad_out = cotangent.astype(F32)
    grad_w_down = dot(hidden, cotangent, ((0,), (0,)))
    grad_pre = pull(dot(cotangent, down_w, ((1,), (1,))))[0].astype(BF16)
    grad_w_up = dot(normed_two, grad_pre, ((0,), (0,)))
    grad_up_bias = lax.psum(jnp.sum(grad_pre.astype(F32), axis=0), "seq")
    grad_two = lax.psum(dot(grad_pre, up_w, ((1,), (1,))), "head")
    grad_middle = grad_out + norm_backward(xhat_two, inv_two, grad_two * gain_two)
    grad_branch = grad_middle.astype(BF16)
    grad_w_out = dot(attended, grad_branch, ((0,), (0,)))
    grad_att = split(dot(grad_branch, out_w, ((1,), (1,))).astype(BF16))
    grad_prob = jnp.einsum("qhd,khd->hqk", grad_att, values, preferred_element_type=F32)
    inner = jnp.sum(chances * grad_prob, axis=-1, keepdims=True)
    grad_logit = (chances * (grad_prob - inner)).astype(BF16)
    dq = scaling * jnp.einsum("hqk,khd->qhd", grad_logit, keys, preferred_element_type=F32)
    dk = scaling * jnp.einsum("hqk,qhd->khd", grad_logit, queries, preferred_element_type=F32)
    dv = jnp.einsum("hqk,qhd->khd", chances_low, grad_att, preferred_element_type=F32)
    part = jnp.stack([dk.reshape(SPAN, tok, -1), dv.reshape(SPAN, tok, -1)], axis=1)
    near = jnp.zeros((2 * SPAN - 1,) + part.shape[1:], F32)
    near = lax.dynamic_update_slice_in_dim(near, part, root, 0)
    owned = near[SPAN - 1]
    for offset in range(1 - SPAN, SPAN):
        if offset:
            owned = owned + shifted(near[offset + SPAN - 1], "seq", offset)
    owned = owned.astype(BF16)
    grad_triple = jnp.stack([dq.reshape(tok, -1).astype(BF16), owned[0], owned[1]], axis=1)
    grad_w_qkv = jnp.einsum("td,tcf->dcf", normed, grad_triple, preferred_element_type=F32)
    grad_one = lax.psum(
        jnp.einsum("tcf,dcf->td", grad_triple, qkv, preferred_element_type=F32), "head"
    )
    x_grad = grad_middle + norm_backward(xhat_one, inv_one, grad_one * gain_one)
    sums = jnp.stack(
        [
            jnp.sum(grad_one * xhat_one, axis=0), jnp.sum(grad_one, axis=0),
            jnp.sum(grad_two * xhat_two, axis=0), jnp.sum(grad_two, axis=0),
            jnp.sum(grad_out, axis=0),
        ],
        axis=0,
    )
    scatter = lambda v, d: lax.psum_scatter(v, "seq", scatter_dimension=d, tiled=True)
    sums = scatter(sums, 1)
    return (
        output, x_grad, scatter(grad_w_qkv, 0), scatter(grad_w_out, 1), sums[0], sums[1], sums[2],
        sums[3], scatter(grad_w_up, 0), grad_up_bias, scatter(grad_w_down, 1), sums[4],
    )


MESH = pl.DeviceIdType.MESH
SEQ = 8
HEAD = 4
LINE = 4
NEAR = 2 * SPAN - 1
QKV_KV, QKV_Q, OUT, UP, DOWN = range(5)
VMEM_BYTES = 60 * 1024 * 1024


def al(value, multiple):
    return pl.multiple_of(value, multiple)


def fused_kernel(names, *refs):
    r = types.SimpleNamespace(**dict(zip(names, refs)))
    s, h = lax.axis_index("seq"), lax.axis_index("head")
    z, y, x, c = lax.div(s, 2), lax.rem(s, 2), lax.div(h, 2), lax.rem(h, 2)
    e = lax.rem(z, 2)
    pair_z = z + 1 - 2 * e
    mate = z * 2 + 1 - y
    pair = pair_z * 2 + y
    twin = x * 2 + 1 - c
    across = (1 - x) * 2 + c
    tokens, width = r.tok.shape
    quarter = tokens // HEAD
    head_w = r.qs.shape[1]
    rows = r.wq.shape[1]
    half = r.wu_all.shape[1]
    sent = []

    def copy(src, dst, ss, rs, **where):
        return pltpu.make_async_remote_copy(
            src_ref=src, dst_ref=dst, send_sem=ss, recv_sem=rs, device_id=where,
            device_id_type=MESH,
        )

    def when(cond, then):
        if cond is None:
            then()
        else:
            pl.when(cond)(lambda: then())

    def send(cond, *args, **where):
        one = copy(*args, **where)
        when(cond, one.start)
        sent.append((cond, one))

    def arrived(cond, dst, rs, like=None):
        when(cond, copy(dst if like is None else like, dst, r.v_ss.at[0], rs, seq=mate).wait_recv)

    barrier = pltpu.get_barrier_semaphore()
    greeted = [{"seq": lax.rem(s + d, SEQ)} for d in range(1, SEQ)]
    greeted += [{"head": lax.rem(h + d, HEAD)} for d in range(1, HEAD)]
    greeted += [{"seq": pair, "head": across}]
    for where in greeted:
        pl.semaphore_signal(barrier, inc=1, device_id=where, device_id_type=MESH)
    for k, ref in enumerate((r.g1, r.b1, r.g2, r.b2, r.b3)):
        r.vec[k : k + 1, :] = ref[...].reshape(1, rows).astype(F32)
    r.vec[5:8, :] = jnp.zeros((3, rows), F32)
    pl.semaphore_wait(barrier, len(greeted))

    def cols(o, size):
        return pl.ds(al(o * size, size), size)

    relay_slot = [
        lambda o: r.wq_all.at[1:3, cols(o, rows), :],
        lambda o: r.wq_all.at[0, cols(o, rows), :],
        lambda o: r.wo_all.at[:, cols(o, rows)],
    ]
    relay_src = [r.wq.at[1:3], r.wq.at[0], r.wo]

    def relay_start(w):
        src, dst, rs = relay_src[w], relay_slot[w](s), r.g_rs.at[w, s]
        send(z < LINE - 1, src, dst, r.g_ss.at[w, 0], rs, seq=s + 2)
        send(z > 0, src, dst, r.g_ss.at[w, 4], rs, seq=s - 2)
        send(None, src, dst, r.g_ss.at[w, 8], rs, seq=mate)

    def relay_round(w, k):
        for sign, first, third in ((-1, 0, 8 + k), (1, 4, 11 + k)):
            from_z = z + sign * k
            there = (from_z >= 0) & (from_z < LINE)
            o = jnp.clip(from_z, 0, LINE - 1) * 2 + y
            ref, rs = relay_slot[w](o), r.g_rs.at[w, o]
            arrived(there, ref, rs)
            onward = (z < LINE - 1) if sign < 0 else (z > 0)
            send(there & onward, ref, ref, r.g_ss.at[w, first + k], rs, seq=s - 2 * sign)
            send(there, ref, ref, r.g_ss.at[w, third], rs, seq=mate)

    def relay_finish(w):
        for d in range(LINE):
            o = lax.rem(z + d, LINE) * 2 + 1 - y
            arrived(None, relay_slot[w](o), r.g_rs.at[w, o])

    low, high = z > 0, z < LINE - 1
    from_mate = 4 - 2 * y

    def token_rows(slot, head):
        return r.nall.at[slot, cols(head, quarter), :]

    def token_send(cond, slot, back, k, to):
        send(cond, token_rows(slot, h), token_rows(back, h), r.t_ns.at[k], r.t_rs.at[back, h], seq=to)

    def token_share(cond, slot):
        ref = token_rows(slot, h)
        arrived(cond, ref, r.t_rs.at[slot, h])
        send(cond, ref, ref, r.t_ss.at[slot, 0], r.t_rs.at[slot, h], head=across)
        send(cond, ref, ref, r.t_ss.at[slot, 1], r.t_rs.at[slot, h], head=twin)

    def token_pass(cond, slot):
        ref = token_rows(slot, across)
        arrived(cond, ref, r.t_rs.at[slot, across])
        send(cond, ref, ref, r.t_ss.at[slot, 2], r.t_rs.at[slot, across], head=twin)

    def token_ready(cond, slot):
        arrived(cond, token_rows(slot, twin), r.t_rs.at[slot, twin])
        other = (1 - x) * 2 + 1 - c
        arrived(cond, token_rows(slot, other), r.t_rs.at[slot, other])

    far_in = jnp.where(y == 0, z >= 2, z <= 1)
    far_slot = 6 * y
    slots = (
        (None, from_mate), (low, 1), (high, 5), (low, 2 - 2 * y), (high, 6 - 2 * y),
        (far_in, far_slot),
    )
    for d in range(1, SEQ):
        send(
            None, r.vec, r.gains.at[:, cols(s, rows)], r.v_ss.at[d - 1], r.v_rs.at[s],
            seq=lax.rem(s + d, SEQ),
        )
    relay_start(0)
    r.gains[:, cols(s, rows)] = r.vec[...]
    for k in range(NEAR):
        other = s + k - (SPAN - 1)

        @pl.when((other < 0) | (other >= SEQ))
        def _():
            r.nall[k] = jnp.zeros(r.nall.shape[1:], BF16)

    for k, cond in enumerate((low & high, high, low, high, low)):

        @pl.when(jnp.logical_not(cond))
        def _():
            r.dkv_recv[k] = jnp.zeros(r.dkv_recv.shape[1:], BF16)

    for d in range(1, SEQ):
        o = lax.rem(s + d, SEQ)
        arrived(None, r.gains.at[:, cols(o, rows)], r.v_rs.at[o], r.vec)

    def normalise(q):
        xhat, _ = norm_parts(r.tok[q, :].astype(F32))
        r.nall[SPAN - 1, q, :] = (xhat * r.gains[0:1, :] + r.gains[1:2, :]).astype(BF16)

    normalise(cols(h, quarter))
    token_send(None, SPAN - 1, 2 + 2 * y, 0, mate)
    token_send(high, SPAN - 1, 1, 1, s + 2)
    token_send(low, SPAN - 1, 5, 2, s - 2)
    for d in range(1, HEAD):
        normalise(cols(lax.rem(h + d, HEAD), quarter))
    token_share(*slots[0])
    token_send(high, from_mate, 2 - 2 * y, 3, s + 2)
    token_send(low, from_mate, 6 - 2 * y, 4, s - 2)
    relay_round(0, 1)
    token_share(*slots[1])
    token_share(*slots[2])
    r.wq_all[:, cols(s, rows), :] = r.wq[...]
    r.wo_all[:, cols(s, rows)] = r.wo[...]
    token_share(*slots[3])
    token_share(*slots[4])
    token_send((y == 0) & low & high, 2, 0, 5, s + 2)
    token_send((y == 1) & low & high, 4, 6, 5, s - 2)
    relay_round(0, 2)
    relay_start(1)
    relay_round(0, 3)
    token_share(*slots[5])
    for cond, slot in slots[:3]:
        token_pass(cond, slot)
    relay_round(1, 1)
    relay_start(2)

    start, leader, span, pad = 0, 0, 0, 0
    for k in range(r.units.shape[0]):
        here = r.units[k]
        inside = (s >= start) & (s < start + here)
        leader = jnp.where(inside, start, leader)
        span = jnp.where(inside, here, span)
        pad = jnp.where(inside, r.pads[k], pad)
        start = start + here
    position = s - leader
    root = jnp.clip(SPAN - 1 - position, 0, SPAN - 1)
    total = span * BLK_DEV
    live = span * tokens - pad

    columns = lax.broadcasted_iota(jnp.int32, (1, SPAN * tokens), 1)
    usable = columns < live
    blocks = lax.div(columns, BLK)
    for hh in range(HEAD):
        for b in range(BLK_DEV):
            query = position * BLK_DEV + b
            count = jnp.zeros((1, SPAN * tokens), F32)
            for wanted in (query - 1, query, query + 1, 0, total - 1):
                count = count + jnp.where(blocks == wanted, 1.0, 0.0)
            for k in range(r.picks.shape[0]):
                raw = r.picks[k, b, hh]
                chosen = lax.rem(raw, BLK_DEV)
                for k_units in range(2, SPAN + 1):
                    chosen = jnp.where(span == k_units, lax.rem(raw, BLK_DEV * k_units), chosen)
                count = count + jnp.where(blocks == chosen, 1.0, 0.0)
            count = jnp.where((query == 0) | (query == total - 1), 1.0, count)
            held = usable & (count > 0)
            bias = jnp.log(jnp.maximum(count, 1.0))
            r.bias[hh, b : b + 1, :] = jnp.where(held, bias, NEGATIVE)

    ffn_src = {
        UP: lambda k: r.wu.at[:, cols(k, half)],
        DOWN: lambda k: r.wd.at[cols(k, half), :],
    }
    ffn_slot = {
        UP: lambda o: r.wu_all.at[cols(o, rows), :],
        DOWN: lambda o: r.wd_all.at[:, cols(o, rows)],
    }

    def ffn_start(w):
        i = w - UP
        for d in range(1, LINE):
            to = lax.rem(z + d, LINE)
            send(
                None, ffn_src[w](lax.rem(to, 2)), ffn_slot[w](s), r.f_ss.at[i, d - 1],
                r.f_rs.at[i, s], seq=to * 2 + y,
            )
        send(
            None, ffn_src[w](e), ffn_slot[w](s), r.f_ss.at[i, 3], r.f_rs.at[i, s], seq=mate
        )

    def by_distance(k):
        up = k + jnp.where(z <= k, 1, 0)
        down = k + jnp.where(LINE - 1 - z <= k, 1, 0)
        return jnp.where(z < LINE // 2, up, LINE - 1 - down)

    def ffn_forward(w, ks=(0, 1, 2)):
        i = w - UP
        for k in ks:
            o = by_distance(k) * 2 + y
            ref = ffn_slot[w](o)
            arrived(None, ref, r.f_rs.at[i, o])
            send(None, ref, ref, r.f_ss.at[i, 4 + k], r.f_rs.at[i, o], seq=mate)

    def ffn_finish(w):
        for d in range(LINE):
            o = lax.rem(z + d, LINE) * 2 + 1 - y
            arrived(None, ffn_slot[w](o), r.f_rs.at[w - UP, o])

    relay_round(1, 2)
    relay_round(2, 1)
    relay_round(1, 3)
    relay_round(2, 2)
    ffn_start(UP)
    relay_round(2, 3)
    for cond, slot in slots[3:]:
        token_pass(cond, slot)
    for ref, src in ((ffn_slot[UP](s), ffn_src[UP](e)), (ffn_slot[DOWN](s), ffn_src[DOWN](e))):
        ref[...] = src[...]

    ffn_start(DOWN)
    for cond, slot in slots:
        token_ready(cond, slot)
    relay_finish(0)
    scaling = HEAD_DIM ** (-0.5)
    for j in range(SPAN):
        q = pl.ds(j * tokens, tokens)
        rows_in = r.nall[root + j]
        r.kwin[q, :] = dot(rows_in, r.wq_all[1], ((1,), (0,))).astype(BF16)
        r.vwin[q, :] = dot(rows_in, r.wq_all[2], ((1,), (0,))).astype(BF16)
    relay_finish(1)
    part = dot(r.nall[SPAN - 1], r.wq_all[0], ((1,), (0,)))
    r.qs[...] = (part.astype(BF16).astype(F32) * scaling).astype(BF16)
    r.cotx[cols(e, tokens), :] = r.cot[...]
    beyond = (1 - x) * 2 + 1 - c

    def block_rows(unit, head):
        return pl.ds(al(unit * tokens + head * quarter, quarter), quarter)

    def cot_rows(unit, head):
        return r.cotx.at[block_rows(unit, head), :]

    send(
        None, r.cot.at[cols(h, quarter), :], cot_rows(e, h), r.c_ss.at[0], r.c_rs.at[h], seq=pair
    )

    def cot_share():
        ref = cot_rows(1 - e, h)
        arrived(None, ref, r.c_rs.at[h])
        send(None, ref, ref, r.c_ss.at[1], r.c_rs.at[h], head=across)
        send(None, ref, ref, r.c_ss.at[2], r.c_rs.at[h], head=twin)

    def cot_pass():
        ref = cot_rows(1 - e, across)
        arrived(None, ref, r.c_rs.at[across])
        send(None, ref, ref, r.c_ss.at[3], r.c_rs.at[across], head=twin)

    lanes = lax.div(lax.broadcasted_iota(jnp.int32, (1, head_w), 1), HEAD_DIM)
    none = jnp.zeros((), BF16)
    r.att[...] = jnp.zeros(r.att.shape, F32)

    def attend(hh, carry):
        mine = lanes == hh
        query = jnp.where(mine, r.qs[...], none)
        for j in range(SPAN):
            k = pl.ds(j * tokens, tokens)
            r.lg[:, k] = dot(query, r.kwin[k, :], ((1,), (1,)))
        for b in range(BLK_DEV):
            q = pl.ds(b * BLK, BLK)
            logits = r.lg[q, :] + r.bias[hh, b : b + 1, :]
            grown = jnp.exp(logits - jnp.max(logits, axis=-1, keepdims=True))
            scale = 1.0 / jnp.sum(grown, axis=-1, keepdims=True)
            r.prob[hh, q, :] = (grown * scale).astype(BF16)
        part = dot(r.prob[hh], r.vwin[...], ((1,), (0,)))
        r.att[...] += jnp.where(mine, part, 0.0)
        return carry

    lax.fori_loop(0, HEAD // 2, attend, 0)
    ffn_forward(UP, (0,))
    lax.fori_loop(HEAD // 2, HEAD, attend, 0)
    ffn_forward(UP, (1,))
    r.att_low[...] = r.att[...].astype(BF16)
    relay_finish(2)

    def rows_of(k):
        return cols(k, quarter)

    def reduce_start(op):
        for v in range(2):
            r.q1_send[op, v] = r.sum_f[rows_of(v * 2 + 1 - c), :].astype(BF16)
        send(None, r.q1_send.at[op], r.q1_recv.at[op], r.q1_ss.at[op], r.q1_rs.at[op], head=twin)

    def reduce_middle(op):
        arrived(None, r.q1_recv.at[op], r.q1_rs.at[op])
        block = r.sum_f[rows_of(across), :] + r.q1_recv[op, 1 - x].astype(F32)
        r.q2_send[op] = block.astype(BF16)
        send(None, r.q2_send.at[op], r.q2_recv.at[op], r.q2_ss.at[op], r.q2_rs.at[op], head=across)
        r.q_own[op] = r.sum_f[rows_of(h), :] + r.q1_recv[op, x].astype(F32)

    def reduce_finish(op):
        arrived(None, r.q2_recv.at[op], r.q2_rs.at[op])
        return r.q_own[op] + r.q2_recv[op].astype(F32)

    def spread_start(op, whole, value):
        whole[rows_of(h), :] = value
        ref = whole.at[rows_of(h), :]
        send(None, ref, ref, r.ag_ss.at[op, 0], r.ag_rs.at[op, h], head=across)
        send(None, ref, ref, r.ag_ss.at[op, 1], r.ag_rs.at[op, h], head=twin)

    def spread_pass(op, whole):
        ref = whole.at[rows_of(across), :]
        arrived(None, ref, r.ag_rs.at[op, across])
        send(None, ref, ref, r.ag_ss.at[op, 2], r.ag_rs.at[op, across], head=twin)

    def spread_finish(op, whole):
        for o in (twin, beyond):
            arrived(None, whole.at[rows_of(o), :], r.ag_rs.at[op, o])

    pair_sum = [r.sum_f, r.sum_g]

    def pair_start(op):
        for u in range(2):
            for v in range(2):
                block = pair_sum[op][block_rows(u, v * 2 + 1 - c), :]
                r.p1_send[op, u * 2 + v] = block.astype(BF16)
        send(None, r.p1_send.at[op], r.p1_recv.at[op], r.p1_ss.at[op], r.p1_rs.at[op], head=twin)

    def pair_middle(op):
        arrived(None, r.p1_recv.at[op], r.p1_rs.at[op])
        for du, dv in ((1, 1), (1, 0), (0, 1), (0, 0)):
            u, v = lax.rem(e + du, 2), lax.rem(x + dv, 2)
            block = pair_sum[op][block_rows(u, v * 2 + c), :] + r.p1_recv[op, u * 2 + v].astype(F32)
            if du or dv:
                k = u * 2 + v
                r.p2_send[op, k] = block.astype(BF16)
                send(
                    None, r.p2_send.at[op, k], r.p2_recv.at[op, e * 2 + x], r.p2_ss.at[op, k],
                    r.p2_rs.at[op, e * 2 + x], seq=pair if du else s, head=across if dv else h,
                )
            else:
                r.p_own[op] = block

    def pair_x(op):
        arrived(None, r.p1_recv.at[op], r.p1_rs.at[op])
        for du in (1, 0):
            u = lax.rem(e + du, 2)
            k = u * 2 + 1 - x
            block = pair_sum[op][block_rows(u, across), :] + r.p1_recv[op, k].astype(F32)
            r.p2_send[op, k] = block.astype(BF16)
            send(
                None, r.p2_send.at[op, k], r.p2_recv.at[op, u], r.p2_ss.at[op, k],
                r.p2_rs.at[op, u], head=across,
            )

    def pair_z(op):
        for du in (1, 0):
            u = lax.rem(e + du, 2)
            arrived(None, r.p2_recv.at[op, u], r.p2_rs.at[op, u])
            block = pair_sum[op][block_rows(u, h), :] + r.p1_recv[op, u * 2 + x].astype(F32)
            block = block + r.p2_recv[op, u].astype(F32)
            if du:
                k = u * 2 + x
                r.p2_send[op, k] = block.astype(BF16)
                send(
                    None, r.p2_send.at[op, k], r.p2_recv.at[op, 2], r.p2_ss.at[op, k],
                    r.p2_rs.at[op, 2], seq=pair,
                )
            else:
                r.p_own[op] = block

    def pair_end(op):
        arrived(None, r.p2_recv.at[op, 2], r.p2_rs.at[op, 2])
        return r.p_own[op] + r.p2_recv[op, 2].astype(F32)

    def pair_finish(op):
        result = r.p_own[op]
        for du, dv in ((0, 1), (1, 0), (1, 1)):
            k = lax.rem(e + du, 2) * 2 + lax.rem(x + dv, 2)
            arrived(None, r.p2_recv.at[op, k], r.p2_rs.at[op, k])
            result = result + r.p2_recv[op, k].astype(F32)
        return result

    r.sum_f[:tokens, :] = dot(r.att_low[...], r.wo_all[...], ((1,), (0,)))
    reduce_start(0)
    reduce_middle(0)
    ffn_forward(UP, (2,))
    ffn_forward(DOWN, (0,))
    middle = r.tok[rows_of(h), :].astype(F32) + reduce_finish(0)
    r.mid_own[...] = middle
    xhat, _ = norm_parts(middle)

    def n2_rows(unit, head):
        return r.n2x.at[block_rows(unit, head), :]

    r.n2x[block_rows(e, h), :] = (xhat * r.gains[2:3, :] + r.gains[3:4, :]).astype(BF16)
    mine, tag = n2_rows(e, h), e * 4 + h
    send(None, mine, mine, r.n2_ss.at[0], r.n2_rs.at[tag], seq=pair)
    send(None, mine, mine, r.n2_ss.at[1], r.n2_rs.at[tag], head=across)
    send(None, mine, mine, r.n2_ss.at[2], r.n2_rs.at[tag], head=twin)
    cot_share()
    ffn_forward(DOWN, (1,))
    for k, (unit, head) in enumerate(((e, across), (1 - e, h), (1 - e, across))):
        ref, tag = n2_rows(unit, head), unit * 4 + head
        arrived(None, ref, r.n2_rs.at[tag])
        if k == 1:
            send(None, ref, ref, r.n2_ss.at[6], r.n2_rs.at[tag], head=across)
        send(None, ref, ref, r.n2_ss.at[3 + k], r.n2_rs.at[tag], head=twin)
    cot_pass()
    ffn_forward(DOWN, (2,))
    ffn_finish(UP)
    ffn_finish(DOWN)
    for unit in (e, 1 - e):
        for head in (x * 2 + 1 - c, (1 - x) * 2 + 1 - c):
            arrived(None, n2_rows(unit, head), r.n2_rs.at[unit * 4 + head])
    for head in (twin, beyond):
        arrived(None, cot_rows(1 - e, head), r.c_rs.at[head])

    root_c = (2.0 / 3.141592653589793) ** 0.5
    r.up_send[half // 128 :, :] = jnp.zeros((8 - half // 128, 128), F32)
    for j in range(half // 256):
        f = pl.ds(j * 256, 256)
        bias = r.upb[:, pl.ds(al(e * half + j * 256, 256), 256)].astype(F32)
        v = dot(r.n2x[...], r.wu_all[:, f], ((1,), (0,))) + bias
        t = jnp.tanh(root_c * (v + 0.044715 * (v * v * v)))
        r.hid[:, f] = (0.5 * v * (1.0 + t)).astype(BF16)
        slope = 0.5 * (1.0 + t) + 0.5 * v * (1.0 - t * t) * (root_c * (1.0 + 0.134145 * v * v))
        low_p = (dot(r.cotx[...], r.wd_all[f, :], ((1,), (1,))) * slope).astype(BF16)
        r.gp[:, f] = low_p
        sums = jnp.sum(low_p.astype(F32), axis=0, keepdims=True)
        r.up_send[2 * j : 2 * j + 1, :] = sums[:, :128]
        r.up_send[2 * j + 1 : 2 * j + 2, :] = sums[:, 128:]

    grad_send = {QKV_KV: r.skv, QKV_Q: r.sq, OUT: r.so, UP: r.su, DOWN: r.sd}
    grad_arrive = {QKV_KV: r.akv, QKV_Q: r.aq, OUT: r.ao, UP: r.au, DOWN: r.ad}
    grad_again = {QKV_KV: r.bkv, QKV_Q: r.bq, OUT: r.bo, UP: r.bu, DOWN: r.bd}
    grad_final = {QKV_KV: r.rkv, QKV_Q: r.rq, OUT: r.ro, UP: r.ru, DOWN: r.rd}

    def tile_of(i):
        return lax.rem(z + 1 + i, LINE)

    def grad_cross(w, zz):
        send(
            None, grad_send[w].at[zz * 2 + 1 - y], grad_arrive[w].at[zz], r.ra_ss.at[w, zz],
            r.ra_rs.at[w, zz], seq=mate,
        )

    def grad_along(w, ks=(1, 2, 3)):
        for d in ks:
            zz = lax.rem(z + d, LINE)
            arrived(None, grad_arrive[w].at[zz], r.ra_rs.at[w, zz])
            both = grad_send[w][zz * 2 + y].astype(F32) + grad_arrive[w][zz].astype(F32)
            grad_again[w][zz] = both.astype(BF16)
            send(
                None, grad_again[w].at[zz], grad_final[w].at[z], r.rb_ss.at[w, zz],
                r.rb_rs.at[w, z], seq=zz * 2 + y,
            )

    def grad_own(w):
        arrived(None, grad_arrive[w].at[z], r.ra_rs.at[w, z])
        return grad_send[w][z * 2 + y].astype(F32) + grad_arrive[w][z].astype(F32)

    def grad_from(w, o):
        arrived(None, grad_final[w].at[o], r.rb_rs.at[w, o])
        return grad_final[w][o].astype(F32)

    def grad_sum(w):
        result = grad_own(w)
        for d in range(1, LINE):
            result = result + grad_from(w, lax.rem(z + d, LINE))
        return result

    def grad_halves(w):
        same = grad_own(w) + grad_from(w, lax.rem(z + 2, LINE))
        other = grad_from(w, lax.rem(z + 1, LINE)) + grad_from(w, lax.rem(z + 3, LINE))
        return same, other

    def down_step(i):
        zz = tile_of(i)
        part = dot(r.hid[...], r.cotx[:, cols(zz, 256)], ((0,), (0,))).astype(BF16)
        r.sd[zz * 2] = part[:, :rows]
        r.sd[zz * 2 + 1] = part[:, rows:]
        grad_cross(DOWN, zz)

    def up_step(i):
        zz = tile_of(i)
        part = dot(r.n2x[:, cols(zz, 256)], r.gp[...], ((0,), (0,))).astype(BF16)
        r.su[zz * 2] = part[:rows]
        r.su[zz * 2 + 1] = part[rows:]
        grad_cross(UP, zz)

    down_step(0)
    r.sum_f[...] = dot(r.gp[...], r.wu_all[...], ((1,), (1,)))
    pair_start(0)
    down_step(1)
    pair_middle(0)
    r.sum_g[...] = dot(r.hid[...], r.wd_all[...], ((1,), (0,)))
    pair_start(1)
    down_step(2)
    down_step(3)
    pair_x(1)
    for i in range(LINE):
        up_step(i)
    for d in range(1, SEQ):
        send(
            None, r.up_send, r.up_recv.at[s], r.up_ss.at[d], r.up_rs.at[s],
            seq=lax.rem(s + d, SEQ),
        )

    grad_two = pair_finish(0)
    xhat, inverse = norm_parts(r.mid_own[...])
    dy = r.cot[rows_of(h), :].astype(F32)
    grad_mid = dy + norm_backward(xhat, inverse, grad_two * r.gains[2:3, :])
    r.gm_own[...] = grad_mid
    spread_start(0, r.gb, grad_mid.astype(BF16))
    r.sm_send[2:3, :] = jnp.sum(grad_two * xhat, axis=0, keepdims=True)
    r.sm_send[3:4, :] = jnp.sum(grad_two, axis=0, keepdims=True)
    r.sm_send[4:5, :] = jnp.sum(dy, axis=0, keepdims=True)
    r.sm_send[5:8, :] = jnp.zeros((3, width), F32)

    grad_along(DOWN)
    pair_z(1)
    spread_pass(0, r.gb)
    spread_finish(0, r.gb)
    r.gatt[...] = dot(r.gb[...], r.wo_all[...], ((1,), (1,))).astype(BF16)
    for i in range(LINE):
        zz = tile_of(i)
        part = dot(r.att_low[...], r.gb[:, cols(zz, 256)], ((0,), (0,))).astype(BF16)
        r.so[zz * 2] = part[:, :rows]
        r.so[zz * 2 + 1] = part[:, rows:]
        grad_cross(OUT, zz)
    grad_along(UP, (1, 2))

    r.dq[...] = jnp.zeros(r.dq.shape, F32)
    r.dk[...] = jnp.zeros(r.dk.shape, F32)
    r.dv[...] = jnp.zeros(r.dv.shape, F32)

    def attend_back(hh, carry):
        mine = lanes == hh
        query = jnp.where(mine, r.qs[...], none)
        grad = jnp.where(mine, r.gatt[...], none)
        for j in range(SPAN):
            k = pl.ds(j * tokens, tokens)
            r.lg[:, k] = dot(grad, r.vwin[k, :], ((1,), (1,)))
        for b in range(BLK_DEV):
            q = pl.ds(b * BLK, BLK)
            chance, grown = r.prob[hh, q, :].astype(F32), r.lg[q, :]
            inner = jnp.sum(chance * grown, axis=-1, keepdims=True)
            r.ds[q, :] = (chance * (grown - inner)).astype(BF16)
        r.dq[...] += jnp.where(mine, dot(r.ds[...], r.kwin[...], ((1,), (0,))), 0.0)
        for j in range(SPAN):
            k = pl.ds(j * tokens, tokens)
            r.dk[k, :] += dot(r.ds[:, k], query, ((0,), (0,)))
            r.dv[k, :] += dot(r.prob[hh, :, k], grad, ((0,), (0,)))
        return carry

    lax.fori_loop(0, HEAD, attend_back, 0)
    for k in range(2 * (SPAN - 1) + SPAN):
        j = k - (SPAN - 1)
        if 0 <= j < SPAN:
            q = pl.ds(j * tokens, tokens)
            r.dkv_pad[k, :, :head_w] = r.dk[q, :].astype(BF16)
            r.dkv_pad[k, :, head_w:] = r.dv[q, :].astype(BF16)
        else:
            r.dkv_pad[k] = jnp.zeros(r.dkv_pad.shape[1:], BF16)
    for k in range(NEAR):
        r.dkv_send[k] = r.dkv_pad[k + SPAN - 1 - root]
    r.gtq[...] = (r.dq[...] * scaling).astype(BF16)

    def grad_hop(cond, slot, into, k, to):
        send(cond, r.dkv_send.at[slot], r.dkv_recv.at[into], r.dkv_ss.at[k], r.dkv_rs.at[into], seq=to)

    def add_to(slot, *froms):
        both = r.dkv_send[slot].astype(F32)
        for k in froms:
            both = both + r.dkv_recv[k].astype(F32)
        r.dkv_send[slot] = both.astype(BF16)

    def grad_wait(cond, into):
        arrived(cond, r.dkv_recv.at[into], r.dkv_rs.at[into])

    FAR, ABOVE, BELOW, LINE_ABOVE, LINE_BELOW, MATE = range(6)
    grad_hop((y == 0) & (z >= 2), 0, FAR, 0, s - 2)
    grad_hop((y == 1) & (z <= 1), 6, FAR, 0, s + 2)
    grad_hop((y == 0) & high, 6, BELOW, 1, s + 2)
    grad_hop((y == 1) & low, 0, ABOVE, 1, s - 2)

    grad_along(UP, (3,))

    for i in range(LINE):
        zz = tile_of(i)
        part = jnp.zeros((256, 2 * head_w), F32)
        for j in range(SPAN):
            part = part + dot(
                r.nall[root + j, :, cols(zz, 256)], r.dkv_pad[j + SPAN - 1], ((0,), (0,))
            )
        part = part.astype(BF16)
        for v in range(2):
            for k in range(2):
                r.skv[zz * 2 + v, k] = part[v * rows : (v + 1) * rows, k * head_w : (k + 1) * head_w]
        grad_cross(QKV_KV, zz)
        if i == 1:
            grad_wait(low & high, FAR)
            add_to(2 + 2 * y, FAR)
            grad_hop((y == 0) & low, 2, ABOVE, 2, s - 2)
            grad_hop((y == 1) & high, 4, BELOW, 2, s + 2)
            grad_hop(low, 1, LINE_ABOVE, 3, s - 2)
            grad_hop(high, 5, LINE_BELOW, 4, s + 2)
    grad_wait(high, ABOVE)
    grad_wait(low, BELOW)
    add_to(from_mate, ABOVE, BELOW)
    grad_hop(None, from_mate, MATE, 5, mate)
    for i in range(LINE):
        zz = tile_of(i)
        part = dot(r.nall[SPAN - 1, :, cols(zz, 256)], r.gtq[...], ((0,), (0,))).astype(BF16)
        r.sq[zz * 2] = part[:rows]
        r.sq[zz * 2 + 1] = part[rows:]
        grad_cross(QKV_Q, zz)
    grad_along(OUT)
    grad_along(QKV_KV)
    ffn = pair_end(1)
    spread_start(1, r.out_o, (r.mid_own[...] + ffn + r.gains[4:5, :]).astype(BF16))
    grad_wait(high, LINE_ABOVE)
    grad_wait(low, LINE_BELOW)
    grad_wait(None, MATE)
    whole = r.dkv_send[SPAN - 1].astype(F32)
    for k in (LINE_ABOVE, LINE_BELOW, MATE):
        whole = whole + r.dkv_recv[k].astype(F32)
    r.gtkv[...] = whole.astype(BF16)

    r.sum_f[:tokens, :] = (
        dot(r.gtq[...], r.wq_all[0], ((1,), (1,)))
        + dot(r.gtkv[:, :head_w], r.wq_all[1], ((1,), (1,)))
        + dot(r.gtkv[:, head_w:], r.wq_all[2], ((1,), (1,)))
    )
    reduce_start(1)
    reduce_middle(1)
    grad_one = reduce_finish(1)
    xhat, inverse = norm_parts(r.tok[rows_of(h), :].astype(F32))
    r.sm_send[0:1, :] = jnp.sum(grad_one * xhat, axis=0, keepdims=True)
    r.sm_send[1:2, :] = jnp.sum(grad_one, axis=0, keepdims=True)
    for d in range(1, SEQ):
        to = lax.rem(s + d, SEQ)
        send(
            None, r.sm_send.at[:, cols(to, rows)], r.sm_recv.at[s], r.sm_ss.at[d], r.sm_rs.at[s],
            seq=to,
        )
    spread_pass(1, r.out_o)
    grad_along(QKV_Q)
    grad_x = r.gm_own[...] + norm_backward(xhat, inverse, grad_one * r.gains[0:1, :])
    spread_start(2, r.xgb, grad_x.astype(BF16))

    same, other = grad_halves(DOWN)
    r.gd_o[cols(e, half), :] = same
    r.gd_o[cols(1 - e, half), :] = other
    same, other = grad_halves(UP)
    r.gu_o[:, cols(e, half)] = same
    r.gu_o[:, cols(1 - e, half)] = other
    spread_pass(2, r.xgb)
    r.go_o[...] = grad_sum(OUT)

    r.sm_recv[s] = r.sm_send[:, cols(s, rows)]
    r.up_recv[s] = r.up_send[...]
    for d in range(1, SEQ):
        o = lax.rem(s + d, SEQ)
        arrived(None, r.sm_recv.at[o], r.sm_rs.at[o], r.vec)
        arrived(None, r.up_recv.at[o], r.up_rs.at[o])
    part = r.sm_recv[0]
    for o in range(1, SEQ):
        part = part + r.sm_recv[o]
    r.sm_own[...] = part
    for d in range(1, HEAD):
        send(
            None, r.sm_own, r.sm_two.at[h], r.sm2_ss.at[d], r.sm2_rs.at[h],
            head=lax.rem(h + d, HEAD),
        )
    r.sm_two[h] = part
    tall = half // 128
    for u in range(2):
        ups = jnp.zeros((tall, 128), F32)
        for o in range(SEQ):
            if (o // 2) % 2 == u:
                ups = ups + r.up_recv[o, :tall, :]
        r.small_o[8 + u * tall : 8 + (u + 1) * tall, :] = ups
    spread_finish(1, r.out_o)
    spread_finish(2, r.xgb)
    r.xg_o[...] = r.xgb[...].astype(F32)
    for d in range(1, HEAD):
        o = lax.rem(h + d, HEAD)
        arrived(None, r.sm_two.at[o], r.sm2_rs.at[o])
    r.small_o[0:8, :] = (r.sm_two[0] + r.sm_two[1]) + (r.sm_two[2] + r.sm_two[3])
    r.gq_o[0] = grad_sum(QKV_Q)
    r.gq_o[1:3] = grad_sum(QKV_KV)

    for cond, one in sent:
        when(cond, one.wait_send)


def local_fused(
    tokens, w_qkv, w_out, ln1_gain, ln1_bias, ln2_gain, ln2_bias, w_up, up_bias, w_down, down_bias,
    seq_units, seq_pad, rand_picks, cotangent,
):
    tok, width = tokens.shape
    rows, _, head_w = w_qkv.shape
    hidden = w_up.shape[1]
    half = hidden // 2
    quarter = tok // HEAD
    keys = SPAN * tok
    smem, vmem = pl.BlockSpec(memory_space=pltpu.SMEM), pl.BlockSpec(memory_space=pltpu.VMEM)
    ins = dict(
        units=seq_units, pads=seq_pad, picks=jnp.transpose(rand_picks, (2, 0, 1)), tok=tokens,
        cot=cotangent, wq=jnp.transpose(w_qkv, (1, 0, 2)), wo=w_out, wu=w_up, wd=w_down,
        g1=ln1_gain, b1=ln1_bias, g2=ln2_gain, b2=ln2_bias, b3=down_bias,
        upb=up_bias.reshape(1, hidden),
    )
    outs = dict(
        out_o=((tok, width), BF16), xg_o=((tok, width), F32), gq_o=((3, rows, head_w), F32),
        go_o=((head_w, rows), F32), gu_o=((rows, hidden), F32), gd_o=((hidden, rows), F32),
        small_o=((16, rows), F32),
    )
    scratch = dict(
        wq_all=((3, width, head_w), BF16), wo_all=((head_w, width), BF16),
        wu_all=((width, half), BF16), wd_all=((half, width), BF16), vec=((8, rows), F32),
        gains=((8, width), F32), nall=((NEAR, tok, width), BF16),
        qs=((tok, head_w), BF16),
        kwin=((keys, head_w), BF16), vwin=((keys, head_w), BF16), lg=((tok, keys), F32),
        prob=((HEAD, tok, keys), BF16), ds=((tok, keys), BF16),
        att=((tok, head_w), F32), att_low=((tok, head_w), BF16), n2x=((2 * tok, width), BF16),
        cotx=((2 * tok, width), BF16), hid=((2 * tok, half), BF16), gp=((2 * tok, half), BF16),
        gb=((tok, width), BF16), xgb=((tok, width), BF16), mid_own=((quarter, width), F32),
        gm_own=((quarter, width), F32), gatt=((tok, head_w), BF16), dq=((tok, head_w), F32),
        dk=((keys, head_w), F32), dv=((keys, head_w), F32),
        dkv_pad=((NEAR + SPAN - 1, tok, 2 * head_w), BF16),
        dkv_send=((NEAR, tok, 2 * head_w), BF16), dkv_recv=((6, tok, 2 * head_w), BF16),
        gtq=((tok, head_w), BF16), gtkv=((tok, 2 * head_w), BF16),
        q1_send=((2, 2, quarter, width), BF16), q1_recv=((2, 2, quarter, width), BF16),
        q2_send=((2, quarter, width), BF16), q2_recv=((2, quarter, width), BF16),
        q_own=((2, quarter, width), F32),
        sum_f=((2 * tok, width), F32), sum_g=((2 * tok, width), F32), bias=((HEAD, 8, keys), F32),
        p1_send=((2, 4, quarter, width), BF16), p1_recv=((2, 4, quarter, width), BF16),
        p2_send=((2, 4, quarter, width), BF16), p2_recv=((2, 4, quarter, width), BF16),
        p_own=((2, quarter, width), F32), sm_send=((8, width), F32),
        sm_recv=((SEQ, 8, rows), F32), sm_own=((8, rows), F32), sm_two=((HEAD, 8, rows), F32),
        up_send=((8, 128), F32), up_recv=((SEQ, 8, 128), F32),
    )
    shards = dict(
        kv=(2, rows, head_w), q=(rows, head_w), o=(head_w, rows), u=(rows, half), d=(half, rows)
    )
    for lead, count in (("s", SEQ), ("a", LINE), ("b", LINE), ("r", LINE)):
        for name, shape in shards.items():
            scratch[lead + name] = ((count,) + shape, BF16)
    semaphores = dict(
        g_ss=(3, 16), g_rs=(3, SEQ), f_ss=(2, 7), f_rs=(2, SEQ), v_ss=(7,), v_rs=(SEQ,),
        t_ns=(6,), t_ss=(NEAR, 3), t_rs=(NEAR, HEAD), dkv_ss=(6,), dkv_rs=(6,), c_ss=(4,), c_rs=(HEAD,),
        q1_ss=(2,), q1_rs=(2,), q2_ss=(2,), q2_rs=(2,), ag_ss=(3, 3), ag_rs=(3, HEAD), n2_ss=(7,),
        n2_rs=(8,), p1_ss=(2,), p1_rs=(2,), p2_ss=(2, 4), p2_rs=(2, 4), ra_ss=(5, LINE),
        ra_rs=(5, LINE), rb_ss=(5, LINE), rb_rs=(5, LINE), sm_ss=(SEQ,), sm_rs=(SEQ,),
        sm2_ss=(HEAD,), sm2_rs=(HEAD,), up_ss=(SEQ,), up_rs=(SEQ,),
    )
    names = [*ins, *outs, *scratch, *semaphores]
    results = pl.pallas_call(
        functools.partial(fused_kernel, names),
        out_shape=[jax.ShapeDtypeStruct(*o) for o in outs.values()],
        in_specs=[smem] * 3 + [vmem] * (len(ins) - 3),
        out_specs=[vmem] * len(outs),
        scratch_shapes=[pltpu.VMEM(*v) for v in scratch.values()]
        + [pltpu.SemaphoreType.DMA(v) for v in semaphores.values()],
        compiler_params=pltpu.CompilerParams(
            collective_id=0, has_side_effects=True, vmem_limit_bytes=VMEM_BYTES
        ),
        name="fused_layer",
    )(*ins.values())
    large = list(outs.values())[:-1]
    handed = pl.pallas_call(
        hand_over_kernel,
        out_shape=[jax.ShapeDtypeStruct(*o) for o in large]
        + [jax.ShapeDtypeStruct((rows,), F32)] * 5
        + [jax.ShapeDtypeStruct((hidden,), F32)],
        in_specs=[vmem] * len(outs),
        out_specs=[vmem] * (len(large) + 6),
        name="hand_over",
    )(*results)
    out, xg, gq, go, gu, gd, g1, b1, g2, b2, b3, upg = handed
    return out, xg, jnp.transpose(gq, (1, 0, 2)), go, g1, b1, g2, b2, gu, upg, gd, b3


def hand_over_kernel(*refs):
    large = (len(refs) - 7) // 2
    small, vectors = refs[large], refs[2 * large + 1 :]
    for k in range(large):
        refs[large + 1 + k][...] = refs[k][...]
    for k in range(5):
        vectors[k][...] = small[k, :]
    for k in range(8):
        vectors[5][pl.ds(k * 128, 128)] = small[8 + k, :]


IN_SPECS = (
    P("seq", None), P("seq", None, "head"), P("head", "seq"), P("seq"), P("seq"), P("seq"),
    P("seq"), P("seq", "head"), P("head"), P("head", "seq"), P("seq"), P(), P(),
    P("seq", "head", None), P("seq", None),
)
OUT_SPECS = (
    P("seq", None), P("seq", None), P("seq", None, "head"), P("head", "seq"), P("seq"), P("seq"),
    P("seq"), P("seq"), P("seq", "head"), P("head"), P("head", "seq"), P("seq"),
)


def solution(mesh):
    fits = mesh.shape["seq"] == SEQ and mesh.shape["head"] == HEAD
    return jax.shard_map(
        local_fused if fits else local_general, mesh=mesh, in_specs=IN_SPECS,
        out_specs=OUT_SPECS, check_vma=False,
    )
```

```python
import functools
import types

import jax
import jax.numpy as jnp
from jax import lax
from jax.experimental import pallas as pl
from jax.experimental.pallas import tpu as pltpu
from jax.sharding import PartitionSpec as P

HEAD_DIM = 64
BLK = 64
SPAN = 4
BLK_DEV = 4
EPSILON = 1e-05
NEGATIVE = -1e30
F32 = jnp.float32
BF16 = jnp.bfloat16


def shifted(value, axis, steps):
    count = lax.axis_size(axis)
    first, last = max(0, -steps), min(count, count - steps)
    return lax.ppermute(value, axis, [(i, i + steps) for i in range(first, last)])


def norm_parts(features):
    average = jnp.mean(features, axis=-1, keepdims=True)
    centred = features - average
    spread = jnp.mean(centred * centred, axis=-1, keepdims=True)
    inverse = lax.rsqrt(spread + EPSILON)
    return centred * inverse, inverse


def norm_backward(xhat, inverse, scaled):
    first = jnp.mean(scaled, axis=-1, keepdims=True)
    second = jnp.mean(scaled * xhat, axis=-1, keepdims=True)
    return inverse * (scaled - first - xhat * second)


def dot(a, b, dims):
    return lax.dot_general(a, b, (dims, ((), ())), preferred_element_type=F32)


def sequence_place(seq_units, seq_pad):
    device = lax.axis_index("seq")
    start, leader, span, pad = 0, 0, 0, 0
    for k in range(seq_units.shape[0]):
        units = seq_units[k]
        inside = (device >= start) & (device < start + units)
        leader = jnp.where(inside, start, leader)
        span = jnp.where(inside, units, span)
        pad = jnp.where(inside, seq_pad[k], pad)
        start = start + units
    return device - leader, span, pad


def key_counts(position, span, picks):
    blocks = lax.broadcasted_iota(jnp.int32, (1, 1, SPAN * BLK_DEV), 2)
    query = position * BLK_DEV + lax.broadcasted_iota(jnp.int32, (BLK_DEV, 1, 1), 0)
    total = span * BLK_DEV
    count = jnp.zeros((BLK_DEV, picks.shape[1], SPAN * BLK_DEV), F32)
    for wanted in (query - 1, query, query + 1, 0, total - 1):
        count = count + (blocks == wanted).astype(F32)
    chosen = picks % total
    for r in range(picks.shape[2]):
        count = count + (blocks == chosen[:, :, r : r + 1]).astype(F32)
    return jnp.where((query == 0) | (query == total - 1), 1.0, count)


def local_general(
    tokens, w_qkv, w_out, ln1_gain, ln1_bias, ln2_gain, ln2_bias, w_up, up_bias, w_down, down_bias,
    seq_units, seq_pad, rand_picks, cotangent,
):
    tok, width = tokens.shape
    heads = w_qkv.shape[2] // HEAD_DIM
    rows = lambda v: lax.all_gather(v, "seq", axis=0, tiled=True)
    cols = lambda v: lax.all_gather(v, "seq", axis=1, tiled=True)
    vectors = jnp.stack([ln1_gain, ln1_bias, ln2_gain, ln2_bias, down_bias], axis=0)
    gain_one, shift_one, gain_two, shift_two, down_shift = [
        v[None].astype(F32) for v in cols(vectors)
    ]
    qkv = rows(w_qkv)
    out_w, up_w, down_w = cols(w_out), rows(w_up), cols(w_down)
    position, span, pad = sequence_place(seq_units, seq_pad)
    root = SPAN - 1 - position
    inputs = tokens.astype(F32)
    xhat_one, inv_one = norm_parts(inputs)
    normed = (xhat_one * gain_one + shift_one).astype(BF16)
    triple = jnp.einsum("td,dcf->tcf", normed, qkv, preferred_element_type=F32).astype(BF16)
    own = jnp.stack([triple[:, 1], triple[:, 2]], axis=0)
    pieces = [own if o == 0 else shifted(own, "seq", -o) for o in range(1 - SPAN, SPAN)]
    nearby = jnp.stack(pieces, axis=0)
    window = lax.dynamic_slice_in_dim(nearby, root, SPAN, 0)
    split = lambda v: v.reshape(v.shape[0], heads, HEAD_DIM)
    keys = split(window[:, 0].reshape(SPAN * tok, -1))
    values = split(window[:, 1].reshape(SPAN * tok, -1))
    queries = split(triple[:, 0])
    scaling = HEAD_DIM ** (-0.5)
    live = jnp.arange(SPAN * tok, dtype=jnp.int32) < span * tok - pad
    count = jnp.repeat(key_counts(position, span, rand_picks), BLK, axis=2)
    count = jnp.where(live[None, None], count, 0.0)
    count = jnp.transpose(jnp.repeat(count, BLK, axis=0), (1, 0, 2))
    logits = jnp.einsum("qhd,khd->hqk", queries, keys, preferred_element_type=F32) * scaling
    logits = jnp.where(count > 0, logits, NEGATIVE)
    grown = jnp.exp(logits - jnp.max(logits, axis=-1, keepdims=True)) * count
    chances = grown / jnp.sum(grown, axis=-1, keepdims=True)
    chances_low = chances.astype(BF16)
    attended = jnp.einsum("hqk,khd->qhd", chances_low, values, preferred_element_type=F32)
    attended = attended.astype(BF16).reshape(tok, heads * HEAD_DIM)
    middle = inputs + lax.psum(dot(attended, out_w, ((1,), (0,))), "head")
    xhat_two, inv_two = norm_parts(middle)
    normed_two = (xhat_two * gain_two + shift_two).astype(BF16)
    pre_act = dot(normed_two, up_w, ((1,), (0,))) + up_bias.astype(F32)[None]
    hidden, pull = jax.vjp(lambda v: jax.nn.gelu(v, approximate=True), pre_act)
    hidden = hidden.astype(BF16)
    ffn = lax.psum(dot(hidden, down_w, ((1,), (0,))).astype(BF16), "head").astype(F32)
    output = (middle + ffn + down_shift).astype(BF16)
    grad_out = cotangent.astype(F32)
    grad_w_down = dot(hidden, cotangent, ((0,), (0,)))
    grad_pre = pull(dot(cotangent, down_w, ((1,), (1,))))[0].astype(BF16)
    grad_w_up = dot(normed_two, grad_pre, ((0,), (0,)))
    grad_up_bias = lax.psum(jnp.sum(grad_pre.astype(F32), axis=0), "seq")
    grad_two = lax.psum(dot(grad_pre, up_w, ((1,), (1,))), "head")
    grad_middle = grad_out + norm_backward(xhat_two, inv_two, grad_two * gain_two)
    grad_branch = grad_middle.astype(BF16)
    grad_w_out = dot(attended, grad_branch, ((0,), (0,)))
    grad_att = split(dot(grad_branch, out_w, ((1,), (1,))).astype(BF16))
    grad_prob = jnp.einsum("qhd,khd->hqk", grad_att, values, preferred_element_type=F32)
    inner = jnp.sum(chances * grad_prob, axis=-1, keepdims=True)
    grad_logit = (chances * (grad_prob - inner)).astype(BF16)
    dq = scaling * jnp.einsum("hqk,khd->qhd", grad_logit, keys, preferred_element_type=F32)
    dk = scaling * jnp.einsum("hqk,qhd->khd", grad_logit, queries, preferred_element_type=F32)
    dv = jnp.einsum("hqk,qhd->khd", chances_low, grad_att, preferred_element_type=F32)
    part = jnp.stack([dk.reshape(SPAN, tok, -1), dv.reshape(SPAN, tok, -1)], axis=1)
    near = jnp.zeros((2 * SPAN - 1,) + part.shape[1:], F32)
    near = lax.dynamic_update_slice_in_dim(near, part, root, 0)
    owned = near[SPAN - 1]
    for offset in range(1 - SPAN, SPAN):
        if offset:
            owned = owned + shifted(near[offset + SPAN - 1], "seq", offset)
    owned = owned.astype(BF16)
    grad_triple = jnp.stack([dq.reshape(tok, -1).astype(BF16), owned[0], owned[1]], axis=1)
    grad_w_qkv = jnp.einsum("td,tcf->dcf", normed, grad_triple, preferred_element_type=F32)
    grad_one = lax.psum(
        jnp.einsum("tcf,dcf->td", grad_triple, qkv, preferred_element_type=F32), "head"
    )
    x_grad = grad_middle + norm_backward(xhat_one, inv_one, grad_one * gain_one)
    sums = jnp.stack(
        [
            jnp.sum(grad_one * xhat_one, axis=0), jnp.sum(grad_one, axis=0),
            jnp.sum(grad_two * xhat_two, axis=0), jnp.sum(grad_two, axis=0),
            jnp.sum(grad_out, axis=0),
        ],
        axis=0,
    )
    scatter = lambda v, d: lax.psum_scatter(v, "seq", scatter_dimension=d, tiled=True)
    sums = scatter(sums, 1)
    return (
        output, x_grad, scatter(grad_w_qkv, 0), scatter(grad_w_out, 1), sums[0], sums[1], sums[2],
        sums[3], scatter(grad_w_up, 0), grad_up_bias, scatter(grad_w_down, 1), sums[4],
    )


MESH = pl.DeviceIdType.MESH
SEQ = 8
HEAD = 4
LINE = 4
NEAR = 2 * SPAN - 1
QKV_KV, QKV_Q, OUT, UP, DOWN = range(5)
VMEM_BYTES = 60 * 1024 * 1024


def al(value, multiple):
    return pl.multiple_of(value, multiple)


def fused_kernel(names, *refs):
    r = types.SimpleNamespace(**dict(zip(names, refs)))
    s, h = lax.axis_index("seq"), lax.axis_index("head")
    z, y, x, c = lax.div(s, 2), lax.rem(s, 2), lax.div(h, 2), lax.rem(h, 2)
    e = lax.rem(z, 2)
    pair_z = z + 1 - 2 * e
    mate = z * 2 + 1 - y
    pair = pair_z * 2 + y
    twin = x * 2 + 1 - c
    across = (1 - x) * 2 + c
    tokens, width = r.tok.shape
    quarter = tokens // HEAD
    head_w = r.qs.shape[1]
    rows = r.wq.shape[1]
    half = r.wu_all.shape[1]
    sent = []

    def copy(src, dst, ss, rs, **where):
        return pltpu.make_async_remote_copy(
            src_ref=src, dst_ref=dst, send_sem=ss, recv_sem=rs, device_id=where,
            device_id_type=MESH,
        )

    def when(cond, then):
        if cond is None:
            then()
        else:
            pl.when(cond)(lambda: then())

    def send(cond, *args, **where):
        one = copy(*args, **where)
        when(cond, one.start)
        sent.append((cond, one))

    def arrived(cond, dst, rs, like=None):
        when(cond, copy(dst if like is None else like, dst, r.v_ss.at[0], rs, seq=mate).wait_recv)

    barrier = pltpu.get_barrier_semaphore()
    greeted = [{"seq": lax.rem(s + d, SEQ)} for d in range(1, SEQ)]
    greeted += [{"head": lax.rem(h + d, HEAD)} for d in range(1, HEAD)]
    greeted += [{"seq": pair, "head": across}]
    for where in greeted:
        pl.semaphore_signal(barrier, inc=1, device_id=where, device_id_type=MESH)
    for k, ref in enumerate((r.g1, r.b1, r.g2, r.b2, r.b3)):
        r.vec[k : k + 1, :] = ref[...].reshape(1, rows).astype(F32)
    r.vec[5:8, :] = jnp.zeros((3, rows), F32)
    pl.semaphore_wait(barrier, len(greeted))

    def cols(o, size):
        return pl.ds(al(o * size, size), size)

    relay_slot = [
        lambda o: r.wq_all.at[1:3, cols(o, rows), :],
        lambda o: r.wq_all.at[0, cols(o, rows), :],
        lambda o: r.wo_all.at[:, cols(o, rows)],
    ]
    relay_src = [r.wq.at[1:3], r.wq.at[0], r.wo]

    def relay_start(w):
        src, dst, rs = relay_src[w], relay_slot[w](s), r.g_rs.at[w, s]
        send(z < LINE - 1, src, dst, r.g_ss.at[w, 0], rs, seq=s + 2)
        send(z > 0, src, dst, r.g_ss.at[w, 4], rs, seq=s - 2)
        send(None, src, dst, r.g_ss.at[w, 8], rs, seq=mate)

    def relay_round(w, k):
        for sign, first, third in ((-1, 0, 8 + k), (1, 4, 11 + k)):
            from_z = z + sign * k
            there = (from_z >= 0) & (from_z < LINE)
            o = jnp.clip(from_z, 0, LINE - 1) * 2 + y
            ref, rs = relay_slot[w](o), r.g_rs.at[w, o]
            arrived(there, ref, rs)
            onward = (z < LINE - 1) if sign < 0 else (z > 0)
            send(there & onward, ref, ref, r.g_ss.at[w, first + k], rs, seq=s - 2 * sign)
            send(there, ref, ref, r.g_ss.at[w, third], rs, seq=mate)

    def relay_finish(w):
        for d in range(LINE):
            o = lax.rem(z + d, LINE) * 2 + 1 - y
            arrived(None, relay_slot[w](o), r.g_rs.at[w, o])

    low, high = z > 0, z < LINE - 1
    from_mate = 4 - 2 * y

    def token_rows(slot, head):
        return r.nall.at[slot, cols(head, quarter), :]

    def token_send(cond, slot, back, k, to):
        send(cond, token_rows(slot, h), token_rows(back, h), r.t_ns.at[k], r.t_rs.at[back, h], seq=to)

    def token_share(cond, slot):
        ref = token_rows(slot, h)
        arrived(cond, ref, r.t_rs.at[slot, h])
        send(cond, ref, ref, r.t_ss.at[slot, 0], r.t_rs.at[slot, h], head=across)
        send(cond, ref, ref, r.t_ss.at[slot, 1], r.t_rs.at[slot, h], head=twin)

    def token_pass(cond, slot):
        ref = token_rows(slot, across)
        arrived(cond, ref, r.t_rs.at[slot, across])
        send(cond, ref, ref, r.t_ss.at[slot, 2], r.t_rs.at[slot, across], head=twin)

    def token_ready(cond, slot):
        arrived(cond, token_rows(slot, twin), r.t_rs.at[slot, twin])
        other = (1 - x) * 2 + 1 - c
        arrived(cond, token_rows(slot, other), r.t_rs.at[slot, other])

    far_in = jnp.where(y == 0, z >= 2, z <= 1)
    far_slot = 6 * y
    slots = (
        (None, from_mate), (low, 1), (high, 5), (low, 2 - 2 * y), (high, 6 - 2 * y),
        (far_in, far_slot),
    )
    for d in range(1, SEQ):
        send(
            None, r.vec, r.gains.at[:, cols(s, rows)], r.v_ss.at[d - 1], r.v_rs.at[s],
            seq=lax.rem(s + d, SEQ),
        )
    relay_start(0)
    r.gains[:, cols(s, rows)] = r.vec[...]
    for k in range(NEAR):
        other = s + k - (SPAN - 1)

        @pl.when((other < 0) | (other >= SEQ))
        def _():
            r.nall[k] = jnp.zeros(r.nall.shape[1:], BF16)

    for k, cond in enumerate((low & high, high, low, high, low)):

        @pl.when(jnp.logical_not(cond))
        def _():
            r.dkv_recv[k] = jnp.zeros(r.dkv_recv.shape[1:], BF16)

    for d in range(1, SEQ):
        o = lax.rem(s + d, SEQ)
        arrived(None, r.gains.at[:, cols(o, rows)], r.v_rs.at[o], r.vec)

    def normalise(q):
        xhat, _ = norm_parts(r.tok[q, :].astype(F32))
        r.nall[SPAN - 1, q, :] = (xhat * r.gains[0:1, :] + r.gains[1:2, :]).astype(BF16)

    normalise(cols(h, quarter))
    token_send(None, SPAN - 1, 2 + 2 * y, 0, mate)
    token_send(high, SPAN - 1, 1, 1, s + 2)
    token_send(low, SPAN - 1, 5, 2, s - 2)
    for d in range(1, HEAD):
        normalise(cols(lax.rem(h + d, HEAD), quarter))
    token_share(*slots[0])
    token_send(high, from_mate, 2 - 2 * y, 3, s + 2)
    token_send(low, from_mate, 6 - 2 * y, 4, s - 2)
    relay_round(0, 1)
    token_share(*slots[1])
    token_share(*slots[2])
    r.wq_all[:, cols(s, rows), :] = r.wq[...]
    r.wo_all[:, cols(s, rows)] = r.wo[...]
    token_share(*slots[3])
    token_share(*slots[4])
    token_send((y == 0) & low & high, 2, 0, 5, s + 2)
    token_send((y == 1) & low & high, 4, 6, 5, s - 2)
    relay_round(0, 2)
    relay_start(1)
    relay_round(0, 3)
    token_share(*slots[5])
    for cond, slot in slots[:3]:
        token_pass(cond, slot)
    relay_round(1, 1)
    relay_start(2)

    start, leader, span, pad = 0, 0, 0, 0
    for k in range(r.units.shape[0]):
        here = r.units[k]
        inside = (s >= start) & (s < start + here)
        leader = jnp.where(inside, start, leader)
        span = jnp.where(inside, here, span)
        pad = jnp.where(inside, r.pads[k], pad)
        start = start + here
    position = s - leader
    root = jnp.clip(SPAN - 1 - position, 0, SPAN - 1)
    total = span * BLK_DEV
    live = span * tokens - pad

    columns = lax.broadcasted_iota(jnp.int32, (1, SPAN * tokens), 1)
    usable = columns < live
    blocks = lax.div(columns, BLK)
    for hh in range(HEAD):
        for b in range(BLK_DEV):
            query = position * BLK_DEV + b
            count = jnp.zeros((1, SPAN * tokens), F32)
            for wanted in (query - 1, query, query + 1, 0, total - 1):
                count = count + jnp.where(blocks == wanted, 1.0, 0.0)
            for k in range(r.picks.shape[0]):
                raw = r.picks[k, b, hh]
                chosen = lax.rem(raw, BLK_DEV)
                for k_units in range(2, SPAN + 1):
                    chosen = jnp.where(span == k_units, lax.rem(raw, BLK_DEV * k_units), chosen)
                count = count + jnp.where(blocks == chosen, 1.0, 0.0)
            count = jnp.where((query == 0) | (query == total - 1), 1.0, count)
            held = usable & (count > 0)
            bias = jnp.log(jnp.maximum(count, 1.0))
            r.bias[hh, b : b + 1, :] = jnp.where(held, bias, NEGATIVE)

    ffn_src = {
        UP: lambda k: r.wu.at[:, cols(k, half)],
        DOWN: lambda k: r.wd.at[cols(k, half), :],
    }
    ffn_slot = {
        UP: lambda o: r.wu_all.at[cols(o, rows), :],
        DOWN: lambda o: r.wd_all.at[:, cols(o, rows)],
    }

    def ffn_start(w):
        i = w - UP
        for d in range(1, LINE):
            to = lax.rem(z + d, LINE)
            send(
                None, ffn_src[w](lax.rem(to, 2)), ffn_slot[w](s), r.f_ss.at[i, d - 1],
                r.f_rs.at[i, s], seq=to * 2 + y,
            )
        send(
            None, ffn_src[w](e), ffn_slot[w](s), r.f_ss.at[i, 3], r.f_rs.at[i, s], seq=mate
        )

    def by_distance(k):
        up = k + jnp.where(z <= k, 1, 0)
        down = k + jnp.where(LINE - 1 - z <= k, 1, 0)
        return jnp.where(z < LINE // 2, up, LINE - 1 - down)

    def ffn_forward(w, ks=(0, 1, 2)):
        i = w - UP
        for k in ks:
            o = by_distance(k) * 2 + y
            ref = ffn_slot[w](o)
            arrived(None, ref, r.f_rs.at[i, o])
            send(None, ref, ref, r.f_ss.at[i, 4 + k], r.f_rs.at[i, o], seq=mate)

    def ffn_finish(w):
        for d in range(LINE):
            o = lax.rem(z + d, LINE) * 2 + 1 - y
            arrived(None, ffn_slot[w](o), r.f_rs.at[w - UP, o])

    relay_round(1, 2)
    relay_round(2, 1)
    relay_round(1, 3)
    relay_round(2, 2)
    ffn_start(UP)
    relay_round(2, 3)
    for cond, slot in slots[3:]:
        token_pass(cond, slot)
    for ref, src in ((ffn_slot[UP](s), ffn_src[UP](e)), (ffn_slot[DOWN](s), ffn_src[DOWN](e))):
        ref[...] = src[...]

    ffn_start(DOWN)
    for cond, slot in slots:
        token_ready(cond, slot)
    relay_finish(0)
    scaling = HEAD_DIM ** (-0.5)
    for j in range(SPAN):
        q = pl.ds(j * tokens, tokens)
        rows_in = r.nall[root + j]
        r.kwin[q, :] = dot(rows_in, r.wq_all[1], ((1,), (0,))).astype(BF16)
        r.vwin[q, :] = dot(rows_in, r.wq_all[2], ((1,), (0,))).astype(BF16)
    relay_finish(1)
    part = dot(r.nall[SPAN - 1], r.wq_all[0], ((1,), (0,)))
    r.qs[...] = (part.astype(BF16).astype(F32) * scaling).astype(BF16)
    r.cotx[cols(e, tokens), :] = r.cot[...]
    beyond = (1 - x) * 2 + 1 - c

    def block_rows(unit, head):
        return pl.ds(al(unit * tokens + head * quarter, quarter), quarter)

    def cot_rows(unit, head):
        return r.cotx.at[block_rows(unit, head), :]

    send(
        None, r.cot.at[cols(h, quarter), :], cot_rows(e, h), r.c_ss.at[0], r.c_rs.at[h], seq=pair
    )

    def cot_share():
        ref = cot_rows(1 - e, h)
        arrived(None, ref, r.c_rs.at[h])
        send(None, ref, ref, r.c_ss.at[1], r.c_rs.at[h], head=across)
        send(None, ref, ref, r.c_ss.at[2], r.c_rs.at[h], head=twin)

    def cot_pass():
        ref = cot_rows(1 - e, across)
        arrived(None, ref, r.c_rs.at[across])
        send(None, ref, ref, r.c_ss.at[3], r.c_rs.at[across], head=twin)

    lanes = lax.div(lax.broadcasted_iota(jnp.int32, (1, head_w), 1), HEAD_DIM)
    none = jnp.zeros((), BF16)
    r.att[...] = jnp.zeros(r.att.shape, F32)

    def attend(hh, carry):
        mine = lanes == hh
        query = jnp.where(mine, r.qs[...], none)
        for j in range(SPAN):
            k = pl.ds(j * tokens, tokens)
            r.lg[:, k] = dot(query, r.kwin[k, :], ((1,), (1,)))
        for b in range(BLK_DEV):
            q = pl.ds(b * BLK, BLK)
            logits = r.lg[q, :] + r.bias[hh, b : b + 1, :]
            grown = jnp.exp(logits - jnp.max(logits, axis=-1, keepdims=True))
            scale = 1.0 / jnp.sum(grown, axis=-1, keepdims=True)
            r.prob[hh, q, :] = (grown * scale).astype(BF16)
        part = dot(r.prob[hh], r.vwin[...], ((1,), (0,)))
        r.att[...] += jnp.where(mine, part, 0.0)
        return carry

    lax.fori_loop(0, HEAD // 2, attend, 0)
    ffn_forward(UP, (0,))
    lax.fori_loop(HEAD // 2, HEAD, attend, 0)
    ffn_forward(UP, (1,))
    r.att_low[...] = r.att[...].astype(BF16)
    relay_finish(2)

    def rows_of(k):
        return cols(k, quarter)

    def reduce_start(op):
        for v in range(2):
            r.q1_send[op, v] = r.sum_f[rows_of(v * 2 + 1 - c), :].astype(BF16)
        send(None, r.q1_send.at[op], r.q1_recv.at[op], r.q1_ss.at[op], r.q1_rs.at[op], head=twin)

    def reduce_middle(op):
        arrived(None, r.q1_recv.at[op], r.q1_rs.at[op])
        block = r.sum_f[rows_of(across), :] + r.q1_recv[op, 1 - x].astype(F32)
        r.q2_send[op] = block.astype(BF16)
        send(None, r.q2_send.at[op], r.q2_recv.at[op], r.q2_ss.at[op], r.q2_rs.at[op], head=across)
        r.q_own[op] = r.sum_f[rows_of(h), :] + r.q1_recv[op, x].astype(F32)

    def reduce_finish(op):
        arrived(None, r.q2_recv.at[op], r.q2_rs.at[op])
        return r.q_own[op] + r.q2_recv[op].astype(F32)

    def spread_start(op, whole, value):
        whole[rows_of(h), :] = value
        ref = whole.at[rows_of(h), :]
        send(None, ref, ref, r.ag_ss.at[op, 0], r.ag_rs.at[op, h], head=across)
        send(None, ref, ref, r.ag_ss.at[op, 1], r.ag_rs.at[op, h], head=twin)

    def spread_pass(op, whole):
        ref = whole.at[rows_of(across), :]
        arrived(None, ref, r.ag_rs.at[op, across])
        send(None, ref, ref, r.ag_ss.at[op, 2], r.ag_rs.at[op, across], head=twin)

    def spread_finish(op, whole):
        for o in (twin, beyond):
            arrived(None, whole.at[rows_of(o), :], r.ag_rs.at[op, o])

    pair_sum = [r.sum_f, r.sum_g]

    def pair_start(op):
        for u in range(2):
            for v in range(2):
                block = pair_sum[op][block_rows(u, v * 2 + 1 - c), :]
                r.p1_send[op, u * 2 + v] = block.astype(BF16)
        send(None, r.p1_send.at[op], r.p1_recv.at[op], r.p1_ss.at[op], r.p1_rs.at[op], head=twin)

    def pair_middle(op):
        arrived(None, r.p1_recv.at[op], r.p1_rs.at[op])
        for du, dv in ((1, 1), (1, 0), (0, 1), (0, 0)):
            u, v = lax.rem(e + du, 2), lax.rem(x + dv, 2)
            block = pair_sum[op][block_rows(u, v * 2 + c), :] + r.p1_recv[op, u * 2 + v].astype(F32)
            if du or dv:
                k = u * 2 + v
                r.p2_send[op, k] = block.astype(BF16)
                send(
                    None, r.p2_send.at[op, k], r.p2_recv.at[op, e * 2 + x], r.p2_ss.at[op, k],
                    r.p2_rs.at[op, e * 2 + x], seq=pair if du else s, head=across if dv else h,
                )
            else:
                r.p_own[op] = block

    def pair_x(op):
        arrived(None, r.p1_recv.at[op], r.p1_rs.at[op])
        for du in (1, 0):
            u = lax.rem(e + du, 2)
            k = u * 2 + 1 - x
            block = pair_sum[op][block_rows(u, across), :] + r.p1_recv[op, k].astype(F32)
            r.p2_send[op, k] = block.astype(BF16)
            send(
                None, r.p2_send.at[op, k], r.p2_recv.at[op, u], r.p2_ss.at[op, k],
                r.p2_rs.at[op, u], head=across,
            )

    def pair_over(op):
        for du in (1, 0):
            u = lax.rem(e + du, 2)
            arrived(None, r.p2_recv.at[op, u], r.p2_rs.at[op, u])
            block = pair_sum[op][block_rows(u, h), :] + r.p1_recv[op, u * 2 + x].astype(F32)
            block = block + r.p2_recv[op, u].astype(F32)
            if du:
                k = u * 2 + x
                r.p2_send[op, k] = block.astype(BF16)
                send(
                    None, r.p2_send.at[op, k], r.p2_recv.at[op, 2], r.p2_ss.at[op, k],
                    r.p2_rs.at[op, 2], seq=pair,
                )
            else:
                r.p_own[op] = block

    def pair_end(op):
        arrived(None, r.p2_recv.at[op, 2], r.p2_rs.at[op, 2])
        return r.p_own[op] + r.p2_recv[op, 2].astype(F32)

    def pair_finish(op):
        result = r.p_own[op]
        for du, dv in ((0, 1), (1, 0), (1, 1)):
            k = lax.rem(e + du, 2) * 2 + lax.rem(x + dv, 2)
            arrived(None, r.p2_recv.at[op, k], r.p2_rs.at[op, k])
            result = result + r.p2_recv[op, k].astype(F32)
        return result

    r.sum_f[:tokens, :] = dot(r.att_low[...], r.wo_all[...], ((1,), (0,)))
    reduce_start(0)
    reduce_middle(0)
    ffn_forward(UP, (2,))
    ffn_forward(DOWN, (0,))
    middle = r.tok[rows_of(h), :].astype(F32) + reduce_finish(0)
    r.mid_own[...] = middle
    xhat, _ = norm_parts(middle)

    def n2_rows(unit, head):
        return r.n2x.at[block_rows(unit, head), :]

    r.n2x[block_rows(e, h), :] = (xhat * r.gains[2:3, :] + r.gains[3:4, :]).astype(BF16)
    mine, tag = n2_rows(e, h), e * 4 + h
    send(None, mine, mine, r.n2_ss.at[0], r.n2_rs.at[tag], seq=pair)
    send(None, mine, mine, r.n2_ss.at[1], r.n2_rs.at[tag], head=across)
    send(None, mine, mine, r.n2_ss.at[2], r.n2_rs.at[tag], head=twin)
    cot_share()
    ffn_forward(DOWN, (1,))
    for k, (unit, head) in enumerate(((e, across), (1 - e, h), (1 - e, across))):
        ref, tag = n2_rows(unit, head), unit * 4 + head
        arrived(None, ref, r.n2_rs.at[tag])
        if k == 1:
            send(None, ref, ref, r.n2_ss.at[6], r.n2_rs.at[tag], head=across)
        send(None, ref, ref, r.n2_ss.at[3 + k], r.n2_rs.at[tag], head=twin)
    cot_pass()
    ffn_forward(DOWN, (2,))
    ffn_finish(UP)
    ffn_finish(DOWN)
    for unit in (e, 1 - e):
        for head in (x * 2 + 1 - c, (1 - x) * 2 + 1 - c):
            arrived(None, n2_rows(unit, head), r.n2_rs.at[unit * 4 + head])
    for head in (twin, beyond):
        arrived(None, cot_rows(1 - e, head), r.c_rs.at[head])

    root_c = (2.0 / 3.141592653589793) ** 0.5
    r.up_send[half // 128 :, :] = jnp.zeros((8 - half // 128, 128), F32)
    for j in range(half // 256):
        f = pl.ds(j * 256, 256)
        bias = r.upb[:, pl.ds(al(e * half + j * 256, 256), 256)].astype(F32)
        v = dot(r.n2x[...], r.wu_all[:, f], ((1,), (0,))) + bias
        t = jnp.tanh(root_c * (v + 0.044715 * (v * v * v)))
        r.hid[:, f] = (0.5 * v * (1.0 + t)).astype(BF16)
        slope = 0.5 * (1.0 + t) + 0.5 * v * (1.0 - t * t) * (root_c * (1.0 + 0.134145 * v * v))
        low_p = (dot(r.cotx[...], r.wd_all[f, :], ((1,), (1,))) * slope).astype(BF16)
        r.gp[:, f] = low_p
        sums = jnp.sum(low_p.astype(F32), axis=0, keepdims=True)
        r.up_send[2 * j : 2 * j + 1, :] = sums[:, :128]
        r.up_send[2 * j + 1 : 2 * j + 2, :] = sums[:, 128:]

    grad_send = {QKV_KV: r.skv, QKV_Q: r.sq, OUT: r.so, UP: r.su, DOWN: r.sd}
    grad_arrive = {QKV_KV: r.akv, QKV_Q: r.aq, OUT: r.ao, UP: r.au, DOWN: r.ad}
    grad_again = {QKV_KV: r.bkv, QKV_Q: r.bq, OUT: r.bo, UP: r.bu, DOWN: r.bd}
    grad_final = {QKV_KV: r.rkv, QKV_Q: r.rq, OUT: r.ro, UP: r.ru, DOWN: r.rd}

    def tile_of(i):
        return lax.rem(z + 1 + i, LINE)

    def grad_cross(w, zz):
        send(
            None, grad_send[w].at[zz * 2 + 1 - y], grad_arrive[w].at[zz], r.ra_ss.at[w, zz],
            r.ra_rs.at[w, zz], seq=mate,
        )

    def grad_along(w, ks=(1, 2, 3)):
        for d in ks:
            zz = lax.rem(z + d, LINE)
            arrived(None, grad_arrive[w].at[zz], r.ra_rs.at[w, zz])
            both = grad_send[w][zz * 2 + y].astype(F32) + grad_arrive[w][zz].astype(F32)
            grad_again[w][zz] = both.astype(BF16)
            send(
                None, grad_again[w].at[zz], grad_final[w].at[z], r.rb_ss.at[w, zz],
                r.rb_rs.at[w, z], seq=zz * 2 + y,
            )

    outer, inner = (z == 0) | (z == LINE - 1), (z == 1) | (z == LINE - 2)
    far_half = 2 - 2 * lax.div(z, 2)
    far_inner = 2 - lax.div(z, 2)
    grad_hold = {QKV_KV: r.hkv, QKV_Q: r.hq, OUT: r.ho}

    def tile_far(i):
        return (far_half, far_half + 1, pair_z, z)[i]

    def grad_first(w):
        for k in range(3):
            zz = tile_far(k)
            arrived(None, grad_arrive[w].at[zz], r.ra_rs.at[w, zz])
            both = grad_send[w][zz * 2 + y].astype(F32) + grad_arrive[w][zz].astype(F32)
            grad_again[w][zz] = both.astype(BF16)
            if k < 2:
                send(
                    outer, grad_again[w].at[zz], grad_hold[w].at[k], r.rh_ss.at[w, k],
                    r.rh_rs.at[w, k], seq=pair,
                )
            else:
                send(
                    None, grad_again[w].at[zz], grad_final[w].at[z], r.rb_ss.at[w, zz],
                    r.rb_rs.at[w, z], seq=pair,
                )

    def grad_second(w):
        for k in range(2):
            zz = tile_far(k)
            arrived(inner, grad_hold[w].at[k], r.rh_rs.at[w, k])

            @pl.when(inner)
            def _():
                both = grad_again[w][zz].astype(F32) + grad_hold[w][k].astype(F32)
                grad_again[w][zz] = both.astype(BF16)

            send(
                inner, grad_again[w].at[zz], grad_final[w].at[z], r.rb_ss.at[w, zz],
                r.rb_rs.at[w, z], seq=zz * 2 + y,
            )

    def grad_own(w):
        arrived(None, grad_arrive[w].at[z], r.ra_rs.at[w, z])
        return grad_send[w][z * 2 + y].astype(F32) + grad_arrive[w][z].astype(F32)

    def grad_from(w, o):
        arrived(None, grad_final[w].at[o], r.rb_rs.at[w, o])
        return grad_final[w][o].astype(F32)

    def grad_sum(w):
        return grad_own(w) + grad_from(w, pair_z) + grad_from(w, far_inner)

    def grad_halves(w):
        same = grad_own(w) + grad_from(w, lax.rem(z + 2, LINE))
        other = grad_from(w, lax.rem(z + 1, LINE)) + grad_from(w, lax.rem(z + 3, LINE))
        return same, other

    def down_step(i):
        zz = tile_of(i)
        part = dot(r.hid[...], r.cotx[:, cols(zz, 256)], ((0,), (0,))).astype(BF16)
        r.sd[zz * 2] = part[:, :rows]
        r.sd[zz * 2 + 1] = part[:, rows:]
        grad_cross(DOWN, zz)

    def up_step(i):
        zz = tile_of(i)
        part = dot(r.n2x[:, cols(zz, 256)], r.gp[...], ((0,), (0,))).astype(BF16)
        r.su[zz * 2] = part[:rows]
        r.su[zz * 2 + 1] = part[rows:]
        grad_cross(UP, zz)

    down_step(0)
    r.sum_f[...] = dot(r.gp[...], r.wu_all[...], ((1,), (1,)))
    pair_start(0)
    down_step(1)
    pair_middle(0)
    r.sum_g[...] = dot(r.hid[...], r.wd_all[...], ((1,), (0,)))
    pair_start(1)
    down_step(2)
    down_step(3)
    pair_x(1)
    for i in range(LINE):
        up_step(i)
    for d in range(1, SEQ):
        send(
            None, r.up_send, r.up_recv.at[s], r.up_ss.at[d], r.up_rs.at[s],
            seq=lax.rem(s + d, SEQ),
        )

    grad_two = pair_finish(0)
    xhat, inverse = norm_parts(r.mid_own[...])
    dy = r.cot[rows_of(h), :].astype(F32)
    grad_mid = dy + norm_backward(xhat, inverse, grad_two * r.gains[2:3, :])
    r.gm_own[...] = grad_mid
    spread_start(0, r.gb, grad_mid.astype(BF16))
    r.sm_send[2:3, :] = jnp.sum(grad_two * xhat, axis=0, keepdims=True)
    r.sm_send[3:4, :] = jnp.sum(grad_two, axis=0, keepdims=True)
    r.sm_send[4:5, :] = jnp.sum(dy, axis=0, keepdims=True)
    r.sm_send[5:8, :] = jnp.zeros((3, width), F32)

    grad_along(DOWN)
    pair_over(1)
    spread_pass(0, r.gb)
    spread_finish(0, r.gb)
    r.gatt[...] = dot(r.gb[...], r.wo_all[...], ((1,), (1,))).astype(BF16)
    for i in range(LINE):
        zz = tile_far(i)
        part = dot(r.att_low[...], r.gb[:, cols(zz, 256)], ((0,), (0,))).astype(BF16)
        r.so[zz * 2] = part[:, :rows]
        r.so[zz * 2 + 1] = part[:, rows:]
        grad_cross(OUT, zz)
    grad_along(UP, (1, 2))

    r.dq[...] = jnp.zeros(r.dq.shape, F32)
    r.dk[...] = jnp.zeros(r.dk.shape, F32)
    r.dv[...] = jnp.zeros(r.dv.shape, F32)

    def attend_back(hh, carry):
        mine = lanes == hh
        query = jnp.where(mine, r.qs[...], none)
        grad = jnp.where(mine, r.gatt[...], none)
        for j in range(SPAN):
            k = pl.ds(j * tokens, tokens)
            r.lg[:, k] = dot(grad, r.vwin[k, :], ((1,), (1,)))
        for b in range(BLK_DEV):
            q = pl.ds(b * BLK, BLK)
            chance, grown = r.prob[hh, q, :].astype(F32), r.lg[q, :]
            inner = jnp.sum(chance * grown, axis=-1, keepdims=True)
            r.ds[q, :] = (chance * (grown - inner)).astype(BF16)
        r.dq[...] += jnp.where(mine, dot(r.ds[...], r.kwin[...], ((1,), (0,))), 0.0)
        for j in range(SPAN):
            k = pl.ds(j * tokens, tokens)
            r.dk[k, :] += dot(r.ds[:, k], query, ((0,), (0,)))
            r.dv[k, :] += dot(r.prob[hh, :, k], grad, ((0,), (0,)))
        return carry

    lax.fori_loop(0, HEAD, attend_back, 0)
    for k in range(2 * (SPAN - 1) + SPAN):
        j = k - (SPAN - 1)
        if 0 <= j < SPAN:
            q = pl.ds(j * tokens, tokens)
            r.dkv_pad[k, :, :head_w] = r.dk[q, :].astype(BF16)
            r.dkv_pad[k, :, head_w:] = r.dv[q, :].astype(BF16)
        else:
            r.dkv_pad[k] = jnp.zeros(r.dkv_pad.shape[1:], BF16)
    for k in range(NEAR):
        r.dkv_send[k] = r.dkv_pad[k + SPAN - 1 - root]
    r.gtq[...] = (r.dq[...] * scaling).astype(BF16)

    def grad_hop(cond, slot, into, k, to):
        send(cond, r.dkv_send.at[slot], r.dkv_recv.at[into], r.dkv_ss.at[k], r.dkv_rs.at[into], seq=to)

    def add_to(slot, *froms):
        both = r.dkv_send[slot].astype(F32)
        for k in froms:
            both = both + r.dkv_recv[k].astype(F32)
        r.dkv_send[slot] = both.astype(BF16)

    def grad_wait(cond, into):
        arrived(cond, r.dkv_recv.at[into], r.dkv_rs.at[into])

    FAR, ABOVE, BELOW, LINE_ABOVE, LINE_BELOW, MATE = range(6)
    grad_hop((y == 0) & (z >= 2), 0, FAR, 0, s - 2)
    grad_hop((y == 1) & (z <= 1), 6, FAR, 0, s + 2)
    grad_hop((y == 0) & high, 6, BELOW, 1, s + 2)
    grad_hop((y == 1) & low, 0, ABOVE, 1, s - 2)

    grad_along(UP, (3,))

    for i in range(LINE):
        zz = tile_far(i)
        part = jnp.zeros((256, 2 * head_w), F32)
        for j in range(SPAN):
            part = part + dot(
                r.nall[root + j, :, cols(zz, 256)], r.dkv_pad[j + SPAN - 1], ((0,), (0,))
            )
        part = part.astype(BF16)
        for v in range(2):
            for k in range(2):
                r.skv[zz * 2 + v, k] = part[v * rows : (v + 1) * rows, k * head_w : (k + 1) * head_w]
        grad_cross(QKV_KV, zz)
        if i == 1:
            grad_wait(low & high, FAR)
            add_to(2 + 2 * y, FAR)
            grad_hop((y == 0) & low, 2, ABOVE, 2, s - 2)
            grad_hop((y == 1) & high, 4, BELOW, 2, s + 2)
            grad_hop(low, 1, LINE_ABOVE, 3, s - 2)
            grad_hop(high, 5, LINE_BELOW, 4, s + 2)
    grad_first(OUT)
    grad_wait(high, ABOVE)
    grad_wait(low, BELOW)
    add_to(from_mate, ABOVE, BELOW)
    grad_hop(None, from_mate, MATE, 5, mate)
    for i in range(LINE):
        zz = tile_far(i)
        part = dot(r.nall[SPAN - 1, :, cols(zz, 256)], r.gtq[...], ((0,), (0,))).astype(BF16)
        r.sq[zz * 2] = part[:rows]
        r.sq[zz * 2 + 1] = part[rows:]
        grad_cross(QKV_Q, zz)
    grad_second(OUT)
    grad_first(QKV_KV)
    ffn = pair_end(1)
    spread_start(1, r.out_o, (r.mid_own[...] + ffn + r.gains[4:5, :]).astype(BF16))
    grad_wait(high, LINE_ABOVE)
    grad_wait(low, LINE_BELOW)
    grad_wait(None, MATE)
    whole = r.dkv_send[SPAN - 1].astype(F32)
    for k in (LINE_ABOVE, LINE_BELOW, MATE):
        whole = whole + r.dkv_recv[k].astype(F32)
    r.gtkv[...] = whole.astype(BF16)

    r.sum_f[:tokens, :] = (
        dot(r.gtq[...], r.wq_all[0], ((1,), (1,)))
        + dot(r.gtkv[:, :head_w], r.wq_all[1], ((1,), (1,)))
        + dot(r.gtkv[:, head_w:], r.wq_all[2], ((1,), (1,)))
    )
    reduce_start(1)
    reduce_middle(1)
    grad_second(QKV_KV)
    grad_one = reduce_finish(1)
    xhat, inverse = norm_parts(r.tok[rows_of(h), :].astype(F32))
    r.sm_send[0:1, :] = jnp.sum(grad_one * xhat, axis=0, keepdims=True)
    r.sm_send[1:2, :] = jnp.sum(grad_one, axis=0, keepdims=True)
    for d in range(1, SEQ):
        to = lax.rem(s + d, SEQ)
        send(
            None, r.sm_send.at[:, cols(to, rows)], r.sm_recv.at[s], r.sm_ss.at[d], r.sm_rs.at[s],
            seq=to,
        )
    spread_pass(1, r.out_o)
    grad_first(QKV_Q)
    grad_x = r.gm_own[...] + norm_backward(xhat, inverse, grad_one * r.gains[0:1, :])
    spread_start(2, r.xgb, grad_x.astype(BF16))

    same, other = grad_halves(DOWN)
    r.gd_o[cols(e, half), :] = same
    r.gd_o[cols(1 - e, half), :] = other
    same, other = grad_halves(UP)
    r.gu_o[:, cols(e, half)] = same
    r.gu_o[:, cols(1 - e, half)] = other
    spread_pass(2, r.xgb)
    grad_second(QKV_Q)
    r.go_o[...] = grad_sum(OUT)

    r.sm_recv[s] = r.sm_send[:, cols(s, rows)]
    r.up_recv[s] = r.up_send[...]
    for d in range(1, SEQ):
        o = lax.rem(s + d, SEQ)
        arrived(None, r.sm_recv.at[o], r.sm_rs.at[o], r.vec)
        arrived(None, r.up_recv.at[o], r.up_rs.at[o])
    part = r.sm_recv[0]
    for o in range(1, SEQ):
        part = part + r.sm_recv[o]
    r.sm_own[...] = part
    for d in range(1, HEAD):
        send(
            None, r.sm_own, r.sm_two.at[h], r.sm2_ss.at[d], r.sm2_rs.at[h],
            head=lax.rem(h + d, HEAD),
        )
    r.sm_two[h] = part
    tall = half // 128
    for u in range(2):
        ups = jnp.zeros((tall, 128), F32)
        for o in range(SEQ):
            if (o // 2) % 2 == u:
                ups = ups + r.up_recv[o, :tall, :]
        r.small_o[8 + u * tall : 8 + (u + 1) * tall, :] = ups
    spread_finish(1, r.out_o)
    spread_finish(2, r.xgb)
    r.xg_o[...] = r.xgb[...].astype(F32)
    for d in range(1, HEAD):
        o = lax.rem(h + d, HEAD)
        arrived(None, r.sm_two.at[o], r.sm2_rs.at[o])
    r.small_o[0:8, :] = (r.sm_two[0] + r.sm_two[1]) + (r.sm_two[2] + r.sm_two[3])
    r.gq_o[0] = grad_sum(QKV_Q)
    r.gq_o[1:3] = grad_sum(QKV_KV)

    for cond, one in sent:
        when(cond, one.wait_send)


def local_fused(
    tokens, w_qkv, w_out, ln1_gain, ln1_bias, ln2_gain, ln2_bias, w_up, up_bias, w_down, down_bias,
    seq_units, seq_pad, rand_picks, cotangent,
):
    tok, width = tokens.shape
    rows, _, head_w = w_qkv.shape
    hidden = w_up.shape[1]
    half = hidden // 2
    quarter = tok // HEAD
    keys = SPAN * tok
    smem, vmem = pl.BlockSpec(memory_space=pltpu.SMEM), pl.BlockSpec(memory_space=pltpu.VMEM)
    ins = dict(
        units=seq_units, pads=seq_pad, picks=jnp.transpose(rand_picks, (2, 0, 1)), tok=tokens,
        cot=cotangent, wq=jnp.transpose(w_qkv, (1, 0, 2)), wo=w_out, wu=w_up, wd=w_down,
        g1=ln1_gain, b1=ln1_bias, g2=ln2_gain, b2=ln2_bias, b3=down_bias,
        upb=up_bias.reshape(1, hidden),
    )
    outs = dict(
        out_o=((tok, width), BF16), xg_o=((tok, width), F32), gq_o=((3, rows, head_w), F32),
        go_o=((head_w, rows), F32), gu_o=((rows, hidden), F32), gd_o=((hidden, rows), F32),
        small_o=((16, rows), F32),
    )
    scratch = dict(
        wq_all=((3, width, head_w), BF16), wo_all=((head_w, width), BF16),
        wu_all=((width, half), BF16), wd_all=((half, width), BF16), vec=((8, rows), F32),
        gains=((8, width), F32), nall=((NEAR, tok, width), BF16),
        qs=((tok, head_w), BF16),
        kwin=((keys, head_w), BF16), vwin=((keys, head_w), BF16), lg=((tok, keys), F32),
        prob=((HEAD, tok, keys), BF16), ds=((tok, keys), BF16),
        att=((tok, head_w), F32), att_low=((tok, head_w), BF16), n2x=((2 * tok, width), BF16),
        cotx=((2 * tok, width), BF16), hid=((2 * tok, half), BF16), gp=((2 * tok, half), BF16),
        gb=((tok, width), BF16), xgb=((tok, width), BF16), mid_own=((quarter, width), F32),
        gm_own=((quarter, width), F32), gatt=((tok, head_w), BF16), dq=((tok, head_w), F32),
        dk=((keys, head_w), F32), dv=((keys, head_w), F32),
        dkv_pad=((NEAR + SPAN - 1, tok, 2 * head_w), BF16),
        dkv_send=((NEAR, tok, 2 * head_w), BF16), dkv_recv=((6, tok, 2 * head_w), BF16),
        gtq=((tok, head_w), BF16), gtkv=((tok, 2 * head_w), BF16),
        q1_send=((2, 2, quarter, width), BF16), q1_recv=((2, 2, quarter, width), BF16),
        q2_send=((2, quarter, width), BF16), q2_recv=((2, quarter, width), BF16),
        q_own=((2, quarter, width), F32),
        sum_f=((2 * tok, width), F32), sum_g=((2 * tok, width), F32), bias=((HEAD, 8, keys), F32),
        p1_send=((2, 4, quarter, width), BF16), p1_recv=((2, 4, quarter, width), BF16),
        p2_send=((2, 4, quarter, width), BF16), p2_recv=((2, 4, quarter, width), BF16),
        p_own=((2, quarter, width), F32), sm_send=((8, width), F32),
        sm_recv=((SEQ, 8, rows), F32), sm_own=((8, rows), F32), sm_two=((HEAD, 8, rows), F32),
        up_send=((8, 128), F32), up_recv=((SEQ, 8, 128), F32),
    )
    shards = dict(
        kv=(2, rows, head_w), q=(rows, head_w), o=(head_w, rows), u=(rows, half), d=(half, rows)
    )
    for lead, count in (("s", SEQ), ("a", LINE), ("b", LINE), ("r", LINE), ("h", 2)):
        for name, shape in shards.items():
            scratch[lead + name] = ((count,) + shape, BF16)
    semaphores = dict(
        g_ss=(3, 16), g_rs=(3, SEQ), f_ss=(2, 7), f_rs=(2, SEQ), v_ss=(7,), v_rs=(SEQ,),
        t_ns=(6,), t_ss=(NEAR, 3), t_rs=(NEAR, HEAD), dkv_ss=(6,), dkv_rs=(6,), c_ss=(4,), c_rs=(HEAD,),
        q1_ss=(2,), q1_rs=(2,), q2_ss=(2,), q2_rs=(2,), ag_ss=(3, 3), ag_rs=(3, HEAD), n2_ss=(7,),
        n2_rs=(8,), p1_ss=(2,), p1_rs=(2,), p2_ss=(2, 4), p2_rs=(2, 4), ra_ss=(5, LINE),
        ra_rs=(5, LINE), rh_ss=(5, 2), rh_rs=(5, 2), rb_ss=(5, LINE), rb_rs=(5, LINE), sm_ss=(SEQ,), sm_rs=(SEQ,),
        sm2_ss=(HEAD,), sm2_rs=(HEAD,), up_ss=(SEQ,), up_rs=(SEQ,),
    )
    names = [*ins, *outs, *scratch, *semaphores]
    results = pl.pallas_call(
        functools.partial(fused_kernel, names),
        out_shape=[jax.ShapeDtypeStruct(*o) for o in outs.values()],
        in_specs=[smem] * 3 + [vmem] * (len(ins) - 3),
        out_specs=[vmem] * len(outs),
        scratch_shapes=[pltpu.VMEM(*v) for v in scratch.values()]
        + [pltpu.SemaphoreType.DMA(v) for v in semaphores.values()],
        compiler_params=pltpu.CompilerParams(
            collective_id=0, has_side_effects=True, vmem_limit_bytes=VMEM_BYTES
        ),
        name="fused_layer",
    )(*ins.values())
    large = list(outs.values())[:-1]
    handed = pl.pallas_call(
        hand_over_kernel,
        out_shape=[jax.ShapeDtypeStruct(*o) for o in large]
        + [jax.ShapeDtypeStruct((rows,), F32)] * 5
        + [jax.ShapeDtypeStruct((hidden,), F32)],
        in_specs=[vmem] * len(outs),
        out_specs=[vmem] * (len(large) + 6),
        name="hand_over",
    )(*results)
    out, xg, gq, go, gu, gd, g1, b1, g2, b2, b3, upg = handed
    return out, xg, jnp.transpose(gq, (1, 0, 2)), go, g1, b1, g2, b2, gu, upg, gd, b3


def hand_over_kernel(*refs):
    large = (len(refs) - 7) // 2
    small, vectors = refs[large], refs[2 * large + 1 :]
    for k in range(large):
        refs[large + 1 + k][...] = refs[k][...]
    for k in range(5):
        vectors[k][...] = small[k, :]
    for k in range(8):
        vectors[5][pl.ds(k * 128, 128)] = small[8 + k, :]


IN_SPECS = (
    P("seq", None), P("seq", None, "head"), P("head", "seq"), P("seq"), P("seq"), P("seq"),
    P("seq"), P("seq", "head"), P("head"), P("head", "seq"), P("seq"), P(), P(),
    P("seq", "head", None), P("seq", None),
)
OUT_SPECS = (
    P("seq", None), P("seq", None), P("seq", None, "head"), P("head", "seq"), P("seq"), P("seq"),
    P("seq"), P("seq"), P("seq", "head"), P("head"), P("head", "seq"), P("seq"),
)


def solution(mesh):
    fits = mesh.shape["seq"] == SEQ and mesh.shape["head"] == HEAD
    return jax.shard_map(
        local_fused if fits else local_general, mesh=mesh, in_specs=IN_SPECS,
        out_specs=OUT_SPECS, check_vma=False,
    )
```

```python
import functools
import types

import jax
import jax.numpy as jnp
from jax import lax
from jax.experimental import pallas as pl
from jax.experimental.pallas import tpu as pltpu
from jax.sharding import PartitionSpec as P

HEAD_DIM = 64
BLK = 64
SPAN = 4
BLK_DEV = 4
EPSILON = 1e-05
NEGATIVE = -1e30
F32 = jnp.float32
BF16 = jnp.bfloat16


def shifted(value, axis, steps):
    count = lax.axis_size(axis)
    first, last = max(0, -steps), min(count, count - steps)
    return lax.ppermute(value, axis, [(i, i + steps) for i in range(first, last)])


def norm_parts(features):
    average = jnp.mean(features, axis=-1, keepdims=True)
    centred = features - average
    spread = jnp.mean(centred * centred, axis=-1, keepdims=True)
    inverse = lax.rsqrt(spread + EPSILON)
    return centred * inverse, inverse


def norm_backward(xhat, inverse, scaled):
    first = jnp.mean(scaled, axis=-1, keepdims=True)
    second = jnp.mean(scaled * xhat, axis=-1, keepdims=True)
    return inverse * (scaled - first - xhat * second)


def dot(a, b, dims):
    return lax.dot_general(a, b, (dims, ((), ())), preferred_element_type=F32)


def sequence_place(seq_units, seq_pad):
    device = lax.axis_index("seq")
    start, leader, span, pad = 0, 0, 0, 0
    for k in range(seq_units.shape[0]):
        units = seq_units[k]
        inside = (device >= start) & (device < start + units)
        leader = jnp.where(inside, start, leader)
        span = jnp.where(inside, units, span)
        pad = jnp.where(inside, seq_pad[k], pad)
        start = start + units
    return device - leader, span, pad


def key_counts(position, span, picks):
    blocks = lax.broadcasted_iota(jnp.int32, (1, 1, SPAN * BLK_DEV), 2)
    query = position * BLK_DEV + lax.broadcasted_iota(jnp.int32, (BLK_DEV, 1, 1), 0)
    total = span * BLK_DEV
    count = jnp.zeros((BLK_DEV, picks.shape[1], SPAN * BLK_DEV), F32)
    for wanted in (query - 1, query, query + 1, 0, total - 1):
        count = count + (blocks == wanted).astype(F32)
    chosen = picks % total
    for r in range(picks.shape[2]):
        count = count + (blocks == chosen[:, :, r : r + 1]).astype(F32)
    return jnp.where((query == 0) | (query == total - 1), 1.0, count)


def local_general(
    tokens, w_qkv, w_out, ln1_gain, ln1_bias, ln2_gain, ln2_bias, w_up, up_bias, w_down, down_bias,
    seq_units, seq_pad, rand_picks, cotangent,
):
    tok, width = tokens.shape
    heads = w_qkv.shape[2] // HEAD_DIM
    rows = lambda v: lax.all_gather(v, "seq", axis=0, tiled=True)
    cols = lambda v: lax.all_gather(v, "seq", axis=1, tiled=True)
    vectors = jnp.stack([ln1_gain, ln1_bias, ln2_gain, ln2_bias, down_bias], axis=0)
    gain_one, shift_one, gain_two, shift_two, down_shift = [
        v[None].astype(F32) for v in cols(vectors)
    ]
    qkv = rows(w_qkv)
    out_w, up_w, down_w = cols(w_out), rows(w_up), cols(w_down)
    position, span, pad = sequence_place(seq_units, seq_pad)
    root = SPAN - 1 - position
    inputs = tokens.astype(F32)
    xhat_one, inv_one = norm_parts(inputs)
    normed = (xhat_one * gain_one + shift_one).astype(BF16)
    triple = jnp.einsum("td,dcf->tcf", normed, qkv, preferred_element_type=F32).astype(BF16)
    own = jnp.stack([triple[:, 1], triple[:, 2]], axis=0)
    pieces = [own if o == 0 else shifted(own, "seq", -o) for o in range(1 - SPAN, SPAN)]
    nearby = jnp.stack(pieces, axis=0)
    window = lax.dynamic_slice_in_dim(nearby, root, SPAN, 0)
    split = lambda v: v.reshape(v.shape[0], heads, HEAD_DIM)
    keys = split(window[:, 0].reshape(SPAN * tok, -1))
    values = split(window[:, 1].reshape(SPAN * tok, -1))
    queries = split(triple[:, 0])
    scaling = HEAD_DIM ** (-0.5)
    live = jnp.arange(SPAN * tok, dtype=jnp.int32) < span * tok - pad
    count = jnp.repeat(key_counts(position, span, rand_picks), BLK, axis=2)
    count = jnp.where(live[None, None], count, 0.0)
    count = jnp.transpose(jnp.repeat(count, BLK, axis=0), (1, 0, 2))
    logits = jnp.einsum("qhd,khd->hqk", queries, keys, preferred_element_type=F32) * scaling
    logits = jnp.where(count > 0, logits, NEGATIVE)
    grown = jnp.exp(logits - jnp.max(logits, axis=-1, keepdims=True)) * count
    chances = grown / jnp.sum(grown, axis=-1, keepdims=True)
    chances_low = chances.astype(BF16)
    attended = jnp.einsum("hqk,khd->qhd", chances_low, values, preferred_element_type=F32)
    attended = attended.astype(BF16).reshape(tok, heads * HEAD_DIM)
    middle = inputs + lax.psum(dot(attended, out_w, ((1,), (0,))), "head")
    xhat_two, inv_two = norm_parts(middle)
    normed_two = (xhat_two * gain_two + shift_two).astype(BF16)
    pre_act = dot(normed_two, up_w, ((1,), (0,))) + up_bias.astype(F32)[None]
    hidden, pull = jax.vjp(lambda v: jax.nn.gelu(v, approximate=True), pre_act)
    hidden = hidden.astype(BF16)
    ffn = lax.psum(dot(hidden, down_w, ((1,), (0,))).astype(BF16), "head").astype(F32)
    output = (middle + ffn + down_shift).astype(BF16)
    grad_out = cotangent.astype(F32)
    grad_w_down = dot(hidden, cotangent, ((0,), (0,)))
    grad_pre = pull(dot(cotangent, down_w, ((1,), (1,))))[0].astype(BF16)
    grad_w_up = dot(normed_two, grad_pre, ((0,), (0,)))
    grad_up_bias = lax.psum(jnp.sum(grad_pre.astype(F32), axis=0), "seq")
    grad_two = lax.psum(dot(grad_pre, up_w, ((1,), (1,))), "head")
    grad_middle = grad_out + norm_backward(xhat_two, inv_two, grad_two * gain_two)
    grad_branch = grad_middle.astype(BF16)
    grad_w_out = dot(attended, grad_branch, ((0,), (0,)))
    grad_att = split(dot(grad_branch, out_w, ((1,), (1,))).astype(BF16))
    grad_prob = jnp.einsum("qhd,khd->hqk", grad_att, values, preferred_element_type=F32)
    inner = jnp.sum(chances * grad_prob, axis=-1, keepdims=True)
    grad_logit = (chances * (grad_prob - inner)).astype(BF16)
    dq = scaling * jnp.einsum("hqk,khd->qhd", grad_logit, keys, preferred_element_type=F32)
    dk = scaling * jnp.einsum("hqk,qhd->khd", grad_logit, queries, preferred_element_type=F32)
    dv = jnp.einsum("hqk,qhd->khd", chances_low, grad_att, preferred_element_type=F32)
    part = jnp.stack([dk.reshape(SPAN, tok, -1), dv.reshape(SPAN, tok, -1)], axis=1)
    near = jnp.zeros((2 * SPAN - 1,) + part.shape[1:], F32)
    near = lax.dynamic_update_slice_in_dim(near, part, root, 0)
    owned = near[SPAN - 1]
    for offset in range(1 - SPAN, SPAN):
        if offset:
            owned = owned + shifted(near[offset + SPAN - 1], "seq", offset)
    owned = owned.astype(BF16)
    grad_triple = jnp.stack([dq.reshape(tok, -1).astype(BF16), owned[0], owned[1]], axis=1)
    grad_w_qkv = jnp.einsum("td,tcf->dcf", normed, grad_triple, preferred_element_type=F32)
    grad_one = lax.psum(
        jnp.einsum("tcf,dcf->td", grad_triple, qkv, preferred_element_type=F32), "head"
    )
    x_grad = grad_middle + norm_backward(xhat_one, inv_one, grad_one * gain_one)
    sums = jnp.stack(
        [
            jnp.sum(grad_one * xhat_one, axis=0), jnp.sum(grad_one, axis=0),
            jnp.sum(grad_two * xhat_two, axis=0), jnp.sum(grad_two, axis=0),
            jnp.sum(grad_out, axis=0),
        ],
        axis=0,
    )
    scatter = lambda v, d: lax.psum_scatter(v, "seq", scatter_dimension=d, tiled=True)
    sums = scatter(sums, 1)
    return (
        output, x_grad, scatter(grad_w_qkv, 0), scatter(grad_w_out, 1), sums[0], sums[1], sums[2],
        sums[3], scatter(grad_w_up, 0), grad_up_bias, scatter(grad_w_down, 1), sums[4],
    )


MESH = pl.DeviceIdType.MESH
SEQ = 8
HEAD = 4
LINE = 4
NEAR = 2 * SPAN - 1
QKV_KV, QKV_Q, OUT, UP, DOWN = range(5)
VMEM_BYTES = 60 * 1024 * 1024


def al(value, multiple):
    return pl.multiple_of(value, multiple)


def fused_kernel(names, *refs):
    r = types.SimpleNamespace(**dict(zip(names, refs)))
    s, h = lax.axis_index("seq"), lax.axis_index("head")
    z, y, x, c = lax.div(s, 2), lax.rem(s, 2), lax.div(h, 2), lax.rem(h, 2)
    e = lax.rem(z, 2)
    pair_z = z + 1 - 2 * e
    mate = z * 2 + 1 - y
    pair = pair_z * 2 + y
    twin = x * 2 + 1 - c
    across = (1 - x) * 2 + c
    tokens, width = r.tok.shape
    quarter = tokens // HEAD
    head_w = r.qs.shape[1]
    rows = r.wq.shape[1]
    half = r.wu_all.shape[1]
    sent = []

    def copy(src, dst, ss, rs, **where):
        return pltpu.make_async_remote_copy(
            src_ref=src, dst_ref=dst, send_sem=ss, recv_sem=rs, device_id=where,
            device_id_type=MESH,
        )

    def when(cond, then):
        if cond is None:
            then()
        else:
            pl.when(cond)(lambda: then())

    def send(cond, *args, **where):
        one = copy(*args, **where)
        when(cond, one.start)
        sent.append((cond, one))

    def arrived(cond, dst, rs, like=None):
        when(cond, copy(dst if like is None else like, dst, r.v_ss.at[0], rs, seq=mate).wait_recv)

    barrier = pltpu.get_barrier_semaphore()
    greeted = [{"seq": lax.rem(s + d, SEQ)} for d in range(1, SEQ)]
    greeted += [{"head": lax.rem(h + d, HEAD)} for d in range(1, HEAD)]
    greeted += [{"seq": pair, "head": across}]
    for where in greeted:
        pl.semaphore_signal(barrier, inc=1, device_id=where, device_id_type=MESH)
    for k, ref in enumerate((r.g1, r.b1, r.g2, r.b2, r.b3)):
        r.vec[k : k + 1, :] = ref[...].reshape(1, rows).astype(F32)
    r.vec[5:8, :] = jnp.zeros((3, rows), F32)
    r.upb_f[...] = r.upb[...].reshape(1, 2 * half).astype(F32)
    pl.semaphore_wait(barrier, len(greeted))

    def cols(o, size):
        return pl.ds(al(o * size, size), size)

    relay_slot = [
        lambda o: r.wq_all.at[1:3, cols(o, rows), :],
        lambda o: r.wq_all.at[0, cols(o, rows), :],
        lambda o: r.wo_all.at[:, cols(o, rows)],
    ]
    relay_src = [r.wq.at[1:3], r.wq.at[0], r.wo]

    def relay_start(w):
        src, dst, rs = relay_src[w], relay_slot[w](s), r.g_rs.at[w, s]
        send(z < LINE - 1, src, dst, r.g_ss.at[w, 0], rs, seq=s + 2)
        send(z > 0, src, dst, r.g_ss.at[w, 4], rs, seq=s - 2)
        send(None, src, dst, r.g_ss.at[w, 8], rs, seq=mate)

    def relay_round(w, k):
        for sign, first, third in ((-1, 0, 8 + k), (1, 4, 11 + k)):
            from_z = z + sign * k
            there = (from_z >= 0) & (from_z < LINE)
            o = jnp.clip(from_z, 0, LINE - 1) * 2 + y
            ref, rs = relay_slot[w](o), r.g_rs.at[w, o]
            arrived(there, ref, rs)
            onward = (z < LINE - 1) if sign < 0 else (z > 0)
            send(there & onward, ref, ref, r.g_ss.at[w, first + k], rs, seq=s - 2 * sign)
            send(there, ref, ref, r.g_ss.at[w, third], rs, seq=mate)

    def relay_finish(w):
        for d in range(LINE):
            o = lax.rem(z + d, LINE) * 2 + 1 - y
            arrived(None, relay_slot[w](o), r.g_rs.at[w, o])

    low, high = z > 0, z < LINE - 1
    from_mate = 4 - 2 * y

    def token_rows(slot, head):
        return r.nall.at[slot, cols(head, quarter), :]

    def token_send(cond, slot, back, k, to):
        send(cond, token_rows(slot, h), token_rows(back, h), r.t_ns.at[k], r.t_rs.at[back, h], seq=to)

    def token_share(cond, slot):
        ref = token_rows(slot, h)
        arrived(cond, ref, r.t_rs.at[slot, h])
        send(cond, ref, ref, r.t_ss.at[slot, 0], r.t_rs.at[slot, h], head=across)
        send(cond, ref, ref, r.t_ss.at[slot, 1], r.t_rs.at[slot, h], head=twin)

    def token_pass(cond, slot):
        ref = token_rows(slot, across)
        arrived(cond, ref, r.t_rs.at[slot, across])
        send(cond, ref, ref, r.t_ss.at[slot, 2], r.t_rs.at[slot, across], head=twin)

    def token_ready(cond, slot):
        arrived(cond, token_rows(slot, twin), r.t_rs.at[slot, twin])
        other = (1 - x) * 2 + 1 - c
        arrived(cond, token_rows(slot, other), r.t_rs.at[slot, other])

    far_in = jnp.where(y == 0, z >= 2, z <= 1)
    far_slot = 6 * y
    slots = (
        (None, from_mate), (low, 1), (high, 5), (low, 2 - 2 * y), (high, 6 - 2 * y),
        (far_in, far_slot),
    )
    for d in range(1, SEQ):
        send(
            None, r.vec, r.gains.at[:, cols(s, rows)], r.v_ss.at[d - 1], r.v_rs.at[s],
            seq=lax.rem(s + d, SEQ),
        )
    relay_start(0)
    r.gains[:, cols(s, rows)] = r.vec[...]
    for k in range(NEAR):
        other = s + k - (SPAN - 1)

        @pl.when((other < 0) | (other >= SEQ))
        def _():
            r.nall[k] = jnp.zeros(r.nall.shape[1:], BF16)

    for k, cond in enumerate((low & high, high, low, high, low)):

        @pl.when(jnp.logical_not(cond))
        def _():
            r.dkv_recv[k] = jnp.zeros(r.dkv_recv.shape[1:], BF16)

    for d in range(1, SEQ):
        o = lax.rem(s + d, SEQ)
        arrived(None, r.gains.at[:, cols(o, rows)], r.v_rs.at[o], r.vec)

    def normalise(q):
        xhat, _ = norm_parts(r.tok[q, :].astype(F32))
        r.nall[SPAN - 1, q, :] = (xhat * r.gains[0:1, :] + r.gains[1:2, :]).astype(BF16)

    normalise(cols(h, quarter))
    token_send(None, SPAN - 1, 2 + 2 * y, 0, mate)
    token_send(high, SPAN - 1, 1, 1, s + 2)
    token_send(low, SPAN - 1, 5, 2, s - 2)
    for d in range(1, HEAD):
        normalise(cols(lax.rem(h + d, HEAD), quarter))
    token_share(*slots[0])
    token_send(high, from_mate, 2 - 2 * y, 3, s + 2)
    token_send(low, from_mate, 6 - 2 * y, 4, s - 2)
    relay_round(0, 1)
    token_share(*slots[1])
    token_share(*slots[2])
    r.wq_all[:, cols(s, rows), :] = r.wq[...]
    r.wo_all[:, cols(s, rows)] = r.wo[...]
    token_share(*slots[3])
    token_share(*slots[4])
    token_send((y == 0) & low & high, 2, 0, 5, s + 2)
    token_send((y == 1) & low & high, 4, 6, 5, s - 2)
    relay_round(0, 2)
    relay_start(1)
    relay_round(0, 3)
    token_share(*slots[5])
    for cond, slot in slots[:3]:
        token_pass(cond, slot)
    relay_round(1, 1)
    relay_start(2)

    start, leader, span, pad = 0, 0, 0, 0
    for k in range(r.units.shape[0]):
        here = r.units[k]
        inside = (s >= start) & (s < start + here)
        leader = jnp.where(inside, start, leader)
        span = jnp.where(inside, here, span)
        pad = jnp.where(inside, r.pads[k], pad)
        start = start + here
    position = s - leader
    root = jnp.clip(SPAN - 1 - position, 0, SPAN - 1)
    total = span * BLK_DEV
    live = span * tokens - pad

    columns = lax.broadcasted_iota(jnp.int32, (1, SPAN * tokens), 1)
    usable = columns < live
    blocks = lax.div(columns, BLK)
    for hh in range(HEAD):
        for b in range(BLK_DEV):
            query = position * BLK_DEV + b
            count = jnp.zeros((1, SPAN * tokens), F32)
            for wanted in (query - 1, query, query + 1, 0, total - 1):
                count = count + jnp.where(blocks == wanted, 1.0, 0.0)
            for k in range(r.picks.shape[0]):
                raw = r.picks[k, b, hh]
                chosen = lax.rem(raw, BLK_DEV)
                for k_units in range(2, SPAN + 1):
                    chosen = jnp.where(span == k_units, lax.rem(raw, BLK_DEV * k_units), chosen)
                count = count + jnp.where(blocks == chosen, 1.0, 0.0)
            count = jnp.where((query == 0) | (query == total - 1), 1.0, count)
            held = usable & (count > 0)
            bias = jnp.log(jnp.maximum(count, 1.0))
            r.bias[hh, b : b + 1, :] = jnp.where(held, bias, NEGATIVE)

    ffn_src = {
        UP: lambda k: r.wu.at[:, cols(k, half)],
        DOWN: lambda k: r.wd.at[cols(k, half), :],
    }
    ffn_slot = {
        UP: lambda o: r.wu_all.at[cols(o, rows), :],
        DOWN: lambda o: r.wd_all.at[:, cols(o, rows)],
    }

    def ffn_start(w):
        i = w - UP
        for d in range(1, LINE):
            to = lax.rem(z + d, LINE)
            send(
                None, ffn_src[w](lax.rem(to, 2)), ffn_slot[w](s), r.f_ss.at[i, d - 1],
                r.f_rs.at[i, s], seq=to * 2 + y,
            )
        send(
            None, ffn_src[w](e), ffn_slot[w](s), r.f_ss.at[i, 3], r.f_rs.at[i, s], seq=mate
        )

    def by_distance(k):
        up = k + jnp.where(z <= k, 1, 0)
        down = k + jnp.where(LINE - 1 - z <= k, 1, 0)
        return jnp.where(z < LINE // 2, up, LINE - 1 - down)

    def ffn_forward(w, ks=(0, 1, 2)):
        i = w - UP
        for k in ks:
            o = by_distance(k) * 2 + y
            ref = ffn_slot[w](o)
            arrived(None, ref, r.f_rs.at[i, o])
            send(None, ref, ref, r.f_ss.at[i, 4 + k], r.f_rs.at[i, o], seq=mate)

    def ffn_finish(w):
        for d in range(LINE):
            o = lax.rem(z + d, LINE) * 2 + 1 - y
            arrived(None, ffn_slot[w](o), r.f_rs.at[w - UP, o])

    relay_round(1, 2)
    relay_round(2, 1)
    relay_round(1, 3)
    relay_round(2, 2)
    ffn_start(UP)
    relay_round(2, 3)
    for cond, slot in slots[3:]:
        token_pass(cond, slot)
    for ref, src in ((ffn_slot[UP](s), ffn_src[UP](e)), (ffn_slot[DOWN](s), ffn_src[DOWN](e))):
        ref[...] = src[...]

    ffn_start(DOWN)
    for cond, slot in slots:
        token_ready(cond, slot)
    relay_finish(0)
    scaling = HEAD_DIM ** (-0.5)
    for j in range(SPAN):
        q = pl.ds(j * tokens, tokens)
        rows_in = r.nall[root + j]
        r.kwin[q, :] = dot(rows_in, r.wq_all[1], ((1,), (0,))).astype(BF16)
        r.vwin[q, :] = dot(rows_in, r.wq_all[2], ((1,), (0,))).astype(BF16)
    relay_finish(1)
    part = dot(r.nall[SPAN - 1], r.wq_all[0], ((1,), (0,)))
    r.qs[...] = (part.astype(BF16).astype(F32) * scaling).astype(BF16)
    r.cotx[cols(e, tokens), :] = r.cot[...]
    beyond = (1 - x) * 2 + 1 - c

    def block_rows(unit, head):
        return pl.ds(al(unit * tokens + head * quarter, quarter), quarter)

    def cot_rows(unit, head):
        return r.cotx.at[block_rows(unit, head), :]

    send(
        None, r.cot.at[cols(h, quarter), :], cot_rows(e, h), r.c_ss.at[0], r.c_rs.at[h], seq=pair
    )

    def cot_share():
        ref = cot_rows(1 - e, h)
        arrived(None, ref, r.c_rs.at[h])
        send(None, ref, ref, r.c_ss.at[1], r.c_rs.at[h], head=across)
        send(None, ref, ref, r.c_ss.at[2], r.c_rs.at[h], head=twin)

    def cot_pass():
        ref = cot_rows(1 - e, across)
        arrived(None, ref, r.c_rs.at[across])
        send(None, ref, ref, r.c_ss.at[3], r.c_rs.at[across], head=twin)

    lanes = lax.div(lax.broadcasted_iota(jnp.int32, (1, head_w), 1), HEAD_DIM)
    none = jnp.zeros((), BF16)
    r.att[...] = jnp.zeros(r.att.shape, F32)

    def attend(hh, carry):
        mine = lanes == hh
        query = jnp.where(mine, r.qs[...], none)
        for j in range(SPAN):
            k = pl.ds(j * tokens, tokens)
            r.lg[:, k] = dot(query, r.kwin[k, :], ((1,), (1,)))
        for b in range(BLK_DEV):
            q = pl.ds(b * BLK, BLK)
            logits = r.lg[q, :] + r.bias[hh, b : b + 1, :]
            grown = jnp.exp(logits - jnp.max(logits, axis=-1, keepdims=True))
            scale = 1.0 / jnp.sum(grown, axis=-1, keepdims=True)
            r.prob[hh, q, :] = (grown * scale).astype(BF16)
        part = dot(r.prob[hh], r.vwin[...], ((1,), (0,)))
        r.att[...] += jnp.where(mine, part, 0.0)
        return carry

    lax.fori_loop(0, HEAD // 2, attend, 0)
    ffn_forward(UP, (0,))
    lax.fori_loop(HEAD // 2, HEAD, attend, 0)
    ffn_forward(UP, (1,))
    r.att_low[...] = r.att[...].astype(BF16)
    relay_finish(2)

    def rows_of(k):
        return cols(k, quarter)

    def reduce_start(op):
        for v in range(2):
            r.q1_send[op, v] = r.sum_f[rows_of(v * 2 + 1 - c), :].astype(BF16)
        send(None, r.q1_send.at[op], r.q1_recv.at[op], r.q1_ss.at[op], r.q1_rs.at[op], head=twin)

    def reduce_middle(op):
        arrived(None, r.q1_recv.at[op], r.q1_rs.at[op])
        block = r.sum_f[rows_of(across), :] + r.q1_recv[op, 1 - x].astype(F32)
        r.q2_send[op] = block.astype(BF16)
        send(None, r.q2_send.at[op], r.q2_recv.at[op], r.q2_ss.at[op], r.q2_rs.at[op], head=across)
        r.q_own[op] = r.sum_f[rows_of(h), :] + r.q1_recv[op, x].astype(F32)

    def reduce_finish(op):
        arrived(None, r.q2_recv.at[op], r.q2_rs.at[op])
        return r.q_own[op] + r.q2_recv[op].astype(F32)

    def spread_start(op, whole, value):
        whole[rows_of(h), :] = value
        ref = whole.at[rows_of(h), :]
        send(None, ref, ref, r.ag_ss.at[op, 0], r.ag_rs.at[op, h], head=across)
        send(None, ref, ref, r.ag_ss.at[op, 1], r.ag_rs.at[op, h], head=twin)

    def spread_pass(op, whole):
        ref = whole.at[rows_of(across), :]
        arrived(None, ref, r.ag_rs.at[op, across])
        send(None, ref, ref, r.ag_ss.at[op, 2], r.ag_rs.at[op, across], head=twin)

    def spread_finish(op, whole):
        for o in (twin, beyond):
            arrived(None, whole.at[rows_of(o), :], r.ag_rs.at[op, o])

    pair_sum = [r.sum_f, r.sum_g]

    def pair_start(op):
        for u in range(2):
            for v in range(2):
                block = pair_sum[op][block_rows(u, v * 2 + 1 - c), :]
                r.p1_send[op, u * 2 + v] = block.astype(BF16)
        send(None, r.p1_send.at[op], r.p1_recv.at[op], r.p1_ss.at[op], r.p1_rs.at[op], head=twin)

    def pair_middle(op):
        arrived(None, r.p1_recv.at[op], r.p1_rs.at[op])
        for du, dv in ((1, 1), (1, 0), (0, 1), (0, 0)):
            u, v = lax.rem(e + du, 2), lax.rem(x + dv, 2)
            block = pair_sum[op][block_rows(u, v * 2 + c), :] + r.p1_recv[op, u * 2 + v].astype(F32)
            if du or dv:
                k = u * 2 + v
                r.p2_send[op, k] = block.astype(BF16)
                send(
                    None, r.p2_send.at[op, k], r.p2_recv.at[op, e * 2 + x], r.p2_ss.at[op, k],
                    r.p2_rs.at[op, e * 2 + x], seq=pair if du else s, head=across if dv else h,
                )
            else:
                r.p_own[op] = block

    def pair_x(op):
        arrived(None, r.p1_recv.at[op], r.p1_rs.at[op])
        for du in (1, 0):
            u = lax.rem(e + du, 2)
            k = u * 2 + 1 - x
            block = pair_sum[op][block_rows(u, across), :] + r.p1_recv[op, k].astype(F32)
            r.p2_send[op, k] = block.astype(BF16)
            send(
                None, r.p2_send.at[op, k], r.p2_recv.at[op, u], r.p2_ss.at[op, k],
                r.p2_rs.at[op, u], head=across,
            )

    def pair_over(op):
        for du in (1, 0):
            u = lax.rem(e + du, 2)
            arrived(None, r.p2_recv.at[op, u], r.p2_rs.at[op, u])
            block = pair_sum[op][block_rows(u, h), :] + r.p1_recv[op, u * 2 + x].astype(F32)
            block = block + r.p2_recv[op, u].astype(F32)
            if du:
                k = u * 2 + x
                r.p2_send[op, k] = block.astype(BF16)
                send(
                    None, r.p2_send.at[op, k], r.p2_recv.at[op, 2], r.p2_ss.at[op, k],
                    r.p2_rs.at[op, 2], seq=pair,
                )
            else:
                r.p_own[op] = block

    def pair_end(op):
        arrived(None, r.p2_recv.at[op, 2], r.p2_rs.at[op, 2])
        return r.p_own[op] + r.p2_recv[op, 2].astype(F32)

    def pair_finish(op):
        result = r.p_own[op]
        for du, dv in ((0, 1), (1, 0), (1, 1)):
            k = lax.rem(e + du, 2) * 2 + lax.rem(x + dv, 2)
            arrived(None, r.p2_recv.at[op, k], r.p2_rs.at[op, k])
            result = result + r.p2_recv[op, k].astype(F32)
        return result

    r.sum_f[:tokens, :] = dot(r.att_low[...], r.wo_all[...], ((1,), (0,)))
    reduce_start(0)
    reduce_middle(0)
    ffn_forward(UP, (2,))
    ffn_forward(DOWN, (0,))
    middle = r.tok[rows_of(h), :].astype(F32) + reduce_finish(0)
    r.mid_own[...] = middle
    xhat, _ = norm_parts(middle)

    def n2_rows(unit, head):
        return r.n2x.at[block_rows(unit, head), :]

    r.n2x[block_rows(e, h), :] = (xhat * r.gains[2:3, :] + r.gains[3:4, :]).astype(BF16)
    mine, tag = n2_rows(e, h), e * 4 + h
    send(None, mine, mine, r.n2_ss.at[0], r.n2_rs.at[tag], seq=pair)
    send(None, mine, mine, r.n2_ss.at[1], r.n2_rs.at[tag], head=across)
    send(None, mine, mine, r.n2_ss.at[2], r.n2_rs.at[tag], head=twin)
    cot_share()
    ffn_forward(DOWN, (1,))
    for k, (unit, head) in enumerate(((e, across), (1 - e, h), (1 - e, across))):
        ref, tag = n2_rows(unit, head), unit * 4 + head
        arrived(None, ref, r.n2_rs.at[tag])
        if k == 1:
            send(None, ref, ref, r.n2_ss.at[6], r.n2_rs.at[tag], head=across)
        send(None, ref, ref, r.n2_ss.at[3 + k], r.n2_rs.at[tag], head=twin)
    cot_pass()
    ffn_forward(DOWN, (2,))
    ffn_finish(UP)
    for unit in (e, 1 - e):
        for head in (x * 2 + 1 - c, (1 - x) * 2 + 1 - c):
            arrived(None, n2_rows(unit, head), r.n2_rs.at[unit * 4 + head])

    root_c = (2.0 / 3.141592653589793) ** 0.5
    r.up_send[half // 128 :, :] = jnp.zeros((8 - half // 128, 128), F32)
    for j in range(half // 256):
        f = pl.ds(j * 256, 256)
        bias = r.upb_f[:, pl.ds(al(e * half + j * 256, 256), 256)]
        v = dot(r.n2x[...], r.wu_all[:, f], ((1,), (0,))) + bias
        t = jnp.tanh(root_c * (v + 0.044715 * (v * v * v)))
        r.hid[:, f] = (0.5 * v * (1.0 + t)).astype(BF16)
        slope = 0.5 * (1.0 + t) + 0.5 * v * (1.0 - t * t) * (root_c * (1.0 + 0.134145 * v * v))
        r.slope[:, f] = slope
    ffn_finish(DOWN)
    for head in (twin, beyond):
        arrived(None, cot_rows(1 - e, head), r.c_rs.at[head])
    for j in range(half // 256):
        f = pl.ds(j * 256, 256)
        low_p = (dot(r.cotx[...], r.wd_all[f, :], ((1,), (1,))) * r.slope[:, f]).astype(BF16)
        r.gp[:, f] = low_p
        sums = jnp.sum(low_p.astype(F32), axis=0, keepdims=True)
        r.up_send[2 * j : 2 * j + 1, :] = sums[:, :128]
        r.up_send[2 * j + 1 : 2 * j + 2, :] = sums[:, 128:]

    grad_send = {QKV_KV: r.skv, QKV_Q: r.sq, OUT: r.so, UP: r.su, DOWN: r.sd}
    grad_arrive = {QKV_KV: r.akv, QKV_Q: r.aq, OUT: r.ao, UP: r.au, DOWN: r.ad}
    grad_again = {QKV_KV: r.bkv, QKV_Q: r.bq, OUT: r.bo, UP: r.bu, DOWN: r.bd}
    grad_final = {QKV_KV: r.rkv, QKV_Q: r.rq, OUT: r.ro, UP: r.ru, DOWN: r.rd}

    def tile_of(i):
        return lax.rem(z + 1 + i, LINE)

    def grad_cross(w, zz):
        send(
            None, grad_send[w].at[zz * 2 + 1 - y], grad_arrive[w].at[zz], r.ra_ss.at[w, zz],
            r.ra_rs.at[w, zz], seq=mate,
        )

    def grad_along(w, ks=(1, 2, 3)):
        for d in ks:
            zz = lax.rem(z + d, LINE)
            arrived(None, grad_arrive[w].at[zz], r.ra_rs.at[w, zz])
            both = grad_send[w][zz * 2 + y].astype(F32) + grad_arrive[w][zz].astype(F32)
            grad_again[w][zz] = both.astype(BF16)
            send(
                None, grad_again[w].at[zz], grad_final[w].at[z], r.rb_ss.at[w, zz],
                r.rb_rs.at[w, z], seq=zz * 2 + y,
            )

    outer, inner = (z == 0) | (z == LINE - 1), (z == 1) | (z == LINE - 2)
    far_half = 2 - 2 * lax.div(z, 2)
    far_inner = 2 - lax.div(z, 2)
    grad_hold = {QKV_KV: r.hkv, QKV_Q: r.hq, OUT: r.ho}

    def tile_far(i):
        return (far_half, far_half + 1, pair_z, z)[i]

    def grad_first(w):
        for k in range(3):
            zz = tile_far(k)
            arrived(None, grad_arrive[w].at[zz], r.ra_rs.at[w, zz])
            both = grad_send[w][zz * 2 + y].astype(F32) + grad_arrive[w][zz].astype(F32)
            grad_again[w][zz] = both.astype(BF16)
            if k < 2:
                send(
                    outer, grad_again[w].at[zz], grad_hold[w].at[k], r.rh_ss.at[w, k],
                    r.rh_rs.at[w, k], seq=pair,
                )
            else:
                send(
                    None, grad_again[w].at[zz], grad_final[w].at[z], r.rb_ss.at[w, zz],
                    r.rb_rs.at[w, z], seq=pair,
                )

    def grad_second(w):
        for k in range(2):
            zz = tile_far(k)
            arrived(inner, grad_hold[w].at[k], r.rh_rs.at[w, k])

            @pl.when(inner)
            def _():
                both = grad_again[w][zz].astype(F32) + grad_hold[w][k].astype(F32)
                grad_again[w][zz] = both.astype(BF16)

            send(
                inner, grad_again[w].at[zz], grad_final[w].at[z], r.rb_ss.at[w, zz],
                r.rb_rs.at[w, z], seq=zz * 2 + y,
            )

    def grad_own(w):
        arrived(None, grad_arrive[w].at[z], r.ra_rs.at[w, z])
        return grad_send[w][z * 2 + y].astype(F32) + grad_arrive[w][z].astype(F32)

    def grad_from(w, o):
        arrived(None, grad_final[w].at[o], r.rb_rs.at[w, o])
        return grad_final[w][o].astype(F32)

    def grad_sum(w):
        return grad_own(w) + grad_from(w, pair_z) + grad_from(w, far_inner)

    def grad_halves(w):
        same = grad_own(w) + grad_from(w, lax.rem(z + 2, LINE))
        other = grad_from(w, lax.rem(z + 1, LINE)) + grad_from(w, lax.rem(z + 3, LINE))
        return same, other

    def down_step(i):
        zz = tile_of(i)
        part = dot(r.hid[...], r.cotx[:, cols(zz, 256)], ((0,), (0,))).astype(BF16)
        r.sd[zz * 2] = part[:, :rows]
        r.sd[zz * 2 + 1] = part[:, rows:]
        grad_cross(DOWN, zz)

    def up_step(i):
        zz = tile_of(i)
        part = dot(r.n2x[:, cols(zz, 256)], r.gp[...], ((0,), (0,))).astype(BF16)
        r.su[zz * 2] = part[:rows]
        r.su[zz * 2 + 1] = part[rows:]
        grad_cross(UP, zz)

    down_step(0)
    r.sum_f[...] = dot(r.gp[...], r.wu_all[...], ((1,), (1,)))
    pair_start(0)
    down_step(1)
    pair_middle(0)
    r.sum_g[...] = dot(r.hid[...], r.wd_all[...], ((1,), (0,)))
    pair_start(1)
    down_step(2)
    down_step(3)
    pair_x(1)
    for i in range(LINE):
        up_step(i)
    for d in range(1, SEQ):
        send(
            None, r.up_send, r.up_recv.at[s], r.up_ss.at[d], r.up_rs.at[s],
            seq=lax.rem(s + d, SEQ),
        )

    grad_two = pair_finish(0)
    xhat, inverse = norm_parts(r.mid_own[...])
    dy = r.cot[rows_of(h), :].astype(F32)
    grad_mid = dy + norm_backward(xhat, inverse, grad_two * r.gains[2:3, :])
    r.gm_own[...] = grad_mid
    spread_start(0, r.gb, grad_mid.astype(BF16))
    r.sm_send[2:3, :] = jnp.sum(grad_two * xhat, axis=0, keepdims=True)
    r.sm_send[3:4, :] = jnp.sum(grad_two, axis=0, keepdims=True)
    r.sm_send[4:5, :] = jnp.sum(dy, axis=0, keepdims=True)
    r.sm_send[5:8, :] = jnp.zeros((3, width), F32)

    grad_along(DOWN)
    pair_over(1)
    spread_pass(0, r.gb)
    spread_finish(0, r.gb)
    r.gatt[...] = dot(r.gb[...], r.wo_all[...], ((1,), (1,))).astype(BF16)
    for i in range(LINE):
        zz = tile_far(i)
        part = dot(r.att_low[...], r.gb[:, cols(zz, 256)], ((0,), (0,))).astype(BF16)
        r.so[zz * 2] = part[:, :rows]
        r.so[zz * 2 + 1] = part[:, rows:]
        grad_cross(OUT, zz)
    grad_along(UP, (1, 2))

    r.dq[...] = jnp.zeros(r.dq.shape, F32)
    r.dk[...] = jnp.zeros(r.dk.shape, F32)
    r.dv[...] = jnp.zeros(r.dv.shape, F32)

    def attend_back(hh, carry):
        mine = lanes == hh
        query = jnp.where(mine, r.qs[...], none)
        grad = jnp.where(mine, r.gatt[...], none)
        for j in range(SPAN):
            k = pl.ds(j * tokens, tokens)
            r.lg[:, k] = dot(grad, r.vwin[k, :], ((1,), (1,)))
        for b in range(BLK_DEV):
            q = pl.ds(b * BLK, BLK)
            chance, grown = r.prob[hh, q, :].astype(F32), r.lg[q, :]
            inner = jnp.sum(chance * grown, axis=-1, keepdims=True)
            r.ds[hh, q, :] = (chance * (grown - inner)).astype(BF16)
        for j in range(SPAN):
            k = pl.ds(j * tokens, tokens)
            r.dk[k, :] += dot(r.ds[hh, :, k], query, ((0,), (0,)))
            r.dv[k, :] += dot(r.prob[hh, :, k], grad, ((0,), (0,)))
        return carry

    lax.fori_loop(0, HEAD, attend_back, 0)
    for k in range(2 * (SPAN - 1) + SPAN):
        j = k - (SPAN - 1)
        if 0 <= j < SPAN:
            q = pl.ds(j * tokens, tokens)
            r.dkv_pad[k, 0] = r.dk[q, :].astype(BF16)
            r.dkv_pad[k, 1] = r.dv[q, :].astype(BF16)
        else:
            r.dkv_pad[k] = jnp.zeros(r.dkv_pad.shape[1:], BF16)
    for k in range(NEAR):
        r.dkv_send[k] = r.dkv_pad[k + SPAN - 1 - root]

    def grad_hop(cond, slot, into, k, to, v):
        send(
            cond, r.dkv_send.at[slot, v], r.dkv_recv.at[into, v], r.dkv_ss.at[k, v],
            r.dkv_rs.at[into, v], seq=to,
        )

    def add_to(v, slot, *froms):
        both = r.dkv_send[slot, v].astype(F32)
        for k in froms:
            both = both + r.dkv_recv[k, v].astype(F32)
        r.dkv_send[slot, v] = both.astype(BF16)

    def grad_wait(cond, into, v):
        arrived(cond, r.dkv_recv.at[into, v], r.dkv_rs.at[into, v])

    FAR, ABOVE, BELOW, LINE_ABOVE, LINE_BELOW, MATE = range(6)
    for v in range(2):
        grad_hop((y == 0) & (z >= 2), 0, FAR, 0, s - 2, v)
        grad_hop((y == 1) & (z <= 1), 6, FAR, 0, s + 2, v)
    for v in range(2):
        grad_hop((y == 0) & high, 6, BELOW, 1, s + 2, v)
        grad_hop((y == 1) & low, 0, ABOVE, 1, s - 2, v)

    def hop_far(v):
        grad_wait(low & high, FAR, v)
        add_to(v, 2 + 2 * y, FAR)
        grad_hop((y == 0) & low, 2, ABOVE, 2, s - 2, v)
        grad_hop((y == 1) & high, 4, BELOW, 2, s + 2, v)

    def hop_line(v):
        grad_hop(low, 1, LINE_ABOVE, 3, s - 2, v)
        grad_hop(high, 5, LINE_BELOW, 4, s + 2, v)

    def hop_mate(v):
        grad_wait(high, ABOVE, v)
        grad_wait(low, BELOW, v)
        add_to(v, from_mate, ABOVE, BELOW)
        grad_hop(None, from_mate, MATE, 5, mate, v)

    def queries_back(hh, carry):
        r.dq[...] += jnp.where(lanes == hh, dot(r.ds[hh], r.kwin[...], ((1,), (0,))), 0.0)
        return carry

    for i in range(LINE):
        zz = tile_far(i)
        for k in range(2):
            part = jnp.zeros((256, head_w), F32)
            for j in range(SPAN):
                part = part + dot(
                    r.nall[root + j, :, cols(zz, 256)], r.dkv_pad[j + SPAN - 1, k], ((0,), (0,))
                )
            part = part.astype(BF16)
            for v in range(2):
                r.skv[zz * 2 + v, k] = part[v * rows : (v + 1) * rows]
        grad_cross(QKV_KV, zz)
        if i == 1:
            hop_far(0)
        if i == 2:
            hop_far(1)
            hop_line(0)
            hop_line(1)
    grad_along(UP, (3,))
    hop_mate(0)
    hop_mate(1)
    grad_first(OUT)
    lax.fori_loop(0, HEAD, queries_back, 0)
    r.gtq[...] = (r.dq[...] * scaling).astype(BF16)
    for i in range(LINE):
        zz = tile_far(i)
        part = dot(r.nall[SPAN - 1, :, cols(zz, 256)], r.gtq[...], ((0,), (0,))).astype(BF16)
        r.sq[zz * 2] = part[:rows]
        r.sq[zz * 2 + 1] = part[rows:]
        grad_cross(QKV_Q, zz)
    grad_second(OUT)
    grad_first(QKV_KV)
    ffn = pair_end(1)
    spread_start(1, r.out_o, (r.mid_own[...] + ffn + r.gains[4:5, :]).astype(BF16))
    for v in range(2):
        grad_wait(high, LINE_ABOVE, v)
        grad_wait(low, LINE_BELOW, v)
        grad_wait(None, MATE, v)
        whole = r.dkv_send[SPAN - 1, v].astype(F32)
        for k in (LINE_ABOVE, LINE_BELOW, MATE):
            whole = whole + r.dkv_recv[k, v].astype(F32)
        r.gtkv[v] = whole.astype(BF16)

    r.sum_f[:tokens, :] = (
        dot(r.gtq[...], r.wq_all[0], ((1,), (1,)))
        + dot(r.gtkv[0], r.wq_all[1], ((1,), (1,)))
        + dot(r.gtkv[1], r.wq_all[2], ((1,), (1,)))
    )
    reduce_start(1)
    reduce_middle(1)
    grad_second(QKV_KV)
    grad_one = reduce_finish(1)
    xhat, inverse = norm_parts(r.tok[rows_of(h), :].astype(F32))
    r.sm_send[0:1, :] = jnp.sum(grad_one * xhat, axis=0, keepdims=True)
    r.sm_send[1:2, :] = jnp.sum(grad_one, axis=0, keepdims=True)
    for d in range(1, SEQ):
        to = lax.rem(s + d, SEQ)
        send(
            None, r.sm_send.at[:, cols(to, rows)], r.sm_recv.at[s], r.sm_ss.at[d], r.sm_rs.at[s],
            seq=to,
        )
    spread_pass(1, r.out_o)
    grad_first(QKV_Q)
    grad_x = r.gm_own[...] + norm_backward(xhat, inverse, grad_one * r.gains[0:1, :])
    spread_start(2, r.xg_o, grad_x.astype(BF16))

    same, other = grad_halves(DOWN)
    r.gd_o[cols(e, half), :] = same
    r.gd_o[cols(1 - e, half), :] = other
    same, other = grad_halves(UP)
    r.gu_o[:, cols(e, half)] = same
    r.gu_o[:, cols(1 - e, half)] = other
    spread_pass(2, r.xg_o)
    grad_second(QKV_Q)
    r.go_o[...] = grad_sum(OUT)

    r.sm_recv[s] = r.sm_send[:, cols(s, rows)]
    r.up_recv[s] = r.up_send[...]
    for d in range(1, SEQ):
        o = lax.rem(s + d, SEQ)
        arrived(None, r.sm_recv.at[o], r.sm_rs.at[o], r.vec)
        arrived(None, r.up_recv.at[o], r.up_rs.at[o])
    part = r.sm_recv[0]
    for o in range(1, SEQ):
        part = part + r.sm_recv[o]
    r.sm_own[...] = part
    for d in range(1, HEAD):
        send(
            None, r.sm_own, r.sm_two.at[h], r.sm2_ss.at[d], r.sm2_rs.at[h],
            head=lax.rem(h + d, HEAD),
        )
    r.sm_two[h] = part
    tall = half // 128
    for u in range(2):
        ups = jnp.zeros((tall, 128), F32)
        for o in range(SEQ):
            if (o // 2) % 2 == u:
                ups = ups + r.up_recv[o, :tall, :]
        r.small_o[8 + u * tall : 8 + (u + 1) * tall, :] = ups
    spread_finish(1, r.out_o)
    spread_finish(2, r.xg_o)
    for d in range(1, HEAD):
        o = lax.rem(h + d, HEAD)
        arrived(None, r.sm_two.at[o], r.sm2_rs.at[o])
    r.small_o[0:8, :] = (r.sm_two[0] + r.sm_two[1]) + (r.sm_two[2] + r.sm_two[3])
    r.gq_o[0] = grad_sum(QKV_Q)
    r.gq_o[1:3] = grad_sum(QKV_KV)

    for cond, one in sent:
        when(cond, one.wait_send)


def local_fused(
    tokens, w_qkv, w_out, ln1_gain, ln1_bias, ln2_gain, ln2_bias, w_up, up_bias, w_down, down_bias,
    seq_units, seq_pad, rand_picks, cotangent,
):
    tok, width = tokens.shape
    rows, _, head_w = w_qkv.shape
    hidden = w_up.shape[1]
    half = hidden // 2
    quarter = tok // HEAD
    keys = SPAN * tok
    smem, vmem = pl.BlockSpec(memory_space=pltpu.SMEM), pl.BlockSpec(memory_space=pltpu.VMEM)
    ins = dict(
        units=seq_units, pads=seq_pad, picks=jnp.transpose(rand_picks, (2, 0, 1)), tok=tokens,
        cot=cotangent, wq=jnp.transpose(w_qkv, (1, 0, 2)), wo=w_out, wu=w_up, wd=w_down,
        g1=ln1_gain, b1=ln1_bias, g2=ln2_gain, b2=ln2_bias, b3=down_bias,
        upb=up_bias,
    )
    outs = dict(
        out_o=((tok, width), BF16), xg_o=((tok, width), BF16), gq_o=((3, rows, head_w), F32),
        go_o=((head_w, rows), F32), gu_o=((rows, hidden), F32), gd_o=((hidden, rows), F32),
        small_o=((16, rows), F32),
    )
    scratch = dict(
        wq_all=((3, width, head_w), BF16), wo_all=((head_w, width), BF16),
        wu_all=((width, half), BF16), wd_all=((half, width), BF16), vec=((8, rows), F32), upb_f=((1, hidden), F32),
        gains=((8, width), F32), nall=((NEAR, tok, width), BF16),
        qs=((tok, head_w), BF16),
        kwin=((keys, head_w), BF16), vwin=((keys, head_w), BF16), lg=((tok, keys), F32),
        prob=((HEAD, tok, keys), BF16), ds=((HEAD, tok, keys), BF16),
        att=((tok, head_w), F32), att_low=((tok, head_w), BF16), n2x=((2 * tok, width), BF16),
        cotx=((2 * tok, width), BF16), hid=((2 * tok, half), BF16), slope=((2 * tok, half), F32), gp=((2 * tok, half), BF16),
        gb=((tok, width), BF16), mid_own=((quarter, width), F32),
        gm_own=((quarter, width), F32), gatt=((tok, head_w), BF16), dq=((tok, head_w), F32),
        dk=((keys, head_w), F32), dv=((keys, head_w), F32),
        dkv_pad=((NEAR + SPAN - 1, 2, tok, head_w), BF16),
        dkv_send=((NEAR, 2, tok, head_w), BF16), dkv_recv=((6, 2, tok, head_w), BF16),
        gtq=((tok, head_w), BF16), gtkv=((2, tok, head_w), BF16),
        q1_send=((2, 2, quarter, width), BF16), q1_recv=((2, 2, quarter, width), BF16),
        q2_send=((2, quarter, width), BF16), q2_recv=((2, quarter, width), BF16),
        q_own=((2, quarter, width), F32),
        sum_f=((2 * tok, width), F32), sum_g=((2 * tok, width), F32), bias=((HEAD, 8, keys), F32),
        p1_send=((2, 4, quarter, width), BF16), p1_recv=((2, 4, quarter, width), BF16),
        p2_send=((2, 4, quarter, width), BF16), p2_recv=((2, 4, quarter, width), BF16),
        p_own=((2, quarter, width), F32), sm_send=((8, width), F32),
        sm_recv=((SEQ, 8, rows), F32), sm_own=((8, rows), F32), sm_two=((HEAD, 8, rows), F32),
        up_send=((8, 128), F32), up_recv=((SEQ, 8, 128), F32),
    )
    shards = dict(
        kv=(2, rows, head_w), q=(rows, head_w), o=(head_w, rows), u=(rows, half), d=(half, rows)
    )
    for lead, count in (("s", SEQ), ("a", LINE), ("b", LINE), ("r", LINE), ("h", 2)):
        for name, shape in shards.items():
            scratch[lead + name] = ((count,) + shape, BF16)
    semaphores = dict(
        g_ss=(3, 16), g_rs=(3, SEQ), f_ss=(2, 7), f_rs=(2, SEQ), v_ss=(7,), v_rs=(SEQ,),
        t_ns=(6,), t_ss=(NEAR, 3), t_rs=(NEAR, HEAD), dkv_ss=(6, 2), dkv_rs=(6, 2), c_ss=(4,), c_rs=(HEAD,),
        q1_ss=(2,), q1_rs=(2,), q2_ss=(2,), q2_rs=(2,), ag_ss=(3, 3), ag_rs=(3, HEAD), n2_ss=(7,),
        n2_rs=(8,), p1_ss=(2,), p1_rs=(2,), p2_ss=(2, 4), p2_rs=(2, 4), ra_ss=(5, LINE),
        ra_rs=(5, LINE), rh_ss=(5, 2), rh_rs=(5, 2), rb_ss=(5, LINE), rb_rs=(5, LINE), sm_ss=(SEQ,), sm_rs=(SEQ,),
        sm2_ss=(HEAD,), sm2_rs=(HEAD,), up_ss=(SEQ,), up_rs=(SEQ,),
    )
    names = [*ins, *outs, *scratch, *semaphores]
    results = pl.pallas_call(
        functools.partial(fused_kernel, names),
        out_shape=[jax.ShapeDtypeStruct(*o) for o in outs.values()],
        in_specs=[smem] * 3 + [vmem] * (len(ins) - 3),
        out_specs=[vmem] * len(outs),
        scratch_shapes=[pltpu.VMEM(*v) for v in scratch.values()]
        + [pltpu.SemaphoreType.DMA(v) for v in semaphores.values()],
        compiler_params=pltpu.CompilerParams(
            collective_id=0, has_side_effects=True, vmem_limit_bytes=VMEM_BYTES
        ),
        name="fused_layer",
    )(*ins.values())
    large = [(v[0], F32 if k == "xg_o" else v[1]) for k, v in outs.items()][:-1]
    handed = pl.pallas_call(
        hand_over_kernel,
        out_shape=[jax.ShapeDtypeStruct(*o) for o in large]
        + [jax.ShapeDtypeStruct((rows,), F32)] * 5
        + [jax.ShapeDtypeStruct((hidden,), F32)],
        in_specs=[vmem] * len(outs),
        out_specs=[vmem] * (len(large) + 6),
        name="hand_over",
    )(*results)
    out, xg, gq, go, gu, gd, g1, b1, g2, b2, b3, upg = handed
    return out, xg, jnp.transpose(gq, (1, 0, 2)), go, g1, b1, g2, b2, gu, upg, gd, b3


def hand_over_kernel(*refs):
    large = (len(refs) - 7) // 2
    small, vectors = refs[large], refs[2 * large + 1 :]
    for k in range(large):
        target = refs[large + 1 + k]
        target[...] = refs[k][...].astype(target.dtype)
    for k in range(5):
        vectors[k][...] = small[k, :]
    for k in range(8):
        vectors[5][pl.ds(k * 128, 128)] = small[8 + k, :]


IN_SPECS = (
    P("seq", None), P("seq", None, "head"), P("head", "seq"), P("seq"), P("seq"), P("seq"),
    P("seq"), P("seq", "head"), P("head"), P("head", "seq"), P("seq"), P(), P(),
    P("seq", "head", None), P("seq", None),
)
OUT_SPECS = (
    P("seq", None), P("seq", None), P("seq", None, "head"), P("head", "seq"), P("seq"), P("seq"),
    P("seq"), P("seq"), P("seq", "head"), P("head"), P("head", "seq"), P("seq"),
)


def solution(mesh):
    fits = mesh.shape["seq"] == SEQ and mesh.shape["head"] == HEAD
    return jax.shard_map(
        local_fused if fits else local_general, mesh=mesh, in_specs=IN_SPECS,
        out_specs=OUT_SPECS, check_vma=False,
    )
```

```python
import functools
import types

import jax
import jax.numpy as jnp
from jax import lax
from jax.experimental import pallas as pl
from jax.experimental.pallas import tpu as pltpu
from jax.sharding import PartitionSpec as P

HEAD_DIM = 64
BLK = 64
SPAN = 4
BLK_DEV = 4
EPSILON = 1e-05
NEGATIVE = -1e30
F32 = jnp.float32
BF16 = jnp.bfloat16


def shifted(value, axis, steps):
    count = lax.axis_size(axis)
    first, last = max(0, -steps), min(count, count - steps)
    return lax.ppermute(value, axis, [(i, i + steps) for i in range(first, last)])


def norm_parts(features):
    average = jnp.mean(features, axis=-1, keepdims=True)
    centred = features - average
    spread = jnp.mean(centred * centred, axis=-1, keepdims=True)
    inverse = lax.rsqrt(spread + EPSILON)
    return centred * inverse, inverse


def norm_backward(xhat, inverse, scaled):
    first = jnp.mean(scaled, axis=-1, keepdims=True)
    second = jnp.mean(scaled * xhat, axis=-1, keepdims=True)
    return inverse * (scaled - first - xhat * second)


def dot(a, b, dims):
    return lax.dot_general(a, b, (dims, ((), ())), preferred_element_type=F32)


def sequence_place(seq_units, seq_pad):
    device = lax.axis_index("seq")
    start, leader, span, pad = 0, 0, 0, 0
    for k in range(seq_units.shape[0]):
        units = seq_units[k]
        inside = (device >= start) & (device < start + units)
        leader = jnp.where(inside, start, leader)
        span = jnp.where(inside, units, span)
        pad = jnp.where(inside, seq_pad[k], pad)
        start = start + units
    return device - leader, span, pad


def key_counts(position, span, picks):
    blocks = lax.broadcasted_iota(jnp.int32, (1, 1, SPAN * BLK_DEV), 2)
    query = position * BLK_DEV + lax.broadcasted_iota(jnp.int32, (BLK_DEV, 1, 1), 0)
    total = span * BLK_DEV
    count = jnp.zeros((BLK_DEV, picks.shape[1], SPAN * BLK_DEV), F32)
    for wanted in (query - 1, query, query + 1, 0, total - 1):
        count = count + (blocks == wanted).astype(F32)
    chosen = picks % total
    for r in range(picks.shape[2]):
        count = count + (blocks == chosen[:, :, r : r + 1]).astype(F32)
    return jnp.where((query == 0) | (query == total - 1), 1.0, count)


def local_general(
    tokens, w_qkv, w_out, ln1_gain, ln1_bias, ln2_gain, ln2_bias, w_up, up_bias, w_down, down_bias,
    seq_units, seq_pad, rand_picks, cotangent,
):
    tok, width = tokens.shape
    heads = w_qkv.shape[2] // HEAD_DIM
    rows = lambda v: lax.all_gather(v, "seq", axis=0, tiled=True)
    cols = lambda v: lax.all_gather(v, "seq", axis=1, tiled=True)
    vectors = jnp.stack([ln1_gain, ln1_bias, ln2_gain, ln2_bias, down_bias], axis=0)
    gain_one, shift_one, gain_two, shift_two, down_shift = [
        v[None].astype(F32) for v in cols(vectors)
    ]
    qkv = rows(w_qkv)
    out_w, up_w, down_w = cols(w_out), rows(w_up), cols(w_down)
    position, span, pad = sequence_place(seq_units, seq_pad)
    root = SPAN - 1 - position
    inputs = tokens.astype(F32)
    xhat_one, inv_one = norm_parts(inputs)
    normed = (xhat_one * gain_one + shift_one).astype(BF16)
    triple = jnp.einsum("td,dcf->tcf", normed, qkv, preferred_element_type=F32).astype(BF16)
    own = jnp.stack([triple[:, 1], triple[:, 2]], axis=0)
    pieces = [own if o == 0 else shifted(own, "seq", -o) for o in range(1 - SPAN, SPAN)]
    nearby = jnp.stack(pieces, axis=0)
    window = lax.dynamic_slice_in_dim(nearby, root, SPAN, 0)
    split = lambda v: v.reshape(v.shape[0], heads, HEAD_DIM)
    keys = split(window[:, 0].reshape(SPAN * tok, -1))
    values = split(window[:, 1].reshape(SPAN * tok, -1))
    queries = split(triple[:, 0])
    scaling = HEAD_DIM ** (-0.5)
    live = jnp.arange(SPAN * tok, dtype=jnp.int32) < span * tok - pad
    count = jnp.repeat(key_counts(position, span, rand_picks), BLK, axis=2)
    count = jnp.where(live[None, None], count, 0.0)
    count = jnp.transpose(jnp.repeat(count, BLK, axis=0), (1, 0, 2))
    logits = jnp.einsum("qhd,khd->hqk", queries, keys, preferred_element_type=F32) * scaling
    logits = jnp.where(count > 0, logits, NEGATIVE)
    grown = jnp.exp(logits - jnp.max(logits, axis=-1, keepdims=True)) * count
    chances = grown / jnp.sum(grown, axis=-1, keepdims=True)
    chances_low = chances.astype(BF16)
    attended = jnp.einsum("hqk,khd->qhd", chances_low, values, preferred_element_type=F32)
    attended = attended.astype(BF16).reshape(tok, heads * HEAD_DIM)
    middle = inputs + lax.psum(dot(attended, out_w, ((1,), (0,))), "head")
    xhat_two, inv_two = norm_parts(middle)
    normed_two = (xhat_two * gain_two + shift_two).astype(BF16)
    pre_act = dot(normed_two, up_w, ((1,), (0,))) + up_bias.astype(F32)[None]
    hidden, pull = jax.vjp(lambda v: jax.nn.gelu(v, approximate=True), pre_act)
    hidden = hidden.astype(BF16)
    ffn = lax.psum(dot(hidden, down_w, ((1,), (0,))).astype(BF16), "head").astype(F32)
    output = (middle + ffn + down_shift).astype(BF16)
    grad_out = cotangent.astype(F32)
    grad_w_down = dot(hidden, cotangent, ((0,), (0,)))
    grad_pre = pull(dot(cotangent, down_w, ((1,), (1,))))[0].astype(BF16)
    grad_w_up = dot(normed_two, grad_pre, ((0,), (0,)))
    grad_up_bias = lax.psum(jnp.sum(grad_pre.astype(F32), axis=0), "seq")
    grad_two = lax.psum(dot(grad_pre, up_w, ((1,), (1,))), "head")
    grad_middle = grad_out + norm_backward(xhat_two, inv_two, grad_two * gain_two)
    grad_branch = grad_middle.astype(BF16)
    grad_w_out = dot(attended, grad_branch, ((0,), (0,)))
    grad_att = split(dot(grad_branch, out_w, ((1,), (1,))).astype(BF16))
    grad_prob = jnp.einsum("qhd,khd->hqk", grad_att, values, preferred_element_type=F32)
    inner = jnp.sum(chances * grad_prob, axis=-1, keepdims=True)
    grad_logit = (chances * (grad_prob - inner)).astype(BF16)
    dq = scaling * jnp.einsum("hqk,khd->qhd", grad_logit, keys, preferred_element_type=F32)
    dk = scaling * jnp.einsum("hqk,qhd->khd", grad_logit, queries, preferred_element_type=F32)
    dv = jnp.einsum("hqk,qhd->khd", chances_low, grad_att, preferred_element_type=F32)
    part = jnp.stack([dk.reshape(SPAN, tok, -1), dv.reshape(SPAN, tok, -1)], axis=1)
    near = jnp.zeros((2 * SPAN - 1,) + part.shape[1:], F32)
    near = lax.dynamic_update_slice_in_dim(near, part, root, 0)
    owned = near[SPAN - 1]
    for offset in range(1 - SPAN, SPAN):
        if offset:
            owned = owned + shifted(near[offset + SPAN - 1], "seq", offset)
    owned = owned.astype(BF16)
    grad_triple = jnp.stack([dq.reshape(tok, -1).astype(BF16), owned[0], owned[1]], axis=1)
    grad_w_qkv = jnp.einsum("td,tcf->dcf", normed, grad_triple, preferred_element_type=F32)
    grad_one = lax.psum(
        jnp.einsum("tcf,dcf->td", grad_triple, qkv, preferred_element_type=F32), "head"
    )
    x_grad = grad_middle + norm_backward(xhat_one, inv_one, grad_one * gain_one)
    sums = jnp.stack(
        [
            jnp.sum(grad_one * xhat_one, axis=0), jnp.sum(grad_one, axis=0),
            jnp.sum(grad_two * xhat_two, axis=0), jnp.sum(grad_two, axis=0),
            jnp.sum(grad_out, axis=0),
        ],
        axis=0,
    )
    scatter = lambda v, d: lax.psum_scatter(v, "seq", scatter_dimension=d, tiled=True)
    sums = scatter(sums, 1)
    return (
        output, x_grad, scatter(grad_w_qkv, 0), scatter(grad_w_out, 1), sums[0], sums[1], sums[2],
        sums[3], scatter(grad_w_up, 0), grad_up_bias, scatter(grad_w_down, 1), sums[4],
    )


MESH = pl.DeviceIdType.MESH
SEQ = 8
HEAD = 4
LINE = 4
NEAR = 2 * SPAN - 1
QKV_KV, QKV_Q, OUT, UP, DOWN = range(5)
VMEM_BYTES = 60 * 1024 * 1024
PIECES = 2


def al(value, multiple):
    return pl.multiple_of(value, multiple)


def fused_kernel(names, *refs):
    r = types.SimpleNamespace(**dict(zip(names, refs)))
    s, h = lax.axis_index("seq"), lax.axis_index("head")
    z, y, x, c = lax.div(s, 2), lax.rem(s, 2), lax.div(h, 2), lax.rem(h, 2)
    e = lax.rem(z, 2)
    pair_z = z + 1 - 2 * e
    mate = z * 2 + 1 - y
    pair = pair_z * 2 + y
    twin = x * 2 + 1 - c
    across = (1 - x) * 2 + c
    tokens, width = r.tok.shape
    quarter = tokens // HEAD
    head_w = r.qs.shape[1]
    rows = r.wq.shape[1]
    half = r.wu_all.shape[1]
    sent = []

    def copy(src, dst, ss, rs, **where):
        return pltpu.make_async_remote_copy(
            src_ref=src, dst_ref=dst, send_sem=ss, recv_sem=rs, device_id=where,
            device_id_type=MESH,
        )

    def when(cond, then):
        if cond is None:
            then()
        else:
            pl.when(cond)(lambda: then())

    def send(cond, *args, **where):
        one = copy(*args, **where)
        when(cond, one.start)
        sent.append((cond, one))

    def arrived(cond, dst, rs, like=None):
        when(cond, copy(dst if like is None else like, dst, r.v_ss.at[0], rs, seq=mate).wait_recv)

    barrier = pltpu.get_barrier_semaphore()
    greeted = [{"seq": lax.rem(s + d, SEQ)} for d in range(1, SEQ)]
    greeted += [{"head": lax.rem(h + d, HEAD)} for d in range(1, HEAD)]
    greeted += [{"seq": pair, "head": across}]
    for where in greeted:
        pl.semaphore_signal(barrier, inc=1, device_id=where, device_id_type=MESH)
    for k, ref in enumerate((r.g1, r.b1, r.g2, r.b2, r.b3)):
        r.vec[k : k + 1, :] = ref[...].reshape(1, rows).astype(F32)
    r.vec[5:8, :] = jnp.zeros((3, rows), F32)
    r.upb_f[...] = r.upb[...].reshape(1, 2 * half).astype(F32)
    pl.semaphore_wait(barrier, len(greeted))

    def cols(o, size):
        return pl.ds(al(o * size, size), size)

    relay_slot = [
        lambda o: r.wq_all.at[1:3, cols(o, rows), :],
        lambda o: r.wq_all.at[0, cols(o, rows), :],
        lambda o: r.wo_all.at[:, cols(o, rows)],
    ]
    relay_src = [r.wq.at[1:3], r.wq.at[0], r.wo]

    def relay_start(w):
        src, dst, rs = relay_src[w], relay_slot[w](s), r.g_rs.at[w, s]
        send(z < LINE - 1, src, dst, r.g_ss.at[w, 0], rs, seq=s + 2)
        send(z > 0, src, dst, r.g_ss.at[w, 4], rs, seq=s - 2)
        send(None, src, dst, r.g_ss.at[w, 8], rs, seq=mate)

    def relay_round(w, k):
        for sign, first, third in ((-1, 0, 8 + k), (1, 4, 11 + k)):
            from_z = z + sign * k
            there = (from_z >= 0) & (from_z < LINE)
            o = jnp.clip(from_z, 0, LINE - 1) * 2 + y
            ref, rs = relay_slot[w](o), r.g_rs.at[w, o]
            arrived(there, ref, rs)
            onward = (z < LINE - 1) if sign < 0 else (z > 0)
            send(there & onward, ref, ref, r.g_ss.at[w, first + k], rs, seq=s - 2 * sign)
            send(there, ref, ref, r.g_ss.at[w, third], rs, seq=mate)

    def relay_finish(w):
        for d in range(LINE):
            o = lax.rem(z + d, LINE) * 2 + 1 - y
            arrived(None, relay_slot[w](o), r.g_rs.at[w, o])

    low, high = z > 0, z < LINE - 1
    from_mate = 4 - 2 * y

    def token_rows(slot, head):
        return r.nall.at[slot, cols(head, quarter), :]

    def token_send(cond, slot, back, k, to):
        send(cond, token_rows(slot, h), token_rows(back, h), r.t_ns.at[k], r.t_rs.at[back, h], seq=to)

    def token_share(cond, slot):
        ref = token_rows(slot, h)
        arrived(cond, ref, r.t_rs.at[slot, h])
        send(cond, ref, ref, r.t_ss.at[slot, 0], r.t_rs.at[slot, h], head=across)
        send(cond, ref, ref, r.t_ss.at[slot, 1], r.t_rs.at[slot, h], head=twin)

    def token_pass(cond, slot):
        ref = token_rows(slot, across)
        arrived(cond, ref, r.t_rs.at[slot, across])
        send(cond, ref, ref, r.t_ss.at[slot, 2], r.t_rs.at[slot, across], head=twin)

    def token_ready(cond, slot):
        arrived(cond, token_rows(slot, twin), r.t_rs.at[slot, twin])
        other = (1 - x) * 2 + 1 - c
        arrived(cond, token_rows(slot, other), r.t_rs.at[slot, other])

    far_in = jnp.where(y == 0, z >= 2, z <= 1)
    far_slot = 6 * y
    slots = (
        (None, from_mate), (low, 1), (high, 5), (low, 2 - 2 * y), (high, 6 - 2 * y),
        (far_in, far_slot),
    )
    for d in range(1, SEQ):
        send(
            None, r.vec, r.gains.at[:, cols(s, rows)], r.v_ss.at[d - 1], r.v_rs.at[s],
            seq=lax.rem(s + d, SEQ),
        )
    relay_start(0)
    r.gains[:, cols(s, rows)] = r.vec[...]
    for k in range(NEAR):
        other = s + k - (SPAN - 1)

        @pl.when((other < 0) | (other >= SEQ))
        def _():
            r.nall[k] = jnp.zeros(r.nall.shape[1:], BF16)

    for k, cond in enumerate((low & high, high, low, high, low)):

        @pl.when(jnp.logical_not(cond))
        def _():
            r.dkv_recv[k] = jnp.zeros(r.dkv_recv.shape[1:], BF16)

    for d in range(1, SEQ):
        o = lax.rem(s + d, SEQ)
        arrived(None, r.gains.at[:, cols(o, rows)], r.v_rs.at[o], r.vec)

    def normalise(q):
        xhat, _ = norm_parts(r.tok[q, :].astype(F32))
        r.nall[SPAN - 1, q, :] = (xhat * r.gains[0:1, :] + r.gains[1:2, :]).astype(BF16)

    normalise(cols(h, quarter))
    token_send(None, SPAN - 1, 2 + 2 * y, 0, mate)
    token_send(high, SPAN - 1, 1, 1, s + 2)
    token_send(low, SPAN - 1, 5, 2, s - 2)
    for d in range(1, HEAD):
        normalise(cols(lax.rem(h + d, HEAD), quarter))
    token_share(*slots[0])
    token_send(high, from_mate, 2 - 2 * y, 3, s + 2)
    token_send(low, from_mate, 6 - 2 * y, 4, s - 2)
    relay_round(0, 1)
    token_share(*slots[1])
    token_share(*slots[2])
    r.wq_all[:, cols(s, rows), :] = r.wq[...]
    r.wo_all[:, cols(s, rows)] = r.wo[...]
    token_share(*slots[3])
    token_share(*slots[4])
    token_send((y == 0) & low & high, 2, 0, 5, s + 2)
    token_send((y == 1) & low & high, 4, 6, 5, s - 2)
    relay_round(0, 2)
    relay_start(1)
    relay_round(0, 3)
    token_share(*slots[5])
    for cond, slot in slots[:3]:
        token_pass(cond, slot)
    relay_round(1, 1)
    relay_start(2)

    start, leader, span, pad = 0, 0, 0, 0
    for k in range(r.units.shape[0]):
        here = r.units[k]
        inside = (s >= start) & (s < start + here)
        leader = jnp.where(inside, start, leader)
        span = jnp.where(inside, here, span)
        pad = jnp.where(inside, r.pads[k], pad)
        start = start + here
    position = s - leader
    root = jnp.clip(SPAN - 1 - position, 0, SPAN - 1)
    total = span * BLK_DEV
    live = span * tokens - pad

    columns = lax.broadcasted_iota(jnp.int32, (1, SPAN * tokens), 1)
    usable = columns < live
    blocks = lax.div(columns, BLK)
    for hh in range(HEAD):
        for b in range(BLK_DEV):
            query = position * BLK_DEV + b
            count = jnp.zeros((1, SPAN * tokens), F32)
            for wanted in (query - 1, query, query + 1, 0, total - 1):
                count = count + jnp.where(blocks == wanted, 1.0, 0.0)
            for k in range(r.picks.shape[0]):
                raw = r.picks[k, b, hh]
                chosen = lax.rem(raw, BLK_DEV)
                for k_units in range(2, SPAN + 1):
                    chosen = jnp.where(span == k_units, lax.rem(raw, BLK_DEV * k_units), chosen)
                count = count + jnp.where(blocks == chosen, 1.0, 0.0)
            count = jnp.where((query == 0) | (query == total - 1), 1.0, count)
            held = usable & (count > 0)
            bias = jnp.log(jnp.maximum(count, 1.0))
            r.bias[hh, b : b + 1, :] = jnp.where(held, bias, NEGATIVE)

    ffn_src = {
        UP: lambda k: r.wu.at[:, cols(k, half)],
        DOWN: lambda k: r.wd.at[cols(k, half), :],
    }
    ffn_slot = {
        UP: lambda o: r.wu_all.at[cols(o, rows), :],
        DOWN: lambda o: r.wd_all.at[:, cols(o, rows)],
    }

    def ffn_start(w):
        i = w - UP
        for d in range(1, LINE):
            to = lax.rem(z + d, LINE)
            send(
                None, ffn_src[w](lax.rem(to, 2)), ffn_slot[w](s), r.f_ss.at[i, d - 1],
                r.f_rs.at[i, s], seq=to * 2 + y,
            )
        send(
            None, ffn_src[w](e), ffn_slot[w](s), r.f_ss.at[i, 3], r.f_rs.at[i, s], seq=mate
        )

    def by_distance(k):
        up = k + jnp.where(z <= k, 1, 0)
        down = k + jnp.where(LINE - 1 - z <= k, 1, 0)
        return jnp.where(z < LINE // 2, up, LINE - 1 - down)

    def ffn_forward(w, ks=(0, 1, 2)):
        i = w - UP
        for k in ks:
            o = by_distance(k) * 2 + y
            ref = ffn_slot[w](o)
            arrived(None, ref, r.f_rs.at[i, o])
            send(None, ref, ref, r.f_ss.at[i, 4 + k], r.f_rs.at[i, o], seq=mate)

    def ffn_finish(w):
        for d in range(LINE):
            o = lax.rem(z + d, LINE) * 2 + 1 - y
            arrived(None, ffn_slot[w](o), r.f_rs.at[w - UP, o])

    relay_round(1, 2)
    relay_round(2, 1)
    relay_round(1, 3)
    relay_round(2, 2)
    ffn_start(UP)
    relay_round(2, 3)
    for cond, slot in slots[3:]:
        token_pass(cond, slot)
    for ref, src in ((ffn_slot[UP](s), ffn_src[UP](e)), (ffn_slot[DOWN](s), ffn_src[DOWN](e))):
        ref[...] = src[...]

    ffn_start(DOWN)
    for cond, slot in slots:
        token_ready(cond, slot)
    relay_finish(0)
    scaling = HEAD_DIM ** (-0.5)
    for j in range(SPAN):
        q = pl.ds(j * tokens, tokens)
        rows_in = r.nall[root + j]
        r.kwin[q, :] = dot(rows_in, r.wq_all[1], ((1,), (0,))).astype(BF16)
        r.vwin[q, :] = dot(rows_in, r.wq_all[2], ((1,), (0,))).astype(BF16)
    relay_finish(1)
    part = dot(r.nall[SPAN - 1], r.wq_all[0], ((1,), (0,)))
    r.qs[...] = (part.astype(BF16).astype(F32) * scaling).astype(BF16)
    r.cotx[cols(e, tokens), :] = r.cot[...]
    beyond = (1 - x) * 2 + 1 - c

    def block_rows(unit, head):
        return pl.ds(al(unit * tokens + head * quarter, quarter), quarter)

    def cot_rows(unit, head):
        return r.cotx.at[block_rows(unit, head), :]

    send(
        None, r.cot.at[cols(h, quarter), :], cot_rows(e, h), r.c_ss.at[0], r.c_rs.at[h], seq=pair
    )

    def cot_share():
        ref = cot_rows(1 - e, h)
        arrived(None, ref, r.c_rs.at[h])
        send(None, ref, ref, r.c_ss.at[1], r.c_rs.at[h], head=across)
        send(None, ref, ref, r.c_ss.at[2], r.c_rs.at[h], head=twin)

    def cot_pass():
        ref = cot_rows(1 - e, across)
        arrived(None, ref, r.c_rs.at[across])
        send(None, ref, ref, r.c_ss.at[3], r.c_rs.at[across], head=twin)

    lanes = lax.div(lax.broadcasted_iota(jnp.int32, (1, head_w), 1), HEAD_DIM)
    none = jnp.zeros((), BF16)
    r.att[...] = jnp.zeros(r.att.shape, F32)

    def attend(hh, carry):
        mine = lanes == hh
        query = jnp.where(mine, r.qs[...], none)
        for j in range(SPAN):
            k = pl.ds(j * tokens, tokens)
            r.lg[:, k] = dot(query, r.kwin[k, :], ((1,), (1,)))
        for b in range(BLK_DEV):
            q = pl.ds(b * BLK, BLK)
            logits = r.lg[q, :] + r.bias[hh, b : b + 1, :]
            grown = jnp.exp(logits - jnp.max(logits, axis=-1, keepdims=True))
            scale = 1.0 / jnp.sum(grown, axis=-1, keepdims=True)
            r.prob[hh, q, :] = (grown * scale).astype(BF16)
        part = dot(r.prob[hh], r.vwin[...], ((1,), (0,)))
        r.att[...] += jnp.where(mine, part, 0.0)
        return carry

    lax.fori_loop(0, HEAD // 2, attend, 0)
    ffn_forward(UP, (0,))
    lax.fori_loop(HEAD // 2, HEAD, attend, 0)
    ffn_forward(UP, (1,))
    r.att_low[...] = r.att[...].astype(BF16)
    relay_finish(2)

    def rows_of(k):
        return cols(k, quarter)

    def reduce_start(op):
        for v in range(2):
            r.q1_send[op, v] = r.sum_f[rows_of(v * 2 + 1 - c), :].astype(BF16)
        send(None, r.q1_send.at[op], r.q1_recv.at[op], r.q1_ss.at[op], r.q1_rs.at[op], head=twin)

    def reduce_middle(op):
        arrived(None, r.q1_recv.at[op], r.q1_rs.at[op])
        block = r.sum_f[rows_of(across), :] + r.q1_recv[op, 1 - x].astype(F32)
        r.q2_send[op] = block.astype(BF16)
        send(None, r.q2_send.at[op], r.q2_recv.at[op], r.q2_ss.at[op], r.q2_rs.at[op], head=across)
        r.q_own[op] = r.sum_f[rows_of(h), :] + r.q1_recv[op, x].astype(F32)

    def reduce_finish(op):
        arrived(None, r.q2_recv.at[op], r.q2_rs.at[op])
        return r.q_own[op] + r.q2_recv[op].astype(F32)

    def spread_start(op, whole, value):
        whole[rows_of(h), :] = value
        ref = whole.at[rows_of(h), :]
        send(None, ref, ref, r.ag_ss.at[op, 0], r.ag_rs.at[op, h], head=across)
        send(None, ref, ref, r.ag_ss.at[op, 1], r.ag_rs.at[op, h], head=twin)

    def spread_pass(op, whole):
        ref = whole.at[rows_of(across), :]
        arrived(None, ref, r.ag_rs.at[op, across])
        send(None, ref, ref, r.ag_ss.at[op, 2], r.ag_rs.at[op, across], head=twin)

    def spread_finish(op, whole):
        for o in (twin, beyond):
            arrived(None, whole.at[rows_of(o), :], r.ag_rs.at[op, o])

    pair_sum = [r.sum_f, r.sum_g]

    def pair_start(op):
        for u in range(2):
            for v in range(2):
                block = pair_sum[op][block_rows(u, v * 2 + 1 - c), :]
                r.p1_send[op, u * 2 + v] = block.astype(BF16)
        send(None, r.p1_send.at[op], r.p1_recv.at[op], r.p1_ss.at[op], r.p1_rs.at[op], head=twin)

    def pair_middle(op):
        arrived(None, r.p1_recv.at[op], r.p1_rs.at[op])
        for du, dv in ((1, 1), (1, 0), (0, 1), (0, 0)):
            u, v = lax.rem(e + du, 2), lax.rem(x + dv, 2)
            block = pair_sum[op][block_rows(u, v * 2 + c), :] + r.p1_recv[op, u * 2 + v].astype(F32)
            if du or dv:
                k = u * 2 + v
                r.p2_send[op, k] = block.astype(BF16)
                send(
                    None, r.p2_send.at[op, k], r.p2_recv.at[op, e * 2 + x], r.p2_ss.at[op, k],
                    r.p2_rs.at[op, e * 2 + x], seq=pair if du else s, head=across if dv else h,
                )
            else:
                r.p_own[op] = block

    def pair_x(op):
        arrived(None, r.p1_recv.at[op], r.p1_rs.at[op])
        for du in (1, 0):
            u = lax.rem(e + du, 2)
            k = u * 2 + 1 - x
            block = pair_sum[op][block_rows(u, across), :] + r.p1_recv[op, k].astype(F32)
            r.p2_send[op, k] = block.astype(BF16)
            send(
                None, r.p2_send.at[op, k], r.p2_recv.at[op, u], r.p2_ss.at[op, k],
                r.p2_rs.at[op, u], head=across,
            )

    def pair_over(op):
        for du in (1, 0):
            u = lax.rem(e + du, 2)
            arrived(None, r.p2_recv.at[op, u], r.p2_rs.at[op, u])
            block = pair_sum[op][block_rows(u, h), :] + r.p1_recv[op, u * 2 + x].astype(F32)
            block = block + r.p2_recv[op, u].astype(F32)
            if du:
                k = u * 2 + x
                r.p2_send[op, k] = block.astype(BF16)
                send(
                    None, r.p2_send.at[op, k], r.p2_recv.at[op, 2], r.p2_ss.at[op, k],
                    r.p2_rs.at[op, 2], seq=pair,
                )
            else:
                r.p_own[op] = block

    def pair_end(op):
        arrived(None, r.p2_recv.at[op, 2], r.p2_rs.at[op, 2])
        return r.p_own[op] + r.p2_recv[op, 2].astype(F32)

    def pair_finish(op):
        result = r.p_own[op]
        for du, dv in ((0, 1), (1, 0), (1, 1)):
            k = lax.rem(e + du, 2) * 2 + lax.rem(x + dv, 2)
            arrived(None, r.p2_recv.at[op, k], r.p2_rs.at[op, k])
            result = result + r.p2_recv[op, k].astype(F32)
        return result

    r.sum_f[:tokens, :] = dot(r.att_low[...], r.wo_all[...], ((1,), (0,)))
    reduce_start(0)
    reduce_middle(0)
    ffn_forward(UP, (2,))
    ffn_forward(DOWN, (0,))
    middle = r.tok[rows_of(h), :].astype(F32) + reduce_finish(0)
    r.mid_own[...] = middle
    xhat, _ = norm_parts(middle)

    def n2_rows(unit, head):
        return r.n2x.at[block_rows(unit, head), :]

    r.n2x[block_rows(e, h), :] = (xhat * r.gains[2:3, :] + r.gains[3:4, :]).astype(BF16)
    mine, tag = n2_rows(e, h), e * 4 + h
    send(None, mine, mine, r.n2_ss.at[0], r.n2_rs.at[tag], seq=pair)
    send(None, mine, mine, r.n2_ss.at[1], r.n2_rs.at[tag], head=across)
    send(None, mine, mine, r.n2_ss.at[2], r.n2_rs.at[tag], head=twin)
    cot_share()
    ffn_forward(DOWN, (1,))
    for k, (unit, head) in enumerate(((e, across), (1 - e, h), (1 - e, across))):
        ref, tag = n2_rows(unit, head), unit * 4 + head
        arrived(None, ref, r.n2_rs.at[tag])
        if k == 1:
            send(None, ref, ref, r.n2_ss.at[6], r.n2_rs.at[tag], head=across)
        send(None, ref, ref, r.n2_ss.at[3 + k], r.n2_rs.at[tag], head=twin)
    cot_pass()
    ffn_forward(DOWN, (2,))
    ffn_finish(UP)
    for unit in (e, 1 - e):
        for head in (x * 2 + 1 - c, (1 - x) * 2 + 1 - c):
            arrived(None, n2_rows(unit, head), r.n2_rs.at[unit * 4 + head])

    root_c = (2.0 / 3.141592653589793) ** 0.5
    r.up_send[half // 128 :, :] = jnp.zeros((8 - half // 128, 128), F32)
    for j in range(half // 256):
        f = pl.ds(j * 256, 256)
        bias = r.upb_f[:, pl.ds(al(e * half + j * 256, 256), 256)]
        v = dot(r.n2x[...], r.wu_all[:, f], ((1,), (0,))) + bias
        t = jnp.tanh(root_c * (v + 0.044715 * (v * v * v)))
        r.hid[:, f] = (0.5 * v * (1.0 + t)).astype(BF16)
        slope = 0.5 * (1.0 + t) + 0.5 * v * (1.0 - t * t) * (root_c * (1.0 + 0.134145 * v * v))
        r.slope[:, f] = slope
    ffn_finish(DOWN)
    for head in (twin, beyond):
        arrived(None, cot_rows(1 - e, head), r.c_rs.at[head])
    for j in range(half // 256):
        f = pl.ds(j * 256, 256)
        low_p = (dot(r.cotx[...], r.wd_all[f, :], ((1,), (1,))) * r.slope[:, f]).astype(BF16)
        r.gp[:, f] = low_p
        sums = jnp.sum(low_p.astype(F32), axis=0, keepdims=True)
        r.up_send[2 * j : 2 * j + 1, :] = sums[:, :128]
        r.up_send[2 * j + 1 : 2 * j + 2, :] = sums[:, 128:]

    grad_send = {QKV_KV: r.skv, QKV_Q: r.sq, OUT: r.so, UP: r.su, DOWN: r.sd}
    grad_arrive = {QKV_KV: r.akv, QKV_Q: r.aq, OUT: r.ao, UP: r.au, DOWN: r.ad}
    grad_again = {QKV_KV: r.bkv, QKV_Q: r.bq, OUT: r.bo, UP: r.bu, DOWN: r.bd}
    grad_final = {QKV_KV: r.rkv, QKV_Q: r.rq, OUT: r.ro, UP: r.ru, DOWN: r.rd}

    def tile_of(i):
        return lax.rem(z + 1 + i, LINE)

    def grad_cross(w, zz):
        send(
            None, grad_send[w].at[zz * 2 + 1 - y], grad_arrive[w].at[zz], r.ra_ss.at[w, zz],
            r.ra_rs.at[w, zz], seq=mate,
        )

    def grad_along(w, ks=(1, 2, 3)):
        for d in ks:
            zz = lax.rem(z + d, LINE)
            arrived(None, grad_arrive[w].at[zz], r.ra_rs.at[w, zz])
            both = grad_send[w][zz * 2 + y].astype(F32) + grad_arrive[w][zz].astype(F32)
            grad_again[w][zz] = both.astype(BF16)
            send(
                None, grad_again[w].at[zz], grad_final[w].at[z], r.rb_ss.at[w, zz],
                r.rb_rs.at[w, z], seq=zz * 2 + y,
            )

    outer, inner = (z == 0) | (z == LINE - 1), (z == 1) | (z == LINE - 2)
    far_half = 2 - 2 * lax.div(z, 2)
    far_inner = 2 - lax.div(z, 2)
    grad_hold = {QKV_KV: r.hkv, QKV_Q: r.hq, OUT: r.ho}

    def tile_far(i):
        return (far_half, far_half + 1, pair_z, z)[i]

    def grad_first(w):
        for k in range(3):
            zz = tile_far(k)
            arrived(None, grad_arrive[w].at[zz], r.ra_rs.at[w, zz])
            both = grad_send[w][zz * 2 + y].astype(F32) + grad_arrive[w][zz].astype(F32)
            grad_again[w][zz] = both.astype(BF16)
            if k < 2:
                send(
                    outer, grad_again[w].at[zz], grad_hold[w].at[k], r.rh_ss.at[w, k],
                    r.rh_rs.at[w, k], seq=pair,
                )
            else:
                send(
                    None, grad_again[w].at[zz], grad_final[w].at[z], r.rb_ss.at[w, zz],
                    r.rb_rs.at[w, z], seq=pair,
                )

    def grad_second(w):
        for k in range(2):
            zz = tile_far(k)
            arrived(inner, grad_hold[w].at[k], r.rh_rs.at[w, k])

            @pl.when(inner)
            def _():
                both = grad_again[w][zz].astype(F32) + grad_hold[w][k].astype(F32)
                grad_again[w][zz] = both.astype(BF16)

            send(
                inner, grad_again[w].at[zz], grad_final[w].at[z], r.rb_ss.at[w, zz],
                r.rb_rs.at[w, z], seq=zz * 2 + y,
            )

    def grad_own(w):
        arrived(None, grad_arrive[w].at[z], r.ra_rs.at[w, z])
        return grad_send[w][z * 2 + y].astype(F32) + grad_arrive[w][z].astype(F32)

    def grad_from(w, o):
        arrived(None, grad_final[w].at[o], r.rb_rs.at[w, o])
        return grad_final[w][o].astype(F32)

    def grad_sum(w):
        return grad_own(w) + grad_from(w, pair_z) + grad_from(w, far_inner)

    def grad_halves(w):
        same = grad_own(w) + grad_from(w, lax.rem(z + 2, LINE))
        other = grad_from(w, lax.rem(z + 1, LINE)) + grad_from(w, lax.rem(z + 3, LINE))
        return same, other

    def down_step(i):
        zz = tile_of(i)
        part = dot(r.hid[...], r.cotx[:, cols(zz, 256)], ((0,), (0,))).astype(BF16)
        r.sd[zz * 2] = part[:, :rows]
        r.sd[zz * 2 + 1] = part[:, rows:]
        grad_cross(DOWN, zz)

    def up_step(i):
        zz = tile_of(i)
        part = dot(r.n2x[:, cols(zz, 256)], r.gp[...], ((0,), (0,))).astype(BF16)
        r.su[zz * 2] = part[:rows]
        r.su[zz * 2 + 1] = part[rows:]
        grad_cross(UP, zz)

    down_step(0)
    r.sum_f[...] = dot(r.gp[...], r.wu_all[...], ((1,), (1,)))
    pair_start(0)
    down_step(1)
    pair_middle(0)
    r.sum_g[...] = dot(r.hid[...], r.wd_all[...], ((1,), (0,)))
    pair_start(1)
    down_step(2)
    down_step(3)
    pair_x(1)
    for i in range(LINE):
        up_step(i)
    for d in range(1, SEQ):
        send(
            None, r.up_send, r.up_recv.at[s], r.up_ss.at[d], r.up_rs.at[s],
            seq=lax.rem(s + d, SEQ),
        )

    grad_two = pair_finish(0)
    xhat, inverse = norm_parts(r.mid_own[...])
    dy = r.cot[rows_of(h), :].astype(F32)
    grad_mid = dy + norm_backward(xhat, inverse, grad_two * r.gains[2:3, :])
    r.gm_own[...] = grad_mid
    spread_start(0, r.gb, grad_mid.astype(BF16))
    r.sm_send[2:3, :] = jnp.sum(grad_two * xhat, axis=0, keepdims=True)
    r.sm_send[3:4, :] = jnp.sum(grad_two, axis=0, keepdims=True)
    r.sm_send[4:5, :] = jnp.sum(dy, axis=0, keepdims=True)
    r.sm_send[5:8, :] = jnp.zeros((3, width), F32)

    grad_along(DOWN)
    pair_over(1)
    spread_pass(0, r.gb)
    spread_finish(0, r.gb)
    r.gatt[...] = dot(r.gb[...], r.wo_all[...], ((1,), (1,))).astype(BF16)
    for i in range(LINE):
        zz = tile_far(i)
        part = dot(r.att_low[...], r.gb[:, cols(zz, 256)], ((0,), (0,))).astype(BF16)
        r.so[zz * 2] = part[:, :rows]
        r.so[zz * 2 + 1] = part[:, rows:]
        grad_cross(OUT, zz)
    grad_along(UP, (1, 2))

    r.dq[...] = jnp.zeros(r.dq.shape, F32)
    r.dk[...] = jnp.zeros(r.dk.shape, F32)
    r.dv[...] = jnp.zeros(r.dv.shape, F32)

    def attend_back(hh, carry):
        mine = lanes == hh
        query = jnp.where(mine, r.qs[...], none)
        grad = jnp.where(mine, r.gatt[...], none)
        for j in range(SPAN):
            k = pl.ds(j * tokens, tokens)
            r.lg[:, k] = dot(grad, r.vwin[k, :], ((1,), (1,)))
        for b in range(BLK_DEV):
            q = pl.ds(b * BLK, BLK)
            chance, grown = r.prob[hh, q, :].astype(F32), r.lg[q, :]
            inner = jnp.sum(chance * grown, axis=-1, keepdims=True)
            r.ds[hh, q, :] = (chance * (grown - inner)).astype(BF16)
        for j in range(SPAN):
            k = pl.ds(j * tokens, tokens)
            r.dk[k, :] += dot(r.ds[hh, :, k], query, ((0,), (0,)))
            r.dv[k, :] += dot(r.prob[hh, :, k], grad, ((0,), (0,)))
        return carry

    lax.fori_loop(0, HEAD, attend_back, 0)
    for k in range(2 * (SPAN - 1) + SPAN):
        j = k - (SPAN - 1)
        if 0 <= j < SPAN:
            q = pl.ds(j * tokens, tokens)
            r.dkv_pad[k, 0] = r.dk[q, :].astype(BF16)
            r.dkv_pad[k, 1] = r.dv[q, :].astype(BF16)
        else:
            r.dkv_pad[k] = jnp.zeros(r.dkv_pad.shape[1:], BF16)
    for k in range(NEAR):
        r.dkv_send[k] = r.dkv_pad[k + SPAN - 1 - root]

    def grad_hop(cond, slot, into, k, to, v):
        send(
            cond, r.dkv_send.at[slot, v], r.dkv_recv.at[into, v], r.dkv_ss.at[k, v],
            r.dkv_rs.at[into, v], seq=to,
        )

    def add_to(v, slot, *froms):
        both = r.dkv_send[slot, v].astype(F32)
        for k in froms:
            both = both + r.dkv_recv[k, v].astype(F32)
        r.dkv_send[slot, v] = both.astype(BF16)

    def grad_wait(cond, into, v):
        arrived(cond, r.dkv_recv.at[into, v], r.dkv_rs.at[into, v])

    FAR, ABOVE, BELOW, LINE_ABOVE, LINE_BELOW, MATE = range(6)
    for v in range(2):
        grad_hop((y == 0) & (z >= 2), 0, FAR, 0, s - 2, v)
        grad_hop((y == 1) & (z <= 1), 6, FAR, 0, s + 2, v)
    for v in range(2):
        grad_hop((y == 0) & high, 6, BELOW, 1, s + 2, v)
        grad_hop((y == 1) & low, 0, ABOVE, 1, s - 2, v)

    def hop_far(v):
        grad_wait(low & high, FAR, v)
        add_to(v, 2 + 2 * y, FAR)
        grad_hop((y == 0) & low, 2, ABOVE, 2, s - 2, v)
        grad_hop((y == 1) & high, 4, BELOW, 2, s + 2, v)

    def hop_line(v):
        grad_hop(low, 1, LINE_ABOVE, 3, s - 2, v)
        grad_hop(high, 5, LINE_BELOW, 4, s + 2, v)

    def hop_mate(v):
        grad_wait(high, ABOVE, v)
        grad_wait(low, BELOW, v)
        add_to(v, from_mate, ABOVE, BELOW)
        grad_hop(None, from_mate, MATE, 5, mate, v)

    def queries_back(hh, carry):
        r.dq[...] += jnp.where(lanes == hh, dot(r.ds[hh], r.kwin[...], ((1,), (0,))), 0.0)
        return carry

    for i in range(LINE):
        zz = tile_far(i)
        for k in range(2):
            part = jnp.zeros((256, head_w), F32)
            for j in range(SPAN):
                part = part + dot(
                    r.nall[root + j, :, cols(zz, 256)], r.dkv_pad[j + SPAN - 1, k], ((0,), (0,))
                )
            part = part.astype(BF16)
            for v in range(2):
                r.skv[zz * 2 + v, k] = part[v * rows : (v + 1) * rows]
        grad_cross(QKV_KV, zz)
        if i == 1:
            hop_far(0)
        if i == 2:
            hop_far(1)
            hop_line(0)
            hop_line(1)
    grad_along(UP, (3,))
    hop_mate(0)
    hop_mate(1)
    grad_first(OUT)
    lax.fori_loop(0, HEAD, queries_back, 0)
    r.gtq[...] = (r.dq[...] * scaling).astype(BF16)
    for i in range(LINE):
        zz = tile_far(i)
        part = dot(r.nall[SPAN - 1, :, cols(zz, 256)], r.gtq[...], ((0,), (0,))).astype(BF16)
        r.sq[zz * 2] = part[:rows]
        r.sq[zz * 2 + 1] = part[rows:]
        grad_cross(QKV_Q, zz)
    grad_second(OUT)
    grad_first(QKV_KV)
    ffn = pair_end(1)
    spread_start(1, r.out_o, (r.mid_own[...] + ffn + r.gains[4:5, :]).astype(BF16))
    for v in range(2):
        grad_wait(high, LINE_ABOVE, v)
        grad_wait(low, LINE_BELOW, v)
        grad_wait(None, MATE, v)
        whole = r.dkv_send[SPAN - 1, v].astype(F32)
        for k in (LINE_ABOVE, LINE_BELOW, MATE):
            whole = whole + r.dkv_recv[k, v].astype(F32)
        r.gtkv[v] = whole.astype(BF16)

    r.sum_f[:tokens, :] = (
        dot(r.gtq[...], r.wq_all[0], ((1,), (1,)))
        + dot(r.gtkv[0], r.wq_all[1], ((1,), (1,)))
        + dot(r.gtkv[1], r.wq_all[2], ((1,), (1,)))
    )
    reduce_start(1)
    reduce_middle(1)
    grad_second(QKV_KV)
    grad_one = reduce_finish(1)
    xhat, inverse = norm_parts(r.tok[rows_of(h), :].astype(F32))
    r.sm_send[0:1, :] = jnp.sum(grad_one * xhat, axis=0, keepdims=True)
    r.sm_send[1:2, :] = jnp.sum(grad_one, axis=0, keepdims=True)
    for d in range(1, SEQ):
        to = lax.rem(s + d, SEQ)
        send(
            None, r.sm_send.at[:, cols(to, rows)], r.sm_recv.at[s], r.sm_ss.at[d], r.sm_rs.at[s],
            seq=to,
        )
    spread_pass(1, r.out_o)
    grad_first(QKV_Q)
    grad_x = r.gm_own[...] + norm_backward(xhat, inverse, grad_one * r.gains[0:1, :])
    spread_start(2, r.xg_o, grad_x.astype(BF16))

    same, other = grad_halves(DOWN)
    r.gd_o[cols(e, half), :] = same
    r.gd_o[cols(1 - e, half), :] = other
    same, other = grad_halves(UP)
    r.gu_o[:, cols(e, half)] = same
    r.gu_o[:, cols(1 - e, half)] = other
    spread_pass(2, r.xg_o)
    grad_second(QKV_Q)
    r.go_o[...] = grad_sum(OUT)

    r.sm_recv[s] = r.sm_send[:, cols(s, rows)]
    r.up_recv[s] = r.up_send[...]
    for d in range(1, SEQ):
        o = lax.rem(s + d, SEQ)
        arrived(None, r.sm_recv.at[o], r.sm_rs.at[o], r.vec)
        arrived(None, r.up_recv.at[o], r.up_rs.at[o])
    part = r.sm_recv[0]
    for o in range(1, SEQ):
        part = part + r.sm_recv[o]
    r.sm_own[...] = part
    for d in range(1, HEAD):
        send(
            None, r.sm_own, r.sm_two.at[h], r.sm2_ss.at[d], r.sm2_rs.at[h],
            head=lax.rem(h + d, HEAD),
        )
    r.sm_two[h] = part
    tall = half // 128
    for u in range(2):
        ups = jnp.zeros((tall, 128), F32)
        for o in range(SEQ):
            if (o // 2) % 2 == u:
                ups = ups + r.up_recv[o, :tall, :]
        r.small_o[8 + u * tall : 8 + (u + 1) * tall, :] = ups
    spread_finish(1, r.out_o)
    spread_finish(2, r.xg_o)
    for d in range(1, HEAD):
        o = lax.rem(h + d, HEAD)
        arrived(None, r.sm_two.at[o], r.sm2_rs.at[o])
    r.small_o[0:8, :] = (r.sm_two[0] + r.sm_two[1]) + (r.sm_two[2] + r.sm_two[3])
    r.gq_o[0] = grad_sum(QKV_Q)
    r.gq_o[1:3] = grad_sum(QKV_KV)

    for cond, one in sent:
        when(cond, one.wait_send)


def local_fused(
    tokens, w_qkv, w_out, ln1_gain, ln1_bias, ln2_gain, ln2_bias, w_up, up_bias, w_down, down_bias,
    seq_units, seq_pad, rand_picks, cotangent,
):
    tok, width = tokens.shape
    rows, _, head_w = w_qkv.shape
    hidden = w_up.shape[1]
    half = hidden // 2
    quarter = tok // HEAD
    keys = SPAN * tok
    smem, vmem = pl.BlockSpec(memory_space=pltpu.SMEM), pl.BlockSpec(memory_space=pltpu.VMEM)
    ins = dict(
        units=seq_units, pads=seq_pad, picks=jnp.transpose(rand_picks, (2, 0, 1)), tok=tokens,
        cot=cotangent, wq=jnp.transpose(w_qkv, (1, 0, 2)), wo=w_out, wu=w_up, wd=w_down,
        g1=ln1_gain, b1=ln1_bias, g2=ln2_gain, b2=ln2_bias, b3=down_bias,
        upb=up_bias,
    )
    outs = dict(
        out_o=((tok, width), BF16), xg_o=((tok, width), BF16), gq_o=((3, rows, head_w), F32),
        go_o=((head_w, rows), F32), gu_o=((rows, hidden), F32), gd_o=((hidden, rows), F32),
        small_o=((16, rows), F32),
    )
    scratch = dict(
        wq_all=((3, width, head_w), BF16), wo_all=((head_w, width), BF16),
        wu_all=((width, half), BF16), wd_all=((half, width), BF16), vec=((8, rows), F32), upb_f=((1, hidden), F32),
        gains=((8, width), F32), nall=((NEAR, tok, width), BF16),
        qs=((tok, head_w), BF16),
        kwin=((keys, head_w), BF16), vwin=((keys, head_w), BF16), lg=((tok, keys), F32),
        prob=((HEAD, tok, keys), BF16), ds=((HEAD, tok, keys), BF16),
        att=((tok, head_w), F32), att_low=((tok, head_w), BF16), n2x=((2 * tok, width), BF16),
        cotx=((2 * tok, width), BF16), hid=((2 * tok, half), BF16), slope=((2 * tok, half), F32), gp=((2 * tok, half), BF16),
        gb=((tok, width), BF16), mid_own=((quarter, width), F32),
        gm_own=((quarter, width), F32), gatt=((tok, head_w), BF16), dq=((tok, head_w), F32),
        dk=((keys, head_w), F32), dv=((keys, head_w), F32),
        dkv_pad=((NEAR + SPAN - 1, 2, tok, head_w), BF16),
        dkv_send=((NEAR, 2, tok, head_w), BF16), dkv_recv=((6, 2, tok, head_w), BF16),
        gtq=((tok, head_w), BF16), gtkv=((2, tok, head_w), BF16),
        q1_send=((2, 2, quarter, width), BF16), q1_recv=((2, 2, quarter, width), BF16),
        q2_send=((2, quarter, width), BF16), q2_recv=((2, quarter, width), BF16),
        q_own=((2, quarter, width), F32),
        sum_f=((2 * tok, width), F32), sum_g=((2 * tok, width), F32), bias=((HEAD, 8, keys), F32),
        p1_send=((2, 4, quarter, width), BF16), p1_recv=((2, 4, quarter, width), BF16),
        p2_send=((2, 4, quarter, width), BF16), p2_recv=((2, 4, quarter, width), BF16),
        p_own=((2, quarter, width), F32), sm_send=((8, width), F32),
        sm_recv=((SEQ, 8, rows), F32), sm_own=((8, rows), F32), sm_two=((HEAD, 8, rows), F32),
        up_send=((8, 128), F32), up_recv=((SEQ, 8, 128), F32),
    )
    shards = dict(
        kv=(2, rows, head_w), q=(rows, head_w), o=(head_w, rows), u=(rows, half), d=(half, rows)
    )
    for lead, count in (("s", SEQ), ("a", LINE), ("b", LINE), ("r", LINE), ("h", 2)):
        for name, shape in shards.items():
            scratch[lead + name] = ((count,) + shape, BF16)
    semaphores = dict(
        g_ss=(3, 16), g_rs=(3, SEQ), f_ss=(2, 7), f_rs=(2, SEQ), v_ss=(7,), v_rs=(SEQ,),
        t_ns=(6,), t_ss=(NEAR, 3), t_rs=(NEAR, HEAD), dkv_ss=(6, 2), dkv_rs=(6, 2), c_ss=(4,), c_rs=(HEAD,),
        q1_ss=(2,), q1_rs=(2,), q2_ss=(2,), q2_rs=(2,), ag_ss=(3, 3), ag_rs=(3, HEAD), n2_ss=(7,),
        n2_rs=(8,), p1_ss=(2,), p1_rs=(2,), p2_ss=(2, 4), p2_rs=(2, 4), ra_ss=(5, LINE),
        ra_rs=(5, LINE), rh_ss=(5, 2), rh_rs=(5, 2), rb_ss=(5, LINE), rb_rs=(5, LINE), sm_ss=(SEQ,), sm_rs=(SEQ,),
        sm2_ss=(HEAD,), sm2_rs=(HEAD,), up_ss=(SEQ,), up_rs=(SEQ,),
    )
    names = [*ins, *outs, *scratch, *semaphores]
    results = pl.pallas_call(
        functools.partial(fused_kernel, names),
        out_shape=[jax.ShapeDtypeStruct(*o) for o in outs.values()],
        in_specs=[smem] * 3 + [vmem] * (len(ins) - 3),
        out_specs=[vmem] * len(outs),
        scratch_shapes=[pltpu.VMEM(*v) for v in scratch.values()]
        + [pltpu.SemaphoreType.DMA(v) for v in semaphores.values()],
        compiler_params=pltpu.CompilerParams(
            collective_id=0, has_side_effects=True, vmem_limit_bytes=VMEM_BYTES
        ),
        name="fused_layer",
    )(*ins.values())
    large = [(v[0], F32 if k == "xg_o" else v[1]) for k, v in outs.items()][:-1]

    def piece(out):
        shape, axis = list(out[0]), len(out[0]) - 2
        shape[axis] //= PIECES
        return pl.BlockSpec(tuple(shape), lambda i: (0,) * axis + (i, 0))

    handed = pl.pallas_call(
        hand_over_kernel,
        out_shape=[jax.ShapeDtypeStruct(*o) for o in large]
        + [jax.ShapeDtypeStruct((rows,), F32)] * 5
        + [jax.ShapeDtypeStruct((hidden,), F32)],
        grid=(PIECES,),
        in_specs=[piece(o) for o in large] + [vmem],
        out_specs=[piece(o) for o in large] + [vmem] * 6,
        name="hand_over",
    )(*results)
    out, xg, gq, go, gu, gd, g1, b1, g2, b2, b3, upg = handed
    return out, xg, jnp.transpose(gq, (1, 0, 2)), go, g1, b1, g2, b2, gu, upg, gd, b3


def hand_over_kernel(*refs):
    large = (len(refs) - 7) // 2
    small, vectors = refs[large], refs[2 * large + 1 :]
    for k in range(large):
        target = refs[large + 1 + k]
        target[...] = refs[k][...].astype(target.dtype)
    for k in range(5):
        vectors[k][...] = small[k, :]
    for k in range(8):
        vectors[5][pl.ds(k * 128, 128)] = small[8 + k, :]


IN_SPECS = (
    P("seq", None), P("seq", None, "head"), P("head", "seq"), P("seq"), P("seq"), P("seq"),
    P("seq"), P("seq", "head"), P("head"), P("head", "seq"), P("seq"), P(), P(),
    P("seq", "head", None), P("seq", None),
)
OUT_SPECS = (
    P("seq", None), P("seq", None), P("seq", None, "head"), P("head", "seq"), P("seq"), P("seq"),
    P("seq"), P("seq"), P("seq", "head"), P("head"), P("head", "seq"), P("seq"),
)


def solution(mesh):
    fits = mesh.shape["seq"] == SEQ and mesh.shape["head"] == HEAD
    return jax.shard_map(
        local_fused if fits else local_general, mesh=mesh, in_specs=IN_SPECS,
        out_specs=OUT_SPECS, check_vma=False,
    )
```

```python
import functools
import types

import jax
import jax.numpy as jnp
from jax import lax
from jax.experimental import pallas as pl
from jax.experimental.pallas import tpu as pltpu
from jax.sharding import PartitionSpec as P

HEAD_DIM = 64
BLK = 64
SPAN = 4
BLK_DEV = 4
EPSILON = 1e-05
NEGATIVE = -1e30
F32 = jnp.float32
BF16 = jnp.bfloat16


def shifted(value, axis, steps):
    count = lax.axis_size(axis)
    first, last = max(0, -steps), min(count, count - steps)
    return lax.ppermute(value, axis, [(i, i + steps) for i in range(first, last)])


def norm_parts(features):
    average = jnp.mean(features, axis=-1, keepdims=True)
    centred = features - average
    spread = jnp.mean(centred * centred, axis=-1, keepdims=True)
    inverse = lax.rsqrt(spread + EPSILON)
    return centred * inverse, inverse


def norm_backward(xhat, inverse, scaled):
    first = jnp.mean(scaled, axis=-1, keepdims=True)
    second = jnp.mean(scaled * xhat, axis=-1, keepdims=True)
    return inverse * (scaled - first - xhat * second)


def dot(a, b, dims):
    return lax.dot_general(a, b, (dims, ((), ())), preferred_element_type=F32)


def sequence_place(seq_units, seq_pad):
    device = lax.axis_index("seq")
    start, leader, span, pad = 0, 0, 0, 0
    for k in range(seq_units.shape[0]):
        units = seq_units[k]
        inside = (device >= start) & (device < start + units)
        leader = jnp.where(inside, start, leader)
        span = jnp.where(inside, units, span)
        pad = jnp.where(inside, seq_pad[k], pad)
        start = start + units
    return device - leader, span, pad


def key_counts(position, span, picks):
    blocks = lax.broadcasted_iota(jnp.int32, (1, 1, SPAN * BLK_DEV), 2)
    query = position * BLK_DEV + lax.broadcasted_iota(jnp.int32, (BLK_DEV, 1, 1), 0)
    total = span * BLK_DEV
    count = jnp.zeros((BLK_DEV, picks.shape[1], SPAN * BLK_DEV), F32)
    for wanted in (query - 1, query, query + 1, 0, total - 1):
        count = count + (blocks == wanted).astype(F32)
    chosen = picks % total
    for r in range(picks.shape[2]):
        count = count + (blocks == chosen[:, :, r : r + 1]).astype(F32)
    return jnp.where((query == 0) | (query == total - 1), 1.0, count)


def local_general(
    tokens, w_qkv, w_out, ln1_gain, ln1_bias, ln2_gain, ln2_bias, w_up, up_bias, w_down, down_bias,
    seq_units, seq_pad, rand_picks, cotangent,
):
    tok, width = tokens.shape
    heads = w_qkv.shape[2] // HEAD_DIM
    rows = lambda v: lax.all_gather(v, "seq", axis=0, tiled=True)
    cols = lambda v: lax.all_gather(v, "seq", axis=1, tiled=True)
    vectors = jnp.stack([ln1_gain, ln1_bias, ln2_gain, ln2_bias, down_bias], axis=0)
    gain_one, shift_one, gain_two, shift_two, down_shift = [
        v[None].astype(F32) for v in cols(vectors)
    ]
    qkv = rows(w_qkv)
    out_w, up_w, down_w = cols(w_out), rows(w_up), cols(w_down)
    position, span, pad = sequence_place(seq_units, seq_pad)
    root = SPAN - 1 - position
    inputs = tokens.astype(F32)
    xhat_one, inv_one = norm_parts(inputs)
    normed = (xhat_one * gain_one + shift_one).astype(BF16)
    triple = jnp.einsum("td,dcf->tcf", normed, qkv, preferred_element_type=F32).astype(BF16)
    own = jnp.stack([triple[:, 1], triple[:, 2]], axis=0)
    pieces = [own if o == 0 else shifted(own, "seq", -o) for o in range(1 - SPAN, SPAN)]
    nearby = jnp.stack(pieces, axis=0)
    window = lax.dynamic_slice_in_dim(nearby, root, SPAN, 0)
    split = lambda v: v.reshape(v.shape[0], heads, HEAD_DIM)
    keys = split(window[:, 0].reshape(SPAN * tok, -1))
    values = split(window[:, 1].reshape(SPAN * tok, -1))
    queries = split(triple[:, 0])
    scaling = HEAD_DIM ** (-0.5)
    live = jnp.arange(SPAN * tok, dtype=jnp.int32) < span * tok - pad
    count = jnp.repeat(key_counts(position, span, rand_picks), BLK, axis=2)
    count = jnp.where(live[None, None], count, 0.0)
    count = jnp.transpose(jnp.repeat(count, BLK, axis=0), (1, 0, 2))
    logits = jnp.einsum("qhd,khd->hqk", queries, keys, preferred_element_type=F32) * scaling
    logits = jnp.where(count > 0, logits, NEGATIVE)
    grown = jnp.exp(logits - jnp.max(logits, axis=-1, keepdims=True)) * count
    chances = grown / jnp.sum(grown, axis=-1, keepdims=True)
    chances_low = chances.astype(BF16)
    attended = jnp.einsum("hqk,khd->qhd", chances_low, values, preferred_element_type=F32)
    attended = attended.astype(BF16).reshape(tok, heads * HEAD_DIM)
    middle = inputs + lax.psum(dot(attended, out_w, ((1,), (0,))), "head")
    xhat_two, inv_two = norm_parts(middle)
    normed_two = (xhat_two * gain_two + shift_two).astype(BF16)
    pre_act = dot(normed_two, up_w, ((1,), (0,))) + up_bias.astype(F32)[None]
    hidden, pull = jax.vjp(lambda v: jax.nn.gelu(v, approximate=True), pre_act)
    hidden = hidden.astype(BF16)
    ffn = lax.psum(dot(hidden, down_w, ((1,), (0,))).astype(BF16), "head").astype(F32)
    output = (middle + ffn + down_shift).astype(BF16)
    grad_out = cotangent.astype(F32)
    grad_w_down = dot(hidden, cotangent, ((0,), (0,)))
    grad_pre = pull(dot(cotangent, down_w, ((1,), (1,))))[0].astype(BF16)
    grad_w_up = dot(normed_two, grad_pre, ((0,), (0,)))
    grad_up_bias = lax.psum(jnp.sum(grad_pre.astype(F32), axis=0), "seq")
    grad_two = lax.psum(dot(grad_pre, up_w, ((1,), (1,))), "head")
    grad_middle = grad_out + norm_backward(xhat_two, inv_two, grad_two * gain_two)
    grad_branch = grad_middle.astype(BF16)
    grad_w_out = dot(attended, grad_branch, ((0,), (0,)))
    grad_att = split(dot(grad_branch, out_w, ((1,), (1,))).astype(BF16))
    grad_prob = jnp.einsum("qhd,khd->hqk", grad_att, values, preferred_element_type=F32)
    inner = jnp.sum(chances * grad_prob, axis=-1, keepdims=True)
    grad_logit = (chances * (grad_prob - inner)).astype(BF16)
    dq = scaling * jnp.einsum("hqk,khd->qhd", grad_logit, keys, preferred_element_type=F32)
    dk = scaling * jnp.einsum("hqk,qhd->khd", grad_logit, queries, preferred_element_type=F32)
    dv = jnp.einsum("hqk,qhd->khd", chances_low, grad_att, preferred_element_type=F32)
    part = jnp.stack([dk.reshape(SPAN, tok, -1), dv.reshape(SPAN, tok, -1)], axis=1)
    near = jnp.zeros((2 * SPAN - 1,) + part.shape[1:], F32)
    near = lax.dynamic_update_slice_in_dim(near, part, root, 0)
    owned = near[SPAN - 1]
    for offset in range(1 - SPAN, SPAN):
        if offset:
            owned = owned + shifted(near[offset + SPAN - 1], "seq", offset)
    owned = owned.astype(BF16)
    grad_triple = jnp.stack([dq.reshape(tok, -1).astype(BF16), owned[0], owned[1]], axis=1)
    grad_w_qkv = jnp.einsum("td,tcf->dcf", normed, grad_triple, preferred_element_type=F32)
    grad_one = lax.psum(
        jnp.einsum("tcf,dcf->td", grad_triple, qkv, preferred_element_type=F32), "head"
    )
    x_grad = grad_middle + norm_backward(xhat_one, inv_one, grad_one * gain_one)
    sums = jnp.stack(
        [
            jnp.sum(grad_one * xhat_one, axis=0), jnp.sum(grad_one, axis=0),
            jnp.sum(grad_two * xhat_two, axis=0), jnp.sum(grad_two, axis=0),
            jnp.sum(grad_out, axis=0),
        ],
        axis=0,
    )
    scatter = lambda v, d: lax.psum_scatter(v, "seq", scatter_dimension=d, tiled=True)
    sums = scatter(sums, 1)
    return (
        output, x_grad, scatter(grad_w_qkv, 0), scatter(grad_w_out, 1), sums[0], sums[1], sums[2],
        sums[3], scatter(grad_w_up, 0), grad_up_bias, scatter(grad_w_down, 1), sums[4],
    )


MESH = pl.DeviceIdType.MESH
SEQ = 8
HEAD = 4
LINE = 4
NEAR = 2 * SPAN - 1
QKV_KV, QKV_Q, OUT, UP, DOWN = range(5)
VMEM_BYTES = 60 * 1024 * 1024
PIECES = 2


def al(value, multiple):
    return pl.multiple_of(value, multiple)


def fused_kernel(names, *refs):
    r = types.SimpleNamespace(**dict(zip(names, refs)))
    s, h = lax.axis_index("seq"), lax.axis_index("head")
    z, y, x, c = lax.div(s, 2), lax.rem(s, 2), lax.div(h, 2), lax.rem(h, 2)
    e = lax.rem(z, 2)
    pair_z = z + 1 - 2 * e
    mate = z * 2 + 1 - y
    pair = pair_z * 2 + y
    twin = x * 2 + 1 - c
    across = (1 - x) * 2 + c
    tokens, width = r.tok.shape
    quarter = tokens // HEAD
    head_w = r.qs.shape[1]
    rows = r.wq.shape[1]
    half = r.wu_all.shape[1]
    sent = []

    def copy(src, dst, ss, rs, **where):
        return pltpu.make_async_remote_copy(
            src_ref=src, dst_ref=dst, send_sem=ss, recv_sem=rs, device_id=where,
            device_id_type=MESH,
        )

    def when(cond, then):
        if cond is None:
            then()
        else:
            pl.when(cond)(lambda: then())

    def send(cond, *args, **where):
        one = copy(*args, **where)
        when(cond, one.start)
        sent.append((cond, one))

    def arrived(cond, dst, rs, like=None):
        when(cond, copy(dst if like is None else like, dst, r.v_ss.at[0], rs, seq=mate).wait_recv)

    barrier = pltpu.get_barrier_semaphore()
    greeted = [{"seq": lax.rem(s + d, SEQ)} for d in range(1, SEQ)]
    greeted += [{"head": lax.rem(h + d, HEAD)} for d in range(1, HEAD)]
    greeted += [{"seq": pair, "head": across}]
    for where in greeted:
        pl.semaphore_signal(barrier, inc=1, device_id=where, device_id_type=MESH)
    for k, ref in enumerate((r.g1, r.b1, r.g2, r.b2, r.b3)):
        r.vec[k : k + 1, :] = ref[...].reshape(1, rows).astype(F32)
    r.vec[5:8, :] = jnp.zeros((3, rows), F32)
    r.upb_f[...] = r.upb[...].reshape(1, 2 * half).astype(F32)
    pl.semaphore_wait(barrier, len(greeted))

    def cols(o, size):
        return pl.ds(al(o * size, size), size)

    relay_slot = [
        lambda o: r.wq_all.at[1:3, cols(o, rows), :],
        lambda o: r.wq_all.at[0, cols(o, rows), :],
        lambda o: r.wo_all.at[:, cols(o, rows)],
    ]
    relay_src = [r.wq.at[1:3], r.wq.at[0], r.wo]

    def relay_start(w):
        src, dst, rs = relay_src[w], relay_slot[w](s), r.g_rs.at[w, s]
        send(z < LINE - 1, src, dst, r.g_ss.at[w, 0], rs, seq=s + 2)
        send(z > 0, src, dst, r.g_ss.at[w, 4], rs, seq=s - 2)
        send(None, src, dst, r.g_ss.at[w, 8], rs, seq=mate)

    def relay_round(w, k):
        for sign, first, third in ((-1, 0, 8 + k), (1, 4, 11 + k)):
            from_z = z + sign * k
            there = (from_z >= 0) & (from_z < LINE)
            o = jnp.clip(from_z, 0, LINE - 1) * 2 + y
            ref, rs = relay_slot[w](o), r.g_rs.at[w, o]
            arrived(there, ref, rs)
            onward = (z < LINE - 1) if sign < 0 else (z > 0)
            send(there & onward, ref, ref, r.g_ss.at[w, first + k], rs, seq=s - 2 * sign)
            send(there, ref, ref, r.g_ss.at[w, third], rs, seq=mate)

    def relay_finish(w):
        for d in range(LINE):
            o = lax.rem(z + d, LINE) * 2 + 1 - y
            arrived(None, relay_slot[w](o), r.g_rs.at[w, o])

    low, high = z > 0, z < LINE - 1
    from_mate = 4 - 2 * y

    def token_rows(slot, head):
        return r.nall.at[slot, cols(head, quarter), :]

    def token_send(cond, slot, back, k, to):
        send(cond, token_rows(slot, h), token_rows(back, h), r.t_ns.at[k], r.t_rs.at[back, h], seq=to)

    def token_share(cond, slot):
        ref = token_rows(slot, h)
        arrived(cond, ref, r.t_rs.at[slot, h])
        send(cond, ref, ref, r.t_ss.at[slot, 0], r.t_rs.at[slot, h], head=across)
        send(cond, ref, ref, r.t_ss.at[slot, 1], r.t_rs.at[slot, h], head=twin)

    def token_pass(cond, slot):
        ref = token_rows(slot, across)
        arrived(cond, ref, r.t_rs.at[slot, across])
        send(cond, ref, ref, r.t_ss.at[slot, 2], r.t_rs.at[slot, across], head=twin)

    def token_ready(cond, slot):
        arrived(cond, token_rows(slot, twin), r.t_rs.at[slot, twin])
        other = (1 - x) * 2 + 1 - c
        arrived(cond, token_rows(slot, other), r.t_rs.at[slot, other])

    far_in = jnp.where(y == 0, z >= 2, z <= 1)
    far_slot = 6 * y
    slots = (
        (None, from_mate), (low, 1), (high, 5), (low, 2 - 2 * y), (high, 6 - 2 * y),
        (far_in, far_slot),
    )
    for d in range(1, SEQ):
        send(
            None, r.vec, r.gains.at[:, cols(s, rows)], r.v_ss.at[d - 1], r.v_rs.at[s],
            seq=lax.rem(s + d, SEQ),
        )
    relay_start(0)
    r.gains[:, cols(s, rows)] = r.vec[...]
    for k in range(NEAR):
        other = s + k - (SPAN - 1)

        @pl.when((other < 0) | (other >= SEQ))
        def _():
            r.nall[k] = jnp.zeros(r.nall.shape[1:], BF16)

    for k, cond in enumerate((low & high, high, low, high, low)):

        @pl.when(jnp.logical_not(cond))
        def _():
            r.dkv_recv[k] = jnp.zeros(r.dkv_recv.shape[1:], BF16)

    for d in range(1, SEQ):
        o = lax.rem(s + d, SEQ)
        arrived(None, r.gains.at[:, cols(o, rows)], r.v_rs.at[o], r.vec)

    def normalise(q):
        xhat, _ = norm_parts(r.tok[q, :].astype(F32))
        r.nall[SPAN - 1, q, :] = (xhat * r.gains[0:1, :] + r.gains[1:2, :]).astype(BF16)

    normalise(cols(h, quarter))
    token_send(None, SPAN - 1, 2 + 2 * y, 0, mate)
    token_send(high, SPAN - 1, 1, 1, s + 2)
    token_send(low, SPAN - 1, 5, 2, s - 2)
    for d in range(1, HEAD):
        normalise(cols(lax.rem(h + d, HEAD), quarter))
    token_share(*slots[0])
    token_send(high, from_mate, 2 - 2 * y, 3, s + 2)
    token_send(low, from_mate, 6 - 2 * y, 4, s - 2)
    relay_round(0, 1)
    token_share(*slots[1])
    token_share(*slots[2])
    r.wq_all[:, cols(s, rows), :] = r.wq[...]
    r.wo_all[:, cols(s, rows)] = r.wo[...]
    token_share(*slots[3])
    token_share(*slots[4])
    token_send((y == 0) & low & high, 2, 0, 5, s + 2)
    token_send((y == 1) & low & high, 4, 6, 5, s - 2)
    relay_round(0, 2)
    relay_start(1)
    relay_round(0, 3)
    token_share(*slots[5])
    for cond, slot in slots[:3]:
        token_pass(cond, slot)
    relay_round(1, 1)
    relay_start(2)

    start, leader, span, pad = 0, 0, 0, 0
    for k in range(r.units.shape[0]):
        here = r.units[k]
        inside = (s >= start) & (s < start + here)
        leader = jnp.where(inside, start, leader)
        span = jnp.where(inside, here, span)
        pad = jnp.where(inside, r.pads[k], pad)
        start = start + here
    position = s - leader
    root = jnp.clip(SPAN - 1 - position, 0, SPAN - 1)
    total = span * BLK_DEV
    live = span * tokens - pad

    columns = lax.broadcasted_iota(jnp.int32, (1, SPAN * tokens), 1)
    usable = columns < live
    blocks = lax.div(columns, BLK)
    for hh in range(HEAD):
        for b in range(BLK_DEV):
            query = position * BLK_DEV + b
            count = jnp.zeros((1, SPAN * tokens), F32)
            for wanted in (query - 1, query, query + 1, 0, total - 1):
                count = count + jnp.where(blocks == wanted, 1.0, 0.0)
            for k in range(r.picks.shape[0]):
                raw = r.picks[k, b, hh]
                chosen = lax.rem(raw, BLK_DEV)
                for k_units in range(2, SPAN + 1):
                    chosen = jnp.where(span == k_units, lax.rem(raw, BLK_DEV * k_units), chosen)
                count = count + jnp.where(blocks == chosen, 1.0, 0.0)
            count = jnp.where((query == 0) | (query == total - 1), 1.0, count)
            held = usable & (count > 0)
            bias = jnp.log(jnp.maximum(count, 1.0))
            r.bias[hh, b : b + 1, :] = jnp.where(held, bias, NEGATIVE)

    ffn_src = {
        UP: lambda k: r.wu.at[:, cols(k, half)],
        DOWN: lambda k: r.wd.at[cols(k, half), :],
    }
    ffn_slot = {
        UP: lambda o: r.wu_all.at[cols(o, rows), :],
        DOWN: lambda o: r.wd_all.at[:, cols(o, rows)],
    }

    def ffn_start(w):
        i = w - UP
        for d in range(1, LINE):
            to = lax.rem(z + d, LINE)
            send(
                None, ffn_src[w](lax.rem(to, 2)), ffn_slot[w](s), r.f_ss.at[i, d - 1],
                r.f_rs.at[i, s], seq=to * 2 + y,
            )
        send(
            None, ffn_src[w](e), ffn_slot[w](s), r.f_ss.at[i, 3], r.f_rs.at[i, s], seq=mate
        )

    def by_distance(k):
        up = k + jnp.where(z <= k, 1, 0)
        down = k + jnp.where(LINE - 1 - z <= k, 1, 0)
        return jnp.where(z < LINE // 2, up, LINE - 1 - down)

    def ffn_forward(w, ks=(0, 1, 2)):
        i = w - UP
        for k in ks:
            o = by_distance(k) * 2 + y
            ref = ffn_slot[w](o)
            arrived(None, ref, r.f_rs.at[i, o])
            send(None, ref, ref, r.f_ss.at[i, 4 + k], r.f_rs.at[i, o], seq=mate)

    def ffn_finish(w):
        for d in range(LINE):
            o = lax.rem(z + d, LINE) * 2 + 1 - y
            arrived(None, ffn_slot[w](o), r.f_rs.at[w - UP, o])

    relay_round(1, 2)
    relay_round(2, 1)
    relay_round(1, 3)
    relay_round(2, 2)
    ffn_start(UP)
    for cond, slot in slots[3:]:
        token_pass(cond, slot)
    relay_round(2, 3)
    for ref, src in ((ffn_slot[UP](s), ffn_src[UP](e)), (ffn_slot[DOWN](s), ffn_src[DOWN](e))):
        ref[...] = src[...]

    ffn_start(DOWN)
    for cond, slot in slots:
        token_ready(cond, slot)
    relay_finish(0)
    scaling = HEAD_DIM ** (-0.5)
    for j in range(SPAN):
        q = pl.ds(j * tokens, tokens)
        rows_in = r.nall[root + j]
        r.kwin[q, :] = dot(rows_in, r.wq_all[1], ((1,), (0,))).astype(BF16)
        r.vwin[q, :] = dot(rows_in, r.wq_all[2], ((1,), (0,))).astype(BF16)
    relay_finish(1)
    part = dot(r.nall[SPAN - 1], r.wq_all[0], ((1,), (0,)))
    r.qs[...] = (part.astype(BF16).astype(F32) * scaling).astype(BF16)
    r.cotx[cols(e, tokens), :] = r.cot[...]
    beyond = (1 - x) * 2 + 1 - c

    def block_rows(unit, head):
        return pl.ds(al(unit * tokens + head * quarter, quarter), quarter)

    def cot_rows(unit, head):
        return r.cotx.at[block_rows(unit, head), :]

    send(
        None, r.cot.at[cols(h, quarter), :], cot_rows(e, h), r.c_ss.at[0], r.c_rs.at[h], seq=pair
    )

    def cot_share():
        ref = cot_rows(1 - e, h)
        arrived(None, ref, r.c_rs.at[h])
        send(None, ref, ref, r.c_ss.at[1], r.c_rs.at[h], head=across)
        send(None, ref, ref, r.c_ss.at[2], r.c_rs.at[h], head=twin)

    def cot_pass():
        ref = cot_rows(1 - e, across)
        arrived(None, ref, r.c_rs.at[across])
        send(None, ref, ref, r.c_ss.at[3], r.c_rs.at[across], head=twin)

    lanes = lax.div(lax.broadcasted_iota(jnp.int32, (1, head_w), 1), HEAD_DIM)
    none = jnp.zeros((), BF16)
    r.att[...] = jnp.zeros(r.att.shape, F32)

    def attend(hh, carry):
        mine = lanes == hh
        query = jnp.where(mine, r.qs[...], none)
        for j in range(SPAN):
            k = pl.ds(j * tokens, tokens)
            r.lg[:, k] = dot(query, r.kwin[k, :], ((1,), (1,)))
        for b in range(BLK_DEV):
            q = pl.ds(b * BLK, BLK)
            logits = r.lg[q, :] + r.bias[hh, b : b + 1, :]
            grown = jnp.exp(logits - jnp.max(logits, axis=-1, keepdims=True))
            scale = 1.0 / jnp.sum(grown, axis=-1, keepdims=True)
            r.prob[hh, q, :] = (grown * scale).astype(BF16)
        part = dot(r.prob[hh], r.vwin[...], ((1,), (0,)))
        r.att[...] += jnp.where(mine, part, 0.0)
        return carry

    lax.fori_loop(0, HEAD // 2, attend, 0)
    ffn_forward(UP, (0,))
    lax.fori_loop(HEAD // 2, HEAD, attend, 0)
    ffn_forward(UP, (1,))
    r.att_low[...] = r.att[...].astype(BF16)
    relay_finish(2)

    def rows_of(k):
        return cols(k, quarter)

    def reduce_start(op):
        for v in range(2):
            r.q1_send[op, v] = r.sum_f[rows_of(v * 2 + 1 - c), :].astype(BF16)
        send(None, r.q1_send.at[op], r.q1_recv.at[op], r.q1_ss.at[op], r.q1_rs.at[op], head=twin)

    def reduce_middle(op):
        arrived(None, r.q1_recv.at[op], r.q1_rs.at[op])
        block = r.sum_f[rows_of(across), :] + r.q1_recv[op, 1 - x].astype(F32)
        r.q2_send[op] = block.astype(BF16)
        send(None, r.q2_send.at[op], r.q2_recv.at[op], r.q2_ss.at[op], r.q2_rs.at[op], head=across)
        r.q_own[op] = r.sum_f[rows_of(h), :] + r.q1_recv[op, x].astype(F32)

    def reduce_finish(op):
        arrived(None, r.q2_recv.at[op], r.q2_rs.at[op])
        return r.q_own[op] + r.q2_recv[op].astype(F32)

    def spread_start(op, whole, value):
        whole[rows_of(h), :] = value
        ref = whole.at[rows_of(h), :]
        send(None, ref, ref, r.ag_ss.at[op, 0], r.ag_rs.at[op, h], head=across)
        send(None, ref, ref, r.ag_ss.at[op, 1], r.ag_rs.at[op, h], head=twin)

    def spread_pass(op, whole):
        ref = whole.at[rows_of(across), :]
        arrived(None, ref, r.ag_rs.at[op, across])
        send(None, ref, ref, r.ag_ss.at[op, 2], r.ag_rs.at[op, across], head=twin)

    def spread_finish(op, whole):
        for o in (twin, beyond):
            arrived(None, whole.at[rows_of(o), :], r.ag_rs.at[op, o])

    pair_sum = [r.sum_f, r.sum_g]

    def pair_start(op):
        for u in range(2):
            for v in range(2):
                block = pair_sum[op][block_rows(u, v * 2 + 1 - c), :]
                r.p1_send[op, u * 2 + v] = block.astype(BF16)
        send(None, r.p1_send.at[op], r.p1_recv.at[op], r.p1_ss.at[op], r.p1_rs.at[op], head=twin)

    def pair_middle(op):
        arrived(None, r.p1_recv.at[op], r.p1_rs.at[op])
        for du, dv in ((1, 1), (1, 0), (0, 1), (0, 0)):
            u, v = lax.rem(e + du, 2), lax.rem(x + dv, 2)
            block = pair_sum[op][block_rows(u, v * 2 + c), :] + r.p1_recv[op, u * 2 + v].astype(F32)
            if du or dv:
                k = u * 2 + v
                r.p2_send[op, k] = block.astype(BF16)
                send(
                    None, r.p2_send.at[op, k], r.p2_recv.at[op, e * 2 + x], r.p2_ss.at[op, k],
                    r.p2_rs.at[op, e * 2 + x], seq=pair if du else s, head=across if dv else h,
                )
            else:
                r.p_own[op] = block

    def pair_x(op):
        arrived(None, r.p1_recv.at[op], r.p1_rs.at[op])
        for du in (1, 0):
            u = lax.rem(e + du, 2)
            k = u * 2 + 1 - x
            block = pair_sum[op][block_rows(u, across), :] + r.p1_recv[op, k].astype(F32)
            r.p2_send[op, k] = block.astype(BF16)
            send(
                None, r.p2_send.at[op, k], r.p2_recv.at[op, u], r.p2_ss.at[op, k],
                r.p2_rs.at[op, u], head=across,
            )

    def pair_over(op):
        for du in (1, 0):
            u = lax.rem(e + du, 2)
            arrived(None, r.p2_recv.at[op, u], r.p2_rs.at[op, u])
            block = pair_sum[op][block_rows(u, h), :] + r.p1_recv[op, u * 2 + x].astype(F32)
            block = block + r.p2_recv[op, u].astype(F32)
            if du:
                k = u * 2 + x
                r.p2_send[op, k] = block.astype(BF16)
                send(
                    None, r.p2_send.at[op, k], r.p2_recv.at[op, 2], r.p2_ss.at[op, k],
                    r.p2_rs.at[op, 2], seq=pair,
                )
            else:
                r.p_own[op] = block

    def pair_end(op):
        arrived(None, r.p2_recv.at[op, 2], r.p2_rs.at[op, 2])
        return r.p_own[op] + r.p2_recv[op, 2].astype(F32)

    def pair_finish(op):
        result = r.p_own[op]
        for du, dv in ((0, 1), (1, 0), (1, 1)):
            k = lax.rem(e + du, 2) * 2 + lax.rem(x + dv, 2)
            arrived(None, r.p2_recv.at[op, k], r.p2_rs.at[op, k])
            result = result + r.p2_recv[op, k].astype(F32)
        return result

    r.sum_f[:tokens, :] = dot(r.att_low[...], r.wo_all[...], ((1,), (0,)))
    reduce_start(0)
    reduce_middle(0)
    ffn_forward(UP, (2,))
    ffn_forward(DOWN, (0,))
    middle = r.tok[rows_of(h), :].astype(F32) + reduce_finish(0)
    r.mid_own[...] = middle
    xhat, _ = norm_parts(middle)

    def n2_rows(unit, head):
        return r.n2x.at[block_rows(unit, head), :]

    r.n2x[block_rows(e, h), :] = (xhat * r.gains[2:3, :] + r.gains[3:4, :]).astype(BF16)
    mine, tag = n2_rows(e, h), e * 4 + h
    send(None, mine, mine, r.n2_ss.at[0], r.n2_rs.at[tag], seq=pair)
    send(None, mine, mine, r.n2_ss.at[1], r.n2_rs.at[tag], head=across)
    send(None, mine, mine, r.n2_ss.at[2], r.n2_rs.at[tag], head=twin)
    cot_share()
    ffn_forward(DOWN, (1,))
    for k, (unit, head) in enumerate(((e, across), (1 - e, h), (1 - e, across))):
        ref, tag = n2_rows(unit, head), unit * 4 + head
        arrived(None, ref, r.n2_rs.at[tag])
        if k == 1:
            send(None, ref, ref, r.n2_ss.at[6], r.n2_rs.at[tag], head=across)
        send(None, ref, ref, r.n2_ss.at[3 + k], r.n2_rs.at[tag], head=twin)
    cot_pass()
    ffn_forward(DOWN, (2,))
    ffn_finish(UP)
    for unit in (e, 1 - e):
        for head in (x * 2 + 1 - c, (1 - x) * 2 + 1 - c):
            arrived(None, n2_rows(unit, head), r.n2_rs.at[unit * 4 + head])

    root_c = (2.0 / 3.141592653589793) ** 0.5
    r.up_send[half // 128 :, :] = jnp.zeros((8 - half // 128, 128), F32)
    for j in range(half // 256):
        f = pl.ds(j * 256, 256)
        bias = r.upb_f[:, pl.ds(al(e * half + j * 256, 256), 256)]
        v = dot(r.n2x[...], r.wu_all[:, f], ((1,), (0,))) + bias
        t = jnp.tanh(root_c * (v + 0.044715 * (v * v * v)))
        r.hid[:, f] = (0.5 * v * (1.0 + t)).astype(BF16)
        slope = 0.5 * (1.0 + t) + 0.5 * v * (1.0 - t * t) * (root_c * (1.0 + 0.134145 * v * v))
        r.slope[:, f] = slope
    ffn_finish(DOWN)
    for head in (twin, beyond):
        arrived(None, cot_rows(1 - e, head), r.c_rs.at[head])
    for j in range(half // 256):
        f = pl.ds(j * 256, 256)
        low_p = (dot(r.cotx[...], r.wd_all[f, :], ((1,), (1,))) * r.slope[:, f]).astype(BF16)
        r.gp[:, f] = low_p
        sums = jnp.sum(low_p.astype(F32), axis=0, keepdims=True)
        r.up_send[2 * j : 2 * j + 1, :] = sums[:, :128]
        r.up_send[2 * j + 1 : 2 * j + 2, :] = sums[:, 128:]

    grad_send = {QKV_KV: r.skv, QKV_Q: r.sq, OUT: r.so, UP: r.su, DOWN: r.sd}
    grad_arrive = {QKV_KV: r.akv, QKV_Q: r.aq, OUT: r.ao, UP: r.au, DOWN: r.ad}
    grad_again = {QKV_KV: r.bkv, QKV_Q: r.bq, OUT: r.bo, UP: r.bu, DOWN: r.bd}
    grad_final = {QKV_KV: r.rkv, QKV_Q: r.rq, OUT: r.ro, UP: r.ru, DOWN: r.rd}

    def tile_of(i):
        return lax.rem(z + 1 + i, LINE)

    def grad_cross(w, zz):
        send(
            None, grad_send[w].at[zz * 2 + 1 - y], grad_arrive[w].at[zz], r.ra_ss.at[w, zz],
            r.ra_rs.at[w, zz], seq=mate,
        )

    def grad_along(w, ks=(1, 2, 3)):
        for d in ks:
            zz = lax.rem(z + d, LINE)
            arrived(None, grad_arrive[w].at[zz], r.ra_rs.at[w, zz])
            both = grad_send[w][zz * 2 + y].astype(F32) + grad_arrive[w][zz].astype(F32)
            grad_again[w][zz] = both.astype(BF16)
            send(
                None, grad_again[w].at[zz], grad_final[w].at[z], r.rb_ss.at[w, zz],
                r.rb_rs.at[w, z], seq=zz * 2 + y,
            )

    outer, inner = (z == 0) | (z == LINE - 1), (z == 1) | (z == LINE - 2)
    far_half = 2 - 2 * lax.div(z, 2)
    far_inner = 2 - lax.div(z, 2)
    grad_hold = {QKV_KV: r.hkv, QKV_Q: r.hq, OUT: r.ho}

    def tile_far(i):
        return (far_half, far_half + 1, pair_z, z)[i]

    def grad_first(w):
        for k in range(3):
            zz = tile_far(k)
            arrived(None, grad_arrive[w].at[zz], r.ra_rs.at[w, zz])
            both = grad_send[w][zz * 2 + y].astype(F32) + grad_arrive[w][zz].astype(F32)
            grad_again[w][zz] = both.astype(BF16)
            if k < 2:
                send(
                    outer, grad_again[w].at[zz], grad_hold[w].at[k], r.rh_ss.at[w, k],
                    r.rh_rs.at[w, k], seq=pair,
                )
            else:
                send(
                    None, grad_again[w].at[zz], grad_final[w].at[z], r.rb_ss.at[w, zz],
                    r.rb_rs.at[w, z], seq=pair,
                )

    def grad_second(w):
        for k in range(2):
            zz = tile_far(k)
            arrived(inner, grad_hold[w].at[k], r.rh_rs.at[w, k])

            @pl.when(inner)
            def _():
                both = grad_again[w][zz].astype(F32) + grad_hold[w][k].astype(F32)
                grad_again[w][zz] = both.astype(BF16)

            send(
                inner, grad_again[w].at[zz], grad_final[w].at[z], r.rb_ss.at[w, zz],
                r.rb_rs.at[w, z], seq=zz * 2 + y,
            )

    def grad_own(w):
        arrived(None, grad_arrive[w].at[z], r.ra_rs.at[w, z])
        return grad_send[w][z * 2 + y].astype(F32) + grad_arrive[w][z].astype(F32)

    def grad_from(w, o):
        arrived(None, grad_final[w].at[o], r.rb_rs.at[w, o])
        return grad_final[w][o].astype(F32)

    def grad_sum(w):
        return grad_own(w) + grad_from(w, pair_z) + grad_from(w, far_inner)

    def grad_halves(w):
        same = grad_own(w) + grad_from(w, lax.rem(z + 2, LINE))
        other = grad_from(w, lax.rem(z + 1, LINE)) + grad_from(w, lax.rem(z + 3, LINE))
        return same, other

    def down_step(i):
        zz = tile_of(i)
        part = dot(r.hid[...], r.cotx[:, cols(zz, 256)], ((0,), (0,))).astype(BF16)
        r.sd[zz * 2] = part[:, :rows]
        r.sd[zz * 2 + 1] = part[:, rows:]
        grad_cross(DOWN, zz)

    def up_step(i):
        zz = tile_of(i)
        part = dot(r.n2x[:, cols(zz, 256)], r.gp[...], ((0,), (0,))).astype(BF16)
        r.su[zz * 2] = part[:rows]
        r.su[zz * 2 + 1] = part[rows:]
        grad_cross(UP, zz)

    down_step(0)
    r.sum_f[...] = dot(r.gp[...], r.wu_all[...], ((1,), (1,)))
    pair_start(0)
    down_step(1)
    pair_middle(0)
    r.sum_g[...] = dot(r.hid[...], r.wd_all[...], ((1,), (0,)))
    pair_start(1)
    down_step(2)
    down_step(3)
    pair_x(1)
    for i in range(LINE):
        up_step(i)
    for d in range(1, SEQ):
        send(
            None, r.up_send, r.up_recv.at[s], r.up_ss.at[d], r.up_rs.at[s],
            seq=lax.rem(s + d, SEQ),
        )

    grad_along(DOWN, (1,))
    grad_two = pair_finish(0)
    xhat, inverse = norm_parts(r.mid_own[...])
    dy = r.cot[rows_of(h), :].astype(F32)
    grad_mid = dy + norm_backward(xhat, inverse, grad_two * r.gains[2:3, :])
    r.gm_own[...] = grad_mid
    spread_start(0, r.gb, grad_mid.astype(BF16))
    r.sm_send[2:3, :] = jnp.sum(grad_two * xhat, axis=0, keepdims=True)
    r.sm_send[3:4, :] = jnp.sum(grad_two, axis=0, keepdims=True)
    r.sm_send[4:5, :] = jnp.sum(dy, axis=0, keepdims=True)
    r.sm_send[5:8, :] = jnp.zeros((3, width), F32)

    grad_along(DOWN, (2, 3))
    pair_over(1)
    spread_pass(0, r.gb)
    spread_finish(0, r.gb)
    r.gatt[...] = dot(r.gb[...], r.wo_all[...], ((1,), (1,))).astype(BF16)
    for i in range(LINE):
        zz = tile_far(i)
        part = dot(r.att_low[...], r.gb[:, cols(zz, 256)], ((0,), (0,))).astype(BF16)
        r.so[zz * 2] = part[:, :rows]
        r.so[zz * 2 + 1] = part[:, rows:]
        grad_cross(OUT, zz)
    grad_along(UP, (1, 2))

    r.dq[...] = jnp.zeros(r.dq.shape, F32)
    r.dk[...] = jnp.zeros(r.dk.shape, F32)
    r.dv[...] = jnp.zeros(r.dv.shape, F32)

    def attend_back(hh, carry):
        mine = lanes == hh
        query = jnp.where(mine, r.qs[...], none)
        grad = jnp.where(mine, r.gatt[...], none)
        for j in range(SPAN):
            k = pl.ds(j * tokens, tokens)
            r.lg[:, k] = dot(grad, r.vwin[k, :], ((1,), (1,)))
        for b in range(BLK_DEV):
            q = pl.ds(b * BLK, BLK)
            chance, grown = r.prob[hh, q, :].astype(F32), r.lg[q, :]
            inner = jnp.sum(chance * grown, axis=-1, keepdims=True)
            r.ds[hh, q, :] = (chance * (grown - inner)).astype(BF16)
        for j in range(SPAN):
            k = pl.ds(j * tokens, tokens)
            r.dk[k, :] += dot(r.ds[hh, :, k], query, ((0,), (0,)))
            r.dv[k, :] += dot(r.prob[hh, :, k], grad, ((0,), (0,)))
        return carry

    lax.fori_loop(0, HEAD, attend_back, 0)
    for k in range(2 * (SPAN - 1) + SPAN):
        j = k - (SPAN - 1)
        if 0 <= j < SPAN:
            q = pl.ds(j * tokens, tokens)
            r.dkv_pad[k, 0] = r.dk[q, :].astype(BF16)
            r.dkv_pad[k, 1] = r.dv[q, :].astype(BF16)
        else:
            r.dkv_pad[k] = jnp.zeros(r.dkv_pad.shape[1:], BF16)
    for k in range(NEAR):
        r.dkv_send[k] = r.dkv_pad[k + SPAN - 1 - root]

    def grad_hop(cond, slot, into, k, to, v):
        send(
            cond, r.dkv_send.at[slot, v], r.dkv_recv.at[into, v], r.dkv_ss.at[k, v],
            r.dkv_rs.at[into, v], seq=to,
        )

    def add_to(v, slot, *froms):
        both = r.dkv_send[slot, v].astype(F32)
        for k in froms:
            both = both + r.dkv_recv[k, v].astype(F32)
        r.dkv_send[slot, v] = both.astype(BF16)

    def grad_wait(cond, into, v):
        arrived(cond, r.dkv_recv.at[into, v], r.dkv_rs.at[into, v])

    FAR, ABOVE, BELOW, LINE_ABOVE, LINE_BELOW, MATE = range(6)
    for v in range(2):
        grad_hop((y == 0) & (z >= 2), 0, FAR, 0, s - 2, v)
        grad_hop((y == 1) & (z <= 1), 6, FAR, 0, s + 2, v)
    for v in range(2):
        grad_hop((y == 0) & high, 6, BELOW, 1, s + 2, v)
        grad_hop((y == 1) & low, 0, ABOVE, 1, s - 2, v)

    def hop_far(v):
        grad_wait(low & high, FAR, v)
        add_to(v, 2 + 2 * y, FAR)
        grad_hop((y == 0) & low, 2, ABOVE, 2, s - 2, v)
        grad_hop((y == 1) & high, 4, BELOW, 2, s + 2, v)

    def hop_line(v):
        grad_hop(low, 1, LINE_ABOVE, 3, s - 2, v)
        grad_hop(high, 5, LINE_BELOW, 4, s + 2, v)

    def hop_mate(v):
        grad_wait(high, ABOVE, v)
        grad_wait(low, BELOW, v)
        add_to(v, from_mate, ABOVE, BELOW)
        grad_hop(None, from_mate, MATE, 5, mate, v)

    def queries_back(hh, carry):
        r.dq[...] += jnp.where(lanes == hh, dot(r.ds[hh], r.kwin[...], ((1,), (0,))), 0.0)
        return carry

    for i in range(LINE):
        zz = tile_far(i)
        for k in range(2):
            part = jnp.zeros((256, head_w), F32)
            for j in range(SPAN):
                part = part + dot(
                    r.nall[root + j, :, cols(zz, 256)], r.dkv_pad[j + SPAN - 1, k], ((0,), (0,))
                )
            part = part.astype(BF16)
            for v in range(2):
                r.skv[zz * 2 + v, k] = part[v * rows : (v + 1) * rows]
        grad_cross(QKV_KV, zz)
        if i == 1:
            hop_far(0)
        if i == 2:
            hop_far(1)
            hop_line(0)
            hop_line(1)
    grad_along(UP, (3,))
    hop_mate(0)
    hop_mate(1)
    grad_first(OUT)
    lax.fori_loop(0, HEAD, queries_back, 0)
    r.gtq[...] = (r.dq[...] * scaling).astype(BF16)
    for i in range(LINE):
        zz = tile_far(i)
        part = dot(r.nall[SPAN - 1, :, cols(zz, 256)], r.gtq[...], ((0,), (0,))).astype(BF16)
        r.sq[zz * 2] = part[:rows]
        r.sq[zz * 2 + 1] = part[rows:]
        grad_cross(QKV_Q, zz)
    grad_second(OUT)
    grad_first(QKV_KV)
    ffn = pair_end(1)
    spread_start(1, r.out_o, (r.mid_own[...] + ffn + r.gains[4:5, :]).astype(BF16))
    for v in range(2):
        grad_wait(high, LINE_ABOVE, v)
        grad_wait(low, LINE_BELOW, v)
        grad_wait(None, MATE, v)
        whole = r.dkv_send[SPAN - 1, v].astype(F32)
        for k in (LINE_ABOVE, LINE_BELOW, MATE):
            whole = whole + r.dkv_recv[k, v].astype(F32)
        r.gtkv[v] = whole.astype(BF16)

    r.sum_f[:tokens, :] = (
        dot(r.gtq[...], r.wq_all[0], ((1,), (1,)))
        + dot(r.gtkv[0], r.wq_all[1], ((1,), (1,)))
        + dot(r.gtkv[1], r.wq_all[2], ((1,), (1,)))
    )
    reduce_start(1)
    reduce_middle(1)
    grad_second(QKV_KV)
    grad_one = reduce_finish(1)
    xhat, inverse = norm_parts(r.tok[rows_of(h), :].astype(F32))
    r.sm_send[0:1, :] = jnp.sum(grad_one * xhat, axis=0, keepdims=True)
    r.sm_send[1:2, :] = jnp.sum(grad_one, axis=0, keepdims=True)
    for d in range(1, SEQ):
        to = lax.rem(s + d, SEQ)
        send(
            None, r.sm_send.at[:, cols(to, rows)], r.sm_recv.at[s], r.sm_ss.at[d], r.sm_rs.at[s],
            seq=to,
        )
    spread_pass(1, r.out_o)
    grad_first(QKV_Q)
    grad_x = r.gm_own[...] + norm_backward(xhat, inverse, grad_one * r.gains[0:1, :])
    spread_start(2, r.xg_o, grad_x.astype(BF16))

    same, other = grad_halves(DOWN)
    r.gd_o[cols(e, half), :] = same
    r.gd_o[cols(1 - e, half), :] = other
    same, other = grad_halves(UP)
    r.gu_o[:, cols(e, half)] = same
    r.gu_o[:, cols(1 - e, half)] = other
    spread_pass(2, r.xg_o)
    grad_second(QKV_Q)
    r.go_o[...] = grad_sum(OUT)

    r.sm_recv[s] = r.sm_send[:, cols(s, rows)]
    r.up_recv[s] = r.up_send[...]
    for d in range(1, SEQ):
        o = lax.rem(s + d, SEQ)
        arrived(None, r.sm_recv.at[o], r.sm_rs.at[o], r.vec)
        arrived(None, r.up_recv.at[o], r.up_rs.at[o])
    part = r.sm_recv[0]
    for o in range(1, SEQ):
        part = part + r.sm_recv[o]
    r.sm_own[...] = part
    for d in range(1, HEAD):
        send(
            None, r.sm_own, r.sm_two.at[h], r.sm2_ss.at[d], r.sm2_rs.at[h],
            head=lax.rem(h + d, HEAD),
        )
    r.sm_two[h] = part
    tall = half // 128
    for u in range(2):
        ups = jnp.zeros((tall, 128), F32)
        for o in range(SEQ):
            if (o // 2) % 2 == u:
                ups = ups + r.up_recv[o, :tall, :]
        r.small_o[8 + u * tall : 8 + (u + 1) * tall, :] = ups
    spread_finish(1, r.out_o)
    spread_finish(2, r.xg_o)
    for d in range(1, HEAD):
        o = lax.rem(h + d, HEAD)
        arrived(None, r.sm_two.at[o], r.sm2_rs.at[o])
    r.small_o[0:8, :] = (r.sm_two[0] + r.sm_two[1]) + (r.sm_two[2] + r.sm_two[3])
    r.gq_o[0] = grad_sum(QKV_Q)
    r.gq_o[1:3] = grad_sum(QKV_KV)

    for cond, one in sent:
        when(cond, one.wait_send)


def local_fused(
    tokens, w_qkv, w_out, ln1_gain, ln1_bias, ln2_gain, ln2_bias, w_up, up_bias, w_down, down_bias,
    seq_units, seq_pad, rand_picks, cotangent,
):
    tok, width = tokens.shape
    rows, _, head_w = w_qkv.shape
    hidden = w_up.shape[1]
    half = hidden // 2
    quarter = tok // HEAD
    keys = SPAN * tok
    smem, vmem = pl.BlockSpec(memory_space=pltpu.SMEM), pl.BlockSpec(memory_space=pltpu.VMEM)
    ins = dict(
        units=seq_units, pads=seq_pad, picks=jnp.transpose(rand_picks, (2, 0, 1)), tok=tokens,
        cot=cotangent, wq=jnp.transpose(w_qkv, (1, 0, 2)), wo=w_out, wu=w_up, wd=w_down,
        g1=ln1_gain, b1=ln1_bias, g2=ln2_gain, b2=ln2_bias, b3=down_bias,
        upb=up_bias,
    )
    outs = dict(
        out_o=((tok, width), BF16), xg_o=((tok, width), BF16), gq_o=((3, rows, head_w), F32),
        go_o=((head_w, rows), F32), gu_o=((rows, hidden), F32), gd_o=((hidden, rows), F32),
        small_o=((16, rows), F32),
    )
    scratch = dict(
        wq_all=((3, width, head_w), BF16), wo_all=((head_w, width), BF16),
        wu_all=((width, half), BF16), wd_all=((half, width), BF16), vec=((8, rows), F32), upb_f=((1, hidden), F32),
        gains=((8, width), F32), nall=((NEAR, tok, width), BF16),
        qs=((tok, head_w), BF16),
        kwin=((keys, head_w), BF16), vwin=((keys, head_w), BF16), lg=((tok, keys), F32),
        prob=((HEAD, tok, keys), BF16), ds=((HEAD, tok, keys), BF16),
        att=((tok, head_w), F32), att_low=((tok, head_w), BF16), n2x=((2 * tok, width), BF16),
        cotx=((2 * tok, width), BF16), hid=((2 * tok, half), BF16), slope=((2 * tok, half), F32), gp=((2 * tok, half), BF16),
        gb=((tok, width), BF16), mid_own=((quarter, width), F32),
        gm_own=((quarter, width), F32), gatt=((tok, head_w), BF16), dq=((tok, head_w), F32),
        dk=((keys, head_w), F32), dv=((keys, head_w), F32),
        dkv_pad=((NEAR + SPAN - 1, 2, tok, head_w), BF16),
        dkv_send=((NEAR, 2, tok, head_w), BF16), dkv_recv=((6, 2, tok, head_w), BF16),
        gtq=((tok, head_w), BF16), gtkv=((2, tok, head_w), BF16),
        q1_send=((2, 2, quarter, width), BF16), q1_recv=((2, 2, quarter, width), BF16),
        q2_send=((2, quarter, width), BF16), q2_recv=((2, quarter, width), BF16),
        q_own=((2, quarter, width), F32),
        sum_f=((2 * tok, width), F32), sum_g=((2 * tok, width), F32), bias=((HEAD, 8, keys), F32),
        p1_send=((2, 4, quarter, width), BF16), p1_recv=((2, 4, quarter, width), BF16),
        p2_send=((2, 4, quarter, width), BF16), p2_recv=((2, 4, quarter, width), BF16),
        p_own=((2, quarter, width), F32), sm_send=((8, width), F32),
        sm_recv=((SEQ, 8, rows), F32), sm_own=((8, rows), F32), sm_two=((HEAD, 8, rows), F32),
        up_send=((8, 128), F32), up_recv=((SEQ, 8, 128), F32),
    )
    shards = dict(
        kv=(2, rows, head_w), q=(rows, head_w), o=(head_w, rows), u=(rows, half), d=(half, rows)
    )
    for lead, count in (("s", SEQ), ("a", LINE), ("b", LINE), ("r", LINE), ("h", 2)):
        for name, shape in shards.items():
            scratch[lead + name] = ((count,) + shape, BF16)
    semaphores = dict(
        g_ss=(3, 16), g_rs=(3, SEQ), f_ss=(2, 7), f_rs=(2, SEQ), v_ss=(7,), v_rs=(SEQ,),
        t_ns=(6,), t_ss=(NEAR, 3), t_rs=(NEAR, HEAD), dkv_ss=(6, 2), dkv_rs=(6, 2), c_ss=(4,), c_rs=(HEAD,),
        q1_ss=(2,), q1_rs=(2,), q2_ss=(2,), q2_rs=(2,), ag_ss=(3, 3), ag_rs=(3, HEAD), n2_ss=(7,),
        n2_rs=(8,), p1_ss=(2,), p1_rs=(2,), p2_ss=(2, 4), p2_rs=(2, 4), ra_ss=(5, LINE),
        ra_rs=(5, LINE), rh_ss=(5, 2), rh_rs=(5, 2), rb_ss=(5, LINE), rb_rs=(5, LINE), sm_ss=(SEQ,), sm_rs=(SEQ,),
        sm2_ss=(HEAD,), sm2_rs=(HEAD,), up_ss=(SEQ,), up_rs=(SEQ,),
    )
    names = [*ins, *outs, *scratch, *semaphores]
    results = pl.pallas_call(
        functools.partial(fused_kernel, names),
        out_shape=[jax.ShapeDtypeStruct(*o) for o in outs.values()],
        in_specs=[smem] * 3 + [vmem] * (len(ins) - 3),
        out_specs=[vmem] * len(outs),
        scratch_shapes=[pltpu.VMEM(*v) for v in scratch.values()]
        + [pltpu.SemaphoreType.DMA(v) for v in semaphores.values()],
        compiler_params=pltpu.CompilerParams(
            collective_id=0, has_side_effects=True, vmem_limit_bytes=VMEM_BYTES
        ),
        name="fused_layer",
    )(*ins.values())
    large = [(v[0], F32 if k == "xg_o" else v[1]) for k, v in outs.items()][:-1]

    def piece(out):
        shape, axis = list(out[0]), len(out[0]) - 2
        shape[axis] //= PIECES
        return pl.BlockSpec(tuple(shape), lambda i: (0,) * axis + (i, 0))

    handed = pl.pallas_call(
        hand_over_kernel,
        out_shape=[jax.ShapeDtypeStruct(*o) for o in large]
        + [jax.ShapeDtypeStruct((rows,), F32)] * 5
        + [jax.ShapeDtypeStruct((hidden,), F32)],
        grid=(PIECES,),
        in_specs=[piece(o) for o in large] + [vmem],
        out_specs=[piece(o) for o in large] + [vmem] * 6,
        name="hand_over",
    )(*results)
    out, xg, gq, go, gu, gd, g1, b1, g2, b2, b3, upg = handed
    return out, xg, jnp.transpose(gq, (1, 0, 2)), go, g1, b1, g2, b2, gu, upg, gd, b3


def hand_over_kernel(*refs):
    large = (len(refs) - 7) // 2
    small, vectors = refs[large], refs[2 * large + 1 :]
    for k in range(large):
        target = refs[large + 1 + k]
        target[...] = refs[k][...].astype(target.dtype)
    for k in range(5):
        vectors[k][...] = small[k, :]
    for k in range(8):
        vectors[5][pl.ds(k * 128, 128)] = small[8 + k, :]


IN_SPECS = (
    P("seq", None), P("seq", None, "head"), P("head", "seq"), P("seq"), P("seq"), P("seq"),
    P("seq"), P("seq", "head"), P("head"), P("head", "seq"), P("seq"), P(), P(),
    P("seq", "head", None), P("seq", None),
)
OUT_SPECS = (
    P("seq", None), P("seq", None), P("seq", None, "head"), P("head", "seq"), P("seq"), P("seq"),
    P("seq"), P("seq"), P("seq", "head"), P("head"), P("head", "seq"), P("seq"),
)


def solution(mesh):
    fits = mesh.shape["seq"] == SEQ and mesh.shape["head"] == HEAD
    return jax.shard_map(
        local_fused if fits else local_general, mesh=mesh, in_specs=IN_SPECS,
        out_specs=OUT_SPECS, check_vma=False,
    )
```

```python
import functools
import types

import jax
import jax.numpy as jnp
from jax import lax
from jax.experimental import pallas as pl
from jax.experimental.pallas import tpu as pltpu
from jax.sharding import PartitionSpec as P

HEAD_DIM = 64
BLK = 64
SPAN = 4
BLK_DEV = 4
EPSILON = 1e-05
NEGATIVE = -1e30
F32 = jnp.float32
BF16 = jnp.bfloat16


def shifted(value, axis, steps):
    count = lax.axis_size(axis)
    first, last = max(0, -steps), min(count, count - steps)
    return lax.ppermute(value, axis, [(i, i + steps) for i in range(first, last)])


def norm_parts(features):
    average = jnp.mean(features, axis=-1, keepdims=True)
    centred = features - average
    spread = jnp.mean(centred * centred, axis=-1, keepdims=True)
    inverse = lax.rsqrt(spread + EPSILON)
    return centred * inverse, inverse


def norm_backward(xhat, inverse, scaled):
    first = jnp.mean(scaled, axis=-1, keepdims=True)
    second = jnp.mean(scaled * xhat, axis=-1, keepdims=True)
    return inverse * (scaled - first - xhat * second)


def dot(a, b, dims):
    return lax.dot_general(a, b, (dims, ((), ())), preferred_element_type=F32)


def sequence_place(seq_units, seq_pad):
    device = lax.axis_index("seq")
    start, leader, span, pad = 0, 0, 0, 0
    for k in range(seq_units.shape[0]):
        units = seq_units[k]
        inside = (device >= start) & (device < start + units)
        leader = jnp.where(inside, start, leader)
        span = jnp.where(inside, units, span)
        pad = jnp.where(inside, seq_pad[k], pad)
        start = start + units
    return device - leader, span, pad


def key_counts(position, span, picks):
    blocks = lax.broadcasted_iota(jnp.int32, (1, 1, SPAN * BLK_DEV), 2)
    query = position * BLK_DEV + lax.broadcasted_iota(jnp.int32, (BLK_DEV, 1, 1), 0)
    total = span * BLK_DEV
    count = jnp.zeros((BLK_DEV, picks.shape[1], SPAN * BLK_DEV), F32)
    for wanted in (query - 1, query, query + 1, 0, total - 1):
        count = count + (blocks == wanted).astype(F32)
    chosen = picks % total
    for r in range(picks.shape[2]):
        count = count + (blocks == chosen[:, :, r : r + 1]).astype(F32)
    return jnp.where((query == 0) | (query == total - 1), 1.0, count)


def local_general(
    tokens, w_qkv, w_out, ln1_gain, ln1_bias, ln2_gain, ln2_bias, w_up, up_bias, w_down, down_bias,
    seq_units, seq_pad, rand_picks, cotangent,
):
    tok, width = tokens.shape
    heads = w_qkv.shape[2] // HEAD_DIM
    rows = lambda v: lax.all_gather(v, "seq", axis=0, tiled=True)
    cols = lambda v: lax.all_gather(v, "seq", axis=1, tiled=True)
    vectors = jnp.stack([ln1_gain, ln1_bias, ln2_gain, ln2_bias, down_bias], axis=0)
    gain_one, shift_one, gain_two, shift_two, down_shift = [
        v[None].astype(F32) for v in cols(vectors)
    ]
    qkv = rows(w_qkv)
    out_w, up_w, down_w = cols(w_out), rows(w_up), cols(w_down)
    position, span, pad = sequence_place(seq_units, seq_pad)
    root = SPAN - 1 - position
    inputs = tokens.astype(F32)
    xhat_one, inv_one = norm_parts(inputs)
    normed = (xhat_one * gain_one + shift_one).astype(BF16)
    triple = jnp.einsum("td,dcf->tcf", normed, qkv, preferred_element_type=F32).astype(BF16)
    own = jnp.stack([triple[:, 1], triple[:, 2]], axis=0)
    pieces = [own if o == 0 else shifted(own, "seq", -o) for o in range(1 - SPAN, SPAN)]
    nearby = jnp.stack(pieces, axis=0)
    window = lax.dynamic_slice_in_dim(nearby, root, SPAN, 0)
    split = lambda v: v.reshape(v.shape[0], heads, HEAD_DIM)
    keys = split(window[:, 0].reshape(SPAN * tok, -1))
    values = split(window[:, 1].reshape(SPAN * tok, -1))
    queries = split(triple[:, 0])
    scaling = HEAD_DIM ** (-0.5)
    live = jnp.arange(SPAN * tok, dtype=jnp.int32) < span * tok - pad
    count = jnp.repeat(key_counts(position, span, rand_picks), BLK, axis=2)
    count = jnp.where(live[None, None], count, 0.0)
    count = jnp.transpose(jnp.repeat(count, BLK, axis=0), (1, 0, 2))
    logits = jnp.einsum("qhd,khd->hqk", queries, keys, preferred_element_type=F32) * scaling
    logits = jnp.where(count > 0, logits, NEGATIVE)
    grown = jnp.exp(logits - jnp.max(logits, axis=-1, keepdims=True)) * count
    chances = grown / jnp.sum(grown, axis=-1, keepdims=True)
    chances_low = chances.astype(BF16)
    attended = jnp.einsum("hqk,khd->qhd", chances_low, values, preferred_element_type=F32)
    attended = attended.astype(BF16).reshape(tok, heads * HEAD_DIM)
    middle = inputs + lax.psum(dot(attended, out_w, ((1,), (0,))), "head")
    xhat_two, inv_two = norm_parts(middle)
    normed_two = (xhat_two * gain_two + shift_two).astype(BF16)
    pre_act = dot(normed_two, up_w, ((1,), (0,))) + up_bias.astype(F32)[None]
    hidden, pull = jax.vjp(lambda v: jax.nn.gelu(v, approximate=True), pre_act)
    hidden = hidden.astype(BF16)
    ffn = lax.psum(dot(hidden, down_w, ((1,), (0,))).astype(BF16), "head").astype(F32)
    output = (middle + ffn + down_shift).astype(BF16)
    grad_out = cotangent.astype(F32)
    grad_w_down = dot(hidden, cotangent, ((0,), (0,)))
    grad_pre = pull(dot(cotangent, down_w, ((1,), (1,))))[0].astype(BF16)
    grad_w_up = dot(normed_two, grad_pre, ((0,), (0,)))
    grad_up_bias = lax.psum(jnp.sum(grad_pre.astype(F32), axis=0), "seq")
    grad_two = lax.psum(dot(grad_pre, up_w, ((1,), (1,))), "head")
    grad_middle = grad_out + norm_backward(xhat_two, inv_two, grad_two * gain_two)
    grad_branch = grad_middle.astype(BF16)
    grad_w_out = dot(attended, grad_branch, ((0,), (0,)))
    grad_att = split(dot(grad_branch, out_w, ((1,), (1,))).astype(BF16))
    grad_prob = jnp.einsum("qhd,khd->hqk", grad_att, values, preferred_element_type=F32)
    inner = jnp.sum(chances * grad_prob, axis=-1, keepdims=True)
    grad_logit = (chances * (grad_prob - inner)).astype(BF16)
    dq = scaling * jnp.einsum("hqk,khd->qhd", grad_logit, keys, preferred_element_type=F32)
    dk = scaling * jnp.einsum("hqk,qhd->khd", grad_logit, queries, preferred_element_type=F32)
    dv = jnp.einsum("hqk,qhd->khd", chances_low, grad_att, preferred_element_type=F32)
    part = jnp.stack([dk.reshape(SPAN, tok, -1), dv.reshape(SPAN, tok, -1)], axis=1)
    near = jnp.zeros((2 * SPAN - 1,) + part.shape[1:], F32)
    near = lax.dynamic_update_slice_in_dim(near, part, root, 0)
    owned = near[SPAN - 1]
    for offset in range(1 - SPAN, SPAN):
        if offset:
            owned = owned + shifted(near[offset + SPAN - 1], "seq", offset)
    owned = owned.astype(BF16)
    grad_triple = jnp.stack([dq.reshape(tok, -1).astype(BF16), owned[0], owned[1]], axis=1)
    grad_w_qkv = jnp.einsum("td,tcf->dcf", normed, grad_triple, preferred_element_type=F32)
    grad_one = lax.psum(
        jnp.einsum("tcf,dcf->td", grad_triple, qkv, preferred_element_type=F32), "head"
    )
    x_grad = grad_middle + norm_backward(xhat_one, inv_one, grad_one * gain_one)
    sums = jnp.stack(
        [
            jnp.sum(grad_one * xhat_one, axis=0), jnp.sum(grad_one, axis=0),
            jnp.sum(grad_two * xhat_two, axis=0), jnp.sum(grad_two, axis=0),
            jnp.sum(grad_out, axis=0),
        ],
        axis=0,
    )
    scatter = lambda v, d: lax.psum_scatter(v, "seq", scatter_dimension=d, tiled=True)
    sums = scatter(sums, 1)
    return (
        output, x_grad, scatter(grad_w_qkv, 0), scatter(grad_w_out, 1), sums[0], sums[1], sums[2],
        sums[3], scatter(grad_w_up, 0), grad_up_bias, scatter(grad_w_down, 1), sums[4],
    )


MESH = pl.DeviceIdType.MESH
SEQ = 8
HEAD = 4
LINE = 4
NEAR = 2 * SPAN - 1
QKV_KV, QKV_Q, OUT, UP, DOWN = range(5)
VMEM_BYTES = 60 * 1024 * 1024
PIECES = 2


def al(value, multiple):
    return pl.multiple_of(value, multiple)


def fused_kernel(names, *refs):
    r = types.SimpleNamespace(**dict(zip(names, refs)))
    s, h = lax.axis_index("seq"), lax.axis_index("head")
    z, y, x, c = lax.div(s, 2), lax.rem(s, 2), lax.div(h, 2), lax.rem(h, 2)
    e = lax.rem(z, 2)
    pair_z = z + 1 - 2 * e
    mate = z * 2 + 1 - y
    pair = pair_z * 2 + y
    twin = x * 2 + 1 - c
    across = (1 - x) * 2 + c
    tokens, width = r.tok.shape
    quarter = tokens // HEAD
    head_w = r.qs.shape[1]
    rows = r.wq.shape[1]
    half = r.wu_all.shape[1]
    sent = []

    def copy(src, dst, ss, rs, **where):
        return pltpu.make_async_remote_copy(
            src_ref=src, dst_ref=dst, send_sem=ss, recv_sem=rs, device_id=where,
            device_id_type=MESH,
        )

    def when(cond, then):
        if cond is None:
            then()
        else:
            pl.when(cond)(lambda: then())

    def send(cond, *args, **where):
        one = copy(*args, **where)
        when(cond, one.start)
        sent.append((cond, one))

    def arrived(cond, dst, rs, like=None):
        when(cond, copy(dst if like is None else like, dst, r.v_ss.at[0], rs, seq=mate).wait_recv)

    barrier = pltpu.get_barrier_semaphore()
    greeted = [{"seq": lax.rem(s + d, SEQ)} for d in range(1, SEQ)]
    greeted += [{"head": lax.rem(h + d, HEAD)} for d in range(1, HEAD)]
    greeted += [{"seq": pair, "head": across}]
    for where in greeted:
        pl.semaphore_signal(barrier, inc=1, device_id=where, device_id_type=MESH)
    for k, ref in enumerate((r.g1, r.b1, r.g2, r.b2, r.b3)):
        r.vec[k : k + 1, :] = ref[...].reshape(1, rows).astype(F32)
    r.vec[5:8, :] = jnp.zeros((3, rows), F32)
    r.upb_f[...] = r.upb[...].reshape(1, 2 * half).astype(F32)
    pl.semaphore_wait(barrier, len(greeted))

    def cols(o, size):
        return pl.ds(al(o * size, size), size)

    relay_slot = [
        lambda o: r.wq_all.at[1:3, cols(o, rows), :],
        lambda o: r.wq_all.at[0, cols(o, rows), :],
        lambda o: r.wo_all.at[:, cols(o, rows)],
    ]
    relay_src = [r.wq.at[1:3], r.wq.at[0], r.wo]

    def relay_start(w):
        src, dst, rs = relay_src[w], relay_slot[w](s), r.g_rs.at[w, s]
        send(z < LINE - 1, src, dst, r.g_ss.at[w, 0], rs, seq=s + 2)
        send(z > 0, src, dst, r.g_ss.at[w, 4], rs, seq=s - 2)
        send(None, src, dst, r.g_ss.at[w, 8], rs, seq=mate)

    def relay_round(w, k):
        for sign, first, third in ((-1, 0, 8 + k), (1, 4, 11 + k)):
            from_z = z + sign * k
            there = (from_z >= 0) & (from_z < LINE)
            o = jnp.clip(from_z, 0, LINE - 1) * 2 + y
            ref, rs = relay_slot[w](o), r.g_rs.at[w, o]
            arrived(there, ref, rs)
            onward = (z < LINE - 1) if sign < 0 else (z > 0)
            send(there & onward, ref, ref, r.g_ss.at[w, first + k], rs, seq=s - 2 * sign)
            send(there, ref, ref, r.g_ss.at[w, third], rs, seq=mate)

    def relay_finish(w):
        for d in range(LINE):
            o = lax.rem(z + d, LINE) * 2 + 1 - y
            arrived(None, relay_slot[w](o), r.g_rs.at[w, o])

    low, high = z > 0, z < LINE - 1
    from_mate = 4 - 2 * y

    def token_rows(slot, head):
        return r.nall.at[slot, cols(head, quarter), :]

    def token_send(cond, slot, back, k, to):
        send(cond, token_rows(slot, h), token_rows(back, h), r.t_ns.at[k], r.t_rs.at[back, h], seq=to)

    def token_share(cond, slot):
        ref = token_rows(slot, h)
        arrived(cond, ref, r.t_rs.at[slot, h])
        send(cond, ref, ref, r.t_ss.at[slot, 0], r.t_rs.at[slot, h], head=across)
        send(cond, ref, ref, r.t_ss.at[slot, 1], r.t_rs.at[slot, h], head=twin)

    def token_pass(cond, slot):
        ref = token_rows(slot, across)
        arrived(cond, ref, r.t_rs.at[slot, across])
        send(cond, ref, ref, r.t_ss.at[slot, 2], r.t_rs.at[slot, across], head=twin)

    def token_ready(cond, slot):
        arrived(cond, token_rows(slot, twin), r.t_rs.at[slot, twin])
        other = (1 - x) * 2 + 1 - c
        arrived(cond, token_rows(slot, other), r.t_rs.at[slot, other])

    far_in = jnp.where(y == 0, z >= 2, z <= 1)
    far_slot = 6 * y
    slots = (
        (None, from_mate), (low, 1), (high, 5), (low, 2 - 2 * y), (high, 6 - 2 * y),
        (far_in, far_slot),
    )
    for d in range(1, SEQ):
        send(
            None, r.vec, r.gains.at[:, cols(s, rows)], r.v_ss.at[d - 1], r.v_rs.at[s],
            seq=lax.rem(s + d, SEQ),
        )
    relay_start(0)
    r.gains[:, cols(s, rows)] = r.vec[...]
    for k in range(NEAR):
        other = s + k - (SPAN - 1)

        @pl.when((other < 0) | (other >= SEQ))
        def _():
            r.nall[k] = jnp.zeros(r.nall.shape[1:], BF16)

    for k, cond in enumerate((low & high, high, low, high, low)):

        @pl.when(jnp.logical_not(cond))
        def _():
            r.dkv_recv[k] = jnp.zeros(r.dkv_recv.shape[1:], BF16)

    for d in range(1, SEQ):
        o = lax.rem(s + d, SEQ)
        arrived(None, r.gains.at[:, cols(o, rows)], r.v_rs.at[o], r.vec)

    def normalise(q):
        xhat, _ = norm_parts(r.tok[q, :].astype(F32))
        r.nall[SPAN - 1, q, :] = (xhat * r.gains[0:1, :] + r.gains[1:2, :]).astype(BF16)

    normalise(cols(h, quarter))
    token_send(None, SPAN - 1, 2 + 2 * y, 0, mate)
    token_send(high, SPAN - 1, 1, 1, s + 2)
    token_send(low, SPAN - 1, 5, 2, s - 2)
    for d in range(1, HEAD):
        normalise(cols(lax.rem(h + d, HEAD), quarter))
    token_share(*slots[0])
    token_send(high, from_mate, 2 - 2 * y, 3, s + 2)
    token_send(low, from_mate, 6 - 2 * y, 4, s - 2)
    relay_round(0, 1)
    token_share(*slots[1])
    token_share(*slots[2])
    r.wq_all[:, cols(s, rows), :] = r.wq[...]
    r.wo_all[:, cols(s, rows)] = r.wo[...]
    token_share(*slots[3])
    token_share(*slots[4])
    token_send((y == 0) & low & high, 2, 0, 5, s + 2)
    token_send((y == 1) & low & high, 4, 6, 5, s - 2)
    relay_round(0, 2)
    relay_start(1)
    relay_round(0, 3)
    token_share(*slots[5])
    for cond, slot in slots[:3]:
        token_pass(cond, slot)
    relay_round(1, 1)
    relay_start(2)

    start, leader, span, pad = 0, 0, 0, 0
    for k in range(r.units.shape[0]):
        here = r.units[k]
        inside = (s >= start) & (s < start + here)
        leader = jnp.where(inside, start, leader)
        span = jnp.where(inside, here, span)
        pad = jnp.where(inside, r.pads[k], pad)
        start = start + here
    position = s - leader
    root = jnp.clip(SPAN - 1 - position, 0, SPAN - 1)
    total = span * BLK_DEV
    live = span * tokens - pad

    columns = lax.broadcasted_iota(jnp.int32, (1, SPAN * tokens), 1)
    usable = columns < live
    blocks = lax.div(columns, BLK)
    for hh in range(HEAD):
        for b in range(BLK_DEV):
            query = position * BLK_DEV + b
            count = jnp.zeros((1, SPAN * tokens), F32)
            for wanted in (query - 1, query, query + 1, 0, total - 1):
                count = count + jnp.where(blocks == wanted, 1.0, 0.0)
            for k in range(r.picks.shape[0]):
                raw = r.picks[k, b, hh]
                chosen = lax.rem(raw, BLK_DEV)
                for k_units in range(2, SPAN + 1):
                    chosen = jnp.where(span == k_units, lax.rem(raw, BLK_DEV * k_units), chosen)
                count = count + jnp.where(blocks == chosen, 1.0, 0.0)
            count = jnp.where((query == 0) | (query == total - 1), 1.0, count)
            held = usable & (count > 0)
            bias = jnp.log(jnp.maximum(count, 1.0))
            r.bias[hh, b : b + 1, :] = jnp.where(held, bias, NEGATIVE)

    ffn_src = {
        UP: lambda k: r.wu.at[:, cols(k, half)],
        DOWN: lambda k: r.wd.at[cols(k, half), :],
    }
    ffn_slot = {
        UP: lambda o: r.wu_all.at[cols(o, rows), :],
        DOWN: lambda o: r.wd_all.at[:, cols(o, rows)],
    }

    def ffn_start(w):
        i = w - UP
        for d in range(1, LINE):
            to = lax.rem(z + d, LINE)
            send(
                None, ffn_src[w](lax.rem(to, 2)), ffn_slot[w](s), r.f_ss.at[i, d - 1],
                r.f_rs.at[i, s], seq=to * 2 + y,
            )
        send(
            None, ffn_src[w](e), ffn_slot[w](s), r.f_ss.at[i, 3], r.f_rs.at[i, s], seq=mate
        )

    def by_distance(k):
        up = k + jnp.where(z <= k, 1, 0)
        down = k + jnp.where(LINE - 1 - z <= k, 1, 0)
        return jnp.where(z < LINE // 2, up, LINE - 1 - down)

    def ffn_forward(w, ks=(0, 1, 2)):
        i = w - UP
        for k in ks:
            o = by_distance(k) * 2 + y
            ref = ffn_slot[w](o)
            arrived(None, ref, r.f_rs.at[i, o])
            send(None, ref, ref, r.f_ss.at[i, 4 + k], r.f_rs.at[i, o], seq=mate)

    def ffn_finish(w):
        for d in range(LINE):
            o = lax.rem(z + d, LINE) * 2 + 1 - y
            arrived(None, ffn_slot[w](o), r.f_rs.at[w - UP, o])

    relay_round(1, 2)
    relay_round(2, 1)
    relay_round(1, 3)
    relay_round(2, 2)
    ffn_start(UP)
    for cond, slot in slots[3:]:
        token_pass(cond, slot)
    relay_round(2, 3)
    own_copies = [
        pltpu.make_async_copy(ffn_src[UP](e), ffn_slot[UP](s), r.l_s.at[0]),
        pltpu.make_async_copy(ffn_src[DOWN](e), ffn_slot[DOWN](s), r.l_s.at[1]),
        pltpu.make_async_copy(r.cot, r.cotx.at[cols(e, tokens), :], r.l_s.at[2]),
    ]
    for one in own_copies:
        one.start()

    ffn_start(DOWN)
    for cond, slot in slots:
        token_ready(cond, slot)
    relay_finish(0)
    scaling = HEAD_DIM ** (-0.5)
    for j in range(SPAN):
        q = pl.ds(j * tokens, tokens)
        rows_in = r.nall[root + j]
        r.kwin[q, :] = dot(rows_in, r.wq_all[1], ((1,), (0,))).astype(BF16)
        r.vwin[q, :] = dot(rows_in, r.wq_all[2], ((1,), (0,))).astype(BF16)
    relay_finish(1)
    part = dot(r.nall[SPAN - 1], r.wq_all[0], ((1,), (0,)))
    r.qs[...] = (part.astype(BF16).astype(F32) * scaling).astype(BF16)
    beyond = (1 - x) * 2 + 1 - c

    def block_rows(unit, head):
        return pl.ds(al(unit * tokens + head * quarter, quarter), quarter)

    def cot_rows(unit, head):
        return r.cotx.at[block_rows(unit, head), :]

    send(
        None, r.cot.at[cols(h, quarter), :], cot_rows(e, h), r.c_ss.at[0], r.c_rs.at[h], seq=pair
    )

    def cot_share():
        ref = cot_rows(1 - e, h)
        arrived(None, ref, r.c_rs.at[h])
        send(None, ref, ref, r.c_ss.at[1], r.c_rs.at[h], head=across)
        send(None, ref, ref, r.c_ss.at[2], r.c_rs.at[h], head=twin)

    def cot_pass():
        ref = cot_rows(1 - e, across)
        arrived(None, ref, r.c_rs.at[across])
        send(None, ref, ref, r.c_ss.at[3], r.c_rs.at[across], head=twin)

    lanes = lax.div(lax.broadcasted_iota(jnp.int32, (1, head_w), 1), HEAD_DIM)
    none = jnp.zeros((), BF16)
    r.att[...] = jnp.zeros(r.att.shape, F32)

    def attend(hh, carry):
        mine = lanes == hh
        query = jnp.where(mine, r.qs[...], none)
        for j in range(SPAN):
            k = pl.ds(j * tokens, tokens)
            r.lg[:, k] = dot(query, r.kwin[k, :], ((1,), (1,)))
        for b in range(BLK_DEV):
            q = pl.ds(b * BLK, BLK)
            logits = r.lg[q, :] + r.bias[hh, b : b + 1, :]
            grown = jnp.exp(logits - jnp.max(logits, axis=-1, keepdims=True))
            scale = 1.0 / jnp.sum(grown, axis=-1, keepdims=True)
            r.prob[hh, q, :] = (grown * scale).astype(BF16)
        part = dot(r.prob[hh], r.vwin[...], ((1,), (0,)))
        r.att[...] += jnp.where(mine, part, 0.0)
        return carry

    lax.fori_loop(0, HEAD // 2, attend, 0)
    ffn_forward(UP, (0,))
    lax.fori_loop(HEAD // 2, HEAD, attend, 0)
    ffn_forward(UP, (1,))
    r.att_low[...] = r.att[...].astype(BF16)
    relay_finish(2)

    def rows_of(k):
        return cols(k, quarter)

    def reduce_start(op):
        for v in range(2):
            r.q1_send[op, v] = r.sum_f[rows_of(v * 2 + 1 - c), :].astype(BF16)
        send(None, r.q1_send.at[op], r.q1_recv.at[op], r.q1_ss.at[op], r.q1_rs.at[op], head=twin)

    def reduce_middle(op):
        arrived(None, r.q1_recv.at[op], r.q1_rs.at[op])
        block = r.sum_f[rows_of(across), :] + r.q1_recv[op, 1 - x].astype(F32)
        r.q2_send[op] = block.astype(BF16)
        send(None, r.q2_send.at[op], r.q2_recv.at[op], r.q2_ss.at[op], r.q2_rs.at[op], head=across)
        r.q_own[op] = r.sum_f[rows_of(h), :] + r.q1_recv[op, x].astype(F32)

    def reduce_finish(op):
        arrived(None, r.q2_recv.at[op], r.q2_rs.at[op])
        return r.q_own[op] + r.q2_recv[op].astype(F32)

    def spread_start(op, whole, value):
        whole[rows_of(h), :] = value
        ref = whole.at[rows_of(h), :]
        send(None, ref, ref, r.ag_ss.at[op, 0], r.ag_rs.at[op, h], head=across)
        send(None, ref, ref, r.ag_ss.at[op, 1], r.ag_rs.at[op, h], head=twin)

    def spread_pass(op, whole):
        ref = whole.at[rows_of(across), :]
        arrived(None, ref, r.ag_rs.at[op, across])
        send(None, ref, ref, r.ag_ss.at[op, 2], r.ag_rs.at[op, across], head=twin)

    def spread_finish(op, whole):
        for o in (twin, beyond):
            arrived(None, whole.at[rows_of(o), :], r.ag_rs.at[op, o])

    pair_sum = [r.sum_f, r.sum_g]

    def pair_start(op):
        for u in range(2):
            for v in range(2):
                block = pair_sum[op][block_rows(u, v * 2 + 1 - c), :]
                r.p1_send[op, u * 2 + v] = block.astype(BF16)
        send(None, r.p1_send.at[op], r.p1_recv.at[op], r.p1_ss.at[op], r.p1_rs.at[op], head=twin)

    def pair_middle(op):
        arrived(None, r.p1_recv.at[op], r.p1_rs.at[op])
        for du, dv in ((1, 1), (1, 0), (0, 1), (0, 0)):
            u, v = lax.rem(e + du, 2), lax.rem(x + dv, 2)
            block = pair_sum[op][block_rows(u, v * 2 + c), :] + r.p1_recv[op, u * 2 + v].astype(F32)
            if du or dv:
                k = u * 2 + v
                r.p2_send[op, k] = block.astype(BF16)
                send(
                    None, r.p2_send.at[op, k], r.p2_recv.at[op, e * 2 + x], r.p2_ss.at[op, k],
                    r.p2_rs.at[op, e * 2 + x], seq=pair if du else s, head=across if dv else h,
                )
            else:
                r.p_own[op] = block

    def pair_x(op):
        arrived(None, r.p1_recv.at[op], r.p1_rs.at[op])
        for du in (1, 0):
            u = lax.rem(e + du, 2)
            k = u * 2 + 1 - x
            block = pair_sum[op][block_rows(u, across), :] + r.p1_recv[op, k].astype(F32)
            r.p2_send[op, k] = block.astype(BF16)
            send(
                None, r.p2_send.at[op, k], r.p2_recv.at[op, u], r.p2_ss.at[op, k],
                r.p2_rs.at[op, u], head=across,
            )

    def pair_over(op):
        for du in (1, 0):
            u = lax.rem(e + du, 2)
            arrived(None, r.p2_recv.at[op, u], r.p2_rs.at[op, u])
            block = pair_sum[op][block_rows(u, h), :] + r.p1_recv[op, u * 2 + x].astype(F32)
            block = block + r.p2_recv[op, u].astype(F32)
            if du:
                k = u * 2 + x
                r.p2_send[op, k] = block.astype(BF16)
                send(
                    None, r.p2_send.at[op, k], r.p2_recv.at[op, 2], r.p2_ss.at[op, k],
                    r.p2_rs.at[op, 2], seq=pair,
                )
            else:
                r.p_own[op] = block

    def pair_end(op):
        arrived(None, r.p2_recv.at[op, 2], r.p2_rs.at[op, 2])
        return r.p_own[op] + r.p2_recv[op, 2].astype(F32)

    def pair_finish(op):
        result = r.p_own[op]
        for du, dv in ((0, 1), (1, 0), (1, 1)):
            k = lax.rem(e + du, 2) * 2 + lax.rem(x + dv, 2)
            arrived(None, r.p2_recv.at[op, k], r.p2_rs.at[op, k])
            result = result + r.p2_recv[op, k].astype(F32)
        return result

    r.sum_f[:tokens, :] = dot(r.att_low[...], r.wo_all[...], ((1,), (0,)))
    reduce_start(0)
    reduce_middle(0)
    ffn_forward(UP, (2,))
    ffn_forward(DOWN, (0,))
    middle = r.tok[rows_of(h), :].astype(F32) + reduce_finish(0)
    r.mid_own[...] = middle
    xhat, _ = norm_parts(middle)

    def n2_rows(unit, head):
        return r.n2x.at[block_rows(unit, head), :]

    r.n2x[block_rows(e, h), :] = (xhat * r.gains[2:3, :] + r.gains[3:4, :]).astype(BF16)
    mine, tag = n2_rows(e, h), e * 4 + h
    send(None, mine, mine, r.n2_ss.at[0], r.n2_rs.at[tag], seq=pair)
    send(None, mine, mine, r.n2_ss.at[1], r.n2_rs.at[tag], head=across)
    send(None, mine, mine, r.n2_ss.at[2], r.n2_rs.at[tag], head=twin)
    cot_share()
    ffn_forward(DOWN, (1,))
    for k, (unit, head) in enumerate(((e, across), (1 - e, h), (1 - e, across))):
        ref, tag = n2_rows(unit, head), unit * 4 + head
        arrived(None, ref, r.n2_rs.at[tag])
        if k == 1:
            send(None, ref, ref, r.n2_ss.at[6], r.n2_rs.at[tag], head=across)
        send(None, ref, ref, r.n2_ss.at[3 + k], r.n2_rs.at[tag], head=twin)
    cot_pass()
    ffn_forward(DOWN, (2,))
    ffn_finish(UP)
    for unit in (e, 1 - e):
        for head in (x * 2 + 1 - c, (1 - x) * 2 + 1 - c):
            arrived(None, n2_rows(unit, head), r.n2_rs.at[unit * 4 + head])

    for one in own_copies:
        one.wait()
    root_c = (2.0 / 3.141592653589793) ** 0.5
    r.up_send[half // 128 :, :] = jnp.zeros((8 - half // 128, 128), F32)
    for j in range(half // 256):
        f = pl.ds(j * 256, 256)
        bias = r.upb_f[:, pl.ds(al(e * half + j * 256, 256), 256)]
        v = dot(r.n2x[...], r.wu_all[:, f], ((1,), (0,))) + bias
        t = jnp.tanh(root_c * (v + 0.044715 * (v * v * v)))
        r.hid[:, f] = (0.5 * v * (1.0 + t)).astype(BF16)
        slope = 0.5 * (1.0 + t) + 0.5 * v * (1.0 - t * t) * (root_c * (1.0 + 0.134145 * v * v))
        r.slope[:, f] = slope
    ffn_finish(DOWN)
    for head in (twin, beyond):
        arrived(None, cot_rows(1 - e, head), r.c_rs.at[head])
    for j in range(half // 256):
        f = pl.ds(j * 256, 256)
        low_p = (dot(r.cotx[...], r.wd_all[f, :], ((1,), (1,))) * r.slope[:, f]).astype(BF16)
        r.gp[:, f] = low_p
        sums = jnp.sum(low_p.astype(F32), axis=0, keepdims=True)
        r.up_send[2 * j : 2 * j + 1, :] = sums[:, :128]
        r.up_send[2 * j + 1 : 2 * j + 2, :] = sums[:, 128:]

    grad_send = {QKV_KV: r.skv, QKV_Q: r.sq, OUT: r.so, UP: r.su, DOWN: r.sd}
    grad_arrive = {QKV_KV: r.akv, QKV_Q: r.aq, OUT: r.ao, UP: r.au, DOWN: r.ad}
    grad_again = {QKV_KV: r.bkv, QKV_Q: r.bq, OUT: r.bo, UP: r.bu, DOWN: r.bd}
    grad_final = {QKV_KV: r.rkv, QKV_Q: r.rq, OUT: r.ro, UP: r.ru, DOWN: r.rd}

    def tile_of(i):
        return lax.rem(z + 1 + i, LINE)

    def grad_cross(w, zz):
        send(
            None, grad_send[w].at[zz * 2 + 1 - y], grad_arrive[w].at[zz], r.ra_ss.at[w, zz],
            r.ra_rs.at[w, zz], seq=mate,
        )

    def grad_along(w, ks=(1, 2, 3)):
        for d in ks:
            zz = lax.rem(z + d, LINE)
            arrived(None, grad_arrive[w].at[zz], r.ra_rs.at[w, zz])
            both = grad_send[w][zz * 2 + y].astype(F32) + grad_arrive[w][zz].astype(F32)
            grad_again[w][zz] = both.astype(BF16)
            send(
                None, grad_again[w].at[zz], grad_final[w].at[z], r.rb_ss.at[w, zz],
                r.rb_rs.at[w, z], seq=zz * 2 + y,
            )

    outer, inner = (z == 0) | (z == LINE - 1), (z == 1) | (z == LINE - 2)
    far_half = 2 - 2 * lax.div(z, 2)
    far_inner = 2 - lax.div(z, 2)
    grad_hold = {QKV_KV: r.hkv, QKV_Q: r.hq, OUT: r.ho}

    def tile_far(i):
        return (far_half, far_half + 1, pair_z, z)[i]

    def grad_first(w):
        for k in range(3):
            zz = tile_far(k)
            arrived(None, grad_arrive[w].at[zz], r.ra_rs.at[w, zz])
            both = grad_send[w][zz * 2 + y].astype(F32) + grad_arrive[w][zz].astype(F32)
            grad_again[w][zz] = both.astype(BF16)
            if k < 2:
                send(
                    outer, grad_again[w].at[zz], grad_hold[w].at[k], r.rh_ss.at[w, k],
                    r.rh_rs.at[w, k], seq=pair,
                )
            else:
                send(
                    None, grad_again[w].at[zz], grad_final[w].at[z], r.rb_ss.at[w, zz],
                    r.rb_rs.at[w, z], seq=pair,
                )

    def grad_second(w):
        for k in range(2):
            zz = tile_far(k)
            arrived(inner, grad_hold[w].at[k], r.rh_rs.at[w, k])

            @pl.when(inner)
            def _():
                both = grad_again[w][zz].astype(F32) + grad_hold[w][k].astype(F32)
                grad_again[w][zz] = both.astype(BF16)

            send(
                inner, grad_again[w].at[zz], grad_final[w].at[z], r.rb_ss.at[w, zz],
                r.rb_rs.at[w, z], seq=zz * 2 + y,
            )

    def grad_own(w):
        arrived(None, grad_arrive[w].at[z], r.ra_rs.at[w, z])
        return grad_send[w][z * 2 + y].astype(F32) + grad_arrive[w][z].astype(F32)

    def grad_from(w, o):
        arrived(None, grad_final[w].at[o], r.rb_rs.at[w, o])
        return grad_final[w][o].astype(F32)

    def grad_sum(w):
        return grad_own(w) + grad_from(w, pair_z) + grad_from(w, far_inner)

    def grad_halves(w):
        same = grad_own(w) + grad_from(w, lax.rem(z + 2, LINE))
        other = grad_from(w, lax.rem(z + 1, LINE)) + grad_from(w, lax.rem(z + 3, LINE))
        return same, other

    def down_step(i):
        zz = tile_of(i)
        part = dot(r.hid[...], r.cotx[:, cols(zz, 256)], ((0,), (0,))).astype(BF16)
        r.sd[zz * 2] = part[:, :rows]
        r.sd[zz * 2 + 1] = part[:, rows:]
        grad_cross(DOWN, zz)

    def up_step(i):
        zz = tile_of(i)
        part = dot(r.n2x[:, cols(zz, 256)], r.gp[...], ((0,), (0,))).astype(BF16)
        r.su[zz * 2] = part[:rows]
        r.su[zz * 2 + 1] = part[rows:]
        grad_cross(UP, zz)

    down_step(0)
    r.sum_f[...] = dot(r.gp[...], r.wu_all[...], ((1,), (1,)))
    pair_start(0)
    down_step(1)
    pair_middle(0)
    r.sum_g[...] = dot(r.hid[...], r.wd_all[...], ((1,), (0,)))
    pair_start(1)
    down_step(2)
    down_step(3)
    pair_x(1)
    for i in range(LINE):
        up_step(i)
    for d in range(1, SEQ):
        send(
            None, r.up_send, r.up_recv.at[s], r.up_ss.at[d], r.up_rs.at[s],
            seq=lax.rem(s + d, SEQ),
        )

    grad_along(DOWN, (1,))
    grad_two = pair_finish(0)
    xhat, inverse = norm_parts(r.mid_own[...])
    dy = r.cotx[block_rows(e, h), :].astype(F32)
    grad_mid = dy + norm_backward(xhat, inverse, grad_two * r.gains[2:3, :])
    r.gm_own[...] = grad_mid
    spread_start(0, r.gb, grad_mid.astype(BF16))
    r.sm_send[2:3, :] = jnp.sum(grad_two * xhat, axis=0, keepdims=True)
    r.sm_send[3:4, :] = jnp.sum(grad_two, axis=0, keepdims=True)
    r.sm_send[4:5, :] = jnp.sum(dy, axis=0, keepdims=True)
    r.sm_send[5:8, :] = jnp.zeros((3, width), F32)

    grad_along(DOWN, (2, 3))
    pair_over(1)
    spread_pass(0, r.gb)
    spread_finish(0, r.gb)
    r.gatt[...] = dot(r.gb[...], r.wo_all[...], ((1,), (1,))).astype(BF16)
    for i in range(LINE):
        zz = tile_far(i)
        part = dot(r.att_low[...], r.gb[:, cols(zz, 256)], ((0,), (0,))).astype(BF16)
        r.so[zz * 2] = part[:, :rows]
        r.so[zz * 2 + 1] = part[:, rows:]
        grad_cross(OUT, zz)
    grad_along(UP, (1, 2))

    r.dq[...] = jnp.zeros(r.dq.shape, F32)
    r.dk[...] = jnp.zeros(r.dk.shape, F32)
    r.dv[...] = jnp.zeros(r.dv.shape, F32)

    def attend_back(hh, carry):
        mine = lanes == hh
        query = jnp.where(mine, r.qs[...], none)
        grad = jnp.where(mine, r.gatt[...], none)
        for j in range(SPAN):
            k = pl.ds(j * tokens, tokens)
            r.lg[:, k] = dot(grad, r.vwin[k, :], ((1,), (1,)))
        for b in range(BLK_DEV):
            q = pl.ds(b * BLK, BLK)
            chance, grown = r.prob[hh, q, :].astype(F32), r.lg[q, :]
            inner = jnp.sum(chance * grown, axis=-1, keepdims=True)
            r.ds[hh, q, :] = (chance * (grown - inner)).astype(BF16)
        for j in range(SPAN):
            k = pl.ds(j * tokens, tokens)
            r.dk[k, :] += dot(r.ds[hh, :, k], query, ((0,), (0,)))
            r.dv[k, :] += dot(r.prob[hh, :, k], grad, ((0,), (0,)))
        return carry

    lax.fori_loop(0, HEAD, attend_back, 0)
    for k in range(2 * (SPAN - 1) + SPAN):
        j = k - (SPAN - 1)
        if 0 <= j < SPAN:
            q = pl.ds(j * tokens, tokens)
            r.dkv_pad[k, 0] = r.dk[q, :].astype(BF16)
            r.dkv_pad[k, 1] = r.dv[q, :].astype(BF16)
        else:
            r.dkv_pad[k] = jnp.zeros(r.dkv_pad.shape[1:], BF16)
    for k in range(NEAR):
        r.dkv_send[k] = r.dkv_pad[k + SPAN - 1 - root]

    def grad_hop(cond, slot, into, k, to, v):
        send(
            cond, r.dkv_send.at[slot, v], r.dkv_recv.at[into, v], r.dkv_ss.at[k, v],
            r.dkv_rs.at[into, v], seq=to,
        )

    def add_to(v, slot, *froms):
        both = r.dkv_send[slot, v].astype(F32)
        for k in froms:
            both = both + r.dkv_recv[k, v].astype(F32)
        r.dkv_send[slot, v] = both.astype(BF16)

    def grad_wait(cond, into, v):
        arrived(cond, r.dkv_recv.at[into, v], r.dkv_rs.at[into, v])

    FAR, ABOVE, BELOW, LINE_ABOVE, LINE_BELOW, MATE = range(6)
    for v in range(2):
        grad_hop((y == 0) & (z >= 2), 0, FAR, 0, s - 2, v)
        grad_hop((y == 1) & (z <= 1), 6, FAR, 0, s + 2, v)
    for v in range(2):
        grad_hop((y == 0) & high, 6, BELOW, 1, s + 2, v)
        grad_hop((y == 1) & low, 0, ABOVE, 1, s - 2, v)

    def hop_far(v):
        grad_wait(low & high, FAR, v)
        add_to(v, 2 + 2 * y, FAR)
        grad_hop((y == 0) & low, 2, ABOVE, 2, s - 2, v)
        grad_hop((y == 1) & high, 4, BELOW, 2, s + 2, v)

    def hop_line(v):
        grad_hop(low, 1, LINE_ABOVE, 3, s - 2, v)
        grad_hop(high, 5, LINE_BELOW, 4, s + 2, v)

    def hop_mate(v):
        grad_wait(high, ABOVE, v)
        grad_wait(low, BELOW, v)
        add_to(v, from_mate, ABOVE, BELOW)
        grad_hop(None, from_mate, MATE, 5, mate, v)

    def queries_back(hh, carry):
        r.dq[...] += jnp.where(lanes == hh, dot(r.ds[hh], r.kwin[...], ((1,), (0,))), 0.0)
        return carry

    for i in range(LINE):
        zz = tile_far(i)
        for k in range(2):
            part = jnp.zeros((256, head_w), F32)
            for j in range(SPAN):
                part = part + dot(
                    r.nall[root + j, :, cols(zz, 256)], r.dkv_pad[j + SPAN - 1, k], ((0,), (0,))
                )
            part = part.astype(BF16)
            for v in range(2):
                r.skv[zz * 2 + v, k] = part[v * rows : (v + 1) * rows]
        grad_cross(QKV_KV, zz)
        if i == 1:
            hop_far(0)
        if i == 2:
            hop_far(1)
            hop_line(0)
            hop_line(1)
    grad_along(UP, (3,))
    hop_mate(0)
    hop_mate(1)
    grad_first(OUT)
    lax.fori_loop(0, HEAD, queries_back, 0)
    r.gtq[...] = (r.dq[...] * scaling).astype(BF16)
    for i in range(LINE):
        zz = tile_far(i)
        part = dot(r.nall[SPAN - 1, :, cols(zz, 256)], r.gtq[...], ((0,), (0,))).astype(BF16)
        r.sq[zz * 2] = part[:rows]
        r.sq[zz * 2 + 1] = part[rows:]
        grad_cross(QKV_Q, zz)
    grad_second(OUT)
    grad_first(QKV_KV)
    ffn = pair_end(1)
    spread_start(1, r.out_o, (r.mid_own[...] + ffn + r.gains[4:5, :]).astype(BF16))
    for v in range(2):
        grad_wait(high, LINE_ABOVE, v)
        grad_wait(low, LINE_BELOW, v)
        grad_wait(None, MATE, v)
        whole = r.dkv_send[SPAN - 1, v].astype(F32)
        for k in (LINE_ABOVE, LINE_BELOW, MATE):
            whole = whole + r.dkv_recv[k, v].astype(F32)
        r.gtkv[v] = whole.astype(BF16)

    r.sum_f[:tokens, :] = (
        dot(r.gtq[...], r.wq_all[0], ((1,), (1,)))
        + dot(r.gtkv[0], r.wq_all[1], ((1,), (1,)))
        + dot(r.gtkv[1], r.wq_all[2], ((1,), (1,)))
    )
    reduce_start(1)
    reduce_middle(1)
    grad_second(QKV_KV)
    grad_one = reduce_finish(1)
    xhat, inverse = norm_parts(r.tok[rows_of(h), :].astype(F32))
    r.sm_send[0:1, :] = jnp.sum(grad_one * xhat, axis=0, keepdims=True)
    r.sm_send[1:2, :] = jnp.sum(grad_one, axis=0, keepdims=True)
    for d in range(1, SEQ):
        to = lax.rem(s + d, SEQ)
        send(
            None, r.sm_send.at[:, cols(to, rows)], r.sm_recv.at[s], r.sm_ss.at[d], r.sm_rs.at[s],
            seq=to,
        )
    spread_pass(1, r.out_o)
    grad_first(QKV_Q)
    grad_x = r.gm_own[...] + norm_backward(xhat, inverse, grad_one * r.gains[0:1, :])
    spread_start(2, r.xg_o, grad_x.astype(BF16))

    same, other = grad_halves(DOWN)
    r.gd_o[cols(e, half), :] = same
    r.gd_o[cols(1 - e, half), :] = other
    same, other = grad_halves(UP)
    r.gu_o[:, cols(e, half)] = same
    r.gu_o[:, cols(1 - e, half)] = other
    spread_pass(2, r.xg_o)
    grad_second(QKV_Q)
    r.go_o[...] = grad_sum(OUT)

    r.sm_recv[s] = r.sm_send[:, cols(s, rows)]
    r.up_recv[s] = r.up_send[...]
    for d in range(1, SEQ):
        o = lax.rem(s + d, SEQ)
        arrived(None, r.sm_recv.at[o], r.sm_rs.at[o], r.vec)
        arrived(None, r.up_recv.at[o], r.up_rs.at[o])
    part = r.sm_recv[0]
    for o in range(1, SEQ):
        part = part + r.sm_recv[o]
    r.sm_own[...] = part
    for d in range(1, HEAD):
        send(
            None, r.sm_own, r.sm_two.at[h], r.sm2_ss.at[d], r.sm2_rs.at[h],
            head=lax.rem(h + d, HEAD),
        )
    r.sm_two[h] = part
    tall = half // 128
    for u in range(2):
        ups = jnp.zeros((tall, 128), F32)
        for o in range(SEQ):
            if (o // 2) % 2 == u:
                ups = ups + r.up_recv[o, :tall, :]
        r.small_o[8 + u * tall : 8 + (u + 1) * tall, :] = ups
    spread_finish(1, r.out_o)
    spread_finish(2, r.xg_o)
    for d in range(1, HEAD):
        o = lax.rem(h + d, HEAD)
        arrived(None, r.sm_two.at[o], r.sm2_rs.at[o])
    r.small_o[0:8, :] = (r.sm_two[0] + r.sm_two[1]) + (r.sm_two[2] + r.sm_two[3])
    r.gq_o[0] = grad_sum(QKV_Q)
    r.gq_o[1:3] = grad_sum(QKV_KV)

    for cond, one in sent:
        when(cond, one.wait_send)


def local_fused(
    tokens, w_qkv, w_out, ln1_gain, ln1_bias, ln2_gain, ln2_bias, w_up, up_bias, w_down, down_bias,
    seq_units, seq_pad, rand_picks, cotangent,
):
    tok, width = tokens.shape
    rows, _, head_w = w_qkv.shape
    hidden = w_up.shape[1]
    half = hidden // 2
    quarter = tok // HEAD
    keys = SPAN * tok
    smem, vmem = pl.BlockSpec(memory_space=pltpu.SMEM), pl.BlockSpec(memory_space=pltpu.VMEM)
    anywhere = pl.BlockSpec(memory_space=pl.ANY)
    ins = dict(
        units=seq_units, pads=seq_pad, picks=jnp.transpose(rand_picks, (2, 0, 1)), tok=tokens,
        cot=cotangent, wq=jnp.transpose(w_qkv, (1, 0, 2)), wo=w_out, wu=w_up, wd=w_down,
        g1=ln1_gain, b1=ln1_bias, g2=ln2_gain, b2=ln2_bias, b3=down_bias,
        upb=up_bias,
    )
    outs = dict(
        out_o=((tok, width), BF16), xg_o=((tok, width), BF16), gq_o=((3, rows, head_w), F32),
        go_o=((head_w, rows), F32), gu_o=((rows, hidden), F32), gd_o=((hidden, rows), F32),
        small_o=((16, rows), F32),
    )
    scratch = dict(
        wq_all=((3, width, head_w), BF16), wo_all=((head_w, width), BF16),
        wu_all=((width, half), BF16), wd_all=((half, width), BF16), vec=((8, rows), F32), upb_f=((1, hidden), F32),
        gains=((8, width), F32), nall=((NEAR, tok, width), BF16),
        qs=((tok, head_w), BF16),
        kwin=((keys, head_w), BF16), vwin=((keys, head_w), BF16), lg=((tok, keys), F32),
        prob=((HEAD, tok, keys), BF16), ds=((HEAD, tok, keys), BF16),
        att=((tok, head_w), F32), att_low=((tok, head_w), BF16), n2x=((2 * tok, width), BF16),
        cotx=((2 * tok, width), BF16), hid=((2 * tok, half), BF16), slope=((2 * tok, half), F32), gp=((2 * tok, half), BF16),
        gb=((tok, width), BF16), mid_own=((quarter, width), F32),
        gm_own=((quarter, width), F32), gatt=((tok, head_w), BF16), dq=((tok, head_w), F32),
        dk=((keys, head_w), F32), dv=((keys, head_w), F32),
        dkv_pad=((NEAR + SPAN - 1, 2, tok, head_w), BF16),
        dkv_send=((NEAR, 2, tok, head_w), BF16), dkv_recv=((6, 2, tok, head_w), BF16),
        gtq=((tok, head_w), BF16), gtkv=((2, tok, head_w), BF16),
        q1_send=((2, 2, quarter, width), BF16), q1_recv=((2, 2, quarter, width), BF16),
        q2_send=((2, quarter, width), BF16), q2_recv=((2, quarter, width), BF16),
        q_own=((2, quarter, width), F32),
        sum_f=((2 * tok, width), F32), sum_g=((2 * tok, width), F32), bias=((HEAD, 8, keys), F32),
        p1_send=((2, 4, quarter, width), BF16), p1_recv=((2, 4, quarter, width), BF16),
        p2_send=((2, 4, quarter, width), BF16), p2_recv=((2, 4, quarter, width), BF16),
        p_own=((2, quarter, width), F32), sm_send=((8, width), F32),
        sm_recv=((SEQ, 8, rows), F32), sm_own=((8, rows), F32), sm_two=((HEAD, 8, rows), F32),
        up_send=((8, 128), F32), up_recv=((SEQ, 8, 128), F32),
    )
    shards = dict(
        kv=(2, rows, head_w), q=(rows, head_w), o=(head_w, rows), u=(rows, half), d=(half, rows)
    )
    for lead, count in (("s", SEQ), ("a", LINE), ("b", LINE), ("r", LINE), ("h", 2)):
        for name, shape in shards.items():
            scratch[lead + name] = ((count,) + shape, BF16)
    semaphores = dict(
        g_ss=(3, 16), g_rs=(3, SEQ), f_ss=(2, 7), f_rs=(2, SEQ), v_ss=(7,), v_rs=(SEQ,),
        t_ns=(6,), t_ss=(NEAR, 3), t_rs=(NEAR, HEAD), dkv_ss=(6, 2), dkv_rs=(6, 2), l_s=(3,), c_ss=(4,), c_rs=(HEAD,),
        q1_ss=(2,), q1_rs=(2,), q2_ss=(2,), q2_rs=(2,), ag_ss=(3, 3), ag_rs=(3, HEAD), n2_ss=(7,),
        n2_rs=(8,), p1_ss=(2,), p1_rs=(2,), p2_ss=(2, 4), p2_rs=(2, 4), ra_ss=(5, LINE),
        ra_rs=(5, LINE), rh_ss=(5, 2), rh_rs=(5, 2), rb_ss=(5, LINE), rb_rs=(5, LINE), sm_ss=(SEQ,), sm_rs=(SEQ,),
        sm2_ss=(HEAD,), sm2_rs=(HEAD,), up_ss=(SEQ,), up_rs=(SEQ,),
    )
    names = [*ins, *outs, *scratch, *semaphores]
    results = pl.pallas_call(
        functools.partial(fused_kernel, names),
        out_shape=[jax.ShapeDtypeStruct(*o) for o in outs.values()],
        in_specs=[smem] * 3 + [anywhere if k in ("cot", "wu", "wd") else vmem for k in list(ins)[3:]],
        out_specs=[vmem] * len(outs),
        scratch_shapes=[pltpu.VMEM(*v) for v in scratch.values()]
        + [pltpu.SemaphoreType.DMA(v) for v in semaphores.values()],
        compiler_params=pltpu.CompilerParams(
            collective_id=0, has_side_effects=True, vmem_limit_bytes=VMEM_BYTES
        ),
        name="fused_layer",
    )(*ins.values())
    large = [(v[0], F32 if k == "xg_o" else v[1]) for k, v in outs.items()][:-1]

    def piece(out):
        shape, axis = list(out[0]), len(out[0]) - 2
        shape[axis] //= PIECES
        return pl.BlockSpec(tuple(shape), lambda i: (0,) * axis + (i, 0))

    handed = pl.pallas_call(
        hand_over_kernel,
        out_shape=[jax.ShapeDtypeStruct(*o) for o in large]
        + [jax.ShapeDtypeStruct((rows,), F32)] * 5
        + [jax.ShapeDtypeStruct((hidden,), F32)],
        grid=(PIECES,),
        in_specs=[piece(o) for o in large] + [vmem],
        out_specs=[piece(o) for o in large] + [vmem] * 6,
        name="hand_over",
    )(*results)
    out, xg, gq, go, gu, gd, g1, b1, g2, b2, b3, upg = handed
    return out, xg, jnp.transpose(gq, (1, 0, 2)), go, g1, b1, g2, b2, gu, upg, gd, b3


def hand_over_kernel(*refs):
    large = (len(refs) - 7) // 2
    small, vectors = refs[large], refs[2 * large + 1 :]
    for k in range(large):
        target = refs[large + 1 + k]
        target[...] = refs[k][...].astype(target.dtype)
    for k in range(5):
        vectors[k][...] = small[k, :]
    for k in range(8):
        vectors[5][pl.ds(k * 128, 128)] = small[8 + k, :]


IN_SPECS = (
    P("seq", None), P("seq", None, "head"), P("head", "seq"), P("seq"), P("seq"), P("seq"),
    P("seq"), P("seq", "head"), P("head"), P("head", "seq"), P("seq"), P(), P(),
    P("seq", "head", None), P("seq", None),
)
OUT_SPECS = (
    P("seq", None), P("seq", None), P("seq", None, "head"), P("head", "seq"), P("seq"), P("seq"),
    P("seq"), P("seq"), P("seq", "head"), P("head"), P("head", "seq"), P("seq"),
)


def solution(mesh):
    fits = mesh.shape["seq"] == SEQ and mesh.shape["head"] == HEAD
    return jax.shard_map(
        local_fused if fits else local_general, mesh=mesh, in_specs=IN_SPECS,
        out_specs=OUT_SPECS, check_vma=False,
    )
```
